32 devices in a mesh: mode: 8 (over z, y), elem: 4 (over x, core).
Axes of the slice: x: 2, y: 2, z: 4, core: 2. Of those that a mesh axis runs over, the one named last changes fastest.
Arguments:
- velocity: float32 [3, 256, 4, 7, 7, 512], P(None, 'mode', None, None, None, 'elem'), may hold values from -0.3 to 0.3
- radial_dx: float32 [4, 7, 7, 512], P(None, None, None, 'elem'), may hold values from 0.5 to 2
- radial_dy: float32 [4, 7, 7, 512], P(None, None, None, 'elem'), may hold values from -0.5 to 0.5
- around_dx: float32 [4, 7, 7, 512], P(None, None, None, 'elem'), may hold values from -0.5 to 0.5
- around_dy: float32 [4, 7, 7, 512], P(None, None, None, 'elem'), may hold values from 0.5 to 2
- jacobian: float32 [4, 7, 7, 512], P(None, None, None, 'elem'), may hold values from 0.5 to 2
Outputs:
- advection: float32 [3, 256, 4, 7, 7, 512], P(None, 'mode', None, None, None, 'elem')
- pressure: float32 [256, 4, 7, 7, 512], P('mode', None, None, None, 'elem')
The draws below stay inside these ranges and needn't reach their ends.
All inputs are finite; a program needn't handle non-finite values.
Results may differ from the reference program's by a relative error of at most 0.0003.
Values sent between devices are 32-bit elements; how exact they have to be, the bound alone decides.
No kernel may reach another device: no remote copies, remote signals or barrier semaphores. Data moves between devices by JAX's collectives and lax.ppermute only.
A program may use at most 256 MiB of HBM per device.

```python
import math
import jax
import jax.numpy as jnp
import numpy as np
from jax import lax

PLANES = 256
NODES = 7
ER = 4
ITERS = 3
ET = 512


def level_of(stream_key, dims, cuts, low, largest):
    def one(position, blocks):
        heights = jax.random.uniform(jax.random.fold_in(jax.random.fold_in(stream_key, 6), position), (blocks,), jnp.float32, low / len(cuts), largest / len(cuts))
        return jnp.repeat(jnp.exp(heights), dims[position] // blocks).reshape((-1,) + (1,) * (len(dims) - position - 1))

    factor_of = one(*cuts[0])
    for cut in cuts[1:]:
        factor_of = factor_of * one(*cut)
    return factor_of


def bell_draw(stream_key, shape, spread, bound, shards=(), kind=jnp.bfloat16):
    gain = level_of(stream_key, shape, shards, -0.22, 0.18) if shards else 1.0
    values = jax.random.normal(stream_key, shape, jnp.float32) * spread * gain
    return jnp.minimum(jnp.maximum(values, -bound), bound).astype(kind)


def setup_inputs(seed: int = 0) -> dict:
    keys = jax.random.split(jax.random.key(seed), 7)
    velocity = bell_draw(keys[0], (3, PLANES, ER, NODES, NODES, ET), 0.05, 0.3, ((1, 8), (5, 4)), jnp.float32)
    radial_dx = jnp.clip(jnp.exp(math.log(2.0) - 1.3862944 * jax.random.uniform(keys[1], (ER, NODES, NODES, ET), jnp.float32) ** level_of(keys[1], (ER, NODES, NODES, ET), ((3, 4),), -0.2, 0.2)), 0.5, 2.0)
    radial_dy = jnp.clip(jax.random.uniform(keys[2], (ER, NODES, NODES, ET), jnp.float32, -0.5, 0.5) * level_of(keys[2], (ER, NODES, NODES, ET), ((3, 4),), -0.4, 0.0), -0.5, 0.5)
    around_dx = jnp.clip(jax.random.uniform(keys[3], (ER, NODES, NODES, ET), jnp.float32, -0.5, 0.5) * level_of(keys[3], (ER, NODES, NODES, ET), ((3, 4),), -0.4, 0.0), -0.5, 0.5)
    around_dy = jnp.clip(jnp.exp(math.log(2.0) - 1.3862944 * jax.random.uniform(keys[4], (ER, NODES, NODES, ET), jnp.float32) ** level_of(keys[4], (ER, NODES, NODES, ET), ((3, 4),), -0.2, 0.2)), 0.5, 2.0)
    jacobian = jnp.clip(jnp.exp(math.log(2.0) - 1.3862944 * jax.random.uniform(keys[5], (ER, NODES, NODES, ET), jnp.float32) ** level_of(keys[5], (ER, NODES, NODES, ET), ((3, 4),), -0.2, 0.2)), 0.5, 2.0)
    return dict(velocity=velocity, radial_dx=radial_dx, radial_dy=radial_dy, around_dx=around_dx, around_dy=around_dy, jacobian=jacobian)


spanwise_wave = 2.0 * math.pi / 64.0
time_step = 0.1


def lobatto_rule(count):
    degree = count - 1
    points = np.cos(np.pi * np.arange(count) / degree)
    legendre = np.zeros((count, count))
    for sweep in range(60):
        legendre[:, 0] = 1.0
        legendre[:, 1] = points
        for order in range(2, count):
            legendre[:, order] = ((2 * order - 1) * points * legendre[:, order - 1] - (order - 1) * legendre[:, order - 2]) / order
        points = points - (points * legendre[:, degree] - legendre[:, degree - 1]) / (count * legendre[:, degree])
    legendre[:, 0] = 1.0
    legendre[:, 1] = points
    for order in range(2, count):
        legendre[:, order] = ((2 * order - 1) * points * legendre[:, order - 1] - (order - 1) * legendre[:, order - 2]) / order
    weights = 2.0 / (degree * count * legendre[:, degree] ** 2)
    return points[::-1].copy(), weights[::-1].copy()


def derivative_table():
    lobatto_nodes = lobatto_rule(NODES)[0]
    total = lobatto_nodes.shape[0]
    scales = np.ones(total)
    for column in range(total):
        for other in range(total):
            if other != column:
                scales[column] = scales[column] / (lobatto_nodes[column] - lobatto_nodes[other])
    table = np.zeros((total, total))
    for row in range(total):
        for column in range(total):
            if row != column:
                table[row, column] = scales[column] / scales[row] / (lobatto_nodes[row] - lobatto_nodes[column])
        table[row, row] = -np.sum(table[row])
    return table


def radial_derivative(table, field):
    return jnp.einsum('ia,...abe->...ibe', table, field, precision=lax.Precision.HIGHEST)


def around_derivative(table, field):
    return jnp.einsum('jb,...abe->...aje', table, field, precision=lax.Precision.HIGHEST)


def radial_transpose(table, field):
    return jnp.einsum('ia,...ibe->...abe', table, field, precision=lax.Precision.HIGHEST)


def around_transpose(table, field):
    return jnp.einsum('jb,...aje->...abe', table, field, precision=lax.Precision.HIGHEST)


def z_derivative(field, first_pair):
    shape = field.shape
    count = shape[1] // 2
    pairs = field.reshape((shape[0], count, 2) + shape[2:])
    waves = (first_pair + jnp.arange(count, dtype=jnp.int32)).astype(jnp.float32) * spanwise_wave
    waves = waves.reshape((1, count) + (1,) * (len(shape) - 2))
    return jnp.stack([waves * pairs[:, :, 1], -waves * pairs[:, :, 0]], axis=2).reshape(shape)


def to_physical(spec):
    planes = spec.shape[1]
    inner_part = (spec[:, 2::2] - 1j * spec[:, 3::2]) * (0.5 * planes)
    spectrum = jnp.concatenate([spec[:, 0:1] * planes + 0j, inner_part, spec[:, 1:2] * planes + 0j], axis=1)
    return jnp.fft.irfft(spectrum, n=planes, axis=1).astype(spec.dtype)


def to_spectral(values):
    planes = values.shape[1]
    half = planes // 2
    spectrum = jnp.fft.rfft(values, axis=1)
    mean = jnp.real(spectrum[:, 0:1]) / planes
    top = jnp.real(spectrum[:, half:half + 1]) / planes
    cosine = jnp.real(spectrum[:, 1:half]) * (2.0 / planes)
    sine = -jnp.imag(spectrum[:, 1:half]) * (2.0 / planes)
    pairs = jnp.stack([cosine, sine], axis=2).reshape((values.shape[0], planes - 2) + values.shape[2:])
    return jnp.concatenate([mean, top, pairs], axis=1).astype(values.dtype)


def geometry(radial_dx, radial_dy, around_dx, around_dy, jacobian):
    lobatto_weights = lobatto_rule(NODES)[1]
    quadrature = jnp.asarray(np.outer(lobatto_weights, lobatto_weights), jnp.float32)[:, :, None]
    mass = quadrature * jacobian
    radial_stiff = mass * (radial_dx * radial_dx + radial_dy * radial_dy)
    cross_stiff = mass * (radial_dx * around_dx + radial_dy * around_dy)
    around_stiff = mass * (around_dx * around_dx + around_dy * around_dy)
    return radial_stiff, cross_stiff, around_stiff, mass


def node_weights(layers):
    layer = jnp.arange(layers, dtype=jnp.int32).reshape(layers, 1, 1, 1)
    node = jnp.arange(NODES, dtype=jnp.int32)
    radial_node = node.reshape(1, NODES, 1, 1)
    around_node = node.reshape(1, 1, NODES, 1)
    shared_radial = ((radial_node == NODES - 1) & (layer < layers - 1)) | ((radial_node == 0) & (layer > 0))
    shared_around = (around_node == 0) | (around_node == NODES - 1)
    multiplicity = (1.0 + shared_radial.astype(jnp.float32)) * (1.0 + shared_around.astype(jnp.float32))
    boundary = (radial_node == NODES - 1) & (layer == layers - 1)
    mask = 1.0 - boundary.astype(jnp.float32)
    return mask, mask / multiplicity


def plane_shift(first_plane, count, planes):
    plane = first_plane + jnp.arange(count, dtype=jnp.int32)
    order = jnp.where(plane == 1, planes // 2, plane // 2)
    wave = order.astype(jnp.float32) * spanwise_wave
    return (wave * wave).reshape(count, 1, 1, 1, 1)


def helmholtz_local(table, field, shift, metrics):
    radial_stiff, cross_stiff, around_stiff, mass = metrics
    radial = radial_derivative(table, field)
    beside_all = around_derivative(table, field)
    return (radial_transpose(table, radial_stiff * radial + cross_stiff * beside_all)
            + around_transpose(table, cross_stiff * radial + around_stiff * beside_all)
            + shift * mass * field)


def assemble(field):
    lower = field[:, :-1, -1] + field[:, 1:, 0]
    field = field.at[:, :-1, -1].set(lower).at[:, 1:, 0].set(lower)
    right = field[:, :, :, -1] + jnp.roll(field[:, :, :, 0], -1, axis=-1)
    return field.at[:, :, :, -1].set(right).at[:, :, :, 0].set(jnp.roll(right, 1, axis=-1))


def inner(first, second, weight):
    return jnp.sum(first * second * weight, axis=(1, 2, 3, 4))


def expand(scalar):
    return scalar.reshape(-1, 1, 1, 1, 1)


def reference(velocity, radial_dx, radial_dy, around_dx, around_dy, jacobian):
    table = jnp.asarray(derivative_table(), jnp.float32)
    width = ET // 16

    def advect_block(start):
        start = start.astype(jnp.int32)
        block = lax.dynamic_slice_in_dim(velocity, start, width, 5)
        metric = [lax.dynamic_slice_in_dim(item, start, width, 3) for item in (radial_dx, radial_dy, around_dx, around_dy)]
        radial = radial_derivative(table, block)
        beside_all = around_derivative(table, block)
        along_x = metric[0] * radial + metric[2] * beside_all
        along_y = metric[1] * radial + metric[3] * beside_all
        along_z = z_derivative(block, 0)
        speed = to_physical(block)
        slope_x = to_physical(along_x)
        slope_y = to_physical(along_y)
        slope_z = to_physical(along_z)
        product = -(speed[0:1] * slope_x + speed[1:2] * slope_y + speed[2:3] * slope_z)
        return to_spectral(product)

    blocks = lax.map(advect_block, jnp.arange(16, dtype=jnp.int32) * width)
    advection = jnp.moveaxis(blocks, 0, 5).reshape(velocity.shape)

    metrics = geometry(radial_dx, radial_dy, around_dx, around_dy, jacobian)
    mask, weight = node_weights(ER)
    group = 16

    def pressure_group(start):
        start = start.astype(jnp.int32)
        predicted = lax.dynamic_slice_in_dim(velocity, start, group, 1) + time_step * lax.dynamic_slice_in_dim(advection, start, group, 1)
        radial = radial_derivative(table, predicted[0:2])
        beside_all = around_derivative(table, predicted[0:2])
        divergence = (radial_dx * radial[0] + around_dx * beside_all[0]) + (radial_dy * radial[1] + around_dy * beside_all[1]) + z_derivative(predicted[2:3], start // 2)[0]
        shift = plane_shift(start, group, PLANES)
        right_side = mask * assemble(-(metrics[3] * divergence) / time_step)
        solution = jnp.zeros_like(right_side)
        residual = right_side
        direction = right_side
        norm_now = inner(residual, residual, weight)
        for turn in range(ITERS):
            image = mask * assemble(helmholtz_local(table, direction, shift, metrics))
            alpha = norm_now / inner(direction, image, weight)
            solution = solution + expand(alpha) * direction
            residual = residual - expand(alpha) * image
            norm_next = inner(residual, residual, weight)
            direction = residual + expand(norm_next / norm_now) * direction
            norm_now = norm_next
        return solution

    groups = lax.map(pressure_group, jnp.arange(PLANES // group, dtype=jnp.int32) * group)
    pressure = groups.reshape((PLANES,) + velocity.shape[2:])
    return advection, pressure
```

```python
import math

import jax
import jax.numpy as jnp
import numpy as np
from jax import lax
from jax.experimental import pallas as pl
from jax.experimental.pallas import tpu as pltpu
from jax.sharding import PartitionSpec as P

NODES = 7
ITERS = 3


spanwise_wave = 2.0 * math.pi / 64.0
time_step = 0.1


def padded_2(value, sides, width):
    for axis, dim in sides:
        size, length = (lax.axis_size(axis), value.shape[dim])
        up = [(i, (i + 1) % size) for i in range(size)]
        down = [(j, i) for i, j in up]
        last = lax.slice_in_dim(value, length - width, length, axis=dim)
        leading = lax.slice_in_dim(value, 0, width, axis=dim)
        before = lax.ppermute(last, axis, up)
        after = lax.ppermute(leading, axis, down)
        value = jnp.concatenate([before, value, after], axis=dim)
    return value


def lobatto_rule(count):
    degree = count - 1
    points = np.cos(np.pi * np.arange(count) / degree)
    legendre = np.zeros((count, count))
    for sweep in range(60):
        legendre[:, 0] = 1.0
        legendre[:, 1] = points
        for order in range(2, count):
            legendre[:, order] = (
                (2 * order - 1) * points * legendre[:, order - 1]
                - (order - 1) * legendre[:, order - 2]
            ) / order
        points = points - (points * legendre[:, degree] - legendre[:, degree - 1]) / (
            count * legendre[:, degree]
        )
    legendre[:, 0] = 1.0
    legendre[:, 1] = points
    for order in range(2, count):
        legendre[:, order] = (
            (2 * order - 1) * points * legendre[:, order - 1] - (order - 1) * legendre[:, order - 2]
        ) / order
    weights = 2.0 / (degree * count * legendre[:, degree] ** 2)
    return (points[::-1].copy(), weights[::-1].copy())


def derivative_table():
    lobatto_nodes = lobatto_rule(NODES)[0]
    total = lobatto_nodes.shape[0]
    scales = np.ones(total)
    for column in range(total):
        for other in range(total):
            if other != column:
                scales[column] = scales[column] / (lobatto_nodes[column] - lobatto_nodes[other])
    table = np.zeros((total, total))
    for row in range(total):
        for column in range(total):
            if row != column:
                table[row, column] = (
                    scales[column] / scales[row] / (lobatto_nodes[row] - lobatto_nodes[column])
                )
        table[row, row] = -np.sum(table[row])
    return table


def radial_derivative(table, field):
    return jnp.einsum("ia,...abe->...ibe", table, field, precision=lax.Precision.HIGHEST)


def around_derivative(table, field):
    return jnp.einsum("jb,...abe->...aje", table, field, precision=lax.Precision.HIGHEST)


def radial_transpose(table, field):
    return jnp.einsum("ia,...ibe->...abe", table, field, precision=lax.Precision.HIGHEST)


def around_transpose(table, field):
    return jnp.einsum("jb,...aje->...abe", table, field, precision=lax.Precision.HIGHEST)


def z_derivative(field, first_pair):
    shape = field.shape
    count = shape[1] // 2
    pairs = field.reshape((shape[0], count, 2) + shape[2:])
    waves = (first_pair + jnp.arange(count, dtype=jnp.int32)).astype(jnp.float32) * spanwise_wave
    waves = waves.reshape((1, count) + (1,) * (len(shape) - 2))
    return jnp.stack([waves * pairs[:, :, 1], -waves * pairs[:, :, 0]], axis=2).reshape(shape)


def transform_tables(planes):
    position = jnp.arange(planes, dtype=jnp.int32)
    plane = jnp.arange(planes, dtype=jnp.int32)
    order = plane // 2
    turns = position[:, None] * order[None, :] % planes
    angle = 2.0 * math.pi / planes * turns.astype(jnp.float32)
    cosine = jnp.cos(angle)
    sine = jnp.sin(angle)
    is_sine = (plane % 2 == 1)[None, :]
    is_top = (plane == 1)[None, :]
    parity = jnp.cos(math.pi * (position % 2).astype(jnp.float32))[:, None]
    basis = jnp.where(is_top, parity, jnp.where(is_sine, sine, cosine))
    scaling = jnp.where(order == 0, 1.0, 2.0).astype(jnp.float32) / planes
    inverse = jnp.transpose(basis * scaling[None, :])
    wave = (order.astype(jnp.float32) * spanwise_wave)[None, :]
    slope = jnp.where(is_sine, wave * cosine, -wave * sine)
    return (basis, inverse, slope)


def geometry(radial_dx, radial_dy, around_dx, around_dy, jacobian):
    lobatto_weights = lobatto_rule(NODES)[1]
    quadrature = jnp.asarray(np.outer(lobatto_weights, lobatto_weights), jnp.float32)[:, :, None]
    mass = quadrature * jacobian
    radial_stiff = mass * (radial_dx * radial_dx + radial_dy * radial_dy)
    cross_stiff = mass * (radial_dx * around_dx + radial_dy * around_dy)
    around_stiff = mass * (around_dx * around_dx + around_dy * around_dy)
    return (radial_stiff, cross_stiff, around_stiff, mass)


def node_weights(layers):
    layer = jnp.arange(layers, dtype=jnp.int32).reshape(layers, 1, 1, 1)
    node = jnp.arange(NODES, dtype=jnp.int32)
    radial_node = node.reshape(1, NODES, 1, 1)
    around_node = node.reshape(1, 1, NODES, 1)
    shared_radial = (radial_node == NODES - 1) & (layer < layers - 1) | (radial_node == 0) & (
        layer > 0
    )
    shared_around = (around_node == 0) | (around_node == NODES - 1)
    multiplicity = (1.0 + shared_radial.astype(jnp.float32)) * (
        1.0 + shared_around.astype(jnp.float32)
    )
    boundary = (radial_node == NODES - 1) & (layer == layers - 1)
    mask = 1.0 - boundary.astype(jnp.float32)
    return (mask, mask / multiplicity)


def plane_shift(first_plane, count, planes):
    plane = first_plane + jnp.arange(count, dtype=jnp.int32)
    order = jnp.where(plane == 1, planes // 2, plane // 2)
    wave = order.astype(jnp.float32) * spanwise_wave
    return (wave * wave).reshape(count, 1, 1, 1, 1)


def helmholtz_local(table, field, shift, metrics):
    radial_stiff, cross_stiff, around_stiff, mass = metrics
    radial = radial_derivative(table, field)
    beside_all = around_derivative(table, field)
    return (
        radial_transpose(table, radial_stiff * radial + cross_stiff * beside_all)
        + around_transpose(table, cross_stiff * radial + around_stiff * beside_all)
        + shift * mass * field
    )


def assemble(field):
    lower = field[:, :-1, -1] + field[:, 1:, 0]
    field = field.at[:, :-1, -1].set(lower).at[:, 1:, 0].set(lower)
    first = field[:, :, :, 0]
    last = field[:, :, :, -1]
    rims = jnp.concatenate([first[..., :1], last[..., -1:]], axis=3)
    padded = padded_2(rims, (("elem", 3),), 1)
    after = jnp.concatenate([first[..., 1:], padded[..., 3:4]], axis=3)
    right = last + after
    left = jnp.concatenate([padded[..., 0:1] + first[..., :1], right[..., :-1]], axis=3)
    return field.at[:, :, :, -1].set(right).at[:, :, :, 0].set(left)


def inner(first, second, weight):
    return jnp.sum(first * second * weight, axis=(1, 2, 3, 4))


def expand(scalar):
    return scalar.reshape(-1, 1, 1, 1, 1)


def squared_norm(residual, weight):
    return lax.psum(inner(residual, residual, weight), "elem")


def on_device(velocity, radial_dx, radial_dy, around_dx, around_dy, jacobian):
    table = jnp.asarray(derivative_table(), jnp.float32)
    modes = lax.axis_size("mode")
    local_planes = velocity.shape[1]
    planes = local_planes * modes
    first_plane = lax.axis_index("mode") * local_planes
    layers = velocity.shape[2]
    columns = velocity.shape[5]
    basis, inverse, slope = transform_tables(planes)
    radial = radial_derivative(table, velocity)
    beside_all = around_derivative(table, velocity)
    along_x = radial_dx * radial + around_dx * beside_all
    along_y = radial_dy * radial + around_dy * beside_all
    fields = jnp.concatenate([velocity, along_x, along_y], axis=0)
    count = fields.shape[0]
    cells = layers * NODES * NODES * columns
    packed = fields.reshape(count, local_planes, modes, cells // modes)
    flat = lax.all_to_all(packed, "mode", split_axis=2, concat_axis=1, tiled=True)[:, :, 0, :]
    values = jnp.einsum("jp,fpc->fjc", basis, flat, precision=lax.Precision.HIGHEST)
    speed = values[0:3]
    slope_x = values[3:6]
    slope_y = values[6:9]
    slope_z = jnp.einsum("jp,fpc->fjc", slope, flat[0:3], precision=lax.Precision.HIGHEST)
    product = -(speed[0:1] * slope_x + speed[1:2] * slope_y + speed[2:3] * slope_z)
    spectral = jnp.einsum("pj,fjc->fpc", inverse, product, precision=lax.Precision.HIGHEST)
    returned = lax.all_to_all(
        spectral[:, :, None, :], "mode", split_axis=1, concat_axis=2, tiled=True
    )
    advection = returned.reshape(velocity.shape)
    metrics = geometry(radial_dx, radial_dy, around_dx, around_dy, jacobian)
    mask, weight = node_weights(layers)
    predicted = velocity + time_step * advection
    radial = radial_derivative(table, predicted[0:2])
    beside_all = around_derivative(table, predicted[0:2])
    divergence = (
        radial_dx * radial[0]
        + around_dx * beside_all[0]
        + (radial_dy * radial[1] + around_dy * beside_all[1])
        + z_derivative(predicted[2:3], first_plane // 2)[0]
    )
    shift = plane_shift(first_plane, local_planes, planes)
    right_side = mask * assemble(-(metrics[3] * divergence) / time_step)
    solution = jnp.zeros_like(right_side)
    residual = right_side
    direction = right_side
    norm_now = squared_norm(residual, weight)
    for turn in range(ITERS):
        image = mask * assemble(helmholtz_local(table, direction, shift, metrics))
        alpha = norm_now / lax.psum(inner(direction, image, weight), "elem")
        solution = solution + expand(alpha) * direction
        residual = residual - expand(alpha) * image
        norm_next = squared_norm(residual, weight)
        direction = residual + expand(norm_next / norm_now) * direction
        norm_now = norm_next
    return (advection, solution)


def split_bf16(table):
    high = table.astype(jnp.bfloat16)
    low = (table - high.astype(np.float64)).astype(jnp.bfloat16)
    return np.concatenate([high, high, low], axis=1)


def paired_tables(planes):
    half = planes // 2
    position = np.arange(planes)
    plane = np.arange(planes)
    order = plane // 2
    angle = 2.0 * np.pi / planes * (position[:, None] * order[None, :] % planes)
    cosine, sine = (np.cos(angle), np.sin(angle))
    odd = (plane % 2 == 1)[None, :]
    parity = (1.0 - 2.0 * (position % 2))[:, None]
    basis = np.where((plane == 1)[None, :], parity, np.where(odd, sine, cosine))
    wave = (order * spanwise_wave)[None, :]
    slope = np.where(odd, wave * cosine, -wave * sine)
    scaling = np.where(order == 0, 1.0, 2.0) / planes
    inverse = -(basis * scaling[None, :]).T

    def columns(matrix, swap):
        even, other = (matrix[:, 0::2], matrix[:, 1::2])
        return np.concatenate([other, even] if swap else [even, other], axis=1)

    forward = np.concatenate(
        [
            columns(basis[:half], False),
            columns(basis[half:], True),
            columns(slope[:half], False),
            columns(slope[half:], True),
        ]
    )
    top, bottom = (inverse[:, :half], inverse[:, half:])
    backward = np.concatenate(
        [
            np.concatenate([top[0::2], bottom[0::2]], axis=1),
            np.concatenate([bottom[1::2], top[1::2]], axis=1),
        ]
    )
    return (split_bf16(forward), split_bf16(backward))


def apply_line(matrix, line):
    n = NODES
    m = n // 2
    sums = [line[a] + line[n - 1 - a] for a in range(m)]
    gaps = [line[a] - line[n - 1 - a] for a in range(m)]

    def total(parts):
        out = parts[0]
        for part in parts[1:]:
            out = out + part
        return out

    out = [None] * n
    for i in range(m + 1):
        plus = total(
            [float(0.5 * (matrix[i, a] - matrix[i, n - 1 - a])) * gaps[a] for a in range(m)]
        )
        if i == m:
            out[i] = plus
            continue
        minus = total(
            [float(0.5 * (matrix[i, a] + matrix[i, n - 1 - a])) * sums[a] for a in range(m)]
            + [float(matrix[i, m]) * line[m]]
        )
        out[i] = plus + minus
        out[n - 1 - i] = plus - minus
    return out


def lanes_of(shape):
    return lax.broadcasted_iota(jnp.int32, shape, len(shape) - 1)


def row_of(ref, row, rows):
    return ref[pl.ds(row, rows, stride=0), :]


def call(body, grid, ins, outs, out_shape, scratch=(), flops=0, moved=0, limit=None):
    return pl.pallas_call(
        body,
        grid=grid,
        in_specs=ins,
        out_specs=outs,
        out_shape=out_shape,
        scratch_shapes=list(scratch),
        compiler_params=pltpu.CompilerParams(
            dimension_semantics=("arbitrary",) * len(grid), vmem_limit_bytes=limit
        ),
        cost_estimate=pl.CostEstimate(
            flops=int(flops), bytes_accessed=int(moved), transcendentals=0
        ),
    )


def whole(shape):
    return pl.BlockSpec(shape, lambda *_: (0,) * len(shape))


def pack(rows, comp, layers, pairs, lanes):
    square = NODES * NODES
    per_plane = square * layers
    half = lanes // 2

    def body(x_ref, o_ref):
        a = pl.program_id(0)
        low = lanes_of((pairs, lanes)) < half

        def layer(e, carry):
            for b in range(NODES):
                start = (a * NODES + b) * layers + e
                cos = x_ref[0, pl.ds(start, pairs, stride=2 * per_plane), :]
                sin = x_ref[0, pl.ds(start + per_plane, pairs, stride=2 * per_plane), :]
                o_ref[2 * e, b] = jnp.where(low, cos, pltpu.roll(sin, half, 1))
                o_ref[2 * e + 1, b] = jnp.where(low, pltpu.roll(cos, half, 1), sin)
            return carry

        lax.fori_loop(0, layers, layer, 0)

    size = rows.shape[1] * lanes * 4
    return call(
        body,
        (NODES,),
        [pl.BlockSpec((1, rows.shape[1], lanes), lambda a: (comp, 0, 0))],
        pl.BlockSpec((2 * layers, NODES, pairs, lanes), lambda a: (0, a, 0, 0)),
        jax.ShapeDtypeStruct((2 * layers, square, pairs, lanes), jnp.float32),
        moved=2 * size,
    )(rows)


def unpack(blocks):
    shares, square, pairs, lanes = blocks.shape
    layers = shares // 2
    per_plane = square * layers
    half = lanes // 2
    count = 2 * pairs * per_plane

    def body(x_ref, o_ref):
        a = pl.program_id(0)
        low = lanes_of((pairs, lanes)) < half

        def layer(e, carry):
            for b in range(NODES):
                start = (a * NODES + b) * layers + e
                left, right = (x_ref[2 * e, b], x_ref[2 * e + 1, b])
                o_ref[pl.ds(start, pairs, stride=2 * per_plane), :] = jnp.where(
                    low, left, pltpu.roll(right, half, 1)
                )
                o_ref[pl.ds(start + per_plane, pairs, stride=2 * per_plane), :] = jnp.where(
                    low, pltpu.roll(left, half, 1), right
                )
            return carry

        lax.fori_loop(0, layers, layer, 0)

    return call(
        body,
        (NODES,),
        [pl.BlockSpec((shares, NODES, pairs, lanes), lambda a: (0, a, 0, 0))],
        whole((count, lanes)),
        jax.ShapeDtypeStruct((count, lanes), jnp.float32),
        moved=2 * count * lanes * 4,
    )(blocks)


def three_pass(rhs_ref, column, tile, rotated, width):
    both = jnp.concatenate([tile, rotated], axis=0)
    high = both.astype(jnp.bfloat16)
    low = (both - high.astype(jnp.float32)).astype(jnp.bfloat16)
    depth = both.shape[0]
    place = pl.ds(column * width, width)
    rhs_ref[pl.ds(0, depth), place] = high
    rhs_ref[pl.ds(depth, depth), place] = low
    rhs_ref[pl.ds(2 * depth, depth), place] = high


def to_points(blocks, table):
    shares, square, pairs, lanes = blocks.shape
    half = lanes // 2
    rows = shares * pairs

    def body(t_ref, x_ref, v_ref, z_ref, rhs_ref):
        for b in range(NODES):
            tile = x_ref[:, b].reshape(rows, lanes)
            three_pass(rhs_ref, b, tile, pltpu.roll(tile, half, 1), lanes)
        rhs = rhs_ref[...]
        low = lanes_of((rows, lanes)) < half
        for place, out in enumerate((v_ref, z_ref)):
            both = [
                jnp.dot(
                    t_ref[pl.ds((2 * place + part) * rows, rows), :],
                    rhs,
                    preferred_element_type=jnp.float32,
                )
                for part in range(2)
            ]
            for b in range(NODES):
                cut = slice(b * lanes, (b + 1) * lanes)
                out[b] = jnp.where(low, both[0][:, cut], both[1][:, cut])

    spec = pl.BlockSpec((NODES, rows, lanes), lambda a: (a, 0, 0))
    shape = jax.ShapeDtypeStruct((square, rows, lanes), jnp.float32)
    return call(
        body,
        (NODES,),
        [
            whole(table.shape),
            pl.BlockSpec((shares, NODES, pairs, lanes), lambda a: (0, a, 0, 0)),
        ],
        [spec, spec],
        [shape, shape],
        scratch=[pltpu.VMEM((table.shape[1], NODES * lanes), jnp.bfloat16)],
        flops=2 * table.shape[0] * table.shape[1] * square * lanes,
        moved=3 * square * rows * lanes * 4,
    )(table, blocks)


def in_plane(speeds, fields, metrics, table):
    square, rows, lanes = speeds[0].shape
    count = len(fields)
    step = 32
    own = [i for i, f in enumerate(fields) if all(f is not s for s in speeds)]
    arrays = list(speeds) + [fields[i] for i in own]

    def body(m_ref, *refs):
        ins, outs = (refs[: len(arrays)], refs[len(arrays) :])
        u_ref, v_ref = ins[:2]
        sources = []
        extra = 2
        for i, f in enumerate(fields):
            if i in own:
                sources.append(ins[extra])
                extra += 1
            else:
                sources.append(u_ref if f is speeds[0] else v_ref)

        def block(s, carry):
            r = pl.ds(s * 8, 8)

            def metric(kind, n):
                return row_of(m_ref, kind * square + n, 8)

            for a in range(NODES):
                ns = [a * NODES + b for b in range(NODES)]
                drift = [
                    u_ref[n, r] * metric(2, n) + v_ref[n, r] * metric(3, n) for n in ns
                ]
                for f in range(count):
                    beside = apply_line(table, [sources[f][n, r] for n in ns])
                    for b, n in enumerate(ns):
                        outs[f][n, r] = drift[b] * beside[b]
            for b in range(NODES):
                ns = [a * NODES + b for a in range(NODES)]
                drift = [
                    u_ref[n, r] * metric(0, n) + v_ref[n, r] * metric(1, n) for n in ns
                ]
                for f in range(count):
                    radial = apply_line(table, [sources[f][n, r] for n in ns])
                    for a, n in enumerate(ns):
                        outs[f][n, r] = outs[f][n, r] + drift[a] * radial[a]
            return carry

        lax.fori_loop(0, step // 8, block, 0)

    spec = pl.BlockSpec((square, step, lanes), lambda i: (0, i, 0))
    shape = jax.ShapeDtypeStruct((square, rows, lanes), jnp.float32)
    return call(
        body,
        (rows // step,),
        [whole(metrics.shape)] + [spec] * len(arrays),
        [spec] * count,
        [shape] * count,
        flops=30 * count * square * rows * lanes,
        moved=(len(arrays) + count) * square * rows * lanes * 4,
    )(metrics, *arrays)


def to_planes(partial, speed_z, slope_z, table, shares):
    square, rows, lanes = partial.shape
    half = lanes // 2
    pairs = rows // shares

    def body(t_ref, g_ref, w_ref, z_ref, o_ref, rhs_ref):
        for b in range(NODES):
            tile = g_ref[b] + w_ref[b] * z_ref[b]
            three_pass(rhs_ref, b, tile, pltpu.roll(tile, half, 1), lanes)
        rhs = rhs_ref[...]
        low = lanes_of((rows, lanes)) < half
        both = [
            jnp.dot(
                t_ref[pl.ds(part * rows, rows), :], rhs, preferred_element_type=jnp.float32
            )
            for part in range(2)
        ]
        for b in range(NODES):
            cut = slice(b * lanes, (b + 1) * lanes)
            out = jnp.where(low, both[0][:, cut], both[1][:, cut])
            o_ref[:, b] = out.reshape(shares, pairs, lanes)

    spec = pl.BlockSpec((NODES, rows, lanes), lambda a: (a, 0, 0))
    return call(
        body,
        (NODES,),
        [whole(table.shape), spec, spec, spec],
        pl.BlockSpec((shares, NODES, pairs, lanes), lambda a: (0, a, 0, 0)),
        jax.ShapeDtypeStruct((shares, square, pairs, lanes), jnp.float32),
        scratch=[pltpu.VMEM((table.shape[1], NODES * lanes), jnp.bfloat16)],
        flops=2 * table.shape[0] * table.shape[1] * square * lanes,
        moved=4 * square * rows * lanes * 4,
    )(table, partial, speed_z, slope_z)


def plane_divergence(sent, returned, metrics, table):
    shares, square, pairs, lanes = sent[0].shape

    def body(m_ref, s0, r0, s1, r1, o_ref, p0, p1):
        d = pl.program_id(0)

        def block(s, carry):
            r = pl.ds(s * 8, 8)
            for n in range(square):
                p0[n] = s0[0, n, r] + time_step * r0[0, n, r]
                p1[n] = s1[0, n, r] + time_step * r1[0, n, r]

            def metric(kind, n):
                return row_of(m_ref, (kind * shares + d) * square + n, 8)

            for a in range(NODES):
                ns = [a * NODES + b for b in range(NODES)]
                first = apply_line(table, [p0[n] for n in ns])
                second = apply_line(table, [p1[n] for n in ns])
                for b, n in enumerate(ns):
                    o_ref[0, n, r] = metric(2, n) * first[b] + metric(3, n) * second[b]
            for b in range(NODES):
                ns = [a * NODES + b for a in range(NODES)]
                first = apply_line(table, [p0[n] for n in ns])
                second = apply_line(table, [p1[n] for n in ns])
                for a, n in enumerate(ns):
                    o_ref[0, n, r] = o_ref[0, n, r] + (
                        metric(0, n) * first[a] + metric(1, n) * second[a]
                    )
            return carry

        lax.fori_loop(0, pairs // 8, block, 0)

    spec = pl.BlockSpec((1, square, pairs, lanes), lambda d: (d, 0, 0, 0))
    return call(
        body,
        (shares,),
        [whole(metrics.shape)] + [spec] * 4,
        spec,
        jax.ShapeDtypeStruct(sent[0].shape, jnp.float32),
        scratch=[pltpu.VMEM((square, 8, lanes), jnp.float32)] * 2,
        flops=50 * shares * square * pairs * lanes,
        moved=5 * shares * square * pairs * lanes * 4,
    )(metrics, sent[0], returned[0], sent[1], returned[1])


def join_layers(y_ref, layers):
    square = NODES * NODES
    last = (NODES - 1) * NODES
    for e in range(layers - 1):
        for b in range(NODES):
            upper, lower = (e * square + last + b, (e + 1) * square + b)
            total = y_ref[upper] + y_ref[lower]
            y_ref[upper] = total
            y_ref[lower] = total
    for b in range(NODES):
        node = (layers - 1) * square + last + b
        y_ref[node] = jnp.zeros_like(y_ref[node])


def rim_messages(read, layers, shape, partials=()):
    lane = lanes_of(shape)
    lanes = shape[-1]
    first = jnp.zeros(shape, jnp.float32)
    last = jnp.zeros(shape, jnp.float32)
    square = NODES * NODES
    for e in range(layers):
        for a in range(NODES):
            spot = e * NODES + a
            here = lane == spot
            node = e * square + a * NODES
            first = jnp.where(here, pltpu.roll(read(node), spot, 1), first)
            last = jnp.where(here, pltpu.roll(read(node + NODES - 1), (spot + 1) % lanes, 1), last)
    for i, partial in enumerate(partials):
        here = lane == layers * NODES + i
        first = jnp.where(here, partial, first)
        last = jnp.where(here, partial, last)
    return (first, last)


def right_side(flat, sent, returned, weights, waves, layers):
    shares, square, pairs, lanes = flat.shape
    half = lanes // 2

    def body(m_ref, k_ref, f_ref, s_ref, r_ref, o_ref, first_ref, last_ref, c0, c1):
        low = lanes_of((8, lanes)) < half
        wave = k_ref[...]

        def layer(e, carry):
            for n in range(square):
                sides = []
                for h in range(2):
                    d = 2 * e + h
                    moved = s_ref[d, n] + time_step * r_ref[d, n]
                    along = pltpu.roll(moved, half, 1) * wave
                    sides.append(f_ref[d, n] + row_of(m_ref, d * square + n, 8) * along)
                c0[e * square + n] = jnp.where(low, sides[0], pltpu.roll(sides[1], half, 1))
                c1[e * square + n] = jnp.where(low, pltpu.roll(sides[0], half, 1), sides[1])
            return carry

        lax.fori_loop(0, layers, layer, 0)
        for part, buffer in enumerate((c0, c1)):
            join_layers(buffer, layers)
            first, last = rim_messages(lambda n: buffer[n], layers, (8, lanes))
            first_ref[part] = first
            last_ref[part] = last

        def copy(e, carry):
            for n in range(square):
                o_ref[e * square + n, 0] = c0[e * square + n]
                o_ref[e * square + n, 1] = c1[e * square + n]
            return carry

        lax.fori_loop(0, layers, copy, 0)

    spec = pl.BlockSpec((shares, square, 8, lanes), lambda i: (0, 0, i, 0))
    nodes = layers * square
    rim = pl.BlockSpec((2, 8, lanes), lambda i: (0, i, 0))
    rim_shape = jax.ShapeDtypeStruct((2, pairs, lanes), jnp.float32)
    out = call(
        body,
        (pairs // 8,),
        [whole(weights.shape), pl.BlockSpec((8, lanes), lambda i: (i, 0)), spec, spec, spec],
        [pl.BlockSpec((nodes, 2, 8, lanes), lambda i: (0, 0, i, 0)), rim, rim],
        [jax.ShapeDtypeStruct((nodes, 2, pairs, lanes), jnp.float32), rim_shape, rim_shape],
        scratch=[pltpu.VMEM((nodes, 8, lanes), jnp.float32)] * 2,
        flops=10 * shares * square * pairs * lanes,
        moved=4 * shares * square * pairs * lanes * 4,
    )(weights, waves, flat, sent, returned)
    planes = 2 * pairs
    return (
        out[0].reshape(nodes, planes, lanes),
        out[1].reshape(planes, lanes),
        out[2].reshape(planes, lanes),
    )


def swap_rims(first, last):
    size = lax.axis_size("elem")
    up = [(i, (i + 1) % size) for i in range(size)]
    down = [(j, i) for i, j in up]
    return (lax.ppermute(last, "elem", up), lax.ppermute(first, "elem", down))


def opposite(first):
    size = lax.axis_size("elem")
    return lax.ppermute(first, "elem", [(i, (i + 2) % size) for i in range(size)])


def join_columns(read, write, before, after, layers):
    lanes = before.shape[-1]
    lane = lanes_of(before.shape)
    square = NODES * NODES
    for e in range(layers):
        for a in range(NODES):
            spot = e * NODES + a
            node = e * square + a * NODES
            first, last = (read(node), read(node + NODES - 1))
            beyond = pltpu.roll(after, lanes - 1 - spot, 1)
            ahead = jnp.where(lane == lanes - 1, beyond, pltpu.roll(first, lanes - 1, 1))
            right = last + ahead
            mine = first + (pltpu.roll(before, lanes - spot, 1) if spot else before)
            write(node + NODES - 1, right)
            write(node, jnp.where(lane == 0, mine, pltpu.roll(right, 1, 1)))


def share_of(layers, e, a, b):
    value = 1.0
    if b in (0, NODES - 1):
        value = 0.5 * value
    if a == 0:
        value = jnp.where(e > 0, 0.5, 1.0) * value
    if a == NODES - 1:
        value = jnp.where(e < layers - 1, 0.5, 0.0) * value
    return value


def helmholtz(r_ref, y_ref, flux_ref, g_ref, shift, layers, table, dot_only=False):
    square = NODES * NODES
    nodes = layers * square
    rows, lanes = shift.shape
    turned = table.T
    zero = jnp.zeros((rows, lanes), jnp.float32)

    def layer(e, carry):
        norm, energy = carry
        base = e * square

        def metric(kind, n):
            return row_of(g_ref, kind * nodes + base + n, rows)

        for b in range(NODES):
            ns = [a * NODES + b for a in range(NODES)]
            radial = apply_line(table, [r_ref[base + n] for n in ns])
            for a, n in enumerate(ns):
                flux_ref[n] = radial[a]
        for a in range(NODES):
            ns = [a * NODES + b for b in range(NODES)]
            line = [r_ref[base + n] for n in ns]
            beside = apply_line(table, line)
            second = []
            part = zero
            for b, n in enumerate(ns):
                radial = flux_ref[n]
                cross = metric(1, n)
                one = metric(0, n) * radial + cross * beside[b]
                two = cross * radial + metric(2, n) * beside[b]
                held = shift * metric(3, n) * line[b]
                weight = 0.5 if b in (0, NODES - 1) else 1.0
                square_here = line[b] * line[b]
                part = part + (square_here * weight if weight != 1.0 else square_here)
                if dot_only:
                    energy = energy + radial * one + beside[b] * two + held * line[b]
                else:
                    flux_ref[n] = one
                    second.append(two)
                    y_ref[base + n] = held
            norm = norm + part * share_of(layers, e, a, 1)
            if not dot_only:
                back = apply_line(turned, second)
                for b, n in enumerate(ns):
                    y_ref[base + n] = y_ref[base + n] + back[b]
        if not dot_only:
            for b in range(NODES):
                ns = [a * NODES + b for a in range(NODES)]
                back = apply_line(turned, [flux_ref[n] for n in ns])
                for a, n in enumerate(ns):
                    value = y_ref[base + n] + back[a]
                    y_ref[base + n] = value
                    energy = energy + value * r_ref[base + n]
        return (norm, energy)

    norm, energy = lax.fori_loop(0, layers, layer, (zero, zero))
    return (
        jnp.sum(norm, axis=1, keepdims=True),
        jnp.sum(energy, axis=1, keepdims=True),
    )


def lane_value(block, lane):
    return block[:, lane : lane + 1]


def sums_from(own, left, right, far, layers):
    total = (own[...] + far[...]) + (left[...] + right[...])
    spot = layers * NODES
    return (lane_value(total, spot), lane_value(total, spot + 1))


def scalars_block(shape, values):
    lane = lanes_of(shape)
    out = jnp.zeros(shape, jnp.float32)
    for i, value in enumerate(values):
        out = jnp.where(lane == i, value, out)
    return out


def solver_specs(nodes, planes, lanes):
    field = pl.BlockSpec((nodes, 8, lanes), lambda i: (0, i, 0))
    small = pl.BlockSpec((8, lanes), lambda i: (i, 0))
    shapes = (
        jax.ShapeDtypeStruct((nodes, planes, lanes), jnp.float32),
        jax.ShapeDtypeStruct((planes, lanes), jnp.float32),
    )
    return (field, small, shapes)


def first_image(raw, before, after, shift, geo, layers, table):
    nodes, planes, lanes = raw.shape
    field, small, (field_shape, small_shape) = solver_specs(nodes, planes, lanes)

    def body(g_ref, k_ref, f_ref, b_ref, a_ref, r_ref, y_ref, first_ref, last_ref, flux):
        def copy(e, carry):
            for n in range(NODES * NODES):
                r_ref[e * NODES * NODES + n] = f_ref[e * NODES * NODES + n]
            return carry

        lax.fori_loop(0, layers, copy, 0)

        def write(n, value):
            r_ref[n] = value

        join_columns(lambda n: f_ref[n], write, b_ref[...], a_ref[...], layers)
        sums = helmholtz(r_ref, y_ref, flux, g_ref, k_ref[...], layers, table)
        join_layers(y_ref, layers)
        first_ref[...], last_ref[...] = rim_messages(
            lambda n: y_ref[n], layers, (8, lanes), sums
        )

    return call(
        body,
        (planes // 8,),
        [whole(geo.shape), small, field, small, small],
        [field, field, small, small],
        [field_shape, field_shape, small_shape, small_shape],
        scratch=[pltpu.VMEM((NODES * NODES, 8, lanes), jnp.float32)],
        flops=80 * nodes * planes * lanes,
        moved=3 * nodes * planes * lanes * 4,
    )(geo, shift, raw, before, after)


def second_image(start, image, messages, shift, geo, layers, table):
    nodes, planes, lanes = start.shape
    field, small, (field_shape, small_shape) = solver_specs(nodes, planes, lanes)

    def body(g_ref, k_ref, r0, y0, own, left, right, far, *rest):
        w_ref, y_ref, first_ref, last_ref, scalar_ref, r1, flux = rest
        norm, energy = sums_from(own, left, right, far, layers)
        alpha = jnp.broadcast_to(norm / energy, (8, lanes))

        def move(e, carry):
            for n in range(NODES * NODES):
                node = e * NODES * NODES + n
                w = y0[node]
                w_ref[node] = w
                r1[node] = r0[node] - alpha * w
            return carry

        lax.fori_loop(0, layers, move, 0)

        def write(n, value):
            w_ref[n] = value
            r1[n] = r0[n] - alpha * value

        join_columns(lambda n: y0[n], write, left[...], right[...], layers)
        sums = helmholtz(r1, y_ref, flux, g_ref, k_ref[...], layers, table)
        join_layers(y_ref, layers)
        first_ref[...], last_ref[...] = rim_messages(
            lambda n: y_ref[n], layers, (8, lanes), sums
        )
        scalar_ref[...] = scalars_block((8, lanes), (alpha, norm, energy))

    return call(
        body,
        (planes // 8,),
        [whole(geo.shape), small, field, field] + [small] * 4,
        [field, field, small, small, small],
        [field_shape, field_shape, small_shape, small_shape, small_shape],
        scratch=[
            pltpu.VMEM((nodes, 8, lanes), jnp.float32),
            pltpu.VMEM((NODES * NODES, 8, lanes), jnp.float32),
        ],
        flops=80 * nodes * planes * lanes,
        moved=4 * nodes * planes * lanes * 4,
    )(geo, shift, start, image, *messages)


def third_energy(start, joined, image, messages, scalars, shift, geo, layers, table):
    nodes, planes, lanes = start.shape
    field, small, (field_shape, small_shape) = solver_specs(nodes, planes, lanes)

    def body(g_ref, k_ref, r0, w0, y1, own, left, right, far, old, *rest):
        r2, d2, sums_ref, scalar_ref, flux = rest
        norm, energy = sums_from(own, left, right, far, layers)
        before = old[...]
        alpha = jnp.broadcast_to(lane_value(before, 0), (8, lanes))
        ratio = norm / lane_value(before, 1)
        curve = energy - ratio * ratio * lane_value(before, 2)
        step = jnp.broadcast_to(norm / curve, (8, lanes))
        beta = jnp.broadcast_to(ratio, (8, lanes))

        def at(node, image_value):
            w = w0[node]
            start_value = r0[node]
            moved = start_value - alpha * w
            d2[node] = moved + beta * start_value
            r2[node] = moved - step * (image_value + beta * w)

        def move(e, carry):
            for n in range(NODES * NODES):
                at(e * NODES * NODES + n, y1[e * NODES * NODES + n])
            return carry

        lax.fori_loop(0, layers, move, 0)
        join_columns(lambda n: y1[n], at, left[...], right[...], layers)
        sums = helmholtz(r2, None, flux, g_ref, k_ref[...], layers, table, dot_only=True)
        lane = lanes_of((8, lanes))
        spot = layers * NODES
        sums_ref[...] = jnp.where(lane == spot, sums[0], jnp.where(lane == spot + 1, sums[1], 0.0))
        scalar_ref[...] = scalars_block((8, lanes), (alpha, norm, curve, step))

    return call(
        body,
        (planes // 8,),
        [whole(geo.shape), small, field, field, field] + [small] * 5,
        [field, field, small, small],
        [field_shape, field_shape, small_shape, small_shape],
        scratch=[pltpu.VMEM((NODES * NODES, 8, lanes), jnp.float32)],
        flops=60 * nodes * planes * lanes,
        moved=5 * nodes * planes * lanes * 4,
    )(geo, shift, start, joined, image, *messages, scalars)


def finish(start, direction, residual, messages, scalars, layers):
    nodes, planes, lanes = start.shape
    square = NODES * NODES
    per_plane = nodes
    pairs = planes // 2
    field, small, _ = solver_specs(nodes, planes, lanes)

    def body(r0, d2, r2, own, left, right, far, old, o_ref):
        i = pl.program_id(0)
        norm, energy = sums_from(own, left, right, far, layers)
        before = old[...]
        ratio = norm / lane_value(before, 1)
        curve = energy - ratio * ratio * lane_value(before, 2)
        step = norm / curve
        third = jnp.broadcast_to(step, (8, lanes))
        second = jnp.broadcast_to(lane_value(before, 3) + step * ratio, (8, lanes))
        first = jnp.broadcast_to(lane_value(before, 0), (8, lanes))
        row = i * 8
        plane = jnp.where(row < pairs, 2 * row, 2 * (row - pairs) + 1)

        def layer(e, carry):
            for n in range(square):
                node = e * square + n
                value = first * r0[node] + second * d2[node] + third * r2[node]
                o_ref[pl.ds(plane * per_plane + n * layers + e, 8, stride=2 * per_plane), :] = value
            return carry

        lax.fori_loop(0, layers, layer, 0)

    return call(
        body,
        (planes // 8,),
        [field] * 3 + [small] * 5,
        whole((planes * nodes, lanes)),
        jax.ShapeDtypeStruct((planes * nodes, lanes), jnp.float32),
        flops=6 * nodes * planes * lanes,
        moved=4 * nodes * planes * lanes * 4,
    )(start, direction, residual, *messages, scalars)


def halves(values, shares):
    half = values.shape[-1] // 2
    parts = [jnp.concatenate([p, p], axis=-1) for p in (values[..., :half], values[..., half:])]
    return jnp.stack(parts, axis=2).reshape(values.shape[0], shares, NODES * NODES, 2 * half)


def on_device_paired(velocity, radial_dx, radial_dy, around_dx, around_dy, jacobian):
    table = derivative_table()
    modes = lax.axis_size("mode")
    mode = lax.axis_index("mode")
    _, local_planes, layers, _, _, lanes = velocity.shape
    planes = local_planes * modes
    pairs = local_planes // 2
    first_plane = mode * local_planes
    square = NODES * NODES
    forward, backward = (jnp.asarray(t) for t in paired_tables(planes))

    rows = velocity.transpose(0, 1, 3, 4, 2, 5).reshape(3, local_planes * square * layers, lanes)
    plain = jnp.stack([radial_dx, radial_dy, around_dx, around_dy]).reshape(
        4, layers, square, lanes
    )
    both = halves(plain, modes)
    here = lax.dynamic_index_in_dim(both, mode, 1, keepdims=False).reshape(4 * square, lanes)
    metrics = geometry(radial_dx, radial_dy, around_dx, around_dy, jacobian)
    geo = jnp.stack(metrics).reshape(4 * layers * square, lanes)
    scaled = halves((metrics[3] * (-1.0 / time_step)).reshape(1, layers, square, lanes), modes)
    flux = (both * scaled).reshape(4 * modes * square, lanes)
    scaled = scaled.reshape(modes * square, lanes)
    pair = (first_plane // 2 + jnp.arange(pairs, dtype=jnp.int32)).astype(jnp.float32)
    wave = pair[:, None] * spanwise_wave
    low = (jnp.arange(lanes) < lanes // 2)[None, :]
    waves = jnp.where(low, wave, -wave)
    shift = plane_shift(first_plane, local_planes, planes).reshape(pairs, 2).T.reshape(-1, 1)
    shift = jnp.broadcast_to(shift, (local_planes, lanes))

    def exchange(blocks):
        return lax.all_to_all(blocks, "mode", split_axis=0, concat_axis=0, tiled=True)

    sent = []
    points = []
    for comp in range(3):
        sent.append(pack(rows, comp, layers, pairs, lanes))
    for comp in range(3):
        points.append(to_points(exchange(sent[comp]), forward))
    speeds = [p[0] for p in points]
    early = in_plane(speeds[:2], speeds[:2], here, table)
    late = in_plane(speeds[:2], speeds[2:], here, table)
    partial = list(early) + list(late)
    returned = []
    for comp in range(3):
        blocks = to_planes(partial[comp], speeds[2], points[comp][1], backward, modes)
        returned.append(exchange(blocks))
    advection = jnp.stack([unpack(r) for r in returned])
    advection = advection.reshape(3, local_planes, NODES, NODES, layers, lanes)
    advection = advection.transpose(0, 1, 4, 2, 3, 5)

    flat = plane_divergence(sent, returned, flux, table)
    raw, first, last = right_side(flat, sent[2], returned[2], scaled, waves, layers)
    before, after = swap_rims(first, last)
    start, image, first, last = first_image(raw, before, after, shift, geo, layers, table)
    messages = (first,) + swap_rims(first, last) + (opposite(first),)
    joined, image, first, last, scalars = second_image(
        start, image, messages, shift, geo, layers, table
    )
    messages = (first,) + swap_rims(first, last) + (opposite(first),)
    residual, direction, sums, scalars = third_energy(
        start, joined, image, messages, scalars, shift, geo, layers, table
    )
    messages = (sums,) + swap_rims(sums, sums) + (opposite(sums),)
    pressure = finish(start, direction, residual, messages, scalars, layers)
    pressure = pressure.reshape(local_planes, NODES, NODES, layers, lanes)
    return (advection, pressure.transpose(0, 3, 1, 2, 4))


def paired_fits(mesh, shape):
    modes, ring = (mesh.shape["mode"], mesh.shape["elem"])
    _, planes, layers, _, _, columns = shape
    return (
        ring == 4
        and columns == 128 * ring
        and modes == 2 * layers
        and planes % (16 * modes) == 0
        and planes == 2 * 128
        and (layers * NODES + 2 <= 128)
    )


def solution(mesh):
    placed = (
        P(None, "mode", None, None, None, "elem"),
        P(None, None, None, "elem"),
        P(None, None, None, "elem"),
        P(None, None, None, "elem"),
        P(None, None, None, "elem"),
        P(None, None, None, "elem"),
    )

    def step(velocity, *rest):
        body = on_device_paired if paired_fits(mesh, velocity.shape) else on_device
        return jax.shard_map(
            body,
            mesh=mesh,
            in_specs=placed,
            out_specs=(
                P(None, "mode", None, None, None, "elem"),
                P("mode", None, None, None, "elem"),
            ),
            check_vma=False,
        )(velocity, *rest)

    return step
```

```python
import math

import jax
import jax.numpy as jnp
import numpy as np
from jax import lax
from jax.experimental import pallas as pl
from jax.experimental.pallas import tpu as pltpu
from jax.sharding import PartitionSpec as P

NODES = 7
ITERS = 3


spanwise_wave = 2.0 * math.pi / 64.0
time_step = 0.1


def padded_2(value, sides, width):
    for axis, dim in sides:
        size, length = (lax.axis_size(axis), value.shape[dim])
        up = [(i, (i + 1) % size) for i in range(size)]
        down = [(j, i) for i, j in up]
        last = lax.slice_in_dim(value, length - width, length, axis=dim)
        leading = lax.slice_in_dim(value, 0, width, axis=dim)
        before = lax.ppermute(last, axis, up)
        after = lax.ppermute(leading, axis, down)
        value = jnp.concatenate([before, value, after], axis=dim)
    return value


def lobatto_rule(count):
    degree = count - 1
    points = np.cos(np.pi * np.arange(count) / degree)
    legendre = np.zeros((count, count))
    for _ in range(60):
        legendre[:, 0] = 1.0
        legendre[:, 1] = points
        for order in range(2, count):
            legendre[:, order] = (
                (2 * order - 1) * points * legendre[:, order - 1]
                - (order - 1) * legendre[:, order - 2]
            ) / order
        points = points - (points * legendre[:, degree] - legendre[:, degree - 1]) / (
            count * legendre[:, degree]
        )
    legendre[:, 0] = 1.0
    legendre[:, 1] = points
    for order in range(2, count):
        legendre[:, order] = (
            (2 * order - 1) * points * legendre[:, order - 1] - (order - 1) * legendre[:, order - 2]
        ) / order
    weights = 2.0 / (degree * count * legendre[:, degree] ** 2)
    return (points[::-1].copy(), weights[::-1].copy())


def derivative_table():
    lobatto_nodes = lobatto_rule(NODES)[0]
    total = lobatto_nodes.shape[0]
    scales = np.ones(total)
    for column in range(total):
        for other in range(total):
            if other != column:
                scales[column] = scales[column] / (lobatto_nodes[column] - lobatto_nodes[other])
    table = np.zeros((total, total))
    for row in range(total):
        for column in range(total):
            if row != column:
                table[row, column] = (
                    scales[column] / scales[row] / (lobatto_nodes[row] - lobatto_nodes[column])
                )
        table[row, row] = -np.sum(table[row])
    return table


def radial_derivative(table, field):
    return jnp.einsum("ia,...abe->...ibe", table, field, precision=lax.Precision.HIGHEST)


def around_derivative(table, field):
    return jnp.einsum("jb,...abe->...aje", table, field, precision=lax.Precision.HIGHEST)


def radial_transpose(table, field):
    return jnp.einsum("ia,...ibe->...abe", table, field, precision=lax.Precision.HIGHEST)


def around_transpose(table, field):
    return jnp.einsum("jb,...aje->...abe", table, field, precision=lax.Precision.HIGHEST)


def z_derivative(field, first_pair):
    shape = field.shape
    count = shape[1] // 2
    pairs = field.reshape((shape[0], count, 2) + shape[2:])
    waves = (first_pair + jnp.arange(count, dtype=jnp.int32)).astype(jnp.float32) * spanwise_wave
    waves = waves.reshape((1, count) + (1,) * (len(shape) - 2))
    return jnp.stack([waves * pairs[:, :, 1], -waves * pairs[:, :, 0]], axis=2).reshape(shape)


def transform_tables(planes):
    position = jnp.arange(planes, dtype=jnp.int32)
    plane = jnp.arange(planes, dtype=jnp.int32)
    order = plane // 2
    turns = position[:, None] * order[None, :] % planes
    angle = 2.0 * math.pi / planes * turns.astype(jnp.float32)
    cosine = jnp.cos(angle)
    sine = jnp.sin(angle)
    is_sine = (plane % 2 == 1)[None, :]
    is_top = (plane == 1)[None, :]
    parity = jnp.cos(math.pi * (position % 2).astype(jnp.float32))[:, None]
    basis = jnp.where(is_top, parity, jnp.where(is_sine, sine, cosine))
    scaling = jnp.where(order == 0, 1.0, 2.0).astype(jnp.float32) / planes
    inverse = jnp.transpose(basis * scaling[None, :])
    wave = (order.astype(jnp.float32) * spanwise_wave)[None, :]
    slope = jnp.where(is_sine, wave * cosine, -wave * sine)
    return (basis, inverse, slope)


def geometry(radial_dx, radial_dy, around_dx, around_dy, jacobian):
    lobatto_weights = lobatto_rule(NODES)[1]
    quadrature = jnp.asarray(np.outer(lobatto_weights, lobatto_weights), jnp.float32)[:, :, None]
    mass = quadrature * jacobian
    radial_stiff = mass * (radial_dx * radial_dx + radial_dy * radial_dy)
    cross_stiff = mass * (radial_dx * around_dx + radial_dy * around_dy)
    around_stiff = mass * (around_dx * around_dx + around_dy * around_dy)
    return (radial_stiff, cross_stiff, around_stiff, mass)


def node_weights(layers):
    layer = jnp.arange(layers, dtype=jnp.int32).reshape(layers, 1, 1, 1)
    node = jnp.arange(NODES, dtype=jnp.int32)
    radial_node = node.reshape(1, NODES, 1, 1)
    around_node = node.reshape(1, 1, NODES, 1)
    shared_radial = (radial_node == NODES - 1) & (layer < layers - 1) | (radial_node == 0) & (
        layer > 0
    )
    shared_around = (around_node == 0) | (around_node == NODES - 1)
    multiplicity = (1.0 + shared_radial.astype(jnp.float32)) * (
        1.0 + shared_around.astype(jnp.float32)
    )
    boundary = (radial_node == NODES - 1) & (layer == layers - 1)
    mask = 1.0 - boundary.astype(jnp.float32)
    return (mask, mask / multiplicity)


def plane_shift(first_plane, count, planes):
    plane = first_plane + jnp.arange(count, dtype=jnp.int32)
    order = jnp.where(plane == 1, planes // 2, plane // 2)
    wave = order.astype(jnp.float32) * spanwise_wave
    return (wave * wave).reshape(count, 1, 1, 1, 1)


def helmholtz_local(table, field, shift, metrics):
    radial_stiff, cross_stiff, around_stiff, mass = metrics
    radial = radial_derivative(table, field)
    beside_all = around_derivative(table, field)
    return (
        radial_transpose(table, radial_stiff * radial + cross_stiff * beside_all)
        + around_transpose(table, cross_stiff * radial + around_stiff * beside_all)
        + shift * mass * field
    )


def assemble(field):
    lower = field[:, :-1, -1] + field[:, 1:, 0]
    field = field.at[:, :-1, -1].set(lower).at[:, 1:, 0].set(lower)
    first = field[:, :, :, 0]
    last = field[:, :, :, -1]
    rims = jnp.concatenate([first[..., :1], last[..., -1:]], axis=3)
    padded = padded_2(rims, (("elem", 3),), 1)
    after = jnp.concatenate([first[..., 1:], padded[..., 3:4]], axis=3)
    right = last + after
    left = jnp.concatenate([padded[..., 0:1] + first[..., :1], right[..., :-1]], axis=3)
    return field.at[:, :, :, -1].set(right).at[:, :, :, 0].set(left)


def inner(first, second, weight):
    return jnp.sum(first * second * weight, axis=(1, 2, 3, 4))


def expand(scalar):
    return scalar.reshape(-1, 1, 1, 1, 1)


def squared_norm(residual, weight):
    return lax.psum(inner(residual, residual, weight), "elem")


def on_device(velocity, radial_dx, radial_dy, around_dx, around_dy, jacobian):
    table = jnp.asarray(derivative_table(), jnp.float32)
    modes = lax.axis_size("mode")
    local_planes = velocity.shape[1]
    planes = local_planes * modes
    first_plane = lax.axis_index("mode") * local_planes
    layers = velocity.shape[2]
    columns = velocity.shape[5]
    basis, inverse, slope = transform_tables(planes)
    radial = radial_derivative(table, velocity)
    beside_all = around_derivative(table, velocity)
    along_x = radial_dx * radial + around_dx * beside_all
    along_y = radial_dy * radial + around_dy * beside_all
    fields = jnp.concatenate([velocity, along_x, along_y], axis=0)
    count = fields.shape[0]
    cells = layers * NODES * NODES * columns
    packed = fields.reshape(count, local_planes, modes, cells // modes)
    flat = lax.all_to_all(packed, "mode", split_axis=2, concat_axis=1, tiled=True)[:, :, 0, :]
    values = jnp.einsum("jp,fpc->fjc", basis, flat, precision=lax.Precision.HIGHEST)
    speed = values[0:3]
    slope_x = values[3:6]
    slope_y = values[6:9]
    slope_z = jnp.einsum("jp,fpc->fjc", slope, flat[0:3], precision=lax.Precision.HIGHEST)
    product = -(speed[0:1] * slope_x + speed[1:2] * slope_y + speed[2:3] * slope_z)
    spectral = jnp.einsum("pj,fjc->fpc", inverse, product, precision=lax.Precision.HIGHEST)
    returned = lax.all_to_all(
        spectral[:, :, None, :], "mode", split_axis=1, concat_axis=2, tiled=True
    )
    advection = returned.reshape(velocity.shape)
    metrics = geometry(radial_dx, radial_dy, around_dx, around_dy, jacobian)
    mask, weight = node_weights(layers)
    predicted = velocity + time_step * advection
    radial = radial_derivative(table, predicted[0:2])
    beside_all = around_derivative(table, predicted[0:2])
    divergence = (
        radial_dx * radial[0]
        + around_dx * beside_all[0]
        + (radial_dy * radial[1] + around_dy * beside_all[1])
        + z_derivative(predicted[2:3], first_plane // 2)[0]
    )
    shift = plane_shift(first_plane, local_planes, planes)
    right_side = mask * assemble(-(metrics[3] * divergence) / time_step)
    solution = jnp.zeros_like(right_side)
    residual = right_side
    direction = right_side
    norm_now = squared_norm(residual, weight)
    for _ in range(ITERS):
        image = mask * assemble(helmholtz_local(table, direction, shift, metrics))
        alpha = norm_now / lax.psum(inner(direction, image, weight), "elem")
        solution = solution + expand(alpha) * direction
        residual = residual - expand(alpha) * image
        norm_next = squared_norm(residual, weight)
        direction = residual + expand(norm_next / norm_now) * direction
        norm_now = norm_next
    return (advection, solution)


def split_bf16(table):
    high = table.astype(jnp.bfloat16)
    low = (table - high.astype(np.float64)).astype(jnp.bfloat16)
    return np.concatenate([high, high, low], axis=1)


def paired_tables(planes):
    position = np.arange(planes)
    plane = np.arange(planes)
    order = plane // 2
    angle = 2.0 * np.pi / planes * (position[:, None] * order[None, :] % planes)
    cosine, sine = (np.cos(angle), np.sin(angle))
    odd = (plane % 2 == 1)[None, :]
    parity = (1.0 - 2.0 * (position % 2))[:, None]
    basis = np.where((plane == 1)[None, :], parity, np.where(odd, sine, cosine))
    wave = (order * spanwise_wave)[None, :]
    slope = np.where(odd, wave * cosine, -wave * sine)
    scaling = np.where(order == 0, 1.0, 2.0) / planes
    inverse = -(basis * scaling[None, :]).T

    def columns(matrix):
        return np.concatenate([matrix[:, 0::2], matrix[:, 1::2]], axis=1)

    forward = np.concatenate([columns(basis), columns(slope)])
    backward = columns(inverse.T).T
    return (split_bf16(forward), split_bf16(backward))


def apply_line(matrix, line):
    n = NODES
    m = n // 2
    sums = [line[a] + line[n - 1 - a] for a in range(m)]
    gaps = [line[a] - line[n - 1 - a] for a in range(m)]

    def total(parts):
        out = parts[0]
        for part in parts[1:]:
            out = out + part
        return out

    out = [None] * n
    for i in range(m + 1):
        plus = total(
            [float(0.5 * (matrix[i, a] - matrix[i, n - 1 - a])) * gaps[a] for a in range(m)]
        )
        if i == m:
            out[i] = plus
            continue
        minus = total(
            [float(0.5 * (matrix[i, a] + matrix[i, n - 1 - a])) * sums[a] for a in range(m)]
            + [float(matrix[i, m]) * line[m]]
        )
        out[i] = plus + minus
        out[n - 1 - i] = plus - minus
    return out


def lanes_of(shape):
    return lax.broadcasted_iota(jnp.int32, shape, len(shape) - 1)


def row_of(ref, row, rows):
    return ref[pl.ds(row, rows, stride=0), :]


def call(body, grid, ins, outs, out_shape, scratch=(), flops=0, moved=0, aliases=None):
    return pl.pallas_call(
        body,
        grid=grid,
        in_specs=ins,
        out_specs=outs,
        out_shape=out_shape,
        scratch_shapes=list(scratch),
        input_output_aliases=aliases or {},
        compiler_params=pltpu.CompilerParams(dimension_semantics=("arbitrary",) * len(grid)),
        cost_estimate=pl.CostEstimate(
            flops=int(flops), bytes_accessed=int(moved), transcendentals=0
        ),
    )


def held(count):
    return [pl.BlockSpec(memory_space=pltpu.VMEM)] * count


def whole(shape):
    return pl.BlockSpec(shape, lambda *_: (0,) * len(shape))


def pack(rows, comp, layers, pairs, lanes):
    square = NODES * NODES
    per_plane = square * layers
    half = lanes // 2

    def body(x_ref, o_ref):
        a = pl.program_id(0)
        low = lanes_of((pairs, lanes)) < half

        def layer(e, carry):
            for b in range(NODES):
                start = (a * NODES + b) * layers + e
                cos = x_ref[0, pl.ds(start, pairs, stride=2 * per_plane), :]
                sin = x_ref[0, pl.ds(start + per_plane, pairs, stride=2 * per_plane), :]
                o_ref[2 * e, b] = jnp.where(low, cos, pltpu.roll(sin, half, 1))
                o_ref[2 * e + 1, b] = jnp.where(low, pltpu.roll(cos, half, 1), sin)
            return carry

        lax.fori_loop(0, layers, layer, 0)

    size = rows.shape[1] * lanes * 4
    return call(
        body,
        (NODES,),
        [pl.BlockSpec((1, rows.shape[1], lanes), lambda a: (comp, 0, 0))],
        pl.BlockSpec((2 * layers, NODES, pairs, lanes), lambda a: (0, a, 0, 0)),
        jax.ShapeDtypeStruct((2 * layers, square, pairs, lanes), jnp.float32),
        moved=2 * size,
    )(rows)


def unpack(blocks, spec, slots, pairs, layers, buffer, total):
    lanes = blocks.shape[-1]
    square = NODES * NODES
    per_plane = square * layers
    half = lanes // 2
    rows = 2 * pairs * per_plane

    def body(x_ref, *refs):
        o_ref = refs[-1]
        a = pl.program_id(1)
        low = lanes_of((pairs, lanes)) < half

        def read(d, b):
            return x_ref[d, b] if len(x_ref.shape) == 4 else x_ref[d, 0, b]

        def layer(e, carry):
            for b in range(NODES):
                start = (a * NODES + b) * layers + e
                left, right = (read(2 * e, b), read(2 * e + 1, b))
                o_ref[pl.ds(start, pairs, stride=2 * per_plane), :] = jnp.where(
                    low, left, pltpu.roll(right, half, 1)
                )
                o_ref[pl.ds(start + per_plane, pairs, stride=2 * per_plane), :] = jnp.where(
                    low, pltpu.roll(left, half, 1), right
                )
            return carry

        lax.fori_loop(0, layers, layer, 0)

    extra = [] if buffer is None else [buffer]
    return call(
        body,
        (2, NODES),
        [spec] + [pl.BlockSpec(memory_space=pl.ANY)] * len(extra),
        pl.BlockSpec((rows, lanes), lambda i, a: (slots[0] + i * slots[1], 0)),
        jax.ShapeDtypeStruct((total, lanes), jnp.float32),
        moved=4 * rows * lanes * 4,
        aliases={1: 0} if extra else None,
    )(blocks, *extra)


def paired_nodes():
    return [(b, min(b + 1, NODES - 1)) for b in range(0, NODES, 2)]


def three_pass(table, rhs_ref, tiles):
    rows, lanes = tiles[0].shape
    half = lanes // 2
    low = lanes_of((rows, lanes)) < half
    depth = 2 * rows
    for place, (one, two) in enumerate(paired_nodes()):
        first, second = (tiles[one], tiles[two])
        cut = pl.ds(place * lanes, lanes)
        for part in range(2):
            if part == 0:
                value = jnp.where(low, first, pltpu.roll(second, half, 1))
            else:
                value = jnp.where(low, pltpu.roll(first, half, 1), second)
            high = value.astype(jnp.bfloat16)
            rest = (value - high.astype(jnp.float32)).astype(jnp.bfloat16)
            rhs_ref[pl.ds(part * rows, rows), cut] = high
            rhs_ref[pl.ds(depth + part * rows, rows), cut] = rest
            rhs_ref[pl.ds(2 * depth + part * rows, rows), cut] = high
    out = jnp.dot(table, rhs_ref[...], preferred_element_type=jnp.float32)
    fields = []
    for field in range(table.shape[0] // depth):
        nodes = [None] * NODES
        for place, (one, two) in enumerate(paired_nodes()):
            cut = slice(place * lanes, (place + 1) * lanes)
            top = out[field * depth : field * depth + rows, cut]
            bottom = out[field * depth + rows : (field + 1) * depth, cut]
            nodes[one] = jnp.where(low, top, pltpu.roll(bottom, half, 1))
            if two != one:
                nodes[two] = jnp.where(low, pltpu.roll(top, half, 1), bottom)
        fields.append(nodes)
    return fields


def rhs_scratch(table, lanes):
    return pltpu.VMEM((table.shape[1], len(paired_nodes()) * lanes), jnp.bfloat16)


def read_tiles(x_ref, rows, lanes):
    return [x_ref[:, b].reshape(rows, lanes) for b in range(NODES)]


def to_points(blocks, table):
    shares, square, pairs, lanes = blocks.shape
    rows = shares * pairs

    def body(t_ref, x_ref, v_ref, z_ref, rhs_ref):
        fields = three_pass(t_ref[...], rhs_ref, read_tiles(x_ref, rows, lanes))
        for b in range(NODES):
            v_ref[b] = fields[0][b]
            z_ref[b] = fields[1][b]

    spec = pl.BlockSpec((NODES, rows, lanes), lambda a: (a, 0, 0))
    shape = jax.ShapeDtypeStruct((square, rows, lanes), jnp.float32)
    return call(
        body,
        (NODES,),
        [
            whole(table.shape),
            pl.BlockSpec((shares, NODES, pairs, lanes), lambda a: (0, a, 0, 0)),
        ],
        [spec, spec],
        [shape, shape],
        scratch=[rhs_scratch(table, lanes)],
        flops=2 * table.shape[0] * table.shape[1] * square * lanes,
        moved=3 * square * rows * lanes * 4,
    )(table, blocks)


def turn_around(blocks, partial, slope_z, table, back):
    shares, square, pairs, lanes = blocks.shape
    rows = shares * pairs

    def body(t_ref, i_ref, x_ref, g_ref, s_ref, w_ref, z_ref, o_ref, rhs_ref):
        fields = three_pass(t_ref[...], rhs_ref, read_tiles(x_ref, rows, lanes))
        for b in range(NODES):
            w_ref[b] = fields[0][b]
            z_ref[b] = fields[1][b]
        tiles = [g_ref[b] + w_ref[b] * s_ref[b] for b in range(NODES)]
        out = three_pass(i_ref[...], rhs_ref, tiles)[0]
        for b in range(NODES):
            o_ref[:, b] = out[b].reshape(shares, pairs, lanes)

    spec = pl.BlockSpec((NODES, rows, lanes), lambda a: (a, 0, 0))
    shape = jax.ShapeDtypeStruct((square, rows, lanes), jnp.float32)
    exchanged = pl.BlockSpec((shares, NODES, pairs, lanes), lambda a: (0, a, 0, 0))
    return call(
        body,
        (NODES,),
        [whole(table.shape), whole(back.shape), exchanged, spec, spec],
        [spec, spec, exchanged],
        [shape, shape, jax.ShapeDtypeStruct(blocks.shape, jnp.float32)],
        scratch=[rhs_scratch(table, lanes)],
        flops=3 * table.shape[0] * table.shape[1] * square * lanes,
        moved=6 * square * rows * lanes * 4,
    )(table, back, blocks, partial, slope_z)


def in_plane(speeds, fields, metrics, table):
    square, rows, lanes = speeds[0].shape
    count = len(fields)
    step = 32
    own = [i for i, f in enumerate(fields) if all(f is not s for s in speeds)]
    arrays = list(speeds) + [fields[i] for i in own]

    def body(m_ref, *refs):
        ins, outs = (refs[: len(arrays)], refs[len(arrays) :])
        u_ref, v_ref = ins[:2]
        sources = []
        extra = 2
        for i, f in enumerate(fields):
            if i in own:
                sources.append(ins[extra])
                extra += 1
            else:
                sources.append(u_ref if f is speeds[0] else v_ref)

        def block(s, carry):
            r = pl.ds(s * 8, 8)

            def metric(kind, n):
                return row_of(m_ref, kind * square + n, 8)

            for a in range(NODES):
                ns = [a * NODES + b for b in range(NODES)]
                drift = [
                    u_ref[n, r] * metric(2, n) + v_ref[n, r] * metric(3, n) for n in ns
                ]
                for f in range(count):
                    beside = apply_line(table, [sources[f][n, r] for n in ns])
                    for b, n in enumerate(ns):
                        outs[f][n, r] = drift[b] * beside[b]
            for b in range(NODES):
                ns = [a * NODES + b for a in range(NODES)]
                drift = [
                    u_ref[n, r] * metric(0, n) + v_ref[n, r] * metric(1, n) for n in ns
                ]
                for f in range(count):
                    radial = apply_line(table, [sources[f][n, r] for n in ns])
                    for a, n in enumerate(ns):
                        outs[f][n, r] = outs[f][n, r] + drift[a] * radial[a]
            return carry

        lax.fori_loop(0, step // 8, block, 0)

    spec = pl.BlockSpec((square, step, lanes), lambda i: (0, i, 0))
    shape = jax.ShapeDtypeStruct((square, rows, lanes), jnp.float32)
    return call(
        body,
        (rows // step,),
        [whole(metrics.shape)] + [spec] * len(arrays),
        [spec] * count,
        [shape] * count,
        flops=30 * count * square * rows * lanes,
        moved=(len(arrays) + count) * square * rows * lanes * 4,
    )(metrics, *arrays)


def to_planes(partial, speed_z, slope_z, table, shares, place, buffers):
    square, rows, lanes = partial.shape
    pairs = rows // shares
    group = pairs // 2

    def body(t_ref, g_ref, w_ref, z_ref, *refs):
        outs, rhs_ref = (refs[-3:-1], refs[-1])
        tiles = [g_ref[b] + w_ref[b] * z_ref[b] for b in range(NODES)]
        nodes = three_pass(t_ref[...], rhs_ref, tiles)[0]
        for b in range(NODES):
            out = nodes[b].reshape(shares, pairs, lanes)
            for i in range(2):
                outs[i][:, 0, b] = out[:, i * group : (i + 1) * group]

    spec = pl.BlockSpec((NODES, rows, lanes), lambda a: (a, 0, 0))
    out_spec = pl.BlockSpec((shares, 1, NODES, group, lanes), lambda a: (0, place, a, 0, 0))
    shape = jax.ShapeDtypeStruct((shares, 2, square, group, lanes), jnp.float32)
    return call(
        body,
        (NODES,),
        [whole(table.shape), spec, spec, spec]
        + [pl.BlockSpec(memory_space=pl.ANY)] * len(buffers),
        [out_spec, out_spec],
        [shape, shape],
        scratch=[rhs_scratch(table, lanes)],
        flops=2 * table.shape[0] * table.shape[1] * square * lanes,
        moved=4 * square * rows * lanes * 4,
        aliases={4: 0, 5: 1} if buffers else None,
    )(table, partial, speed_z, slope_z, *buffers)


def first_part(sent, returned, metrics, table):
    shares, square, pairs, lanes = sent.shape

    def body(m_ref, s0, r0, o_ref, p0):
        d = pl.program_id(0)

        def block(s, carry):
            r = pl.ds(s * 8, 8)
            for n in range(square):
                p0[n] = s0[0, n, r] + time_step * r0[0, n, r]

            def metric(kind, n):
                return row_of(m_ref, (kind * shares + d) * square + n, 8)

            for a in range(NODES):
                ns = [a * NODES + b for b in range(NODES)]
                line = apply_line(table, [p0[n] for n in ns])
                for b, n in enumerate(ns):
                    o_ref[0, n, r] = metric(2, n) * line[b]
            for b in range(NODES):
                ns = [a * NODES + b for a in range(NODES)]
                line = apply_line(table, [p0[n] for n in ns])
                for a, n in enumerate(ns):
                    o_ref[0, n, r] = o_ref[0, n, r] + metric(0, n) * line[a]
            return carry

        lax.fori_loop(0, pairs // 8, block, 0)

    spec = pl.BlockSpec((1, square, pairs, lanes), lambda d: (d, 0, 0, 0))
    return call(
        body,
        (shares,),
        [whole(metrics.shape), spec, spec],
        spec,
        jax.ShapeDtypeStruct(sent.shape, jnp.float32),
        scratch=[pltpu.VMEM((square, 8, lanes), jnp.float32)],
        flops=30 * shares * square * pairs * lanes,
        moved=3 * shares * square * pairs * lanes * 4,
    )(metrics, sent, returned)


def join_layers(y_ref, layers):
    square = NODES * NODES
    last = (NODES - 1) * NODES
    for e in range(layers - 1):
        for b in range(NODES):
            upper, lower = (e * square + last + b, (e + 1) * square + b)
            total = y_ref[upper] + y_ref[lower]
            y_ref[upper] = total
            y_ref[lower] = total
    for b in range(NODES):
        node = (layers - 1) * square + last + b
        y_ref[node] = jnp.zeros_like(y_ref[node])


def rim_messages(read, layers, shape, partials):
    lane = lanes_of(shape)
    lanes = shape[-1]
    axis = len(shape) - 1
    first = jnp.zeros(shape, jnp.float32)
    last = jnp.zeros(shape, jnp.float32)
    square = NODES * NODES
    for e in range(layers):
        for a in range(NODES):
            spot = e * NODES + a
            here = lane == spot
            node = e * square + a * NODES
            first = jnp.where(here, pltpu.roll(read(node), spot, axis), first)
            last = jnp.where(
                here, pltpu.roll(read(node + NODES - 1), (spot + 1) % lanes, axis), last
            )
    for i, partial in enumerate(partials):
        here = lane == layers * NODES + i
        first = jnp.where(here, partial, first)
        last = jnp.where(here, partial, last)
    return (first, last)


def right_side(flat, sent, returned, metrics, weights, waves, table, layers, place):
    shares, square, _, lanes = flat.shape
    half = lanes // 2

    def body(m_ref, q_ref, k_ref, f_ref, s1, s2, r_ref, o_ref, first_ref, last_ref, p1, c0, c1):
        e = pl.program_id(0)
        lane = lanes_of((8, lanes))
        low = lane < half
        wave = k_ref[...]
        sides = (c0, c1)

        @pl.when(e == 0)
        def _():
            first_ref[...] = jnp.zeros_like(first_ref)
            last_ref[...] = jnp.zeros_like(last_ref)

        for h in range(2):
            d = 2 * e + h
            side = sides[h]
            for n in range(square):
                p1[n] = s1[h, n] + time_step * r_ref[h, 0, n]
                moved = s2[h, n] + time_step * r_ref[h, 1, n]
                along = pltpu.roll(moved, half, 1) * wave
                side[n] = f_ref[h, n] + row_of(q_ref, d * square + n, 8) * along

            def metric(kind, n):
                return row_of(m_ref, (kind * shares + d) * square + n, 8)

            for a in range(NODES):
                ns = [a * NODES + b for b in range(NODES)]
                line = apply_line(table, [p1[n] for n in ns])
                for b, n in enumerate(ns):
                    side[n] = side[n] + metric(3, n) * line[b]
            for b in range(NODES):
                ns = [a * NODES + b for a in range(NODES)]
                line = apply_line(table, [p1[n] for n in ns])
                for a, n in enumerate(ns):
                    side[n] = side[n] + metric(1, n) * line[a]
        rims = [[first_ref[0], last_ref[0]], [first_ref[1], last_ref[1]]]
        for n in range(square):
            left, right = (c0[n], c1[n])
            parts = (
                jnp.where(low, left, pltpu.roll(right, half, 1)),
                jnp.where(low, pltpu.roll(left, half, 1), right),
            )
            for i in range(2):
                o_ref[n, i] = parts[i]
                a, b = divmod(n, NODES)
                spot = e * NODES + a
                if b == 0:
                    rims[i][0] = jnp.where(lane == spot, pltpu.roll(parts[i], spot, 1), rims[i][0])
                if b == NODES - 1:
                    rims[i][1] = jnp.where(
                        lane == spot, pltpu.roll(parts[i], spot + 1, 1), rims[i][1]
                    )
        for i in range(2):
            first_ref[i] = rims[i][0]
            last_ref[i] = rims[i][1]

    spec = pl.BlockSpec((2, square, 8, lanes), lambda e: (e, 0, place, 0))
    nodes = layers * square
    rim_shape = jax.ShapeDtypeStruct((2, 8, lanes), jnp.float32)
    scratch = pltpu.VMEM((square, 8, lanes), jnp.float32)
    return call(
        body,
        (layers,),
        [
            whole(metrics.shape),
            whole(weights.shape),
            pl.BlockSpec((8, lanes), lambda e: (place, 0)),
            spec,
            spec,
            spec,
            pl.BlockSpec((2, 2, square, 8, lanes), lambda e: (e, 0, 0, 0, 0)),
        ],
        [
            pl.BlockSpec((square, 2, 8, lanes), lambda e: (e, 0, 0, 0)),
            whole((2, 8, lanes)),
            whole((2, 8, lanes)),
        ],
        [jax.ShapeDtypeStruct((nodes, 2, 8, lanes), jnp.float32), rim_shape, rim_shape],
        scratch=[scratch] * 3,
        flops=40 * shares * square * 8 * lanes,
        moved=6 * shares * square * 8 * lanes * 4,
    )(metrics, weights, waves, flat, sent[1], sent[2], returned)


def swap_rims(first, last):
    size = lax.axis_size("elem")
    up = [(i, (i + 1) % size) for i in range(size)]
    down = [(j, i) for i, j in up]
    return (lax.ppermute(last, "elem", up), lax.ppermute(first, "elem", down))


def opposite(first):
    size = lax.axis_size("elem")
    return lax.ppermute(first, "elem", [(i, (i + 2) % size) for i in range(size)])


def join_columns(read, ref, before, after, layers):
    lanes = before.shape[-1]
    axis = len(before.shape) - 1
    lane = lanes_of(before.shape)
    square = NODES * NODES
    for e in range(layers):
        for a in range(NODES):
            spot = e * NODES + a
            node = e * square + a * NODES
            first, last = (read(node), read(node + NODES - 1))
            beyond = pltpu.roll(after, lanes - 1 - spot, axis)
            ahead = jnp.where(lane == lanes - 1, beyond, pltpu.roll(first, lanes - 1, axis))
            right = last + ahead
            mine = first + (pltpu.roll(before, lanes - spot, axis) if spot else before)
            ref[node + NODES - 1] = right
            ref[node] = jnp.where(lane == 0, mine, pltpu.roll(right, 1, axis))


def join(source, ref, before, after, layers):
    square = NODES * NODES

    def copy(e, carry):
        for n in range(square):
            if 0 < n % NODES < NODES - 1:
                ref[e * square + n] = source[e * square + n]
        return carry

    lax.fori_loop(0, layers, copy, 0)
    join_columns(lambda n: source[n], ref, before, after, layers)
    join_layers(ref, layers)


def each_node(layers, step):
    def layer(e, carry):
        for n in range(NODES * NODES):
            step(e * NODES * NODES + n)
        return carry

    lax.fori_loop(0, layers, layer, 0)


def share_of(layers, e, a):
    if a == 0:
        return jnp.where(e > 0, 0.5, 1.0)
    if a == NODES - 1:
        return jnp.where(e < layers - 1, 0.5, 0.0)
    return 1.0


def helmholtz(r_ref, y_ref, flux_ref, g_ref, shift, layers, table, dot_only=False):
    square = NODES * NODES
    nodes = layers * square
    turned = table.T
    zero = jnp.zeros(shift.shape, jnp.float32)

    def layer(e, carry):
        norm, energy = carry
        base = e * square

        def metric(kind, n):
            return row_of(g_ref, kind * nodes + base + n, 8)

        for b in range(NODES):
            ns = [a * NODES + b for a in range(NODES)]
            radial = apply_line(table, [r_ref[base + n] for n in ns])
            for a, n in enumerate(ns):
                flux_ref[n] = radial[a]
        for a in range(NODES):
            ns = [a * NODES + b for b in range(NODES)]
            line = [r_ref[base + n] for n in ns]
            beside = apply_line(table, line)
            second = []
            rest = []
            part = zero
            for b, n in enumerate(ns):
                radial = flux_ref[n]
                cross = metric(1, n)
                one = metric(0, n) * radial + cross * beside[b]
                two = cross * radial + metric(2, n) * beside[b]
                same = shift * metric(3, n) * line[b]
                whole_weight = line[b] * line[b]
                part = part + (0.5 * whole_weight if b in (0, NODES - 1) else whole_weight)
                if dot_only:
                    energy = energy + (radial * one + beside[b] * two + same * line[b])
                else:
                    flux_ref[n] = one
                    second.append(two)
                    rest.append(same)
            norm = norm + part * share_of(layers, e, a)
            if not dot_only:
                back = apply_line(turned, second)
                for b, n in enumerate(ns):
                    y_ref[base + n] = rest[b] + back[b]
        if not dot_only:
            for b in range(NODES):
                ns = [a * NODES + b for a in range(NODES)]
                back = apply_line(turned, [flux_ref[n] for n in ns])
                for a, n in enumerate(ns):
                    value = y_ref[base + n] + back[a]
                    y_ref[base + n] = value
                    energy = energy + value * r_ref[base + n]
        return (norm, energy)

    norm, energy = lax.fori_loop(0, layers, layer, (zero, zero))
    axis = len(shift.shape) - 1
    return (
        jnp.sum(norm, axis=axis, keepdims=True),
        jnp.sum(energy, axis=axis, keepdims=True),
    )


def lane_value(block, lane):
    return block[..., lane : lane + 1]


def sums_from(own, left, right, far, layers):
    total = (own[...] + far[...]) + (left[...] + right[...])
    spot = layers * NODES
    return (lane_value(total, spot), lane_value(total, spot + 1))


def scalars_block(shape, values, spot=0):
    lane = lanes_of(shape)
    out = jnp.zeros(shape, jnp.float32)
    for i, value in enumerate(values):
        out = jnp.where(lane == spot + i, value, out)
    return out


def shapes_of(field):
    return (
        jax.ShapeDtypeStruct(field.shape, jnp.float32),
        jax.ShapeDtypeStruct(field.shape[1:], jnp.float32),
        pltpu.VMEM((NODES * NODES,) + field.shape[1:], jnp.float32),
    )


def first_image(raw, before, after, shift, geo, layers, table):
    field, small, flux_scratch = shapes_of(raw)
    shape = raw.shape[1:]

    def body(g_ref, k_ref, f_ref, b_ref, a_ref, r_ref, y_ref, first_ref, last_ref, flux):
        join(f_ref, r_ref, b_ref[...], a_ref[...], layers)
        sums = helmholtz(r_ref, y_ref, flux, g_ref, k_ref[...], layers, table)
        first_ref[...], last_ref[...] = rim_messages(lambda n: y_ref[n], layers, shape, sums)

    return call(
        body,
        (),
        held(5),
        held(4),
        [field, field, small, small],
        scratch=[flux_scratch],
        flops=80 * raw.size,
        moved=12 * raw.size,
    )(geo, shift, raw, before, after)


def second_image(start, image, messages, shift, geo, layers, table):
    field, small, flux_scratch = shapes_of(start)
    shape = start.shape[1:]

    def body(g_ref, k_ref, r0, y0, own, left, right, far, *rest):
        w_ref, y_ref, first_ref, last_ref, scalar_ref, r1, flux = rest
        norm, energy = sums_from(own, left, right, far, layers)
        alpha = jnp.broadcast_to(norm / energy, shape)
        join(y0, w_ref, left[...], right[...], layers)

        def move(node):
            r1[node] = r0[node] - alpha * w_ref[node]

        each_node(layers, move)
        sums = helmholtz(r1, y_ref, flux, g_ref, k_ref[...], layers, table)
        first_ref[...], last_ref[...] = rim_messages(lambda n: y_ref[n], layers, shape, sums)
        scalar_ref[...] = scalars_block(shape, (alpha, norm, energy))

    return call(
        body,
        (),
        held(8),
        held(5),
        [field, field, small, small, small],
        scratch=[pltpu.VMEM(start.shape, jnp.float32), flux_scratch],
        flops=80 * start.size,
        moved=16 * start.size,
    )(geo, shift, start, image, *messages)


def third_energy(start, joined, image, messages, scalars, shift, geo, layers, table):
    field, small, flux_scratch = shapes_of(start)
    shape = start.shape[1:]

    def body(g_ref, k_ref, r0, w0, y1, own, left, right, far, old, *rest):
        r2, d2, sums_ref, scalar_ref, w1, flux = rest
        norm, energy = sums_from(own, left, right, far, layers)
        before = old[...]
        alpha = jnp.broadcast_to(lane_value(before, 0), shape)
        ratio = norm / lane_value(before, 1)
        curve = energy - ratio * ratio * lane_value(before, 2)
        step = jnp.broadcast_to(norm / curve, shape)
        beta = jnp.broadcast_to(ratio, shape)
        join(y1, w1, left[...], right[...], layers)

        def move(node):
            w = w0[node]
            start_value = r0[node]
            moved = start_value - alpha * w
            d2[node] = moved + beta * start_value
            r2[node] = moved - step * (w1[node] + beta * w)

        each_node(layers, move)
        sums = helmholtz(r2, None, flux, g_ref, k_ref[...], layers, table, dot_only=True)
        sums_ref[...] = scalars_block(shape, sums, layers * NODES)
        scalar_ref[...] = scalars_block(shape, (alpha, norm, curve, step))

    return call(
        body,
        (),
        held(10),
        held(4),
        [field, field, small, small],
        scratch=[pltpu.VMEM(start.shape, jnp.float32), flux_scratch],
        flops=60 * start.size,
        moved=20 * start.size,
    )(geo, shift, start, joined, image, *messages, scalars)


def finish(start, direction, residual, messages, scalars, layers, place, buffer, total):
    nodes, _, rows, lanes = start.shape
    shape = start.shape[1:]
    square = NODES * NODES

    def body(r0, d2, r2, own, left, right, far, old, *refs):
        o_ref = refs[-1]
        norm, energy = sums_from(own, left, right, far, layers)
        before = old[...]
        ratio = norm / lane_value(before, 1)
        curve = energy - ratio * ratio * lane_value(before, 2)
        step = norm / curve
        third = jnp.broadcast_to(step, shape)
        second = jnp.broadcast_to(lane_value(before, 3) + step * ratio, shape)
        first = jnp.broadcast_to(lane_value(before, 0), shape)

        def layer(e, carry):
            for n in range(square):
                node = e * square + n
                value = first * r0[node] + second * d2[node] + third * r2[node]
                for i in range(2):
                    o_ref[pl.ds(i * nodes + n * layers + e, rows, stride=2 * nodes), :] = value[i]
            return carry

        lax.fori_loop(0, layers, layer, 0)

    extra = [] if buffer is None else [buffer]
    return call(
        body,
        (1,),
        [whole(start.shape)] * 3
        + [whole(shape)] * 5
        + [pl.BlockSpec(memory_space=pl.ANY)] * len(extra),
        pl.BlockSpec((2 * rows * nodes, lanes), lambda i: (place, 0)),
        jax.ShapeDtypeStruct((total, lanes), jnp.float32),
        flops=6 * start.size,
        moved=16 * start.size,
        aliases={8: 0} if extra else None,
    )(start, direction, residual, *messages, scalars, *extra)


def halves(values, shares):
    half = values.shape[-1] // 2
    parts = [jnp.concatenate([p, p], axis=-1) for p in (values[..., :half], values[..., half:])]
    return jnp.stack(parts, axis=2).reshape(values.shape[0], shares, NODES * NODES, 2 * half)


def on_device_paired(*arrays):
    return paired_step(*arrays)


def paired_step(velocity, radial_dx, radial_dy, around_dx, around_dy, jacobian):
    table = derivative_table()
    modes = lax.axis_size("mode")
    mode = lax.axis_index("mode")
    _, local_planes, layers, _, _, lanes = velocity.shape
    planes = local_planes * modes
    pairs = local_planes // 2
    first_plane = mode * local_planes
    square = NODES * NODES
    forward, backward = (jnp.asarray(t) for t in paired_tables(planes))

    rows = velocity.transpose(0, 1, 3, 4, 2, 5).reshape(3, local_planes * square * layers, lanes)
    plain = jnp.stack([radial_dx, radial_dy, around_dx, around_dy]).reshape(
        4, layers, square, lanes
    )
    both = halves(plain, modes)
    here = lax.dynamic_index_in_dim(both, mode, 1, keepdims=False).reshape(4 * square, lanes)
    metrics = geometry(radial_dx, radial_dy, around_dx, around_dy, jacobian)
    geo = jnp.stack(metrics).reshape(4 * layers * square, lanes)
    scaled = halves((metrics[3] * (-1.0 / time_step)).reshape(1, layers, square, lanes), modes)
    flux = (both * scaled).reshape(4 * modes * square, lanes)
    scaled = scaled.reshape(modes * square, lanes)
    pair = (first_plane // 2 + jnp.arange(pairs, dtype=jnp.int32)).astype(jnp.float32)
    wave = pair[:, None] * spanwise_wave
    low = (jnp.arange(lanes) < lanes // 2)[None, :]
    waves = jnp.where(low, wave, -wave)
    shift = plane_shift(first_plane, local_planes, planes).reshape(pairs, 2).T
    shift = jnp.broadcast_to(shift.reshape(2, 2, pairs // 2, 1), (2, 2, pairs // 2, lanes))

    def exchange(blocks):
        return lax.all_to_all(blocks, "mode", split_axis=0, concat_axis=0, tiled=True)

    sent = [pack(rows, comp, layers, pairs, lanes) for comp in range(3)]
    arrived = [exchange(blocks) for blocks in sent]
    speed_x, slope_0 = to_points(arrived[0], forward)
    speed_y, slope_1 = to_points(arrived[1], forward)
    speeds = [speed_x, speed_y]
    partial = in_plane(speeds, speeds, here, table)
    speed_z, slope_2, blocks = turn_around(arrived[2], partial[0], slope_0, forward, backward)
    returned = [exchange(blocks)]
    last = in_plane(speeds, [speed_z], here, table)[0]
    blocks = to_planes(partial[1], speed_z, slope_1, backward, modes, 0, ())
    blocks = to_planes(last, speed_z, slope_2, backward, modes, 1, blocks)
    returned.append(exchange(blocks[0]))
    returned.append(exchange(blocks[1]))

    group = pairs // 2
    own_rows = local_planes * square * layers
    whole_spec = pl.BlockSpec((modes, NODES, group, lanes), lambda i, a: (0, a, i, 0))
    part_spec = pl.BlockSpec((modes, 1, NODES, group, lanes), lambda i, a: (0, i, a, 0, 0))
    advection = unpack(returned[0], whole_spec, (0, 1), group, layers, None, 3 * own_rows)
    flat = first_part(sent[0], returned[0], flux, table)

    def solve(place, flat, buffer):
        own_shift = shift[:, place]
        raw, first, last = right_side(
            flat, sent, returned[1 + place], flux, scaled, waves, table, layers, place
        )
        before, after = swap_rims(first, last)
        start, image, first, last = first_image(raw, before, after, own_shift, geo, layers, table)
        messages = (first,) + swap_rims(first, last) + (opposite(first),)
        joined, image, first, last, scalars = second_image(
            start, image, messages, own_shift, geo, layers, table
        )
        messages = (first,) + swap_rims(first, last) + (opposite(first),)
        residual, direction, sums, scalars = third_energy(
            start, joined, image, messages, scalars, own_shift, geo, layers, table
        )
        messages = (sums,) + swap_rims(sums, sums) + (opposite(sums),)
        return finish(
            start, direction, residual, messages, scalars, layers, place, buffer, own_rows
        )

    pressure = solve(0, flat, None)
    advection = unpack(returned[1], part_spec, (2, 2), group, layers, advection, 3 * own_rows)
    flat, pressure, advection = lax.optimization_barrier((flat, pressure, advection))
    pressure = solve(1, flat, pressure)
    advection = unpack(returned[2], part_spec, (3, 2), group, layers, advection, 3 * own_rows)
    advection = advection.reshape(3, local_planes, NODES, NODES, layers, lanes)
    pressure = pressure.reshape(local_planes, NODES, NODES, layers, lanes)
    return (advection.transpose(0, 1, 4, 2, 3, 5), pressure.transpose(0, 3, 1, 2, 4))


def paired_fits(mesh, shape):
    modes, ring = (mesh.shape["mode"], mesh.shape["elem"])
    _, planes, layers, _, _, columns = shape
    return (
        ring == 4
        and columns == 128 * ring
        and modes == 2 * layers
        and planes % (16 * modes) == 0
        and planes == 2 * 128
        and (layers * NODES + 2 <= 128)
    )


def solution(mesh):
    placed = (
        P(None, "mode", None, None, None, "elem"),
        P(None, None, None, "elem"),
        P(None, None, None, "elem"),
        P(None, None, None, "elem"),
        P(None, None, None, "elem"),
        P(None, None, None, "elem"),
    )


    def step(velocity, *rest):
        body = on_device_paired if paired_fits(mesh, velocity.shape) else on_device
        return jax.shard_map(
            body,
            mesh=mesh,
            in_specs=placed,
            out_specs=(
                P(None, "mode", None, None, None, "elem"),
                P("mode", None, None, None, "elem"),
            ),
            check_vma=False,
        )(velocity, *rest)

    return step
```

```python
import math

import jax
import jax.numpy as jnp
import numpy as np
from jax import lax
from jax.experimental import pallas as pl
from jax.experimental.pallas import tpu as pltpu
from jax.sharding import PartitionSpec as P

NODES = 7
ITERS = 3
GRANT = 24 * 2**20
WHOLE_GRANT = 67043328


spanwise_wave = 2.0 * math.pi / 64.0
time_step = 0.1


def padded_2(value, sides, width):
    for axis, dim in sides:
        size, length = (lax.axis_size(axis), value.shape[dim])
        up = [(i, (i + 1) % size) for i in range(size)]
        down = [(j, i) for i, j in up]
        last = lax.slice_in_dim(value, length - width, length, axis=dim)
        leading = lax.slice_in_dim(value, 0, width, axis=dim)
        before = lax.ppermute(last, axis, up)
        after = lax.ppermute(leading, axis, down)
        value = jnp.concatenate([before, value, after], axis=dim)
    return value


def lobatto_rule(count):
    degree = count - 1
    points = np.cos(np.pi * np.arange(count) / degree)
    legendre = np.zeros((count, count))
    for _ in range(60):
        legendre[:, 0] = 1.0
        legendre[:, 1] = points
        for order in range(2, count):
            legendre[:, order] = (
                (2 * order - 1) * points * legendre[:, order - 1]
                - (order - 1) * legendre[:, order - 2]
            ) / order
        points = points - (points * legendre[:, degree] - legendre[:, degree - 1]) / (
            count * legendre[:, degree]
        )
    legendre[:, 0] = 1.0
    legendre[:, 1] = points
    for order in range(2, count):
        legendre[:, order] = (
            (2 * order - 1) * points * legendre[:, order - 1] - (order - 1) * legendre[:, order - 2]
        ) / order
    weights = 2.0 / (degree * count * legendre[:, degree] ** 2)
    return (points[::-1].copy(), weights[::-1].copy())


def derivative_table():
    lobatto_nodes = lobatto_rule(NODES)[0]
    total = lobatto_nodes.shape[0]
    scales = np.ones(total)
    for column in range(total):
        for other in range(total):
            if other != column:
                scales[column] = scales[column] / (lobatto_nodes[column] - lobatto_nodes[other])
    table = np.zeros((total, total))
    for row in range(total):
        for column in range(total):
            if row != column:
                table[row, column] = (
                    scales[column] / scales[row] / (lobatto_nodes[row] - lobatto_nodes[column])
                )
        table[row, row] = -np.sum(table[row])
    return table


def radial_derivative(table, field):
    return jnp.einsum("ia,...abe->...ibe", table, field, precision=lax.Precision.HIGHEST)


def around_derivative(table, field):
    return jnp.einsum("jb,...abe->...aje", table, field, precision=lax.Precision.HIGHEST)


def radial_transpose(table, field):
    return jnp.einsum("ia,...ibe->...abe", table, field, precision=lax.Precision.HIGHEST)


def around_transpose(table, field):
    return jnp.einsum("jb,...aje->...abe", table, field, precision=lax.Precision.HIGHEST)


def z_derivative(field, first_pair):
    shape = field.shape
    count = shape[1] // 2
    pairs = field.reshape((shape[0], count, 2) + shape[2:])
    waves = (first_pair + jnp.arange(count, dtype=jnp.int32)).astype(jnp.float32) * spanwise_wave
    waves = waves.reshape((1, count) + (1,) * (len(shape) - 2))
    return jnp.stack([waves * pairs[:, :, 1], -waves * pairs[:, :, 0]], axis=2).reshape(shape)


def transform_tables(planes):
    position = jnp.arange(planes, dtype=jnp.int32)
    plane = jnp.arange(planes, dtype=jnp.int32)
    order = plane // 2
    turns = position[:, None] * order[None, :] % planes
    angle = 2.0 * math.pi / planes * turns.astype(jnp.float32)
    cosine = jnp.cos(angle)
    sine = jnp.sin(angle)
    is_sine = (plane % 2 == 1)[None, :]
    is_top = (plane == 1)[None, :]
    parity = jnp.cos(math.pi * (position % 2).astype(jnp.float32))[:, None]
    basis = jnp.where(is_top, parity, jnp.where(is_sine, sine, cosine))
    scaling = jnp.where(order == 0, 1.0, 2.0).astype(jnp.float32) / planes
    inverse = jnp.transpose(basis * scaling[None, :])
    wave = (order.astype(jnp.float32) * spanwise_wave)[None, :]
    slope = jnp.where(is_sine, wave * cosine, -wave * sine)
    return (basis, inverse, slope)


def geometry(radial_dx, radial_dy, around_dx, around_dy, jacobian):
    lobatto_weights = lobatto_rule(NODES)[1]
    quadrature = jnp.asarray(np.outer(lobatto_weights, lobatto_weights), jnp.float32)[:, :, None]
    mass = quadrature * jacobian
    radial_stiff = mass * (radial_dx * radial_dx + radial_dy * radial_dy)
    cross_stiff = mass * (radial_dx * around_dx + radial_dy * around_dy)
    around_stiff = mass * (around_dx * around_dx + around_dy * around_dy)
    return (radial_stiff, cross_stiff, around_stiff, mass)


def node_weights(layers):
    layer = jnp.arange(layers, dtype=jnp.int32).reshape(layers, 1, 1, 1)
    node = jnp.arange(NODES, dtype=jnp.int32)
    radial_node = node.reshape(1, NODES, 1, 1)
    around_node = node.reshape(1, 1, NODES, 1)
    shared_radial = (radial_node == NODES - 1) & (layer < layers - 1) | (radial_node == 0) & (
        layer > 0
    )
    shared_around = (around_node == 0) | (around_node == NODES - 1)
    multiplicity = (1.0 + shared_radial.astype(jnp.float32)) * (
        1.0 + shared_around.astype(jnp.float32)
    )
    boundary = (radial_node == NODES - 1) & (layer == layers - 1)
    mask = 1.0 - boundary.astype(jnp.float32)
    return (mask, mask / multiplicity)


def plane_shift(first_plane, count, planes):
    plane = first_plane + jnp.arange(count, dtype=jnp.int32)
    order = jnp.where(plane == 1, planes // 2, plane // 2)
    wave = order.astype(jnp.float32) * spanwise_wave
    return (wave * wave).reshape(count, 1, 1, 1, 1)


def helmholtz_local(table, field, shift, metrics):
    radial_stiff, cross_stiff, around_stiff, mass = metrics
    radial = radial_derivative(table, field)
    beside_all = around_derivative(table, field)
    return (
        radial_transpose(table, radial_stiff * radial + cross_stiff * beside_all)
        + around_transpose(table, cross_stiff * radial + around_stiff * beside_all)
        + shift * mass * field
    )


def assemble(field):
    lower = field[:, :-1, -1] + field[:, 1:, 0]
    field = field.at[:, :-1, -1].set(lower).at[:, 1:, 0].set(lower)
    first = field[:, :, :, 0]
    last = field[:, :, :, -1]
    rims = jnp.concatenate([first[..., :1], last[..., -1:]], axis=3)
    padded = padded_2(rims, (("elem", 3),), 1)
    after = jnp.concatenate([first[..., 1:], padded[..., 3:4]], axis=3)
    right = last + after
    left = jnp.concatenate([padded[..., 0:1] + first[..., :1], right[..., :-1]], axis=3)
    return field.at[:, :, :, -1].set(right).at[:, :, :, 0].set(left)


def inner(first, second, weight):
    return jnp.sum(first * second * weight, axis=(1, 2, 3, 4))


def expand(scalar):
    return scalar.reshape(-1, 1, 1, 1, 1)


def squared_norm(residual, weight):
    return lax.psum(inner(residual, residual, weight), "elem")


def on_device(velocity, radial_dx, radial_dy, around_dx, around_dy, jacobian):
    table = jnp.asarray(derivative_table(), jnp.float32)
    modes = lax.axis_size("mode")
    local_planes = velocity.shape[1]
    planes = local_planes * modes
    first_plane = lax.axis_index("mode") * local_planes
    layers = velocity.shape[2]
    columns = velocity.shape[5]
    basis, inverse, slope = transform_tables(planes)
    radial = radial_derivative(table, velocity)
    beside_all = around_derivative(table, velocity)
    along_x = radial_dx * radial + around_dx * beside_all
    along_y = radial_dy * radial + around_dy * beside_all
    fields = jnp.concatenate([velocity, along_x, along_y], axis=0)
    count = fields.shape[0]
    cells = layers * NODES * NODES * columns
    packed = fields.reshape(count, local_planes, modes, cells // modes)
    flat = lax.all_to_all(packed, "mode", split_axis=2, concat_axis=1, tiled=True)[:, :, 0, :]
    values = jnp.einsum("jp,fpc->fjc", basis, flat, precision=lax.Precision.HIGHEST)
    speed = values[0:3]
    slope_x = values[3:6]
    slope_y = values[6:9]
    slope_z = jnp.einsum("jp,fpc->fjc", slope, flat[0:3], precision=lax.Precision.HIGHEST)
    product = -(speed[0:1] * slope_x + speed[1:2] * slope_y + speed[2:3] * slope_z)
    spectral = jnp.einsum("pj,fjc->fpc", inverse, product, precision=lax.Precision.HIGHEST)
    returned = lax.all_to_all(
        spectral[:, :, None, :], "mode", split_axis=1, concat_axis=2, tiled=True
    )
    advection = returned.reshape(velocity.shape)
    metrics = geometry(radial_dx, radial_dy, around_dx, around_dy, jacobian)
    mask, weight = node_weights(layers)
    predicted = velocity + time_step * advection
    radial = radial_derivative(table, predicted[0:2])
    beside_all = around_derivative(table, predicted[0:2])
    divergence = (
        radial_dx * radial[0]
        + around_dx * beside_all[0]
        + (radial_dy * radial[1] + around_dy * beside_all[1])
        + z_derivative(predicted[2:3], first_plane // 2)[0]
    )
    shift = plane_shift(first_plane, local_planes, planes)
    right_side = mask * assemble(-(metrics[3] * divergence) / time_step)
    solution = jnp.zeros_like(right_side)
    residual = right_side
    direction = right_side
    norm_now = squared_norm(residual, weight)
    for _ in range(ITERS):
        image = mask * assemble(helmholtz_local(table, direction, shift, metrics))
        alpha = norm_now / lax.psum(inner(direction, image, weight), "elem")
        solution = solution + expand(alpha) * direction
        residual = residual - expand(alpha) * image
        norm_next = squared_norm(residual, weight)
        direction = residual + expand(norm_next / norm_now) * direction
        norm_now = norm_next
    return (advection, solution)


def split_bf16(table):
    high = table.astype(jnp.bfloat16)
    low = (table - high.astype(np.float64)).astype(jnp.bfloat16)
    return np.concatenate([high, high, low], axis=1)


def paired_tables(planes):
    position = np.arange(planes)
    plane = np.arange(planes)
    order = plane // 2
    angle = 2.0 * np.pi / planes * (position[:, None] * order[None, :] % planes)
    cosine, sine = (np.cos(angle), np.sin(angle))
    odd = (plane % 2 == 1)[None, :]
    parity = (1.0 - 2.0 * (position % 2))[:, None]
    basis = np.where((plane == 1)[None, :], parity, np.where(odd, sine, cosine))
    wave = (order * spanwise_wave)[None, :]
    slope = np.where(odd, wave * cosine, -wave * sine)
    scaling = np.where(order == 0, 1.0, 2.0) / planes
    inverse = -(basis * scaling[None, :]).T

    def columns(matrix):
        return np.concatenate([matrix[:, 0::2], matrix[:, 1::2]], axis=1)

    forward = np.concatenate([columns(basis), columns(slope)])
    backward = columns(inverse.T).T
    return (split_bf16(forward), split_bf16(backward))


def apply_line(matrix, line):
    n = NODES
    m = n // 2
    sums = [line[a] + line[n - 1 - a] for a in range(m)]
    gaps = [line[a] - line[n - 1 - a] for a in range(m)]

    def total(parts):
        out = parts[0]
        for part in parts[1:]:
            out = out + part
        return out

    out = [None] * n
    for i in range(m + 1):
        plus = total(
            [float(0.5 * (matrix[i, a] - matrix[i, n - 1 - a])) * gaps[a] for a in range(m)]
        )
        if i == m:
            out[i] = plus
            continue
        minus = total(
            [float(0.5 * (matrix[i, a] + matrix[i, n - 1 - a])) * sums[a] for a in range(m)]
            + [float(matrix[i, m]) * line[m]]
        )
        out[i] = plus + minus
        out[n - 1 - i] = plus - minus
    return out


def lanes_of(shape):
    return lax.broadcasted_iota(jnp.int32, shape, len(shape) - 1)


def row_of(ref, row, rows):
    return ref[pl.ds(row, rows, stride=0), :]


def call(body, grid, ins, outs, out_shape, scratch=(), flops=0, moved=0, aliases=None, grant=GRANT):
    return pl.pallas_call(
        body,
        grid=grid,
        in_specs=ins,
        out_specs=outs,
        out_shape=out_shape,
        scratch_shapes=list(scratch),
        input_output_aliases=aliases or {},
        compiler_params=pltpu.CompilerParams(
            dimension_semantics=("arbitrary",) * len(grid), vmem_limit_bytes=grant
        ),
        cost_estimate=pl.CostEstimate(
            flops=int(flops), bytes_accessed=int(moved), transcendentals=0
        ),
    )


def held(count):
    return [pl.BlockSpec(memory_space=pltpu.VMEM)] * count


def whole(shape):
    return pl.BlockSpec(shape, lambda *_: (0,) * len(shape))


def turn(tiles):
    tiles = list(tiles)
    sub = lax.broadcasted_iota(jnp.int32, tiles[0].shape, 0)
    size = len(tiles)
    step = size // 2
    while step:
        keep = (sub & step) == 0
        for i in range(size):
            if not i & step:
                one, two = (tiles[i], tiles[i + step])
                tiles[i] = jnp.where(keep, one, pltpu.roll(two, step, 0))
                tiles[i + step] = jnp.where(keep, pltpu.roll(one, size - step, 0), two)
        step //= 2
    return tiles


def turn_all(read, write, count):
    def some(s, carry):
        for i in range(NODES):
            t = s * NODES + i
            for r, tile in enumerate(turn([read(k, t) for k in range(8)])):
                write(t, r, tile)
        return carry

    lax.fori_loop(0, count // NODES, some, 0)


def rows_at(k, unit, t):
    return pl.ds(pl.multiple_of(k * unit + 8 * t, 8), 8)


def pack(rows, comp, layers, pairs, lanes):
    square = NODES * NODES
    per_plane = square * layers
    unit = 2 * per_plane
    half = lanes // 2

    def body(x_ref, o_ref, mid):
        low = lanes_of((8, lanes)) < half

        def write(t, r, tile):
            mid[8 * t + r] = tile

        turn_all(lambda k, t: x_ref[0, rows_at(k, unit, t), :], write, unit // 8)

        def layer(e, carry):
            for n in range(square):
                cos = mid[n * layers + e]
                sin = mid[per_plane + n * layers + e]
                o_ref[2 * e, n] = jnp.where(low, cos, pltpu.roll(sin, half, 1))
                o_ref[2 * e + 1, n] = jnp.where(low, pltpu.roll(cos, half, 1), sin)
            return carry

        lax.fori_loop(0, layers, layer, 0)

    size = rows.shape[1] * lanes * 4
    return call(
        body,
        (pairs // 8,),
        [pl.BlockSpec((1, 8 * unit, lanes), lambda g: (comp, g, 0))],
        pl.BlockSpec((2 * layers, square, 8, lanes), lambda g: (0, 0, g, 0)),
        jax.ShapeDtypeStruct((2 * layers, square, pairs, lanes), jnp.float32),
        scratch=[pltpu.VMEM((unit, 8, lanes), jnp.float32)],
        grant=WHOLE_GRANT,
        moved=2 * size,
    )(rows)


def unpack(blocks, spec, slots, layers, buffer, total):
    lanes = blocks.shape[-1]
    square = NODES * NODES
    per_plane = square * layers
    unit = 2 * per_plane
    half = lanes // 2

    def body(x_ref, *refs):
        o_ref, mid = refs[-2:]
        low = lanes_of((8, lanes)) < half

        def read(d, n):
            return x_ref[d, n] if len(x_ref.shape) == 4 else x_ref[d, 0, n]

        def layer(e, carry):
            for n in range(square):
                left, right = (read(2 * e, n), read(2 * e + 1, n))
                mid[n * layers + e] = jnp.where(low, left, pltpu.roll(right, half, 1))
                mid[per_plane + n * layers + e] = jnp.where(low, pltpu.roll(left, half, 1), right)
            return carry

        lax.fori_loop(0, layers, layer, 0)

        def write(t, r, tile):
            o_ref[rows_at(r, unit, t), :] = tile

        turn_all(lambda k, t: mid[8 * t + k], write, unit // 8)

    extra = [] if buffer is None else [buffer]
    return call(
        body,
        (2,),
        [spec] + [pl.BlockSpec(memory_space=pl.ANY)] * len(extra),
        pl.BlockSpec((8 * unit, lanes), lambda i: (slots[0] + i * slots[1], 0)),
        jax.ShapeDtypeStruct((total, lanes), jnp.float32),
        scratch=[pltpu.VMEM((unit, 8, lanes), jnp.float32)],
        moved=4 * 8 * unit * lanes * 4,
        aliases={1: 0} if extra else None,
    )(blocks, *extra)


def paired_nodes():
    return [(b, min(b + 1, NODES - 1)) for b in range(0, NODES, 2)]


def three_pass(table, rhs_ref, tiles):
    rows, lanes = tiles[0].shape
    half = lanes // 2
    low = lanes_of((rows, lanes)) < half
    depth = 2 * rows
    for place, (one, two) in enumerate(paired_nodes()):
        first, second = (tiles[one], tiles[two])
        cut = pl.ds(place * lanes, lanes)
        for part in range(2):
            if part == 0:
                value = jnp.where(low, first, pltpu.roll(second, half, 1))
            else:
                value = jnp.where(low, pltpu.roll(first, half, 1), second)
            high = value.astype(jnp.bfloat16)
            rest = (value - high.astype(jnp.float32)).astype(jnp.bfloat16)
            rhs_ref[pl.ds(part * rows, rows), cut] = high
            rhs_ref[pl.ds(depth + part * rows, rows), cut] = rest
            rhs_ref[pl.ds(2 * depth + part * rows, rows), cut] = high
    out = jnp.dot(table, rhs_ref[...], preferred_element_type=jnp.float32)
    fields = []
    for field in range(table.shape[0] // depth):
        nodes = [None] * NODES
        for place, (one, two) in enumerate(paired_nodes()):
            cut = slice(place * lanes, (place + 1) * lanes)
            top = out[field * depth : field * depth + rows, cut]
            bottom = out[field * depth + rows : (field + 1) * depth, cut]
            nodes[one] = jnp.where(low, top, pltpu.roll(bottom, half, 1))
            if two != one:
                nodes[two] = jnp.where(low, pltpu.roll(top, half, 1), bottom)
        fields.append(nodes)
    return fields


def rhs_scratch(table, lanes):
    return pltpu.VMEM((table.shape[1], len(paired_nodes()) * lanes), jnp.bfloat16)


def read_tiles(x_ref, rows, lanes):
    return [x_ref[:, b].reshape(rows, lanes) for b in range(NODES)]


def to_points(blocks, table):
    shares, square, pairs, lanes = blocks.shape
    rows = shares * pairs

    def body(t_ref, x_ref, v_ref, z_ref, rhs_ref):
        fields = three_pass(t_ref[...], rhs_ref, read_tiles(x_ref, rows, lanes))
        for b in range(NODES):
            v_ref[b] = fields[0][b]
            z_ref[b] = fields[1][b]

    spec = pl.BlockSpec((NODES, rows, lanes), lambda a: (a, 0, 0))
    shape = jax.ShapeDtypeStruct((square, rows, lanes), jnp.float32)
    return call(
        body,
        (NODES,),
        [
            whole(table.shape),
            pl.BlockSpec((shares, NODES, pairs, lanes), lambda a: (0, a, 0, 0)),
        ],
        [spec, spec],
        [shape, shape],
        scratch=[rhs_scratch(table, lanes)],
        flops=2 * table.shape[0] * table.shape[1] * square * lanes,
        grant=WHOLE_GRANT,
        moved=3 * square * rows * lanes * 4,
    )(table, blocks)


def turn_around(blocks, partial, slope_z, table, back):
    shares, square, pairs, lanes = blocks.shape
    rows = shares * pairs

    def body(t_ref, i_ref, x_ref, g_ref, s_ref, w_ref, z_ref, o_ref, rhs_ref):
        fields = three_pass(t_ref[...], rhs_ref, read_tiles(x_ref, rows, lanes))
        for b in range(NODES):
            w_ref[b] = fields[0][b]
            z_ref[b] = fields[1][b]
        tiles = [g_ref[b] + w_ref[b] * s_ref[b] for b in range(NODES)]
        out = three_pass(i_ref[...], rhs_ref, tiles)[0]
        for b in range(NODES):
            o_ref[:, b] = out[b].reshape(shares, pairs, lanes)

    spec = pl.BlockSpec((NODES, rows, lanes), lambda a: (a, 0, 0))
    shape = jax.ShapeDtypeStruct((square, rows, lanes), jnp.float32)
    exchanged = pl.BlockSpec((shares, NODES, pairs, lanes), lambda a: (0, a, 0, 0))
    return call(
        body,
        (NODES,),
        [whole(table.shape), whole(back.shape), exchanged, spec, spec],
        [spec, spec, exchanged],
        [shape, shape, jax.ShapeDtypeStruct(blocks.shape, jnp.float32)],
        scratch=[rhs_scratch(table, lanes)],
        flops=3 * table.shape[0] * table.shape[1] * square * lanes,
        grant=WHOLE_GRANT,
        moved=6 * square * rows * lanes * 4,
    )(table, back, blocks, partial, slope_z)


def in_plane(speeds, fields, metrics, table):
    square, rows, lanes = speeds[0].shape
    count = len(fields)
    step = 32
    own = [i for i, f in enumerate(fields) if all(f is not s for s in speeds)]
    arrays = list(speeds) + [fields[i] for i in own]

    def body(m_ref, *refs):
        ins, outs = (refs[: len(arrays)], refs[len(arrays) :])
        u_ref, v_ref = ins[:2]
        sources = []
        extra = 2
        for i, f in enumerate(fields):
            if i in own:
                sources.append(ins[extra])
                extra += 1
            else:
                sources.append(u_ref if f is speeds[0] else v_ref)

        def block(s, carry):
            r = pl.ds(s * 8, 8)

            def metric(kind, n):
                return row_of(m_ref, kind * square + n, 8)

            for a in range(NODES):
                ns = [a * NODES + b for b in range(NODES)]
                drift = [
                    u_ref[n, r] * metric(2, n) + v_ref[n, r] * metric(3, n) for n in ns
                ]
                for f in range(count):
                    beside = apply_line(table, [sources[f][n, r] for n in ns])
                    for b, n in enumerate(ns):
                        outs[f][n, r] = drift[b] * beside[b]
            for b in range(NODES):
                ns = [a * NODES + b for a in range(NODES)]
                drift = [
                    u_ref[n, r] * metric(0, n) + v_ref[n, r] * metric(1, n) for n in ns
                ]
                for f in range(count):
                    radial = apply_line(table, [sources[f][n, r] for n in ns])
                    for a, n in enumerate(ns):
                        outs[f][n, r] = outs[f][n, r] + drift[a] * radial[a]
            return carry

        lax.fori_loop(0, step // 8, block, 0)

    spec = pl.BlockSpec((square, step, lanes), lambda i: (0, i, 0))
    shape = jax.ShapeDtypeStruct((square, rows, lanes), jnp.float32)
    return call(
        body,
        (rows // step,),
        [whole(metrics.shape)] + [spec] * len(arrays),
        [spec] * count,
        [shape] * count,
        flops=30 * count * square * rows * lanes,
        grant=WHOLE_GRANT,
        moved=(len(arrays) + count) * square * rows * lanes * 4,
    )(metrics, *arrays)


def to_planes(partial, speed_z, slope_z, table, shares, place, buffers):
    square, rows, lanes = partial.shape
    pairs = rows // shares
    group = pairs // 2

    def body(t_ref, g_ref, w_ref, z_ref, *refs):
        outs, rhs_ref = (refs[-3:-1], refs[-1])
        tiles = [g_ref[b] + w_ref[b] * z_ref[b] for b in range(NODES)]
        nodes = three_pass(t_ref[...], rhs_ref, tiles)[0]
        for b in range(NODES):
            out = nodes[b].reshape(shares, pairs, lanes)
            for i in range(2):
                outs[i][:, 0, b] = out[:, i * group : (i + 1) * group]

    spec = pl.BlockSpec((NODES, rows, lanes), lambda a: (a, 0, 0))
    out_spec = pl.BlockSpec((shares, 1, NODES, group, lanes), lambda a: (0, place, a, 0, 0))
    shape = jax.ShapeDtypeStruct((shares, 2, square, group, lanes), jnp.float32)
    return call(
        body,
        (NODES,),
        [whole(table.shape), spec, spec, spec]
        + [pl.BlockSpec(memory_space=pl.ANY)] * len(buffers),
        [out_spec, out_spec],
        [shape, shape],
        scratch=[rhs_scratch(table, lanes)],
        flops=2 * table.shape[0] * table.shape[1] * square * lanes,
        grant=WHOLE_GRANT,
        moved=4 * square * rows * lanes * 4,
        aliases={4: 0, 5: 1} if buffers else None,
    )(table, partial, speed_z, slope_z, *buffers)


def first_part(sent, returned, metrics, table):
    shares, square, pairs, lanes = sent.shape

    def body(m_ref, s0, r0, o_ref, p0):
        d = pl.program_id(0)

        def block(s, carry):
            r = pl.ds(s * 8, 8)
            for n in range(square):
                p0[n] = s0[0, n, r] + time_step * r0[0, n, r]

            def metric(kind, n):
                return row_of(m_ref, (kind * shares + d) * square + n, 8)

            for a in range(NODES):
                ns = [a * NODES + b for b in range(NODES)]
                line = apply_line(table, [p0[n] for n in ns])
                for b, n in enumerate(ns):
                    o_ref[0, n, r] = metric(2, n) * line[b]
            for b in range(NODES):
                ns = [a * NODES + b for a in range(NODES)]
                line = apply_line(table, [p0[n] for n in ns])
                for a, n in enumerate(ns):
                    o_ref[0, n, r] = o_ref[0, n, r] + metric(0, n) * line[a]
            return carry

        lax.fori_loop(0, pairs // 8, block, 0)

    spec = pl.BlockSpec((1, square, pairs, lanes), lambda d: (d, 0, 0, 0))
    return call(
        body,
        (shares,),
        [whole(metrics.shape), spec, spec],
        spec,
        jax.ShapeDtypeStruct(sent.shape, jnp.float32),
        scratch=[pltpu.VMEM((square, 8, lanes), jnp.float32)],
        flops=30 * shares * square * pairs * lanes,
        grant=WHOLE_GRANT,
        moved=3 * shares * square * pairs * lanes * 4,
    )(metrics, sent, returned)


def join_layers(y_ref, layers):
    square = NODES * NODES
    last = (NODES - 1) * NODES
    for e in range(layers - 1):
        for b in range(NODES):
            upper, lower = (e * square + last + b, (e + 1) * square + b)
            total = y_ref[upper] + y_ref[lower]
            y_ref[upper] = total
            y_ref[lower] = total
    for b in range(NODES):
        node = (layers - 1) * square + last + b
        y_ref[node] = jnp.zeros_like(y_ref[node])


def rim_messages(read, layers, shape, partials):
    lane = lanes_of(shape)
    lanes = shape[-1]
    axis = len(shape) - 1
    first = jnp.zeros(shape, jnp.float32)
    last = jnp.zeros(shape, jnp.float32)
    square = NODES * NODES
    for e in range(layers):
        for a in range(NODES):
            spot = e * NODES + a
            here = lane == spot
            node = e * square + a * NODES
            first = jnp.where(here, pltpu.roll(read(node), spot, axis), first)
            last = jnp.where(
                here, pltpu.roll(read(node + NODES - 1), (spot + 1) % lanes, axis), last
            )
    for i, partial in enumerate(partials):
        here = lane == layers * NODES + i
        first = jnp.where(here, partial, first)
        last = jnp.where(here, partial, last)
    return (first, last)


def right_side(flat, sent, returned, metrics, weights, waves, table, layers, place):
    shares, square, _, lanes = flat.shape
    half = lanes // 2

    def body(m_ref, q_ref, k_ref, f_ref, s1, s2, r_ref, o_ref, first_ref, last_ref, p1, c0, c1):
        e = pl.program_id(0)
        lane = lanes_of((8, lanes))
        low = lane < half
        wave = k_ref[...]
        sides = (c0, c1)

        @pl.when(e == 0)
        def _():
            first_ref[...] = jnp.zeros_like(first_ref)
            last_ref[...] = jnp.zeros_like(last_ref)

        for h in range(2):
            d = 2 * e + h
            side = sides[h]
            for n in range(square):
                p1[n] = s1[h, n] + time_step * r_ref[h, 0, n]
                moved = s2[h, n] + time_step * r_ref[h, 1, n]
                along = pltpu.roll(moved, half, 1) * wave
                side[n] = f_ref[h, n] + row_of(q_ref, d * square + n, 8) * along

            def metric(kind, n):
                return row_of(m_ref, (kind * shares + d) * square + n, 8)

            for a in range(NODES):
                ns = [a * NODES + b for b in range(NODES)]
                line = apply_line(table, [p1[n] for n in ns])
                for b, n in enumerate(ns):
                    side[n] = side[n] + metric(3, n) * line[b]
            for b in range(NODES):
                ns = [a * NODES + b for a in range(NODES)]
                line = apply_line(table, [p1[n] for n in ns])
                for a, n in enumerate(ns):
                    side[n] = side[n] + metric(1, n) * line[a]
        rims = [[first_ref[0], last_ref[0]], [first_ref[1], last_ref[1]]]
        for n in range(square):
            left, right = (c0[n], c1[n])
            parts = (
                jnp.where(low, left, pltpu.roll(right, half, 1)),
                jnp.where(low, pltpu.roll(left, half, 1), right),
            )
            for i in range(2):
                o_ref[n, i] = parts[i]
                a, b = divmod(n, NODES)
                spot = e * NODES + a
                if b == 0:
                    rims[i][0] = jnp.where(lane == spot, pltpu.roll(parts[i], spot, 1), rims[i][0])
                if b == NODES - 1:
                    rims[i][1] = jnp.where(
                        lane == spot, pltpu.roll(parts[i], spot + 1, 1), rims[i][1]
                    )
        for i in range(2):
            first_ref[i] = rims[i][0]
            last_ref[i] = rims[i][1]

    spec = pl.BlockSpec((2, square, 8, lanes), lambda e: (e, 0, place, 0))
    nodes = layers * square
    rim_shape = jax.ShapeDtypeStruct((2, 8, lanes), jnp.float32)
    scratch = pltpu.VMEM((square, 8, lanes), jnp.float32)
    return call(
        body,
        (layers,),
        [
            whole(metrics.shape),
            whole(weights.shape),
            pl.BlockSpec((8, lanes), lambda e: (place, 0)),
            spec,
            spec,
            spec,
            pl.BlockSpec((2, 2, square, 8, lanes), lambda e: (e, 0, 0, 0, 0)),
        ],
        [
            pl.BlockSpec((square, 2, 8, lanes), lambda e: (e, 0, 0, 0)),
            whole((2, 8, lanes)),
            whole((2, 8, lanes)),
        ],
        [jax.ShapeDtypeStruct((nodes, 2, 8, lanes), jnp.float32), rim_shape, rim_shape],
        scratch=[scratch] * 3,
        flops=40 * shares * square * 8 * lanes,
        grant=WHOLE_GRANT,
        moved=6 * shares * square * 8 * lanes * 4,
    )(metrics, weights, waves, flat, sent[1], sent[2], returned)


def swap_rims(first, last):
    size = lax.axis_size("elem")
    up = [(i, (i + 1) % size) for i in range(size)]
    down = [(j, i) for i, j in up]
    return (lax.ppermute(last, "elem", up), lax.ppermute(first, "elem", down))


def opposite(first):
    size = lax.axis_size("elem")
    return lax.ppermute(first, "elem", [(i, (i + 2) % size) for i in range(size)])


def join_columns(read, ref, before, after, layers):
    lanes = before.shape[-1]
    axis = len(before.shape) - 1
    lane = lanes_of(before.shape)
    square = NODES * NODES
    for e in range(layers):
        for a in range(NODES):
            spot = e * NODES + a
            node = e * square + a * NODES
            first, last = (read(node), read(node + NODES - 1))
            beyond = pltpu.roll(after, lanes - 1 - spot, axis)
            ahead = jnp.where(lane == lanes - 1, beyond, pltpu.roll(first, lanes - 1, axis))
            right = last + ahead
            mine = first + (pltpu.roll(before, lanes - spot, axis) if spot else before)
            ref[node + NODES - 1] = right
            ref[node] = jnp.where(lane == 0, mine, pltpu.roll(right, 1, axis))


def join(source, ref, before, after, layers):
    square = NODES * NODES

    def copy(e, carry):
        for n in range(square):
            if 0 < n % NODES < NODES - 1:
                ref[e * square + n] = source[e * square + n]
        return carry

    lax.fori_loop(0, layers, copy, 0)
    join_columns(lambda n: source[n], ref, before, after, layers)
    join_layers(ref, layers)


def each_node(layers, step):
    def layer(e, carry):
        for n in range(NODES * NODES):
            step(e * NODES * NODES + n)
        return carry

    lax.fori_loop(0, layers, layer, 0)


def share_of(layers, e, a):
    if a == 0:
        return jnp.where(e > 0, 0.5, 1.0)
    if a == NODES - 1:
        return jnp.where(e < layers - 1, 0.5, 0.0)
    return 1.0


def helmholtz(r_ref, y_ref, flux_ref, g_ref, shift, layers, table, dot_only=False):
    square = NODES * NODES
    nodes = layers * square
    turned = table.T
    zero = jnp.zeros(shift.shape, jnp.float32)

    def layer(e, carry):
        norm, energy = carry
        base = e * square

        def metric(kind, n):
            return row_of(g_ref, kind * nodes + base + n, 8)

        for b in range(NODES):
            ns = [a * NODES + b for a in range(NODES)]
            radial = apply_line(table, [r_ref[base + n] for n in ns])
            for a, n in enumerate(ns):
                flux_ref[n] = radial[a]
        for a in range(NODES):
            ns = [a * NODES + b for b in range(NODES)]
            line = [r_ref[base + n] for n in ns]
            beside = apply_line(table, line)
            second = []
            rest = []
            part = zero
            for b, n in enumerate(ns):
                radial = flux_ref[n]
                cross = metric(1, n)
                one = metric(0, n) * radial + cross * beside[b]
                two = cross * radial + metric(2, n) * beside[b]
                same = shift * metric(3, n) * line[b]
                whole_weight = line[b] * line[b]
                part = part + (0.5 * whole_weight if b in (0, NODES - 1) else whole_weight)
                if dot_only:
                    energy = energy + (radial * one + beside[b] * two + same * line[b])
                else:
                    flux_ref[n] = one
                    second.append(two)
                    rest.append(same)
            norm = norm + part * share_of(layers, e, a)
            if not dot_only:
                back = apply_line(turned, second)
                for b, n in enumerate(ns):
                    y_ref[base + n] = rest[b] + back[b]
        if not dot_only:
            for b in range(NODES):
                ns = [a * NODES + b for a in range(NODES)]
                back = apply_line(turned, [flux_ref[n] for n in ns])
                for a, n in enumerate(ns):
                    value = y_ref[base + n] + back[a]
                    y_ref[base + n] = value
                    energy = energy + value * r_ref[base + n]
        return (norm, energy)

    norm, energy = lax.fori_loop(0, layers, layer, (zero, zero))
    axis = len(shift.shape) - 1
    return (
        jnp.sum(norm, axis=axis, keepdims=True),
        jnp.sum(energy, axis=axis, keepdims=True),
    )


def lane_value(block, lane):
    return block[..., lane : lane + 1]


def sums_from(own, left, right, far, layers):
    total = (own[...] + far[...]) + (left[...] + right[...])
    spot = layers * NODES
    return (lane_value(total, spot), lane_value(total, spot + 1))


def scalars_block(shape, values, spot=0):
    lane = lanes_of(shape)
    out = jnp.zeros(shape, jnp.float32)
    for i, value in enumerate(values):
        out = jnp.where(lane == spot + i, value, out)
    return out


def shapes_of(field):
    return (
        jax.ShapeDtypeStruct(field.shape, jnp.float32),
        jax.ShapeDtypeStruct(field.shape[1:], jnp.float32),
        pltpu.VMEM((NODES * NODES,) + field.shape[1:], jnp.float32),
    )


def first_image(raw, before, after, shift, geo, layers, table):
    field, small, flux_scratch = shapes_of(raw)
    shape = raw.shape[1:]

    def body(g_ref, k_ref, f_ref, b_ref, a_ref, r_ref, y_ref, first_ref, last_ref, flux):
        join(f_ref, r_ref, b_ref[...], a_ref[...], layers)
        sums = helmholtz(r_ref, y_ref, flux, g_ref, k_ref[...], layers, table)
        first_ref[...], last_ref[...] = rim_messages(lambda n: y_ref[n], layers, shape, sums)

    return call(
        body,
        (),
        held(5),
        held(4),
        [field, field, small, small],
        scratch=[flux_scratch],
        flops=80 * raw.size,
        moved=12 * raw.size,
    )(geo, shift, raw, before, after)


def second_image(start, image, messages, shift, geo, layers, table):
    field, small, flux_scratch = shapes_of(start)
    shape = start.shape[1:]

    def body(g_ref, k_ref, r0, y0, own, left, right, far, *rest):
        w_ref, y_ref, first_ref, last_ref, scalar_ref, r1, flux = rest
        norm, energy = sums_from(own, left, right, far, layers)
        alpha = jnp.broadcast_to(norm / energy, shape)
        join(y0, w_ref, left[...], right[...], layers)

        def move(node):
            r1[node] = r0[node] - alpha * w_ref[node]

        each_node(layers, move)
        sums = helmholtz(r1, y_ref, flux, g_ref, k_ref[...], layers, table)
        first_ref[...], last_ref[...] = rim_messages(lambda n: y_ref[n], layers, shape, sums)
        scalar_ref[...] = scalars_block(shape, (alpha, norm, energy))

    return call(
        body,
        (),
        held(8),
        held(5),
        [field, field, small, small, small],
        scratch=[pltpu.VMEM(start.shape, jnp.float32), flux_scratch],
        flops=80 * start.size,
        moved=16 * start.size,
    )(geo, shift, start, image, *messages)


def third_energy(start, joined, image, messages, scalars, shift, geo, layers, table):
    field, small, flux_scratch = shapes_of(start)
    shape = start.shape[1:]

    def body(g_ref, k_ref, r0, w0, y1, own, left, right, far, old, *rest):
        r2, d2, sums_ref, scalar_ref, w1, flux = rest
        norm, energy = sums_from(own, left, right, far, layers)
        before = old[...]
        alpha = jnp.broadcast_to(lane_value(before, 0), shape)
        ratio = norm / lane_value(before, 1)
        curve = energy - ratio * ratio * lane_value(before, 2)
        step = jnp.broadcast_to(norm / curve, shape)
        beta = jnp.broadcast_to(ratio, shape)
        join(y1, w1, left[...], right[...], layers)

        def move(node):
            w = w0[node]
            start_value = r0[node]
            moved = start_value - alpha * w
            d2[node] = moved + beta * start_value
            r2[node] = moved - step * (w1[node] + beta * w)

        each_node(layers, move)
        sums = helmholtz(r2, None, flux, g_ref, k_ref[...], layers, table, dot_only=True)
        sums_ref[...] = scalars_block(shape, sums, layers * NODES)
        scalar_ref[...] = scalars_block(shape, (alpha, norm, curve, step))

    return call(
        body,
        (),
        held(10),
        held(4),
        [field, field, small, small],
        scratch=[pltpu.VMEM(start.shape, jnp.float32), flux_scratch],
        flops=60 * start.size,
        moved=20 * start.size,
    )(geo, shift, start, joined, image, *messages, scalars)


def finish(start, direction, residual, messages, scalars, layers, place, buffer, total):
    nodes, _, rows, lanes = start.shape
    shape = start.shape[1:]
    square = NODES * NODES

    unit = 2 * nodes

    def body(r0, d2, r2, own, left, right, far, old, *refs):
        o_ref, mid = refs[-2:]
        norm, energy = sums_from(own, left, right, far, layers)
        before = old[...]
        ratio = norm / lane_value(before, 1)
        curve = energy - ratio * ratio * lane_value(before, 2)
        step = norm / curve
        third = jnp.broadcast_to(step, shape)
        second = jnp.broadcast_to(lane_value(before, 3) + step * ratio, shape)
        first = jnp.broadcast_to(lane_value(before, 0), shape)

        def layer(e, carry):
            for n in range(square):
                node = e * square + n
                value = first * r0[node] + second * d2[node] + third * r2[node]
                for i in range(2):
                    mid[i * nodes + n * layers + e] = value[i]
            return carry

        lax.fori_loop(0, layers, layer, 0)

        def write(t, r, tile):
            o_ref[rows_at(r, unit, t), :] = tile

        turn_all(lambda k, t: mid[8 * t + k], write, unit // 8)

    extra = [] if buffer is None else [buffer]
    return call(
        body,
        (1,),
        [whole(start.shape)] * 3
        + [whole(shape)] * 5
        + [pl.BlockSpec(memory_space=pl.ANY)] * len(extra),
        pl.BlockSpec((2 * rows * nodes, lanes), lambda i: (place, 0)),
        jax.ShapeDtypeStruct((total, lanes), jnp.float32),
        scratch=[pltpu.VMEM((unit, rows, lanes), jnp.float32)],
        flops=6 * start.size,
        moved=16 * start.size,
        aliases={8: 0} if extra else None,
    )(start, direction, residual, *messages, scalars, *extra)


def halves(values, shares):
    half = values.shape[-1] // 2
    parts = [jnp.concatenate([p, p], axis=-1) for p in (values[..., :half], values[..., half:])]
    return jnp.stack(parts, axis=2).reshape(values.shape[0], shares, NODES * NODES, 2 * half)


def on_device_paired(*arrays):
    return paired_step(*arrays)


def paired_step(velocity, radial_dx, radial_dy, around_dx, around_dy, jacobian):
    table = derivative_table()
    modes = lax.axis_size("mode")
    mode = lax.axis_index("mode")
    _, local_planes, layers, _, _, lanes = velocity.shape
    planes = local_planes * modes
    pairs = local_planes // 2
    first_plane = mode * local_planes
    square = NODES * NODES
    forward, backward = (jnp.asarray(t) for t in paired_tables(planes))

    rows = velocity.transpose(0, 1, 3, 4, 2, 5).reshape(3, local_planes * square * layers, lanes)
    plain = jnp.stack([radial_dx, radial_dy, around_dx, around_dy]).reshape(
        4, layers, square, lanes
    )
    both = halves(plain, modes)
    here = lax.dynamic_index_in_dim(both, mode, 1, keepdims=False).reshape(4 * square, lanes)
    metrics = geometry(radial_dx, radial_dy, around_dx, around_dy, jacobian)
    geo = jnp.stack(metrics).reshape(4 * layers * square, lanes)
    scaled = halves((metrics[3] * (-1.0 / time_step)).reshape(1, layers, square, lanes), modes)
    flux = (both * scaled).reshape(4 * modes * square, lanes)
    scaled = scaled.reshape(modes * square, lanes)
    pair = (first_plane // 2 + jnp.arange(pairs, dtype=jnp.int32)).astype(jnp.float32)
    wave = pair[:, None] * spanwise_wave
    low = (jnp.arange(lanes) < lanes // 2)[None, :]
    waves = jnp.where(low, wave, -wave)
    shift = plane_shift(first_plane, local_planes, planes).reshape(pairs, 2).T
    shift = jnp.broadcast_to(shift.reshape(2, 2, pairs // 2, 1), (2, 2, pairs // 2, lanes))

    def exchange(blocks):
        return lax.all_to_all(blocks, "mode", split_axis=0, concat_axis=0, tiled=True)

    sent = [pack(rows, comp, layers, pairs, lanes) for comp in range(3)]
    arrived = [exchange(blocks) for blocks in sent]
    speed_x, slope_0 = to_points(arrived[0], forward)
    speed_y, slope_1 = to_points(arrived[1], forward)
    speeds = [speed_x, speed_y]
    partial = in_plane(speeds, speeds, here, table)
    speed_z, slope_2, blocks = turn_around(arrived[2], partial[0], slope_0, forward, backward)
    returned = [exchange(blocks)]
    last = in_plane(speeds, [speed_z], here, table)[0]
    blocks = to_planes(partial[1], speed_z, slope_1, backward, modes, 0, ())
    blocks = to_planes(last, speed_z, slope_2, backward, modes, 1, blocks)
    returned.append(exchange(blocks[0]))
    returned.append(exchange(blocks[1]))

    group = pairs // 2
    own_rows = local_planes * square * layers
    whole_spec = pl.BlockSpec((modes, square, group, lanes), lambda i: (0, 0, i, 0))
    part_spec = pl.BlockSpec((modes, 1, square, group, lanes), lambda i: (0, i, 0, 0, 0))
    advection = unpack(returned[0], whole_spec, (0, 1), layers, None, 3 * own_rows)
    flat = first_part(sent[0], returned[0], flux, table)

    def solve(place, flat, buffer):
        own_shift = shift[:, place]
        raw, first, last = right_side(
            flat, sent, returned[1 + place], flux, scaled, waves, table, layers, place
        )
        before, after = swap_rims(first, last)
        start, image, first, last = first_image(raw, before, after, own_shift, geo, layers, table)
        messages = (first,) + swap_rims(first, last) + (opposite(first),)
        joined, image, first, last, scalars = second_image(
            start, image, messages, own_shift, geo, layers, table
        )
        messages = (first,) + swap_rims(first, last) + (opposite(first),)
        residual, direction, sums, scalars = third_energy(
            start, joined, image, messages, scalars, own_shift, geo, layers, table
        )
        messages = (sums,) + swap_rims(sums, sums) + (opposite(sums),)
        return finish(
            start, direction, residual, messages, scalars, layers, place, buffer, own_rows
        )

    pressure = solve(0, flat, None)
    advection = unpack(returned[1], part_spec, (2, 2), layers, advection, 3 * own_rows)
    flat, pressure, advection = lax.optimization_barrier((flat, pressure, advection))
    pressure = solve(1, flat, pressure)
    advection = unpack(returned[2], part_spec, (3, 2), layers, advection, 3 * own_rows)
    advection = advection.reshape(3, local_planes, NODES, NODES, layers, lanes)
    pressure = pressure.reshape(local_planes, NODES, NODES, layers, lanes)
    return (advection.transpose(0, 1, 4, 2, 3, 5), pressure.transpose(0, 3, 1, 2, 4))


def paired_fits(mesh, shape):
    modes, ring = (mesh.shape["mode"], mesh.shape["elem"])
    _, planes, layers, _, _, columns = shape
    return (
        ring == 4
        and columns == 128 * ring
        and modes == 2 * layers
        and layers % 4 == 0
        and planes == 32 * modes
        and (layers * NODES + 2 <= 128)
    )


def solution(mesh):
    placed = (
        P(None, "mode", None, None, None, "elem"),
        P(None, None, None, "elem"),
        P(None, None, None, "elem"),
        P(None, None, None, "elem"),
        P(None, None, None, "elem"),
        P(None, None, None, "elem"),
    )


    def step(velocity, *rest):
        body = on_device_paired if paired_fits(mesh, velocity.shape) else on_device
        return jax.shard_map(
            body,
            mesh=mesh,
            in_specs=placed,
            out_specs=(
                P(None, "mode", None, None, None, "elem"),
                P("mode", None, None, None, "elem"),
            ),
            check_vma=False,
        )(velocity, *rest)

    return step
```

```python
import functools
import math

import jax
import jax.numpy as jnp
import numpy as np
from jax import lax
from jax.experimental import pallas as pl
from jax.experimental.pallas import tpu as pltpu
from jax.sharding import PartitionSpec as P

NODES = 7
ITERS = 3
GRANT = 24 * 2**20
WHOLE_GRANT = 67043328


spanwise_wave = 2.0 * math.pi / 64.0
time_step = 0.1


def padded_2(value, sides, width):
    for axis, dim in sides:
        size, length = (lax.axis_size(axis), value.shape[dim])
        up = [(i, (i + 1) % size) for i in range(size)]
        down = [(j, i) for i, j in up]
        last = lax.slice_in_dim(value, length - width, length, axis=dim)
        leading = lax.slice_in_dim(value, 0, width, axis=dim)
        before = lax.ppermute(last, axis, up)
        after = lax.ppermute(leading, axis, down)
        value = jnp.concatenate([before, value, after], axis=dim)
    return value


def lobatto_rule(count):
    degree = count - 1
    points = np.cos(np.pi * np.arange(count) / degree)
    legendre = np.zeros((count, count))
    for _ in range(60):
        legendre[:, 0] = 1.0
        legendre[:, 1] = points
        for order in range(2, count):
            legendre[:, order] = (
                (2 * order - 1) * points * legendre[:, order - 1]
                - (order - 1) * legendre[:, order - 2]
            ) / order
        points = points - (points * legendre[:, degree] - legendre[:, degree - 1]) / (
            count * legendre[:, degree]
        )
    legendre[:, 0] = 1.0
    legendre[:, 1] = points
    for order in range(2, count):
        legendre[:, order] = (
            (2 * order - 1) * points * legendre[:, order - 1] - (order - 1) * legendre[:, order - 2]
        ) / order
    weights = 2.0 / (degree * count * legendre[:, degree] ** 2)
    return (points[::-1].copy(), weights[::-1].copy())


def derivative_table():
    lobatto_nodes = lobatto_rule(NODES)[0]
    total = lobatto_nodes.shape[0]
    scales = np.ones(total)
    for column in range(total):
        for other in range(total):
            if other != column:
                scales[column] = scales[column] / (lobatto_nodes[column] - lobatto_nodes[other])
    table = np.zeros((total, total))
    for row in range(total):
        for column in range(total):
            if row != column:
                table[row, column] = (
                    scales[column] / scales[row] / (lobatto_nodes[row] - lobatto_nodes[column])
                )
        table[row, row] = -np.sum(table[row])
    return table


def radial_derivative(table, field):
    return jnp.einsum("ia,...abe->...ibe", table, field, precision=lax.Precision.HIGHEST)


def around_derivative(table, field):
    return jnp.einsum("jb,...abe->...aje", table, field, precision=lax.Precision.HIGHEST)


def radial_transpose(table, field):
    return jnp.einsum("ia,...ibe->...abe", table, field, precision=lax.Precision.HIGHEST)


def around_transpose(table, field):
    return jnp.einsum("jb,...aje->...abe", table, field, precision=lax.Precision.HIGHEST)


def z_derivative(field, first_pair):
    shape = field.shape
    count = shape[1] // 2
    pairs = field.reshape((shape[0], count, 2) + shape[2:])
    waves = (first_pair + jnp.arange(count, dtype=jnp.int32)).astype(jnp.float32) * spanwise_wave
    waves = waves.reshape((1, count) + (1,) * (len(shape) - 2))
    return jnp.stack([waves * pairs[:, :, 1], -waves * pairs[:, :, 0]], axis=2).reshape(shape)


def transform_tables(planes):
    position = jnp.arange(planes, dtype=jnp.int32)
    plane = jnp.arange(planes, dtype=jnp.int32)
    order = plane // 2
    turns = position[:, None] * order[None, :] % planes
    angle = 2.0 * math.pi / planes * turns.astype(jnp.float32)
    cosine = jnp.cos(angle)
    sine = jnp.sin(angle)
    is_sine = (plane % 2 == 1)[None, :]
    is_top = (plane == 1)[None, :]
    parity = jnp.cos(math.pi * (position % 2).astype(jnp.float32))[:, None]
    basis = jnp.where(is_top, parity, jnp.where(is_sine, sine, cosine))
    scaling = jnp.where(order == 0, 1.0, 2.0).astype(jnp.float32) / planes
    inverse = jnp.transpose(basis * scaling[None, :])
    wave = (order.astype(jnp.float32) * spanwise_wave)[None, :]
    slope = jnp.where(is_sine, wave * cosine, -wave * sine)
    return (basis, inverse, slope)


def geometry(radial_dx, radial_dy, around_dx, around_dy, jacobian):
    lobatto_weights = lobatto_rule(NODES)[1]
    quadrature = jnp.asarray(np.outer(lobatto_weights, lobatto_weights), jnp.float32)[:, :, None]
    mass = quadrature * jacobian
    radial_stiff = mass * (radial_dx * radial_dx + radial_dy * radial_dy)
    cross_stiff = mass * (radial_dx * around_dx + radial_dy * around_dy)
    around_stiff = mass * (around_dx * around_dx + around_dy * around_dy)
    return (radial_stiff, cross_stiff, around_stiff, mass)


def node_weights(layers):
    layer = jnp.arange(layers, dtype=jnp.int32).reshape(layers, 1, 1, 1)
    node = jnp.arange(NODES, dtype=jnp.int32)
    radial_node = node.reshape(1, NODES, 1, 1)
    around_node = node.reshape(1, 1, NODES, 1)
    shared_radial = (radial_node == NODES - 1) & (layer < layers - 1) | (radial_node == 0) & (
        layer > 0
    )
    shared_around = (around_node == 0) | (around_node == NODES - 1)
    multiplicity = (1.0 + shared_radial.astype(jnp.float32)) * (
        1.0 + shared_around.astype(jnp.float32)
    )
    boundary = (radial_node == NODES - 1) & (layer == layers - 1)
    mask = 1.0 - boundary.astype(jnp.float32)
    return (mask, mask / multiplicity)


def plane_shift(first_plane, count, planes):
    plane = first_plane + jnp.arange(count, dtype=jnp.int32)
    order = jnp.where(plane == 1, planes // 2, plane // 2)
    wave = order.astype(jnp.float32) * spanwise_wave
    return (wave * wave).reshape(count, 1, 1, 1, 1)


def helmholtz_local(table, field, shift, metrics):
    radial_stiff, cross_stiff, around_stiff, mass = metrics
    radial = radial_derivative(table, field)
    beside_all = around_derivative(table, field)
    return (
        radial_transpose(table, radial_stiff * radial + cross_stiff * beside_all)
        + around_transpose(table, cross_stiff * radial + around_stiff * beside_all)
        + shift * mass * field
    )


def assemble(field):
    lower = field[:, :-1, -1] + field[:, 1:, 0]
    field = field.at[:, :-1, -1].set(lower).at[:, 1:, 0].set(lower)
    first = field[:, :, :, 0]
    last = field[:, :, :, -1]
    rims = jnp.concatenate([first[..., :1], last[..., -1:]], axis=3)
    padded = padded_2(rims, (("elem", 3),), 1)
    after = jnp.concatenate([first[..., 1:], padded[..., 3:4]], axis=3)
    right = last + after
    left = jnp.concatenate([padded[..., 0:1] + first[..., :1], right[..., :-1]], axis=3)
    return field.at[:, :, :, -1].set(right).at[:, :, :, 0].set(left)


def inner(first, second, weight):
    return jnp.sum(first * second * weight, axis=(1, 2, 3, 4))


def expand(scalar):
    return scalar.reshape(-1, 1, 1, 1, 1)


def squared_norm(residual, weight):
    return lax.psum(inner(residual, residual, weight), "elem")


def on_device(velocity, radial_dx, radial_dy, around_dx, around_dy, jacobian):
    table = jnp.asarray(derivative_table(), jnp.float32)
    modes = lax.axis_size("mode")
    local_planes = velocity.shape[1]
    planes = local_planes * modes
    first_plane = lax.axis_index("mode") * local_planes
    layers = velocity.shape[2]
    columns = velocity.shape[5]
    basis, inverse, slope = transform_tables(planes)
    radial = radial_derivative(table, velocity)
    beside_all = around_derivative(table, velocity)
    along_x = radial_dx * radial + around_dx * beside_all
    along_y = radial_dy * radial + around_dy * beside_all
    fields = jnp.concatenate([velocity, along_x, along_y], axis=0)
    count = fields.shape[0]
    cells = layers * NODES * NODES * columns
    packed = fields.reshape(count, local_planes, modes, cells // modes)
    flat = lax.all_to_all(packed, "mode", split_axis=2, concat_axis=1, tiled=True)[:, :, 0, :]
    values = jnp.einsum("jp,fpc->fjc", basis, flat, precision=lax.Precision.HIGHEST)
    speed = values[0:3]
    slope_x = values[3:6]
    slope_y = values[6:9]
    slope_z = jnp.einsum("jp,fpc->fjc", slope, flat[0:3], precision=lax.Precision.HIGHEST)
    product = -(speed[0:1] * slope_x + speed[1:2] * slope_y + speed[2:3] * slope_z)
    spectral = jnp.einsum("pj,fjc->fpc", inverse, product, precision=lax.Precision.HIGHEST)
    returned = lax.all_to_all(
        spectral[:, :, None, :], "mode", split_axis=1, concat_axis=2, tiled=True
    )
    advection = returned.reshape(velocity.shape)
    metrics = geometry(radial_dx, radial_dy, around_dx, around_dy, jacobian)
    mask, weight = node_weights(layers)
    predicted = velocity + time_step * advection
    radial = radial_derivative(table, predicted[0:2])
    beside_all = around_derivative(table, predicted[0:2])
    divergence = (
        radial_dx * radial[0]
        + around_dx * beside_all[0]
        + (radial_dy * radial[1] + around_dy * beside_all[1])
        + z_derivative(predicted[2:3], first_plane // 2)[0]
    )
    shift = plane_shift(first_plane, local_planes, planes)
    right_side = mask * assemble(-(metrics[3] * divergence) / time_step)
    solution = jnp.zeros_like(right_side)
    residual = right_side
    direction = right_side
    norm_now = squared_norm(residual, weight)
    for _ in range(ITERS):
        image = mask * assemble(helmholtz_local(table, direction, shift, metrics))
        alpha = norm_now / lax.psum(inner(direction, image, weight), "elem")
        solution = solution + expand(alpha) * direction
        residual = residual - expand(alpha) * image
        norm_next = squared_norm(residual, weight)
        direction = residual + expand(norm_next / norm_now) * direction
        norm_now = norm_next
    return (advection, solution)


def split_bf16(table):
    high = table.astype(jnp.bfloat16)
    low = (table - high.astype(np.float64)).astype(jnp.bfloat16)
    return np.concatenate([high, high, low], axis=1)


def paired_tables(planes):
    position = np.arange(planes)
    plane = np.arange(planes)
    order = plane // 2
    angle = 2.0 * np.pi / planes * (position[:, None] * order[None, :] % planes)
    cosine, sine = (np.cos(angle), np.sin(angle))
    odd = (plane % 2 == 1)[None, :]
    parity = (1.0 - 2.0 * (position % 2))[:, None]
    basis = np.where((plane == 1)[None, :], parity, np.where(odd, sine, cosine))
    wave = (order * spanwise_wave)[None, :]
    slope = np.where(odd, wave * cosine, -wave * sine)
    scaling = np.where(order == 0, 1.0, 2.0) / planes
    inverse = -(basis * scaling[None, :]).T

    def columns(matrix):
        return np.concatenate([matrix[:, 0::2], matrix[:, 1::2]], axis=1)

    forward = np.concatenate([columns(basis), columns(slope)])
    backward = columns(inverse.T).T
    return (split_bf16(forward), split_bf16(backward))


def apply_line(matrix, line):
    n = NODES
    m = n // 2
    sums = [line[a] + line[n - 1 - a] for a in range(m)]
    gaps = [line[a] - line[n - 1 - a] for a in range(m)]

    def total(parts):
        out = parts[0]
        for part in parts[1:]:
            out = out + part
        return out

    out = [None] * n
    for i in range(m + 1):
        plus = total(
            [float(0.5 * (matrix[i, a] - matrix[i, n - 1 - a])) * gaps[a] for a in range(m)]
        )
        if i == m:
            out[i] = plus
            continue
        minus = total(
            [float(0.5 * (matrix[i, a] + matrix[i, n - 1 - a])) * sums[a] for a in range(m)]
            + [float(matrix[i, m]) * line[m]]
        )
        out[i] = plus + minus
        out[n - 1 - i] = plus - minus
    return out


def lanes_of(shape):
    return lax.broadcasted_iota(jnp.int32, shape, len(shape) - 1)


def row_of(ref, row, rows):
    return ref[pl.ds(row, rows, stride=0), :]


def call(body, grid, ins, outs, out_shape, scratch=(), flops=0, moved=0, aliases=None, grant=GRANT):
    return pl.pallas_call(
        body,
        grid=grid,
        in_specs=ins,
        out_specs=outs,
        out_shape=out_shape,
        scratch_shapes=list(scratch),
        input_output_aliases=aliases or {},
        compiler_params=pltpu.CompilerParams(
            dimension_semantics=("arbitrary",) * len(grid), vmem_limit_bytes=grant
        ),
        cost_estimate=pl.CostEstimate(
            flops=int(flops), bytes_accessed=int(moved), transcendentals=0
        ),
    )


def held(count):
    return [pl.BlockSpec(memory_space=pltpu.VMEM)] * count


def whole(shape):
    return pl.BlockSpec(shape, lambda *_: (0,) * len(shape))


def turn(tiles):
    tiles = list(tiles)
    sub = lax.broadcasted_iota(jnp.int32, tiles[0].shape, 0)
    size = len(tiles)
    step = size // 2
    while step:
        keep = (sub & step) == 0
        for i in range(size):
            if not i & step:
                one, two = (tiles[i], tiles[i + step])
                tiles[i] = jnp.where(keep, one, pltpu.roll(two, step, 0))
                tiles[i + step] = jnp.where(keep, pltpu.roll(one, size - step, 0), two)
        step //= 2
    return tiles


def turn_all(read, write, count):
    def some(s, carry):
        for i in range(NODES):
            t = s * NODES + i
            for r, tile in enumerate(turn([read(k, t) for k in range(8)])):
                write(t, r, tile)
        return carry

    lax.fori_loop(0, count // NODES, some, 0)


def rows_at(k, unit, t):
    return pl.ds(pl.multiple_of(k * unit + 8 * t, 8), 8)


def pack_one(x_ref, write_out, mid, layers, lanes):
    square = NODES * NODES
    per_plane = square * layers
    unit = 2 * per_plane
    half = lanes // 2
    low = lanes_of((8, lanes)) < half

    def write(t, r, tile):
        mid[8 * t + r] = tile

    turn_all(lambda k, t: x_ref[0, rows_at(k, unit, t), :], write, unit // 8)

    def layer(e, carry):
        for n in range(square):
            cos = mid[n * layers + e]
            sin = mid[per_plane + n * layers + e]
            write_out(2 * e, n, jnp.where(low, cos, pltpu.roll(sin, half, 1)))
            write_out(2 * e + 1, n, jnp.where(low, pltpu.roll(cos, half, 1), sin))
        return carry

    lax.fori_loop(0, layers, layer, 0)


def pack_specs(layers, pairs, lanes, nodes):
    return (
        pl.BlockSpec((2 * layers, nodes, 8, lanes), lambda g: (0, 0, g, 0)),
        jax.ShapeDtypeStruct((2 * layers, nodes, pairs, lanes), jnp.float32),
    )


def pack_first(rows, layers, pairs, lanes):
    square = NODES * NODES
    unit = 2 * square * layers

    def body(x_ref, o_ref, mid):
        def write(d, n, value):
            o_ref[d, n] = value

        pack_one(x_ref, write, mid, layers, lanes)

    spec, shape = pack_specs(layers, pairs, lanes, square)
    return call(
        body,
        (pairs // 8,),
        [pl.BlockSpec((1, 8 * unit, lanes), lambda g: (0, g, 0))],
        spec,
        shape,
        scratch=[pltpu.VMEM((unit, 8, lanes), jnp.float32)],
        grant=WHOLE_GRANT,
        moved=2 * rows.shape[1] * lanes * 4,
    )(rows)


def pack_rest(rows, layers, pairs, lanes, early):
    square = NODES * NODES
    unit = 2 * square * layers

    def body(x_ref, y_ref, o_ref, late_ref, whole_ref, mid):
        def first(d, n, value):
            o_ref[d, n] = value

        def second(d, n, value):
            whole_ref[d, n] = value
            if n < early:
                o_ref[d, square + n] = value
            else:
                late_ref[d, n - early] = value

        pack_one(x_ref, first, mid, layers, lanes)
        pack_one(y_ref, second, mid, layers, lanes)

    parts = [
        pack_specs(layers, pairs, lanes, nodes)
        for nodes in (square + early, square - early, square)
    ]
    return call(
        body,
        (pairs // 8,),
        [
            pl.BlockSpec((1, 8 * unit, lanes), lambda g: (1, g, 0)),
            pl.BlockSpec((1, 8 * unit, lanes), lambda g: (2, g, 0)),
        ],
        [part[0] for part in parts],
        [part[1] for part in parts],
        scratch=[pltpu.VMEM((unit, 8, lanes), jnp.float32)],
        grant=WHOLE_GRANT,
        moved=5 * rows.shape[1] * lanes * 4,
    )(rows, rows)


def unpack(arrays, specs, read_from, slots, layers, buffer, total):
    lanes = arrays[0].shape[-1]
    square = NODES * NODES
    per_plane = square * layers
    unit = 2 * per_plane
    half = lanes // 2

    def body(*refs):
        o_ref, mid = refs[-2:]
        low = lanes_of((8, lanes)) < half
        read = read_from(refs, pl.program_id(0))

        def layer(e, carry):
            for n in range(square):
                left, right = (read(2 * e, n), read(2 * e + 1, n))
                mid[n * layers + e] = jnp.where(low, left, pltpu.roll(right, half, 1))
                mid[per_plane + n * layers + e] = jnp.where(low, pltpu.roll(left, half, 1), right)
            return carry

        lax.fori_loop(0, layers, layer, 0)

        def write(t, r, tile):
            o_ref[rows_at(r, unit, t), :] = tile

        turn_all(lambda k, t: mid[8 * t + k], write, unit // 8)

    extra = [] if buffer is None else [buffer]
    return call(
        body,
        (2,),
        list(specs) + [pl.BlockSpec(memory_space=pl.ANY)] * len(extra),
        pl.BlockSpec((8 * unit, lanes), lambda i: (slots[0] + i * slots[1], 0)),
        jax.ShapeDtypeStruct((total, lanes), jnp.float32),
        scratch=[pltpu.VMEM((unit, 8, lanes), jnp.float32)],
        moved=4 * 8 * unit * lanes * 4,
        aliases={len(arrays): 0} if extra else None,
    )(*arrays, *extra)


def paired_nodes():
    return [(b, min(b + 1, NODES - 1)) for b in range(0, NODES, 2)]


def three_pass(table, rhs_ref, tiles):
    rows, lanes = tiles[0].shape
    half = lanes // 2
    low = lanes_of((rows, lanes)) < half
    depth = 2 * rows
    for place, (one, two) in enumerate(paired_nodes()):
        first, second = (tiles[one], tiles[two])
        cut = pl.ds(place * lanes, lanes)
        for part in range(2):
            if part == 0:
                value = jnp.where(low, first, pltpu.roll(second, half, 1))
            else:
                value = jnp.where(low, pltpu.roll(first, half, 1), second)
            high = value.astype(jnp.bfloat16)
            rest = (value - high.astype(jnp.float32)).astype(jnp.bfloat16)
            rhs_ref[pl.ds(part * rows, rows), cut] = high
            rhs_ref[pl.ds(depth + part * rows, rows), cut] = rest
            rhs_ref[pl.ds(2 * depth + part * rows, rows), cut] = high
    out = jnp.dot(table, rhs_ref[...], preferred_element_type=jnp.float32)
    fields = []
    for field in range(table.shape[0] // depth):
        nodes = [None] * NODES
        for place, (one, two) in enumerate(paired_nodes()):
            cut = slice(place * lanes, (place + 1) * lanes)
            top = out[field * depth : field * depth + rows, cut]
            bottom = out[field * depth + rows : (field + 1) * depth, cut]
            nodes[one] = jnp.where(low, top, pltpu.roll(bottom, half, 1))
            if two != one:
                nodes[two] = jnp.where(low, pltpu.roll(top, half, 1), bottom)
        fields.append(nodes)
    return fields


def rhs_scratch(table, lanes):
    return pltpu.VMEM((table.shape[1], len(paired_nodes()) * lanes), jnp.bfloat16)


def read_tiles(x_ref, rows, lanes):
    return [x_ref[:, b].reshape(rows, lanes) for b in range(NODES)]


def to_points(blocks, table):
    shares, _, pairs, lanes = blocks.shape
    square = NODES * NODES
    rows = shares * pairs

    def body(t_ref, x_ref, v_ref, z_ref, rhs_ref):
        fields = three_pass(t_ref[...], rhs_ref, read_tiles(x_ref, rows, lanes))
        for b in range(NODES):
            v_ref[b] = fields[0][b]
            z_ref[b] = fields[1][b]

    spec = pl.BlockSpec((NODES, rows, lanes), lambda a: (a, 0, 0))
    shape = jax.ShapeDtypeStruct((square, rows, lanes), jnp.float32)
    return call(
        body,
        (NODES,),
        [
            whole(table.shape),
            pl.BlockSpec((shares, NODES, pairs, lanes), lambda a: (0, a, 0, 0)),
        ],
        [spec, spec],
        [shape, shape],
        scratch=[rhs_scratch(table, lanes)],
        flops=2 * table.shape[0] * table.shape[1] * square * lanes,
        grant=WHOLE_GRANT,
        moved=3 * square * rows * lanes * 4,
    )(table, blocks)


def turn_around(blocks, skip, start, count, partial, slope_z, table, back, fields, out):
    shares, _, pairs, lanes = blocks.shape
    rows = shares * pairs
    square = NODES * NODES
    group = pairs // 2
    shape = jax.ShapeDtypeStruct((square, rows, lanes), jnp.float32)

    def body(t_ref, i_ref, x_ref, g_ref, s_ref, *refs):
        w_ref, z_ref, o_ref, rhs_ref = refs[-4:]
        points = three_pass(t_ref[...], rhs_ref, read_tiles(x_ref, rows, lanes))
        for b in range(NODES):
            w_ref[b] = points[0][b]
            z_ref[b] = points[1][b]
        tiles = [g_ref[b] + w_ref[b] * s_ref[b] for b in range(NODES)]
        spectral = three_pass(i_ref[...], rhs_ref, tiles)[0]
        for b in range(NODES):
            value = spectral[b].reshape(shares, pairs, lanes)
            if out is None:
                o_ref[:, b] = value
            else:
                for g in range(2):
                    o_ref[:, g * NODES + b] = value[:, g * group : (g + 1) * group]

    spec = pl.BlockSpec((NODES, rows, lanes), lambda a: (start + a, 0, 0))
    if out is None:
        out_spec = pl.BlockSpec((shares, NODES, pairs, lanes), lambda a: (0, a, 0, 0))
        out_shape = jax.ShapeDtypeStruct((shares, count * NODES, pairs, lanes), jnp.float32)
    else:
        first = out[1]
        out_spec = pl.BlockSpec((shares, 2 * NODES, group, lanes), lambda a: (0, first + a, 0, 0))
        out_shape = jax.ShapeDtypeStruct(out[0], jnp.float32)
    return call(
        body,
        (count,),
        [
            whole(table.shape),
            whole(back.shape),
            pl.BlockSpec((shares, NODES, pairs, lanes), lambda a: (0, skip + a, 0, 0)),
            spec,
            spec,
        ]
        + [pl.BlockSpec(memory_space=pl.ANY)] * len(fields),
        [spec, spec, out_spec],
        [shape, shape, out_shape],
        scratch=[rhs_scratch(table, lanes)],
        flops=3 * table.shape[0] * table.shape[1] * count * NODES * lanes,
        aliases={5: 0, 6: 1} if fields else None,
        grant=WHOLE_GRANT,
        moved=6 * count * NODES * rows * lanes * 4,
    )(table, back, blocks, partial, slope_z, *fields)


def in_plane(speeds, fields, metrics, table):
    square, rows, lanes = speeds[0].shape
    count = len(fields)
    step = 32
    own = [i for i, f in enumerate(fields) if all(f is not s for s in speeds)]
    arrays = list(speeds) + [fields[i] for i in own]

    def body(m_ref, *refs):
        ins, outs = (refs[: len(arrays)], refs[len(arrays) :])
        u_ref, v_ref = ins[:2]
        sources = []
        extra = 2
        for i, f in enumerate(fields):
            if i in own:
                sources.append(ins[extra])
                extra += 1
            else:
                sources.append(u_ref if f is speeds[0] else v_ref)

        def block(s, carry):
            r = pl.ds(s * 8, 8)

            def metric(kind, n):
                return row_of(m_ref, kind * square + n, 8)

            for a in range(NODES):
                ns = [a * NODES + b for b in range(NODES)]
                drift = [
                    u_ref[n, r] * metric(2, n) + v_ref[n, r] * metric(3, n) for n in ns
                ]
                for f in range(count):
                    beside = apply_line(table, [sources[f][n, r] for n in ns])
                    for b, n in enumerate(ns):
                        outs[f][n, r] = drift[b] * beside[b]
            for b in range(NODES):
                ns = [a * NODES + b for a in range(NODES)]
                drift = [
                    u_ref[n, r] * metric(0, n) + v_ref[n, r] * metric(1, n) for n in ns
                ]
                for f in range(count):
                    radial = apply_line(table, [sources[f][n, r] for n in ns])
                    for a, n in enumerate(ns):
                        outs[f][n, r] = outs[f][n, r] + drift[a] * radial[a]
            return carry

        lax.fori_loop(0, step // 8, block, 0)

    spec = pl.BlockSpec((square, step, lanes), lambda i: (0, i, 0))
    shape = jax.ShapeDtypeStruct((square, rows, lanes), jnp.float32)
    return call(
        body,
        (rows // step,),
        [whole(metrics.shape)] + [spec] * len(arrays),
        [spec] * count,
        [shape] * count,
        flops=30 * count * square * rows * lanes,
        grant=WHOLE_GRANT,
        moved=(len(arrays) + count) * square * rows * lanes * 4,
    )(metrics, *arrays)


def to_planes(partial, speed_z, slope_z, table, shares, place, shapes, buffers):
    square, rows, lanes = partial.shape
    pairs = rows // shares
    group = pairs // 2

    def body(t_ref, g_ref, w_ref, z_ref, *refs):
        outs, rhs_ref = (refs[-3:-1], refs[-1])
        tiles = [g_ref[b] + w_ref[b] * z_ref[b] for b in range(NODES)]
        nodes = three_pass(t_ref[...], rhs_ref, tiles)[0]
        for b in range(NODES):
            out = nodes[b].reshape(shares, pairs, lanes)
            for i in range(2):
                outs[i][:, b] = out[:, i * group : (i + 1) * group]

    spec = pl.BlockSpec((NODES, rows, lanes), lambda a: (a, 0, 0))
    out_spec = pl.BlockSpec((shares, NODES, group, lanes), lambda a: (0, place * NODES + a, 0, 0))
    shapes = [jax.ShapeDtypeStruct(shape, jnp.float32) for shape in shapes]
    return call(
        body,
        (NODES,),
        [whole(table.shape), spec, spec, spec]
        + [pl.BlockSpec(memory_space=pl.ANY)] * len(buffers),
        [out_spec, out_spec],
        shapes,
        scratch=[rhs_scratch(table, lanes)],
        flops=2 * table.shape[0] * table.shape[1] * square * lanes,
        grant=WHOLE_GRANT,
        moved=4 * square * rows * lanes * 4,
        aliases={4 + k: k for k in range(len(buffers))},
    )(table, partial, speed_z, slope_z, *buffers)


def first_part(sent, early, rest, rest_at, metrics, table):
    shares, square, pairs, lanes = sent.shape

    some = early.shape[1]
    count = (square - some) // NODES
    group = pairs // 2

    def body(m_ref, s0, r0, *refs):
        others, (o_ref, p0) = (refs[:count], refs[count:])
        d = pl.program_id(0)

        def block(s, carry):
            r = pl.ds(s * 8, 8)
            for n in range(square):
                if n < some:
                    home = r0[0, n, r]
                else:
                    a, b = divmod(n - some, NODES)
                    home = others[a][0, s * NODES + b]
                p0[n] = s0[0, n, r] + time_step * home

            def metric(kind, n):
                return row_of(m_ref, (kind * shares + d) * square + n, 8)

            for a in range(NODES):
                ns = [a * NODES + b for b in range(NODES)]
                line = apply_line(table, [p0[n] for n in ns])
                for b, n in enumerate(ns):
                    o_ref[0, n, r] = metric(2, n) * line[b]
            for b in range(NODES):
                ns = [a * NODES + b for a in range(NODES)]
                line = apply_line(table, [p0[n] for n in ns])
                for a, n in enumerate(ns):
                    o_ref[0, n, r] = o_ref[0, n, r] + metric(0, n) * line[a]
            return carry

        lax.fori_loop(0, pairs // 8, block, 0)

    spec = pl.BlockSpec((1, square, pairs, lanes), lambda d: (d, 0, 0, 0))
    return call(
        body,
        (shares,),
        [whole(metrics.shape), spec, pl.BlockSpec((1, some, pairs, lanes), lambda d: (d, 0, 0, 0))]
        + [
            pl.BlockSpec(
                (1, 2 * NODES, group, lanes), functools.partial(lambda i, d: (d, i, 0, 0), rest_at + k)
            )
            for k in range(count)
        ],
        spec,
        jax.ShapeDtypeStruct(sent.shape, jnp.float32),
        scratch=[pltpu.VMEM((square, 8, lanes), jnp.float32)],
        flops=30 * shares * square * pairs * lanes,
        grant=WHOLE_GRANT,
        moved=3 * shares * square * pairs * lanes * 4,
    )(metrics, sent, early, *[rest] * count)


def join_layers(y_ref, layers):
    square = NODES * NODES
    last = (NODES - 1) * NODES
    for e in range(layers - 1):
        for b in range(NODES):
            upper, lower = (e * square + last + b, (e + 1) * square + b)
            total = y_ref[upper] + y_ref[lower]
            y_ref[upper] = total
            y_ref[lower] = total
    for b in range(NODES):
        node = (layers - 1) * square + last + b
        y_ref[node] = jnp.zeros_like(y_ref[node])


def rim_messages(read, layers, shape, partials):
    lane = lanes_of(shape)
    lanes = shape[-1]
    axis = len(shape) - 1
    first = jnp.zeros(shape, jnp.float32)
    last = jnp.zeros(shape, jnp.float32)
    square = NODES * NODES
    for e in range(layers):
        for a in range(NODES):
            spot = e * NODES + a
            here = lane == spot
            node = e * square + a * NODES
            first = jnp.where(here, pltpu.roll(read(node), spot, axis), first)
            last = jnp.where(
                here, pltpu.roll(read(node + NODES - 1), (spot + 1) % lanes, axis), last
            )
    for i, partial in enumerate(partials):
        here = lane == layers * NODES + i
        first = jnp.where(here, partial, first)
        last = jnp.where(here, partial, last)
    return (first, last)


def right_side(flat, sent, returned, metrics, weights, waves, table, layers, place):
    shares, square, _, lanes = flat.shape
    half = lanes // 2

    def body(m_ref, q_ref, k_ref, f_ref, s1, s2, r1, r2, o_ref, first_ref, last_ref, p1, c0, c1):
        e = pl.program_id(0)
        lane = lanes_of((8, lanes))
        low = lane < half
        wave = k_ref[...]
        sides = (c0, c1)

        @pl.when(e == 0)
        def _():
            first_ref[...] = jnp.zeros_like(first_ref)
            last_ref[...] = jnp.zeros_like(last_ref)

        for h in range(2):
            d = 2 * e + h
            side = sides[h]
            for n in range(square):
                p1[n] = s1[h, n] + time_step * r1[h, n]
                moved = s2[h, n] + time_step * r2[h, n]
                along = pltpu.roll(moved, half, 1) * wave
                side[n] = f_ref[h, n] + row_of(q_ref, d * square + n, 8) * along

            def metric(kind, n):
                return row_of(m_ref, (kind * shares + d) * square + n, 8)

            for a in range(NODES):
                ns = [a * NODES + b for b in range(NODES)]
                line = apply_line(table, [p1[n] for n in ns])
                for b, n in enumerate(ns):
                    side[n] = side[n] + metric(3, n) * line[b]
            for b in range(NODES):
                ns = [a * NODES + b for a in range(NODES)]
                line = apply_line(table, [p1[n] for n in ns])
                for a, n in enumerate(ns):
                    side[n] = side[n] + metric(1, n) * line[a]
        rims = [[first_ref[0], last_ref[0]], [first_ref[1], last_ref[1]]]
        for n in range(square):
            left, right = (c0[n], c1[n])
            parts = (
                jnp.where(low, left, pltpu.roll(right, half, 1)),
                jnp.where(low, pltpu.roll(left, half, 1), right),
            )
            for i in range(2):
                o_ref[n, i] = parts[i]
                a, b = divmod(n, NODES)
                spot = e * NODES + a
                if b == 0:
                    rims[i][0] = jnp.where(lane == spot, pltpu.roll(parts[i], spot, 1), rims[i][0])
                if b == NODES - 1:
                    rims[i][1] = jnp.where(
                        lane == spot, pltpu.roll(parts[i], spot + 1, 1), rims[i][1]
                    )
        for i in range(2):
            first_ref[i] = rims[i][0]
            last_ref[i] = rims[i][1]

    spec = pl.BlockSpec((2, square, 8, lanes), lambda e: (e, 0, place, 0))
    nodes = layers * square
    rim_shape = jax.ShapeDtypeStruct((2, 8, lanes), jnp.float32)
    scratch = pltpu.VMEM((square, 8, lanes), jnp.float32)
    return call(
        body,
        (layers,),
        [
            whole(metrics.shape),
            whole(weights.shape),
            pl.BlockSpec((8, lanes), lambda e: (place, 0)),
            spec,
            spec,
            spec,
            pl.BlockSpec((2, square, 8, lanes), lambda e: (e, 0, 0, 0)),
            pl.BlockSpec((2, square, 8, lanes), lambda e: (e, 1, 0, 0)),
        ],
        [
            pl.BlockSpec((square, 2, 8, lanes), lambda e: (e, 0, 0, 0)),
            whole((2, 8, lanes)),
            whole((2, 8, lanes)),
        ],
        [jax.ShapeDtypeStruct((nodes, 2, 8, lanes), jnp.float32), rim_shape, rim_shape],
        scratch=[scratch] * 3,
        flops=40 * shares * square * 8 * lanes,
        grant=WHOLE_GRANT - 2 * 2**20,
        moved=6 * shares * square * 8 * lanes * 4,
    )(metrics, weights, waves, flat, *sent, returned, returned)


def swap_rims(first, last):
    size = lax.axis_size("elem")
    up = [(i, (i + 1) % size) for i in range(size)]
    down = [(j, i) for i, j in up]
    return (lax.ppermute(last, "elem", up), lax.ppermute(first, "elem", down))


def opposite(first):
    size = lax.axis_size("elem")
    return lax.ppermute(first, "elem", [(i, (i + 2) % size) for i in range(size)])


def join_columns(read, ref, before, after, layers):
    lanes = before.shape[-1]
    axis = len(before.shape) - 1
    lane = lanes_of(before.shape)
    square = NODES * NODES
    for e in range(layers):
        for a in range(NODES):
            spot = e * NODES + a
            node = e * square + a * NODES
            first, last = (read(node), read(node + NODES - 1))
            beyond = pltpu.roll(after, lanes - 1 - spot, axis)
            ahead = jnp.where(lane == lanes - 1, beyond, pltpu.roll(first, lanes - 1, axis))
            right = last + ahead
            mine = first + (pltpu.roll(before, lanes - spot, axis) if spot else before)
            ref[node + NODES - 1] = right
            ref[node] = jnp.where(lane == 0, mine, pltpu.roll(right, 1, axis))


def join(source, ref, before, after, layers):
    square = NODES * NODES

    def copy(e, carry):
        for n in range(square):
            if 0 < n % NODES < NODES - 1:
                ref[e * square + n] = source[e * square + n]
        return carry

    lax.fori_loop(0, layers, copy, 0)
    join_columns(lambda n: source[n], ref, before, after, layers)
    join_layers(ref, layers)


def each_node(layers, step):
    def layer(e, carry):
        for n in range(NODES * NODES):
            step(e * NODES * NODES + n)
        return carry

    lax.fori_loop(0, layers, layer, 0)


def share_of(layers, e, a):
    if a == 0:
        return jnp.where(e > 0, 0.5, 1.0)
    if a == NODES - 1:
        return jnp.where(e < layers - 1, 0.5, 0.0)
    return 1.0


def helmholtz(r_ref, y_ref, flux_ref, g_ref, shift, layers, table, dot_only=False):
    square = NODES * NODES
    nodes = layers * square
    turned = table.T
    zero = jnp.zeros(shift.shape, jnp.float32)

    def layer(e, carry):
        norm, energy = carry
        base = e * square

        def metric(kind, n):
            return row_of(g_ref, kind * nodes + base + n, 8)

        for b in range(NODES):
            ns = [a * NODES + b for a in range(NODES)]
            radial = apply_line(table, [r_ref[base + n] for n in ns])
            for a, n in enumerate(ns):
                flux_ref[n] = radial[a]
        for a in range(NODES):
            ns = [a * NODES + b for b in range(NODES)]
            line = [r_ref[base + n] for n in ns]
            beside = apply_line(table, line)
            second = []
            rest = []
            part = zero
            for b, n in enumerate(ns):
                radial = flux_ref[n]
                cross = metric(1, n)
                one = metric(0, n) * radial + cross * beside[b]
                two = cross * radial + metric(2, n) * beside[b]
                same = shift * metric(3, n) * line[b]
                whole_weight = line[b] * line[b]
                part = part + (0.5 * whole_weight if b in (0, NODES - 1) else whole_weight)
                if dot_only:
                    energy = energy + (radial * one + beside[b] * two + same * line[b])
                else:
                    flux_ref[n] = one
                    second.append(two)
                    rest.append(same)
            norm = norm + part * share_of(layers, e, a)
            if not dot_only:
                back = apply_line(turned, second)
                for b, n in enumerate(ns):
                    y_ref[base + n] = rest[b] + back[b]
        if not dot_only:
            for b in range(NODES):
                ns = [a * NODES + b for a in range(NODES)]
                back = apply_line(turned, [flux_ref[n] for n in ns])
                for a, n in enumerate(ns):
                    value = y_ref[base + n] + back[a]
                    y_ref[base + n] = value
                    energy = energy + value * r_ref[base + n]
        return (norm, energy)

    norm, energy = lax.fori_loop(0, layers, layer, (zero, zero))
    axis = len(shift.shape) - 1
    return (
        jnp.sum(norm, axis=axis, keepdims=True),
        jnp.sum(energy, axis=axis, keepdims=True),
    )


def lane_value(block, lane):
    return block[..., lane : lane + 1]


def sums_from(own, left, right, far, layers):
    total = (own[...] + far[...]) + (left[...] + right[...])
    spot = layers * NODES
    return (lane_value(total, spot), lane_value(total, spot + 1))


def scalars_block(shape, values, spot=0):
    lane = lanes_of(shape)
    out = jnp.zeros(shape, jnp.float32)
    for i, value in enumerate(values):
        out = jnp.where(lane == spot + i, value, out)
    return out


def shapes_of(field):
    return (
        jax.ShapeDtypeStruct(field.shape, jnp.float32),
        jax.ShapeDtypeStruct(field.shape[1:], jnp.float32),
        pltpu.VMEM((NODES * NODES,) + field.shape[1:], jnp.float32),
    )


def first_image(raw, before, after, shift, geo, layers, table):
    field, small, flux_scratch = shapes_of(raw)
    shape = raw.shape[1:]

    def body(g_ref, k_ref, f_ref, b_ref, a_ref, r_ref, y_ref, first_ref, last_ref, flux):
        join(f_ref, r_ref, b_ref[...], a_ref[...], layers)
        sums = helmholtz(r_ref, y_ref, flux, g_ref, k_ref[...], layers, table)
        first_ref[...], last_ref[...] = rim_messages(lambda n: y_ref[n], layers, shape, sums)

    return call(
        body,
        (),
        held(5),
        held(4),
        [field, field, small, small],
        scratch=[flux_scratch],
        flops=80 * raw.size,
        moved=12 * raw.size,
    )(geo, shift, raw, before, after)


def second_image(start, image, messages, shift, geo, layers, table):
    field, small, flux_scratch = shapes_of(start)
    shape = start.shape[1:]

    def body(g_ref, k_ref, r0, y0, own, left, right, far, *rest):
        w_ref, y_ref, first_ref, last_ref, scalar_ref, r1, flux = rest
        norm, energy = sums_from(own, left, right, far, layers)
        alpha = jnp.broadcast_to(norm / energy, shape)
        join(y0, w_ref, left[...], right[...], layers)

        def move(node):
            r1[node] = r0[node] - alpha * w_ref[node]

        each_node(layers, move)
        sums = helmholtz(r1, y_ref, flux, g_ref, k_ref[...], layers, table)
        first_ref[...], last_ref[...] = rim_messages(lambda n: y_ref[n], layers, shape, sums)
        scalar_ref[...] = scalars_block(shape, (alpha, norm, energy))

    return call(
        body,
        (),
        held(8),
        held(5),
        [field, field, small, small, small],
        scratch=[pltpu.VMEM(start.shape, jnp.float32), flux_scratch],
        flops=80 * start.size,
        moved=16 * start.size,
    )(geo, shift, start, image, *messages)


def third_energy(start, joined, image, messages, scalars, shift, geo, layers, table):
    field, small, flux_scratch = shapes_of(start)
    shape = start.shape[1:]

    def body(g_ref, k_ref, r0, w0, y1, own, left, right, far, old, *rest):
        r2, d2, sums_ref, scalar_ref, w1, flux = rest
        norm, energy = sums_from(own, left, right, far, layers)
        before = old[...]
        alpha = jnp.broadcast_to(lane_value(before, 0), shape)
        ratio = norm / lane_value(before, 1)
        curve = energy - ratio * ratio * lane_value(before, 2)
        step = jnp.broadcast_to(norm / curve, shape)
        beta = jnp.broadcast_to(ratio, shape)
        join(y1, w1, left[...], right[...], layers)

        def move(node):
            w = w0[node]
            start_value = r0[node]
            moved = start_value - alpha * w
            d2[node] = moved + beta * start_value
            r2[node] = moved - step * (w1[node] + beta * w)

        each_node(layers, move)
        sums = helmholtz(r2, None, flux, g_ref, k_ref[...], layers, table, dot_only=True)
        sums_ref[...] = scalars_block(shape, sums, layers * NODES)
        scalar_ref[...] = scalars_block(shape, (alpha, norm, curve, step))

    return call(
        body,
        (),
        held(10),
        held(4),
        [field, field, small, small],
        scratch=[pltpu.VMEM(start.shape, jnp.float32), flux_scratch],
        flops=60 * start.size,
        moved=20 * start.size,
    )(geo, shift, start, joined, image, *messages, scalars)


def finish(start, direction, residual, messages, scalars, layers, place, buffer, total):
    nodes, _, rows, lanes = start.shape
    shape = start.shape[1:]
    square = NODES * NODES

    unit = 2 * nodes

    def body(r0, d2, r2, own, left, right, far, old, *refs):
        o_ref, mid = refs[-2:]
        norm, energy = sums_from(own, left, right, far, layers)
        before = old[...]
        ratio = norm / lane_value(before, 1)
        curve = energy - ratio * ratio * lane_value(before, 2)
        step = norm / curve
        third = jnp.broadcast_to(step, shape)
        second = jnp.broadcast_to(lane_value(before, 3) + step * ratio, shape)
        first = jnp.broadcast_to(lane_value(before, 0), shape)

        def layer(e, carry):
            for n in range(square):
                node = e * square + n
                value = first * r0[node] + second * d2[node] + third * r2[node]
                for i in range(2):
                    mid[i * nodes + n * layers + e] = value[i]
            return carry

        lax.fori_loop(0, layers, layer, 0)

        def write(t, r, tile):
            o_ref[rows_at(r, unit, t), :] = tile

        turn_all(lambda k, t: mid[8 * t + k], write, unit // 8)

    extra = [] if buffer is None else [buffer]
    return call(
        body,
        (1,),
        [whole(start.shape)] * 3
        + [whole(shape)] * 5
        + [pl.BlockSpec(memory_space=pl.ANY)] * len(extra),
        pl.BlockSpec((2 * rows * nodes, lanes), lambda i: (place, 0)),
        jax.ShapeDtypeStruct((total, lanes), jnp.float32),
        scratch=[pltpu.VMEM((unit, rows, lanes), jnp.float32)],
        flops=6 * start.size,
        moved=16 * start.size,
        aliases={8: 0} if extra else None,
    )(start, direction, residual, *messages, scalars, *extra)


def halves(values, shares):
    half = values.shape[-1] // 2
    parts = [jnp.concatenate([p, p], axis=-1) for p in (values[..., :half], values[..., half:])]
    return jnp.stack(parts, axis=2).reshape(values.shape[0], shares, NODES * NODES, 2 * half)


def on_device_paired(*arrays):
    return paired_step(*arrays)


def paired_step(velocity, radial_dx, radial_dy, around_dx, around_dy, jacobian):
    table = derivative_table()
    modes = lax.axis_size("mode")
    mode = lax.axis_index("mode")
    _, local_planes, layers, _, _, lanes = velocity.shape
    planes = local_planes * modes
    pairs = local_planes // 2
    first_plane = mode * local_planes
    square = NODES * NODES
    forward, backward = (jnp.asarray(t) for t in paired_tables(planes))

    rows = velocity.transpose(0, 1, 3, 4, 2, 5).reshape(3, local_planes * square * layers, lanes)
    plain = jnp.stack([radial_dx, radial_dy, around_dx, around_dy]).reshape(
        4, layers, square, lanes
    )
    both = halves(plain, modes)
    here = lax.dynamic_index_in_dim(both, mode, 1, keepdims=False).reshape(4 * square, lanes)
    metrics = geometry(radial_dx, radial_dy, around_dx, around_dy, jacobian)
    geo = jnp.stack(metrics).reshape(4 * layers * square, lanes)
    scaled = halves((metrics[3] * (-1.0 / time_step)).reshape(1, layers, square, lanes), modes)
    flux = (both * scaled).reshape(4 * modes * square, lanes)
    scaled = scaled.reshape(modes * square, lanes)
    pair = (first_plane // 2 + jnp.arange(pairs, dtype=jnp.int32)).astype(jnp.float32)
    wave = pair[:, None] * spanwise_wave
    low = (jnp.arange(lanes) < lanes // 2)[None, :]
    waves = jnp.where(low, wave, -wave)
    shift = plane_shift(first_plane, local_planes, planes).reshape(pairs, 2).T
    shift = jnp.broadcast_to(shift.reshape(2, 2, pairs // 2, 1), (2, 2, pairs // 2, lanes))
    shift = (shift[:, 0], shift[:, 1])

    def exchange(blocks):
        return lax.all_to_all(blocks, "mode", split_axis=0, concat_axis=0, tiled=True)

    some = (NODES // 2 + 1) * NODES
    group = pairs // 2
    first_shape = (modes, 4 * square - 2 * some, group, lanes)
    second_shape = (modes, 2 * square, group, lanes)
    sent_0 = pack_first(rows, layers, pairs, lanes)
    sent_1, late_2, sent_2 = pack_rest(rows, layers, pairs, lanes, some)
    arrived_0 = exchange(sent_0)
    sent_1, here, geo, flux, scaled, waves, shift = lax.optimization_barrier(
        (sent_1, here, geo, flux, scaled, waves, shift)
    )
    arrived_1 = exchange(sent_1)
    arrived_2 = exchange(late_2)
    speed_x, slope_0 = to_points(arrived_0, forward)
    speed_y, slope_1 = to_points(arrived_1, forward)
    speeds = [speed_x, speed_y]
    partial = in_plane(speeds, speeds, here, table)
    rows_early = some // NODES
    speed_z, slope_2, blocks = turn_around(
        arrived_1, NODES, 0, rows_early, partial[0], slope_0, forward, backward, (), None
    )
    home_0 = exchange(blocks)
    speed_z, slope_2, first_buffer = turn_around(
        arrived_2,
        0,
        rows_early,
        NODES - rows_early,
        partial[0],
        slope_0,
        forward,
        backward,
        (speed_z, slope_2),
        (first_shape, NODES),
    )
    last = in_plane(speeds, [speed_z], here, table)[0]
    shapes = (first_shape, second_shape)
    blocks = to_planes(partial[1], speed_z, slope_1, backward, modes, 0, shapes, (first_buffer,))
    blocks = to_planes(last, speed_z, slope_2, backward, modes, 1, shapes, blocks)
    home_1 = exchange(blocks[0])
    home_2 = exchange(blocks[1])
    returned = (home_1, home_2)
    sent = (sent_1, sent_2)

    own_rows = local_planes * square * layers

    def read_first(refs, g):
        def read(d, n):
            if n < some:
                return refs[0][d, n]
            a, b = divmod(n - some, NODES)
            return refs[1 + a][d, g * NODES + b]

        return read

    def read_part(refs, i):
        return lambda d, n: refs[0][d, n]

    first_specs = [pl.BlockSpec((modes, some, group, lanes), lambda i: (0, 0, i, 0))] + [
        pl.BlockSpec(
            (modes, 2 * NODES, group, lanes), functools.partial(lambda k, i: (0, k, 0, 0), NODES + k)
        )
        for k in range(NODES - rows_early)
    ]
    part_specs = [pl.BlockSpec((modes, square, group, lanes), lambda i: (0, i, 0, 0))]
    advection = unpack(
        [home_0] + [home_1] * (NODES - rows_early),
        first_specs,
        read_first,
        (0, 1),
        layers,
        None,
        3 * own_rows,
    )
    flat = first_part(sent_0, home_0, home_1, NODES, flux, table)

    def solve(place, flat, own_shift, buffer):
        raw, first, last = right_side(
            flat, sent, returned[place], flux, scaled, waves, table, layers, place
        )
        before, after = swap_rims(first, last)
        start, image, first, last = first_image(raw, before, after, own_shift, geo, layers, table)
        messages = (first,) + swap_rims(first, last) + (opposite(first),)
        joined, image, first, last, scalars = second_image(
            start, image, messages, own_shift, geo, layers, table
        )
        messages = (first,) + swap_rims(first, last) + (opposite(first),)
        residual, direction, sums, scalars = third_energy(
            start, joined, image, messages, scalars, own_shift, geo, layers, table
        )
        messages = (sums,) + swap_rims(sums, sums) + (opposite(sums),)
        return finish(
            start, direction, residual, messages, scalars, layers, place, buffer, own_rows
        )

    pressure = solve(0, flat, shift[0], None)
    advection = unpack(
        [home_1], part_specs, read_part, (2, 2), layers, advection, 3 * own_rows
    )
    flat, pressure, advection, shift = lax.optimization_barrier(
        (flat, pressure, advection, shift)
    )
    pressure = solve(1, flat, shift[1], pressure)
    advection = unpack(
        [home_2], part_specs, read_part, (3, 2), layers, advection, 3 * own_rows
    )
    advection = advection.reshape(3, local_planes, NODES, NODES, layers, lanes)
    pressure = pressure.reshape(local_planes, NODES, NODES, layers, lanes)
    return (advection.transpose(0, 1, 4, 2, 3, 5), pressure.transpose(0, 3, 1, 2, 4))


def paired_fits(mesh, shape):
    modes, ring = (mesh.shape["mode"], mesh.shape["elem"])
    _, planes, layers, _, _, columns = shape
    return (
        ring == 4
        and columns == 128 * ring
        and modes == 2 * layers
        and layers % 4 == 0
        and planes == 32 * modes
        and (layers * NODES + 2 <= 128)
    )


def solution(mesh):
    placed = (
        P(None, "mode", None, None, None, "elem"),
        P(None, None, None, "elem"),
        P(None, None, None, "elem"),
        P(None, None, None, "elem"),
        P(None, None, None, "elem"),
        P(None, None, None, "elem"),
    )


    def step(velocity, *rest):
        body = on_device_paired if paired_fits(mesh, velocity.shape) else on_device
        return jax.shard_map(
            body,
            mesh=mesh,
            in_specs=placed,
            out_specs=(
                P(None, "mode", None, None, None, "elem"),
                P("mode", None, None, None, "elem"),
            ),
            check_vma=False,
        )(velocity, *rest)

    return step
```

```python
import functools
import math

import jax
import jax.numpy as jnp
import numpy as np
from jax import lax
from jax.experimental import pallas as pl
from jax.experimental.pallas import tpu as pltpu
from jax.sharding import PartitionSpec as P

NODES = 7
ITERS = 3
GRANT = 24 * 2**20
WHOLE_GRANT = 67043328


spanwise_wave = 2.0 * math.pi / 64.0
time_step = 0.1


def padded_2(value, sides, width):
    for axis, dim in sides:
        size, length = (lax.axis_size(axis), value.shape[dim])
        up = [(i, (i + 1) % size) for i in range(size)]
        down = [(j, i) for i, j in up]
        last = lax.slice_in_dim(value, length - width, length, axis=dim)
        leading = lax.slice_in_dim(value, 0, width, axis=dim)
        before = lax.ppermute(last, axis, up)
        after = lax.ppermute(leading, axis, down)
        value = jnp.concatenate([before, value, after], axis=dim)
    return value


def lobatto_rule(count):
    degree = count - 1
    points = np.cos(np.pi * np.arange(count) / degree)
    legendre = np.zeros((count, count))
    for _ in range(60):
        legendre[:, 0] = 1.0
        legendre[:, 1] = points
        for order in range(2, count):
            legendre[:, order] = (
                (2 * order - 1) * points * legendre[:, order - 1]
                - (order - 1) * legendre[:, order - 2]
            ) / order
        points = points - (points * legendre[:, degree] - legendre[:, degree - 1]) / (
            count * legendre[:, degree]
        )
    legendre[:, 0] = 1.0
    legendre[:, 1] = points
    for order in range(2, count):
        legendre[:, order] = (
            (2 * order - 1) * points * legendre[:, order - 1] - (order - 1) * legendre[:, order - 2]
        ) / order
    weights = 2.0 / (degree * count * legendre[:, degree] ** 2)
    return (points[::-1].copy(), weights[::-1].copy())


def derivative_table():
    lobatto_nodes = lobatto_rule(NODES)[0]
    total = lobatto_nodes.shape[0]
    scales = np.ones(total)
    for column in range(total):
        for other in range(total):
            if other != column:
                scales[column] = scales[column] / (lobatto_nodes[column] - lobatto_nodes[other])
    table = np.zeros((total, total))
    for row in range(total):
        for column in range(total):
            if row != column:
                table[row, column] = (
                    scales[column] / scales[row] / (lobatto_nodes[row] - lobatto_nodes[column])
                )
        table[row, row] = -np.sum(table[row])
    return table


def radial_derivative(table, field):
    return jnp.einsum("ia,...abe->...ibe", table, field, precision=lax.Precision.HIGHEST)


def around_derivative(table, field):
    return jnp.einsum("jb,...abe->...aje", table, field, precision=lax.Precision.HIGHEST)


def radial_transpose(table, field):
    return jnp.einsum("ia,...ibe->...abe", table, field, precision=lax.Precision.HIGHEST)


def around_transpose(table, field):
    return jnp.einsum("jb,...aje->...abe", table, field, precision=lax.Precision.HIGHEST)


def z_derivative(field, first_pair):
    shape = field.shape
    count = shape[1] // 2
    pairs = field.reshape((shape[0], count, 2) + shape[2:])
    waves = (first_pair + jnp.arange(count, dtype=jnp.int32)).astype(jnp.float32) * spanwise_wave
    waves = waves.reshape((1, count) + (1,) * (len(shape) - 2))
    return jnp.stack([waves * pairs[:, :, 1], -waves * pairs[:, :, 0]], axis=2).reshape(shape)


def transform_tables(planes):
    position = jnp.arange(planes, dtype=jnp.int32)
    plane = jnp.arange(planes, dtype=jnp.int32)
    order = plane // 2
    turns = position[:, None] * order[None, :] % planes
    angle = 2.0 * math.pi / planes * turns.astype(jnp.float32)
    cosine = jnp.cos(angle)
    sine = jnp.sin(angle)
    is_sine = (plane % 2 == 1)[None, :]
    is_top = (plane == 1)[None, :]
    parity = jnp.cos(math.pi * (position % 2).astype(jnp.float32))[:, None]
    basis = jnp.where(is_top, parity, jnp.where(is_sine, sine, cosine))
    scaling = jnp.where(order == 0, 1.0, 2.0).astype(jnp.float32) / planes
    inverse = jnp.transpose(basis * scaling[None, :])
    wave = (order.astype(jnp.float32) * spanwise_wave)[None, :]
    slope = jnp.where(is_sine, wave * cosine, -wave * sine)
    return (basis, inverse, slope)


def geometry(radial_dx, radial_dy, around_dx, around_dy, jacobian):
    lobatto_weights = lobatto_rule(NODES)[1]
    quadrature = jnp.asarray(np.outer(lobatto_weights, lobatto_weights), jnp.float32)[:, :, None]
    mass = quadrature * jacobian
    radial_stiff = mass * (radial_dx * radial_dx + radial_dy * radial_dy)
    cross_stiff = mass * (radial_dx * around_dx + radial_dy * around_dy)
    around_stiff = mass * (around_dx * around_dx + around_dy * around_dy)
    return (radial_stiff, cross_stiff, around_stiff, mass)


def node_weights(layers):
    layer = jnp.arange(layers, dtype=jnp.int32).reshape(layers, 1, 1, 1)
    node = jnp.arange(NODES, dtype=jnp.int32)
    radial_node = node.reshape(1, NODES, 1, 1)
    around_node = node.reshape(1, 1, NODES, 1)
    shared_radial = (radial_node == NODES - 1) & (layer < layers - 1) | (radial_node == 0) & (
        layer > 0
    )
    shared_around = (around_node == 0) | (around_node == NODES - 1)
    multiplicity = (1.0 + shared_radial.astype(jnp.float32)) * (
        1.0 + shared_around.astype(jnp.float32)
    )
    boundary = (radial_node == NODES - 1) & (layer == layers - 1)
    mask = 1.0 - boundary.astype(jnp.float32)
    return (mask, mask / multiplicity)


def plane_shift(first_plane, count, planes):
    plane = first_plane + jnp.arange(count, dtype=jnp.int32)
    order = jnp.where(plane == 1, planes // 2, plane // 2)
    wave = order.astype(jnp.float32) * spanwise_wave
    return (wave * wave).reshape(count, 1, 1, 1, 1)


def helmholtz_local(table, field, shift, metrics):
    radial_stiff, cross_stiff, around_stiff, mass = metrics
    radial = radial_derivative(table, field)
    beside_all = around_derivative(table, field)
    return (
        radial_transpose(table, radial_stiff * radial + cross_stiff * beside_all)
        + around_transpose(table, cross_stiff * radial + around_stiff * beside_all)
        + shift * mass * field
    )


def assemble(field):
    lower = field[:, :-1, -1] + field[:, 1:, 0]
    field = field.at[:, :-1, -1].set(lower).at[:, 1:, 0].set(lower)
    first = field[:, :, :, 0]
    last = field[:, :, :, -1]
    rims = jnp.concatenate([first[..., :1], last[..., -1:]], axis=3)
    padded = padded_2(rims, (("elem", 3),), 1)
    after = jnp.concatenate([first[..., 1:], padded[..., 3:4]], axis=3)
    right = last + after
    left = jnp.concatenate([padded[..., 0:1] + first[..., :1], right[..., :-1]], axis=3)
    return field.at[:, :, :, -1].set(right).at[:, :, :, 0].set(left)


def inner(first, second, weight):
    return jnp.sum(first * second * weight, axis=(1, 2, 3, 4))


def expand(scalar):
    return scalar.reshape(-1, 1, 1, 1, 1)


def squared_norm(residual, weight):
    return lax.psum(inner(residual, residual, weight), "elem")


def on_device(velocity, radial_dx, radial_dy, around_dx, around_dy, jacobian):
    table = jnp.asarray(derivative_table(), jnp.float32)
    modes = lax.axis_size("mode")
    local_planes = velocity.shape[1]
    planes = local_planes * modes
    first_plane = lax.axis_index("mode") * local_planes
    layers = velocity.shape[2]
    columns = velocity.shape[5]
    basis, inverse, slope = transform_tables(planes)
    radial = radial_derivative(table, velocity)
    beside_all = around_derivative(table, velocity)
    along_x = radial_dx * radial + around_dx * beside_all
    along_y = radial_dy * radial + around_dy * beside_all
    fields = jnp.concatenate([velocity, along_x, along_y], axis=0)
    count = fields.shape[0]
    cells = layers * NODES * NODES * columns
    packed = fields.reshape(count, local_planes, modes, cells // modes)
    flat = lax.all_to_all(packed, "mode", split_axis=2, concat_axis=1, tiled=True)[:, :, 0, :]
    values = jnp.einsum("jp,fpc->fjc", basis, flat, precision=lax.Precision.HIGHEST)
    speed = values[0:3]
    slope_x = values[3:6]
    slope_y = values[6:9]
    slope_z = jnp.einsum("jp,fpc->fjc", slope, flat[0:3], precision=lax.Precision.HIGHEST)
    product = -(speed[0:1] * slope_x + speed[1:2] * slope_y + speed[2:3] * slope_z)
    spectral = jnp.einsum("pj,fjc->fpc", inverse, product, precision=lax.Precision.HIGHEST)
    returned = lax.all_to_all(
        spectral[:, :, None, :], "mode", split_axis=1, concat_axis=2, tiled=True
    )
    advection = returned.reshape(velocity.shape)
    metrics = geometry(radial_dx, radial_dy, around_dx, around_dy, jacobian)
    mask, weight = node_weights(layers)
    predicted = velocity + time_step * advection
    radial = radial_derivative(table, predicted[0:2])
    beside_all = around_derivative(table, predicted[0:2])
    divergence = (
        radial_dx * radial[0]
        + around_dx * beside_all[0]
        + (radial_dy * radial[1] + around_dy * beside_all[1])
        + z_derivative(predicted[2:3], first_plane // 2)[0]
    )
    shift = plane_shift(first_plane, local_planes, planes)
    right_side = mask * assemble(-(metrics[3] * divergence) / time_step)
    solution = jnp.zeros_like(right_side)
    residual = right_side
    direction = right_side
    norm_now = squared_norm(residual, weight)
    for _ in range(ITERS):
        image = mask * assemble(helmholtz_local(table, direction, shift, metrics))
        alpha = norm_now / lax.psum(inner(direction, image, weight), "elem")
        solution = solution + expand(alpha) * direction
        residual = residual - expand(alpha) * image
        norm_next = squared_norm(residual, weight)
        direction = residual + expand(norm_next / norm_now) * direction
        norm_now = norm_next
    return (advection, solution)


def split_bf16(table):
    high = table.astype(jnp.bfloat16)
    low = (table - high.astype(np.float64)).astype(jnp.bfloat16)
    return np.concatenate([high, high, low], axis=1)


def paired_tables(planes):
    position = np.arange(planes)
    plane = np.arange(planes)
    order = plane // 2
    angle = 2.0 * np.pi / planes * (position[:, None] * order[None, :] % planes)
    cosine, sine = (np.cos(angle), np.sin(angle))
    odd = (plane % 2 == 1)[None, :]
    parity = (1.0 - 2.0 * (position % 2))[:, None]
    basis = np.where((plane == 1)[None, :], parity, np.where(odd, sine, cosine))
    wave = (order * spanwise_wave)[None, :]
    slope = np.where(odd, wave * cosine, -wave * sine)
    scaling = np.where(order == 0, 1.0, 2.0) / planes
    inverse = -(basis * scaling[None, :]).T

    def columns(matrix):
        return np.concatenate([matrix[:, 0::2], matrix[:, 1::2]], axis=1)

    forward = np.concatenate([columns(basis), columns(slope)])
    backward = columns(inverse.T).T
    return (split_bf16(forward), split_bf16(backward))


def apply_line(matrix, line):
    n = NODES
    m = n // 2
    sums = [line[a] + line[n - 1 - a] for a in range(m)]
    gaps = [line[a] - line[n - 1 - a] for a in range(m)]

    def total(parts):
        out = parts[0]
        for part in parts[1:]:
            out = out + part
        return out

    out = [None] * n
    for i in range(m + 1):
        plus = total(
            [float(0.5 * (matrix[i, a] - matrix[i, n - 1 - a])) * gaps[a] for a in range(m)]
        )
        if i == m:
            out[i] = plus
            continue
        minus = total(
            [float(0.5 * (matrix[i, a] + matrix[i, n - 1 - a])) * sums[a] for a in range(m)]
            + [float(matrix[i, m]) * line[m]]
        )
        out[i] = plus + minus
        out[n - 1 - i] = plus - minus
    return out


def lanes_of(shape):
    return lax.broadcasted_iota(jnp.int32, shape, len(shape) - 1)


def row_of(ref, row, rows):
    return ref[pl.ds(row, rows, stride=0), :]


def call(body, grid, ins, outs, out_shape, scratch=(), flops=0, moved=0, aliases=None, grant=GRANT):
    return pl.pallas_call(
        body,
        grid=grid,
        in_specs=ins,
        out_specs=outs,
        out_shape=out_shape,
        scratch_shapes=list(scratch),
        input_output_aliases=aliases or {},
        compiler_params=pltpu.CompilerParams(
            dimension_semantics=("arbitrary",) * len(grid), vmem_limit_bytes=grant
        ),
        cost_estimate=pl.CostEstimate(
            flops=int(flops), bytes_accessed=int(moved), transcendentals=0
        ),
    )


def held(count):
    return [pl.BlockSpec(memory_space=pltpu.VMEM)] * count


def whole(shape):
    return pl.BlockSpec(shape, lambda *_: (0,) * len(shape))


def turn(tiles):
    tiles = list(tiles)
    sub = lax.broadcasted_iota(jnp.int32, tiles[0].shape, 0)
    size = len(tiles)
    step = size // 2
    while step:
        keep = (sub & step) == 0
        for i in range(size):
            if not i & step:
                one, two = (tiles[i], tiles[i + step])
                tiles[i] = jnp.where(keep, one, pltpu.roll(two, step, 0))
                tiles[i + step] = jnp.where(keep, pltpu.roll(one, size - step, 0), two)
        step //= 2
    return tiles


def turn_all(read, write, count):
    def some(s, carry):
        for i in range(NODES):
            t = s * NODES + i
            for r, tile in enumerate(turn([read(k, t) for k in range(8)])):
                write(t, r, tile)
        return carry

    lax.fori_loop(0, count // NODES, some, 0)


def rows_at(k, unit, t):
    return pl.ds(pl.multiple_of(k * unit + 8 * t, 8), 8)


def pack_one(x_ref, write_out, mid, layers, lanes):
    square = NODES * NODES
    per_plane = square * layers
    unit = 2 * per_plane
    half = lanes // 2
    low = lanes_of((8, lanes)) < half

    def write(t, r, tile):
        mid[8 * t + r] = tile

    turn_all(lambda k, t: x_ref[0, rows_at(k, unit, t), :], write, unit // 8)

    def layer(e, carry):
        for n in range(square):
            cos = mid[n * layers + e]
            sin = mid[per_plane + n * layers + e]
            write_out(2 * e, n, jnp.where(low, cos, pltpu.roll(sin, half, 1)))
            write_out(2 * e + 1, n, jnp.where(low, pltpu.roll(cos, half, 1), sin))
        return carry

    lax.fori_loop(0, layers, layer, 0)


def pack_specs(layers, pairs, lanes, nodes):
    return (
        pl.BlockSpec((2 * layers, nodes, 8, lanes), lambda g: (0, 0, g, 0)),
        jax.ShapeDtypeStruct((2 * layers, nodes, pairs, lanes), jnp.float32),
    )


def pack_first(rows, layers, pairs, lanes):
    square = NODES * NODES
    unit = 2 * square * layers

    def body(x_ref, o_ref, mid):
        def write(d, n, value):
            o_ref[d, n] = value

        pack_one(x_ref, write, mid, layers, lanes)

    spec, shape = pack_specs(layers, pairs, lanes, square)
    return call(
        body,
        (pairs // 8,),
        [pl.BlockSpec((1, 8 * unit, lanes), lambda g: (0, g, 0))],
        spec,
        shape,
        scratch=[pltpu.VMEM((unit, 8, lanes), jnp.float32)],
        grant=WHOLE_GRANT,
        moved=2 * rows.shape[1] * lanes * 4,
    )(rows)


def pack_rest(rows, layers, pairs, lanes, early):
    square = NODES * NODES
    unit = 2 * square * layers

    def body(x_ref, y_ref, o_ref, late_ref, whole_ref, mid):
        def first(d, n, value):
            o_ref[d, n] = value

        def second(d, n, value):
            whole_ref[d, n] = value
            if n < early:
                o_ref[d, square + n] = value
            else:
                late_ref[d, n - early] = value

        pack_one(x_ref, first, mid, layers, lanes)
        pack_one(y_ref, second, mid, layers, lanes)

    parts = [
        pack_specs(layers, pairs, lanes, nodes)
        for nodes in (square + early, square - early, square)
    ]
    return call(
        body,
        (pairs // 8,),
        [
            pl.BlockSpec((1, 8 * unit, lanes), lambda g: (1, g, 0)),
            pl.BlockSpec((1, 8 * unit, lanes), lambda g: (2, g, 0)),
        ],
        [part[0] for part in parts],
        [part[1] for part in parts],
        scratch=[pltpu.VMEM((unit, 8, lanes), jnp.float32)],
        grant=WHOLE_GRANT,
        moved=5 * rows.shape[1] * lanes * 4,
    )(rows, rows)


def unpack(arrays, specs, read_from, slots, layers, buffer, total, steps=2):
    lanes = arrays[0].shape[-1]
    square = NODES * NODES
    per_plane = square * layers
    unit = 2 * per_plane
    half = lanes // 2

    def body(*refs):
        o_ref, mid = refs[-2:]
        low = lanes_of((8, lanes)) < half
        read = read_from(refs, pl.program_id(0))

        def layer(e, carry):
            for n in range(square):
                left, right = (read(2 * e, n), read(2 * e + 1, n))
                mid[n * layers + e] = jnp.where(low, left, pltpu.roll(right, half, 1))
                mid[per_plane + n * layers + e] = jnp.where(low, pltpu.roll(left, half, 1), right)
            return carry

        lax.fori_loop(0, layers, layer, 0)

        def write(t, r, tile):
            o_ref[rows_at(r, unit, t), :] = tile

        turn_all(lambda k, t: mid[8 * t + k], write, unit // 8)

    extra = [] if buffer is None else [buffer]
    return call(
        body,
        (steps,),
        list(specs) + [pl.BlockSpec(memory_space=pl.ANY)] * len(extra),
        pl.BlockSpec((8 * unit, lanes), lambda i: (slots[0] + i * slots[1], 0)),
        jax.ShapeDtypeStruct((total, lanes), jnp.float32),
        scratch=[pltpu.VMEM((unit, 8, lanes), jnp.float32)],
        moved=4 * 8 * unit * lanes * 4,
        aliases={len(arrays): 0} if extra else None,
    )(*arrays, *extra)


def paired_nodes():
    return [(b, min(b + 1, NODES - 1)) for b in range(0, NODES, 2)]


def three_pass(table, rhs_ref, tiles):
    rows, lanes = tiles[0].shape
    half = lanes // 2
    low = lanes_of((rows, lanes)) < half
    depth = 2 * rows
    for place, (one, two) in enumerate(paired_nodes()):
        first, second = (tiles[one], tiles[two])
        cut = pl.ds(place * lanes, lanes)
        for part in range(2):
            if part == 0:
                value = jnp.where(low, first, pltpu.roll(second, half, 1))
            else:
                value = jnp.where(low, pltpu.roll(first, half, 1), second)
            high = value.astype(jnp.bfloat16)
            rest = (value - high.astype(jnp.float32)).astype(jnp.bfloat16)
            rhs_ref[pl.ds(part * rows, rows), cut] = high
            rhs_ref[pl.ds(depth + part * rows, rows), cut] = rest
            rhs_ref[pl.ds(2 * depth + part * rows, rows), cut] = high
    out = jnp.dot(table, rhs_ref[...], preferred_element_type=jnp.float32)
    fields = []
    for field in range(table.shape[0] // depth):
        nodes = [None] * NODES
        for place, (one, two) in enumerate(paired_nodes()):
            cut = slice(place * lanes, (place + 1) * lanes)
            top = out[field * depth : field * depth + rows, cut]
            bottom = out[field * depth + rows : (field + 1) * depth, cut]
            nodes[one] = jnp.where(low, top, pltpu.roll(bottom, half, 1))
            if two != one:
                nodes[two] = jnp.where(low, pltpu.roll(top, half, 1), bottom)
        fields.append(nodes)
    return fields


def rhs_scratch(table, lanes):
    return pltpu.VMEM((table.shape[1], len(paired_nodes()) * lanes), jnp.bfloat16)


def read_tiles(x_ref, rows, lanes):
    return [x_ref[:, b].reshape(rows, lanes) for b in range(NODES)]


def to_points(blocks, table):
    shares, _, pairs, lanes = blocks.shape
    square = NODES * NODES
    rows = shares * pairs

    def body(t_ref, x_ref, v_ref, z_ref, rhs_ref):
        fields = three_pass(t_ref[...], rhs_ref, read_tiles(x_ref, rows, lanes))
        for b in range(NODES):
            v_ref[b] = fields[0][b]
            z_ref[b] = fields[1][b]

    spec = pl.BlockSpec((NODES, rows, lanes), lambda a: (a, 0, 0))
    shape = jax.ShapeDtypeStruct((square, rows, lanes), jnp.float32)
    return call(
        body,
        (NODES,),
        [
            whole(table.shape),
            pl.BlockSpec((shares, NODES, pairs, lanes), lambda a: (0, a, 0, 0)),
        ],
        [spec, spec],
        [shape, shape],
        scratch=[rhs_scratch(table, lanes)],
        flops=2 * table.shape[0] * table.shape[1] * square * lanes,
        grant=WHOLE_GRANT,
        moved=3 * square * rows * lanes * 4,
    )(table, blocks)


def turn_around(blocks, skip, start, count, partial, slope_z, table, back, fields, out):
    shares, _, pairs, lanes = blocks.shape
    rows = shares * pairs
    square = NODES * NODES
    group = pairs // 2
    shape = jax.ShapeDtypeStruct((square, rows, lanes), jnp.float32)

    def body(t_ref, i_ref, x_ref, g_ref, s_ref, *refs):
        w_ref, z_ref, o_ref, rhs_ref = refs[-4:]
        points = three_pass(t_ref[...], rhs_ref, read_tiles(x_ref, rows, lanes))
        for b in range(NODES):
            w_ref[b] = points[0][b]
            z_ref[b] = points[1][b]
        tiles = [g_ref[b] + w_ref[b] * s_ref[b] for b in range(NODES)]
        spectral = three_pass(i_ref[...], rhs_ref, tiles)[0]
        for b in range(NODES):
            value = spectral[b].reshape(shares, pairs, lanes)
            if out is None:
                o_ref[:, b] = value
            else:
                for g in range(2):
                    o_ref[:, g * NODES + b] = value[:, g * group : (g + 1) * group]

    spec = pl.BlockSpec((NODES, rows, lanes), lambda a: (start + a, 0, 0))
    if out is None:
        out_spec = pl.BlockSpec((shares, NODES, pairs, lanes), lambda a: (0, a, 0, 0))
        out_shape = jax.ShapeDtypeStruct((shares, count * NODES, pairs, lanes), jnp.float32)
    else:
        first = out[1]
        out_spec = pl.BlockSpec((shares, 2 * NODES, group, lanes), lambda a: (0, first + a, 0, 0))
        out_shape = jax.ShapeDtypeStruct(out[0], jnp.float32)
    return call(
        body,
        (count,),
        [
            whole(table.shape),
            whole(back.shape),
            pl.BlockSpec((shares, NODES, pairs, lanes), lambda a: (0, skip + a, 0, 0)),
            spec,
            spec,
        ]
        + [pl.BlockSpec(memory_space=pl.ANY)] * len(fields),
        [spec, spec, out_spec],
        [shape, shape, out_shape],
        scratch=[rhs_scratch(table, lanes)],
        flops=3 * table.shape[0] * table.shape[1] * count * NODES * lanes,
        aliases={5: 0, 6: 1} if fields else None,
        grant=WHOLE_GRANT,
        moved=6 * count * NODES * rows * lanes * 4,
    )(table, back, blocks, partial, slope_z, *fields)


def in_plane(speeds, fields, metrics, table):
    square, rows, lanes = speeds[0].shape
    count = len(fields)
    step = 32
    own = [i for i, f in enumerate(fields) if all(f is not s for s in speeds)]
    arrays = list(speeds) + [fields[i] for i in own]

    def body(m_ref, *refs):
        ins, outs = (refs[: len(arrays)], refs[len(arrays) :])
        u_ref, v_ref = ins[:2]
        sources = []
        extra = 2
        for i, f in enumerate(fields):
            if i in own:
                sources.append(ins[extra])
                extra += 1
            else:
                sources.append(u_ref if f is speeds[0] else v_ref)

        def block(s, carry):
            r = pl.ds(s * 8, 8)

            def metric(kind, n):
                return row_of(m_ref, kind * square + n, 8)

            for a in range(NODES):
                ns = [a * NODES + b for b in range(NODES)]
                drift = [
                    u_ref[n, r] * metric(2, n) + v_ref[n, r] * metric(3, n) for n in ns
                ]
                for f in range(count):
                    beside = apply_line(table, [sources[f][n, r] for n in ns])
                    for b, n in enumerate(ns):
                        outs[f][n, r] = drift[b] * beside[b]
            for b in range(NODES):
                ns = [a * NODES + b for a in range(NODES)]
                drift = [
                    u_ref[n, r] * metric(0, n) + v_ref[n, r] * metric(1, n) for n in ns
                ]
                for f in range(count):
                    radial = apply_line(table, [sources[f][n, r] for n in ns])
                    for a, n in enumerate(ns):
                        outs[f][n, r] = outs[f][n, r] + drift[a] * radial[a]
            return carry

        lax.fori_loop(0, step // 8, block, 0)

    spec = pl.BlockSpec((square, step, lanes), lambda i: (0, i, 0))
    shape = jax.ShapeDtypeStruct((square, rows, lanes), jnp.float32)
    return call(
        body,
        (rows // step,),
        [whole(metrics.shape)] + [spec] * len(arrays),
        [spec] * count,
        [shape] * count,
        flops=30 * count * square * rows * lanes,
        grant=WHOLE_GRANT,
        moved=(len(arrays) + count) * square * rows * lanes * 4,
    )(metrics, *arrays)


def to_planes(partial, speed_z, slope_z, table, shares, place, shapes, buffers):
    square, rows, lanes = partial.shape
    pairs = rows // shares
    group = pairs // 2

    def body(t_ref, g_ref, w_ref, z_ref, *refs):
        outs, rhs_ref = (refs[-3:-1], refs[-1])
        tiles = [g_ref[b] + w_ref[b] * z_ref[b] for b in range(NODES)]
        nodes = three_pass(t_ref[...], rhs_ref, tiles)[0]
        for b in range(NODES):
            out = nodes[b].reshape(shares, pairs, lanes)
            for i in range(2):
                outs[i][:, b] = out[:, i * group : (i + 1) * group]

    spec = pl.BlockSpec((NODES, rows, lanes), lambda a: (a, 0, 0))
    out_spec = pl.BlockSpec((shares, NODES, group, lanes), lambda a: (0, place * NODES + a, 0, 0))
    shapes = [jax.ShapeDtypeStruct(shape, jnp.float32) for shape in shapes]
    return call(
        body,
        (NODES,),
        [whole(table.shape), spec, spec, spec]
        + [pl.BlockSpec(memory_space=pl.ANY)] * len(buffers),
        [out_spec, out_spec],
        shapes,
        scratch=[rhs_scratch(table, lanes)],
        flops=2 * table.shape[0] * table.shape[1] * square * lanes,
        grant=WHOLE_GRANT,
        moved=4 * square * rows * lanes * 4,
        aliases={4 + k: k for k in range(len(buffers))},
    )(table, partial, speed_z, slope_z, *buffers)


def velocity_part(sent, metrics, weights, waves, table):
    shares, square, pairs, lanes = sent[0].shape
    half = lanes // 2

    def body(m_ref, q_ref, k_ref, s0, s1, s2, o_ref):
        d = pl.program_id(0)

        def rows_of(s):
            r = pl.ds(s * 8, 8)
            wave = k_ref[r]

            def metric(kind, n):
                return row_of(m_ref, (kind * shares + d) * square + n, 8)

            for a in range(NODES):
                ns = [a * NODES + b for b in range(NODES)]
                first = apply_line(table, [s0[0, n, r] for n in ns])
                second = apply_line(table, [s1[0, n, r] for n in ns])
                for b, n in enumerate(ns):
                    along = pltpu.roll(s2[0, n, r], half, 1) * wave
                    o_ref[0, n, r] = (
                        metric(2, n) * first[b]
                        + metric(3, n) * second[b]
                        + row_of(q_ref, d * square + n, 8) * along
                    )
            for b in range(NODES):
                ns = [a * NODES + b for a in range(NODES)]
                first = apply_line(table, [s0[0, n, r] for n in ns])
                second = apply_line(table, [s1[0, n, r] for n in ns])
                for a, n in enumerate(ns):
                    o_ref[0, n, r] = o_ref[0, n, r] + (
                        metric(0, n) * first[a] + metric(1, n) * second[a]
                    )

        lax.fori_loop(0, pairs // 8, lambda s, carry: (rows_of(s), carry)[1], 0)

    spec = pl.BlockSpec((1, square, pairs, lanes), lambda d: (d, 0, 0, 0))
    return call(
        body,
        (shares,),
        [whole(metrics.shape), whole(weights.shape), whole(waves.shape)] + [spec] * 3,
        spec,
        jax.ShapeDtypeStruct(sent[0].shape, jnp.float32),
        flops=60 * shares * square * pairs * lanes,
        grant=WHOLE_GRANT,
        moved=4 * shares * square * pairs * lanes * 4,
    )(metrics, weights, waves, *sent)


def first_part(base, early, rest, rest_at, metrics, table):
    shares, square, pairs, lanes = base.shape

    some = early.shape[1]
    count = (square - some) // NODES
    group = pairs // 2

    def body(m_ref, s0, r0, *refs):
        others, (o_ref, p0) = (refs[:count], refs[count:])
        d = pl.program_id(0)

        def block(s, carry):
            r = pl.ds(s * 8, 8)
            for n in range(square):
                if n < some:
                    home = r0[0, n, r]
                else:
                    a, b = divmod(n - some, NODES)
                    home = others[a][0, s * NODES + b]
                p0[n] = home

            def metric(kind, n):
                return row_of(m_ref, (kind * shares + d) * square + n, 8)

            for a in range(NODES):
                ns = [a * NODES + b for b in range(NODES)]
                line = apply_line(table, [p0[n] for n in ns])
                for b, n in enumerate(ns):
                    o_ref[0, n, r] = s0[0, n, r] + metric(2, n) * line[b]
            for b in range(NODES):
                ns = [a * NODES + b for a in range(NODES)]
                line = apply_line(table, [p0[n] for n in ns])
                for a, n in enumerate(ns):
                    o_ref[0, n, r] = o_ref[0, n, r] + metric(0, n) * line[a]
            return carry

        lax.fori_loop(0, pairs // 8, block, 0)

    spec = pl.BlockSpec((1, square, pairs, lanes), lambda d: (d, 0, 0, 0))
    return call(
        body,
        (shares,),
        [whole(metrics.shape), spec, pl.BlockSpec((1, some, pairs, lanes), lambda d: (d, 0, 0, 0))]
        + [
            pl.BlockSpec(
                (1, 2 * NODES, group, lanes), functools.partial(lambda i, d: (d, i, 0, 0), rest_at + k)
            )
            for k in range(count)
        ],
        spec,
        jax.ShapeDtypeStruct(base.shape, jnp.float32),
        scratch=[pltpu.VMEM((square, 8, lanes), jnp.float32)],
        flops=30 * shares * square * pairs * lanes,
        grant=WHOLE_GRANT,
        moved=3 * shares * square * pairs * lanes * 4,
    )(metrics, base, early, *[rest] * count)


def join_layers(y_ref, layers):
    square = NODES * NODES
    last = (NODES - 1) * NODES
    for e in range(layers - 1):
        for b in range(NODES):
            upper, lower = (e * square + last + b, (e + 1) * square + b)
            total = y_ref[upper] + y_ref[lower]
            y_ref[upper] = total
            y_ref[lower] = total
    for b in range(NODES):
        node = (layers - 1) * square + last + b
        y_ref[node] = jnp.zeros_like(y_ref[node])


def rim_messages(read, layers, shape, partials):
    lane = lanes_of(shape)
    lanes = shape[-1]
    axis = len(shape) - 1
    first = jnp.zeros(shape, jnp.float32)
    last = jnp.zeros(shape, jnp.float32)
    square = NODES * NODES
    for e in range(layers):
        for a in range(NODES):
            spot = e * NODES + a
            here = lane == spot
            node = e * square + a * NODES
            first = jnp.where(here, pltpu.roll(read(node), spot, axis), first)
            last = jnp.where(
                here, pltpu.roll(read(node + NODES - 1), (spot + 1) % lanes, axis), last
            )
    for i, partial in enumerate(partials):
        here = lane == layers * NODES + i
        first = jnp.where(here, partial, first)
        last = jnp.where(here, partial, last)
    return (first, last)


def right_side(flat, returned, metrics, weights, waves, table, layers, place):
    shares, square, _, lanes = flat.shape
    half = lanes // 2

    def body(m_ref, q_ref, k_ref, f_ref, r1, r2, o_ref, first_ref, last_ref, c0, c1):
        e = pl.program_id(0)
        lane = lanes_of((8, lanes))
        low = lane < half
        wave = k_ref[...]
        sides = (c0, c1)

        @pl.when(e == 0)
        def _():
            first_ref[...] = jnp.zeros_like(first_ref)
            last_ref[...] = jnp.zeros_like(last_ref)

        for h in range(2):
            d = 2 * e + h
            side = sides[h]
            for n in range(square):
                along = pltpu.roll(r2[h, n], half, 1) * wave
                side[n] = f_ref[h, n] + row_of(q_ref, d * square + n, 8) * along

            def metric(kind, n):
                return row_of(m_ref, (kind * shares + d) * square + n, 8)

            for a in range(NODES):
                ns = [a * NODES + b for b in range(NODES)]
                line = apply_line(table, [r1[h, n] for n in ns])
                for b, n in enumerate(ns):
                    side[n] = side[n] + metric(3, n) * line[b]
            for b in range(NODES):
                ns = [a * NODES + b for a in range(NODES)]
                line = apply_line(table, [r1[h, n] for n in ns])
                for a, n in enumerate(ns):
                    side[n] = side[n] + metric(1, n) * line[a]
        rims = [[first_ref[0], last_ref[0]], [first_ref[1], last_ref[1]]]
        for n in range(square):
            left, right = (c0[n], c1[n])
            parts = (
                jnp.where(low, left, pltpu.roll(right, half, 1)),
                jnp.where(low, pltpu.roll(left, half, 1), right),
            )
            for i in range(2):
                o_ref[n, i] = parts[i]
                a, b = divmod(n, NODES)
                spot = e * NODES + a
                if b == 0:
                    rims[i][0] = jnp.where(lane == spot, pltpu.roll(parts[i], spot, 1), rims[i][0])
                if b == NODES - 1:
                    rims[i][1] = jnp.where(
                        lane == spot, pltpu.roll(parts[i], spot + 1, 1), rims[i][1]
                    )
        for i in range(2):
            first_ref[i] = rims[i][0]
            last_ref[i] = rims[i][1]

    spec = pl.BlockSpec((2, square, 8, lanes), lambda e: (e, 0, place, 0))
    nodes = layers * square
    rim_shape = jax.ShapeDtypeStruct((2, 8, lanes), jnp.float32)
    scratch = pltpu.VMEM((square, 8, lanes), jnp.float32)
    return call(
        body,
        (layers,),
        [
            whole(metrics.shape),
            whole(weights.shape),
            pl.BlockSpec((8, lanes), lambda e: (place, 0)),
            spec,
            pl.BlockSpec((2, square, 8, lanes), lambda e: (e, 0, 0, 0)),
            pl.BlockSpec((2, square, 8, lanes), lambda e: (e, 1, 0, 0)),
        ],
        [
            pl.BlockSpec((square, 2, 8, lanes), lambda e: (e, 0, 0, 0)),
            whole((2, 8, lanes)),
            whole((2, 8, lanes)),
        ],
        [jax.ShapeDtypeStruct((nodes, 2, 8, lanes), jnp.float32), rim_shape, rim_shape],
        scratch=[scratch] * 2,
        flops=40 * shares * square * 8 * lanes,
        moved=4 * shares * square * 8 * lanes * 4,
    )(metrics, weights, waves, flat, returned, returned)


def swap_rims(first, last):
    size = lax.axis_size("elem")
    up = [(i, (i + 1) % size) for i in range(size)]
    down = [(j, i) for i, j in up]
    return (lax.ppermute(last, "elem", up), lax.ppermute(first, "elem", down))


def opposite(first):
    size = lax.axis_size("elem")
    return lax.ppermute(first, "elem", [(i, (i + 2) % size) for i in range(size)])


def join_columns(read, ref, before, after, layers):
    lanes = before.shape[-1]
    axis = len(before.shape) - 1
    lane = lanes_of(before.shape)
    square = NODES * NODES
    for e in range(layers):
        for a in range(NODES):
            spot = e * NODES + a
            node = e * square + a * NODES
            first, last = (read(node), read(node + NODES - 1))
            beyond = pltpu.roll(after, lanes - 1 - spot, axis)
            ahead = jnp.where(lane == lanes - 1, beyond, pltpu.roll(first, lanes - 1, axis))
            right = last + ahead
            mine = first + (pltpu.roll(before, lanes - spot, axis) if spot else before)
            ref[node + NODES - 1] = right
            ref[node] = jnp.where(lane == 0, mine, pltpu.roll(right, 1, axis))


def join(source, ref, before, after, layers):
    square = NODES * NODES

    def copy(e, carry):
        for n in range(square):
            if 0 < n % NODES < NODES - 1:
                ref[e * square + n] = source[e * square + n]
        return carry

    lax.fori_loop(0, layers, copy, 0)
    join_columns(lambda n: source[n], ref, before, after, layers)
    join_layers(ref, layers)


def each_node(layers, step):
    def layer(e, carry):
        for n in range(NODES * NODES):
            step(e * NODES * NODES + n)
        return carry

    lax.fori_loop(0, layers, layer, 0)


def share_of(layers, e, a):
    if a == 0:
        return jnp.where(e > 0, 0.5, 1.0)
    if a == NODES - 1:
        return jnp.where(e < layers - 1, 0.5, 0.0)
    return 1.0


def helmholtz(r_ref, y_ref, flux_ref, g_ref, shift, layers, table, dot_only=False):
    square = NODES * NODES
    nodes = layers * square
    turned = table.T
    zero = jnp.zeros(shift.shape, jnp.float32)

    def layer(e, carry):
        norm, energy = carry
        base = e * square

        def metric(kind, n):
            return row_of(g_ref, kind * nodes + base + n, 8)

        for b in range(NODES):
            ns = [a * NODES + b for a in range(NODES)]
            radial = apply_line(table, [r_ref[base + n] for n in ns])
            for a, n in enumerate(ns):
                flux_ref[n] = radial[a]
        for a in range(NODES):
            ns = [a * NODES + b for b in range(NODES)]
            line = [r_ref[base + n] for n in ns]
            beside = apply_line(table, line)
            second = []
            rest = []
            part = zero
            for b, n in enumerate(ns):
                radial = flux_ref[n]
                cross = metric(1, n)
                one = metric(0, n) * radial + cross * beside[b]
                two = cross * radial + metric(2, n) * beside[b]
                same = shift * metric(3, n) * line[b]
                whole_weight = line[b] * line[b]
                part = part + (0.5 * whole_weight if b in (0, NODES - 1) else whole_weight)
                if dot_only:
                    energy = energy + (radial * one + beside[b] * two + same * line[b])
                else:
                    flux_ref[n] = one
                    second.append(two)
                    rest.append(same)
            norm = norm + part * share_of(layers, e, a)
            if not dot_only:
                back = apply_line(turned, second)
                for b, n in enumerate(ns):
                    y_ref[base + n] = rest[b] + back[b]
        if not dot_only:
            for b in range(NODES):
                ns = [a * NODES + b for a in range(NODES)]
                back = apply_line(turned, [flux_ref[n] for n in ns])
                for a, n in enumerate(ns):
                    value = y_ref[base + n] + back[a]
                    y_ref[base + n] = value
                    energy = energy + value * r_ref[base + n]
        return (norm, energy)

    norm, energy = lax.fori_loop(0, layers, layer, (zero, zero))
    axis = len(shift.shape) - 1
    return (
        jnp.sum(norm, axis=axis, keepdims=True),
        jnp.sum(energy, axis=axis, keepdims=True),
    )


def lane_value(block, lane):
    return block[..., lane : lane + 1]


def sums_from(own, left, right, far, layers):
    total = (own[...] + far[...]) + (left[...] + right[...])
    spot = layers * NODES
    return (lane_value(total, spot), lane_value(total, spot + 1))


def scalars_block(shape, values, spot=0):
    lane = lanes_of(shape)
    out = jnp.zeros(shape, jnp.float32)
    for i, value in enumerate(values):
        out = jnp.where(lane == spot + i, value, out)
    return out


def shapes_of(field):
    return (
        jax.ShapeDtypeStruct(field.shape, jnp.float32),
        jax.ShapeDtypeStruct(field.shape[1:], jnp.float32),
        pltpu.VMEM((NODES * NODES,) + field.shape[1:], jnp.float32),
    )


def first_image(raw, before, after, shift, geo, layers, table):
    field, small, flux_scratch = shapes_of(raw)
    shape = raw.shape[1:]

    def body(g_ref, k_ref, f_ref, b_ref, a_ref, r_ref, y_ref, first_ref, last_ref, flux):
        join(f_ref, r_ref, b_ref[...], a_ref[...], layers)
        sums = helmholtz(r_ref, y_ref, flux, g_ref, k_ref[...], layers, table)
        first_ref[...], last_ref[...] = rim_messages(lambda n: y_ref[n], layers, shape, sums)

    return call(
        body,
        (),
        held(5),
        held(4),
        [field, field, small, small],
        scratch=[flux_scratch],
        flops=80 * raw.size,
        moved=12 * raw.size,
    )(geo, shift, raw, before, after)


def second_image(start, image, messages, shift, geo, layers, table):
    field, small, flux_scratch = shapes_of(start)
    shape = start.shape[1:]

    def body(g_ref, k_ref, r0, y0, own, left, right, far, *rest):
        w_ref, y_ref, first_ref, last_ref, scalar_ref, r1, flux = rest
        norm, energy = sums_from(own, left, right, far, layers)
        alpha = jnp.broadcast_to(norm / energy, shape)
        join(y0, w_ref, left[...], right[...], layers)

        def move(node):
            r1[node] = r0[node] - alpha * w_ref[node]

        each_node(layers, move)
        sums = helmholtz(r1, y_ref, flux, g_ref, k_ref[...], layers, table)
        first_ref[...], last_ref[...] = rim_messages(lambda n: y_ref[n], layers, shape, sums)
        scalar_ref[...] = scalars_block(shape, (alpha, norm, energy))

    return call(
        body,
        (),
        held(8),
        held(5),
        [field, field, small, small, small],
        scratch=[pltpu.VMEM(start.shape, jnp.float32), flux_scratch],
        flops=80 * start.size,
        moved=16 * start.size,
    )(geo, shift, start, image, *messages)


def third_energy(start, joined, image, messages, scalars, shift, geo, layers, table):
    field, small, flux_scratch = shapes_of(start)
    shape = start.shape[1:]

    def body(g_ref, k_ref, r0, w0, y1, own, left, right, far, old, *rest):
        r2, d2, sums_ref, scalar_ref, w1, flux = rest
        norm, energy = sums_from(own, left, right, far, layers)
        before = old[...]
        alpha = jnp.broadcast_to(lane_value(before, 0), shape)
        ratio = norm / lane_value(before, 1)
        curve = energy - ratio * ratio * lane_value(before, 2)
        step = jnp.broadcast_to(norm / curve, shape)
        beta = jnp.broadcast_to(ratio, shape)
        join(y1, w1, left[...], right[...], layers)

        def move(node):
            w = w0[node]
            start_value = r0[node]
            moved = start_value - alpha * w
            d2[node] = moved + beta * start_value
            r2[node] = moved - step * (w1[node] + beta * w)

        each_node(layers, move)
        sums = helmholtz(r2, None, flux, g_ref, k_ref[...], layers, table, dot_only=True)
        sums_ref[...] = scalars_block(shape, sums, layers * NODES)
        scalar_ref[...] = scalars_block(shape, (alpha, norm, curve, step))

    return call(
        body,
        (),
        held(10),
        held(4),
        [field, field, small, small],
        scratch=[pltpu.VMEM(start.shape, jnp.float32), flux_scratch],
        flops=60 * start.size,
        moved=20 * start.size,
    )(geo, shift, start, joined, image, *messages, scalars)


def finish(start, direction, residual, messages, scalars, layers, place, buffer, total):
    nodes, _, rows, lanes = start.shape
    shape = start.shape[1:]
    square = NODES * NODES

    unit = 2 * nodes

    def body(r0, d2, r2, own, left, right, far, old, *refs):
        o_ref, mid = refs[-2:]
        norm, energy = sums_from(own, left, right, far, layers)
        before = old[...]
        ratio = norm / lane_value(before, 1)
        curve = energy - ratio * ratio * lane_value(before, 2)
        step = norm / curve
        third = jnp.broadcast_to(step, shape)
        second = jnp.broadcast_to(lane_value(before, 3) + step * ratio, shape)
        first = jnp.broadcast_to(lane_value(before, 0), shape)

        def layer(e, carry):
            for n in range(square):
                node = e * square + n
                value = first * r0[node] + second * d2[node] + third * r2[node]
                for i in range(2):
                    mid[i * nodes + n * layers + e] = value[i]
            return carry

        lax.fori_loop(0, layers, layer, 0)

        def write(t, r, tile):
            o_ref[rows_at(r, unit, t), :] = tile

        turn_all(lambda k, t: mid[8 * t + k], write, unit // 8)

    extra = [] if buffer is None else [buffer]
    return call(
        body,
        (1,),
        [whole(start.shape)] * 3
        + [whole(shape)] * 5
        + [pl.BlockSpec(memory_space=pl.ANY)] * len(extra),
        pl.BlockSpec((2 * rows * nodes, lanes), lambda i: (place, 0)),
        jax.ShapeDtypeStruct((total, lanes), jnp.float32),
        scratch=[pltpu.VMEM((unit, rows, lanes), jnp.float32)],
        flops=6 * start.size,
        moved=16 * start.size,
        aliases={8: 0} if extra else None,
    )(start, direction, residual, *messages, scalars, *extra)


def halves(values, shares):
    half = values.shape[-1] // 2
    parts = [jnp.concatenate([p, p], axis=-1) for p in (values[..., :half], values[..., half:])]
    return jnp.stack(parts, axis=2).reshape(values.shape[0], shares, NODES * NODES, 2 * half)


def on_device_paired(*arrays):
    return paired_step(*arrays)


def paired_step(velocity, radial_dx, radial_dy, around_dx, around_dy, jacobian):
    table = derivative_table()
    modes = lax.axis_size("mode")
    mode = lax.axis_index("mode")
    _, local_planes, layers, _, _, lanes = velocity.shape
    planes = local_planes * modes
    pairs = local_planes // 2
    first_plane = mode * local_planes
    square = NODES * NODES
    forward, backward = (jnp.asarray(t) for t in paired_tables(planes))

    rows = velocity.transpose(0, 1, 3, 4, 2, 5).reshape(3, local_planes * square * layers, lanes)
    plain = jnp.stack([radial_dx, radial_dy, around_dx, around_dy]).reshape(
        4, layers, square, lanes
    )
    both = halves(plain, modes)
    here = lax.dynamic_index_in_dim(both, mode, 1, keepdims=False).reshape(4 * square, lanes)
    metrics = geometry(radial_dx, radial_dy, around_dx, around_dy, jacobian)
    geo = jnp.stack(metrics).reshape(4 * layers * square, lanes)
    scaled = halves((metrics[3] * (-1.0 / time_step)).reshape(1, layers, square, lanes), modes)
    flux = (both * scaled).reshape(4 * modes * square, lanes)
    small_flux = flux * time_step
    scaled = scaled.reshape(modes * square, lanes)
    pair = (first_plane // 2 + jnp.arange(pairs, dtype=jnp.int32)).astype(jnp.float32)
    wave = pair[:, None] * spanwise_wave
    low = (jnp.arange(lanes) < lanes // 2)[None, :]
    waves = jnp.where(low, wave, -wave)
    small_waves = waves * time_step
    shift = plane_shift(first_plane, local_planes, planes).reshape(pairs, 2).T
    shift = jnp.broadcast_to(shift.reshape(2, 2, pairs // 2, 1), (2, 2, pairs // 2, lanes))
    shift = (shift[:, 0], shift[:, 1])

    def exchange(blocks):
        return lax.all_to_all(blocks, "mode", split_axis=0, concat_axis=0, tiled=True)

    some = (NODES // 2 + 1) * NODES
    group = pairs // 2
    first_shape = (modes, 4 * square - 2 * some, group, lanes)
    second_shape = (modes, 2 * square, group, lanes)
    sent_0 = pack_first(rows, layers, pairs, lanes)
    sent_1, late_2, sent_2 = pack_rest(rows, layers, pairs, lanes, some)
    arrived_0 = exchange(sent_0)
    sent_1, here, geo, flux, small_flux, scaled, waves, small_waves, shift = (
        lax.optimization_barrier(
            (sent_1, here, geo, flux, small_flux, scaled, waves, small_waves, shift)
        )
    )
    arrived_1 = exchange(sent_1)
    arrived_2 = exchange(late_2)
    speed_x, slope_0 = to_points(arrived_0, forward)
    speed_y, slope_1 = to_points(arrived_1, forward)
    speeds = [speed_x, speed_y]
    partial = in_plane(speeds, speeds, here, table)
    rows_early = some // NODES
    speed_z, slope_2, blocks = turn_around(
        arrived_1, NODES, 0, rows_early, partial[0], slope_0, forward, backward, (), None
    )
    home_0 = exchange(blocks)
    speed_z, slope_2, first_buffer = turn_around(
        arrived_2,
        0,
        rows_early,
        NODES - rows_early,
        partial[0],
        slope_0,
        forward,
        backward,
        (speed_z, slope_2),
        (first_shape, NODES),
    )
    last = in_plane(speeds, [speed_z], here, table)[0]
    shapes = (first_shape, second_shape)
    blocks = to_planes(partial[1], speed_z, slope_1, backward, modes, 0, shapes, (first_buffer,))
    blocks = to_planes(last, speed_z, slope_2, backward, modes, 1, shapes, blocks)
    home_1 = exchange(blocks[0])
    home_2 = exchange(blocks[1])
    returned = (home_1, home_2)
    base = velocity_part((sent_0, sent_1, sent_2), flux, scaled, waves, table)

    own_rows = local_planes * square * layers

    def read_first(refs, g):
        def read(d, n):
            if n < some:
                return refs[0][d, n]
            a, b = divmod(n - some, NODES)
            return refs[1 + a][d, g * NODES + b]

        return read

    def read_part(refs, i):
        return lambda d, n: refs[0][d, n]

    first_specs = [pl.BlockSpec((modes, some, group, lanes), lambda i: (0, 0, i, 0))] + [
        pl.BlockSpec(
            (modes, 2 * NODES, group, lanes), functools.partial(lambda k, i: (0, k, 0, 0), NODES + k)
        )
        for k in range(NODES - rows_early)
    ]
    part_specs = [pl.BlockSpec((modes, square, group, lanes), lambda i: (0, i, 0, 0))]
    advection = unpack(
        [home_0] + [home_1] * (NODES - rows_early),
        first_specs,
        read_first,
        (0, 1),
        layers,
        None,
        3 * own_rows,
    )
    flat = first_part(base, home_0, home_1, NODES, small_flux, table)

    def solve(place, flat, own_shift, buffer):
        raw, first, last = right_side(
            flat, returned[place], small_flux, scaled, small_waves, table, layers, place
        )
        before, after = swap_rims(first, last)
        start, image, first, last = first_image(raw, before, after, own_shift, geo, layers, table)
        messages = (first,) + swap_rims(first, last) + (opposite(first),)
        joined, image, first, last, scalars = second_image(
            start, image, messages, own_shift, geo, layers, table
        )
        messages = (first,) + swap_rims(first, last) + (opposite(first),)
        residual, direction, sums, scalars = third_energy(
            start, joined, image, messages, scalars, own_shift, geo, layers, table
        )
        messages = (sums,) + swap_rims(sums, sums) + (opposite(sums),)
        return finish(
            start, direction, residual, messages, scalars, layers, place, buffer, own_rows
        )

    pressure = solve(0, flat, shift[0], None)
    advection = unpack(
        [home_1], part_specs, read_part, (2, 2), layers, advection, 3 * own_rows
    )
    flat, pressure, advection, shift = lax.optimization_barrier(
        (flat, pressure, advection, shift)
    )

    def unpack_late(comp, buffer):
        spec = pl.BlockSpec((modes, square, group, lanes), lambda i: (0, comp, 0, 0))
        return unpack(
            [home_2], [spec], read_part, (3 + 2 * comp, 1), layers, buffer, 3 * own_rows, 1
        )

    pressure = solve(1, flat, shift[1], pressure)
    advection = unpack_late(1, unpack_late(0, advection))
    advection = advection.reshape(3, local_planes, NODES, NODES, layers, lanes)
    pressure = pressure.reshape(local_planes, NODES, NODES, layers, lanes)
    return (advection.transpose(0, 1, 4, 2, 3, 5), pressure.transpose(0, 3, 1, 2, 4))


def paired_fits(mesh, shape):
    modes, ring = (mesh.shape["mode"], mesh.shape["elem"])
    _, planes, layers, _, _, columns = shape
    return (
        ring == 4
        and columns == 128 * ring
        and modes == 2 * layers
        and layers % 4 == 0
        and planes == 32 * modes
        and (layers * NODES + 2 <= 128)
    )


def solution(mesh):
    placed = (
        P(None, "mode", None, None, None, "elem"),
        P(None, None, None, "elem"),
        P(None, None, None, "elem"),
        P(None, None, None, "elem"),
        P(None, None, None, "elem"),
        P(None, None, None, "elem"),
    )


    def step(velocity, *rest):
        body = on_device_paired if paired_fits(mesh, velocity.shape) else on_device
        return jax.shard_map(
            body,
            mesh=mesh,
            in_specs=placed,
            out_specs=(
                P(None, "mode", None, None, None, "elem"),
                P("mode", None, None, None, "elem"),
            ),
            check_vma=False,
        )(velocity, *rest)

    return step
```

```python
import functools
import math

import jax
import jax.numpy as jnp
import numpy as np
from jax import lax
from jax.experimental import pallas as pl
from jax.experimental.pallas import tpu as pltpu
from jax.sharding import PartitionSpec as P

NODES = 7
ITERS = 3
GRANT = 24 * 2**20
WHOLE_GRANT = 67043328


spanwise_wave = 2.0 * math.pi / 64.0
time_step = 0.1


def padded_2(value, sides, width):
    for axis, dim in sides:
        size, length = (lax.axis_size(axis), value.shape[dim])
        up = [(i, (i + 1) % size) for i in range(size)]
        down = [(j, i) for i, j in up]
        last = lax.slice_in_dim(value, length - width, length, axis=dim)
        leading = lax.slice_in_dim(value, 0, width, axis=dim)
        before = lax.ppermute(last, axis, up)
        after = lax.ppermute(leading, axis, down)
        value = jnp.concatenate([before, value, after], axis=dim)
    return value


def lobatto_rule(count):
    degree = count - 1
    points = np.cos(np.pi * np.arange(count) / degree)
    legendre = np.zeros((count, count))
    for _ in range(60):
        legendre[:, 0] = 1.0
        legendre[:, 1] = points
        for order in range(2, count):
            legendre[:, order] = (
                (2 * order - 1) * points * legendre[:, order - 1]
                - (order - 1) * legendre[:, order - 2]
            ) / order
        points = points - (points * legendre[:, degree] - legendre[:, degree - 1]) / (
            count * legendre[:, degree]
        )
    legendre[:, 0] = 1.0
    legendre[:, 1] = points
    for order in range(2, count):
        legendre[:, order] = (
            (2 * order - 1) * points * legendre[:, order - 1] - (order - 1) * legendre[:, order - 2]
        ) / order
    weights = 2.0 / (degree * count * legendre[:, degree] ** 2)
    return (points[::-1].copy(), weights[::-1].copy())


def derivative_table():
    lobatto_nodes = lobatto_rule(NODES)[0]
    total = lobatto_nodes.shape[0]
    scales = np.ones(total)
    for column in range(total):
        for other in range(total):
            if other != column:
                scales[column] = scales[column] / (lobatto_nodes[column] - lobatto_nodes[other])
    table = np.zeros((total, total))
    for row in range(total):
        for column in range(total):
            if row != column:
                table[row, column] = (
                    scales[column] / scales[row] / (lobatto_nodes[row] - lobatto_nodes[column])
                )
        table[row, row] = -np.sum(table[row])
    return table


def radial_derivative(table, field):
    return jnp.einsum("ia,...abe->...ibe", table, field, precision=lax.Precision.HIGHEST)


def around_derivative(table, field):
    return jnp.einsum("jb,...abe->...aje", table, field, precision=lax.Precision.HIGHEST)


def radial_transpose(table, field):
    return jnp.einsum("ia,...ibe->...abe", table, field, precision=lax.Precision.HIGHEST)


def around_transpose(table, field):
    return jnp.einsum("jb,...aje->...abe", table, field, precision=lax.Precision.HIGHEST)


def z_derivative(field, first_pair):
    shape = field.shape
    count = shape[1] // 2
    pairs = field.reshape((shape[0], count, 2) + shape[2:])
    waves = (first_pair + jnp.arange(count, dtype=jnp.int32)).astype(jnp.float32) * spanwise_wave
    waves = waves.reshape((1, count) + (1,) * (len(shape) - 2))
    return jnp.stack([waves * pairs[:, :, 1], -waves * pairs[:, :, 0]], axis=2).reshape(shape)


def transform_tables(planes):
    position = jnp.arange(planes, dtype=jnp.int32)
    plane = jnp.arange(planes, dtype=jnp.int32)
    order = plane // 2
    turns = position[:, None] * order[None, :] % planes
    angle = 2.0 * math.pi / planes * turns.astype(jnp.float32)
    cosine = jnp.cos(angle)
    sine = jnp.sin(angle)
    is_sine = (plane % 2 == 1)[None, :]
    is_top = (plane == 1)[None, :]
    parity = jnp.cos(math.pi * (position % 2).astype(jnp.float32))[:, None]
    basis = jnp.where(is_top, parity, jnp.where(is_sine, sine, cosine))
    scaling = jnp.where(order == 0, 1.0, 2.0).astype(jnp.float32) / planes
    inverse = jnp.transpose(basis * scaling[None, :])
    wave = (order.astype(jnp.float32) * spanwise_wave)[None, :]
    slope = jnp.where(is_sine, wave * cosine, -wave * sine)
    return (basis, inverse, slope)


def geometry(radial_dx, radial_dy, around_dx, around_dy, jacobian):
    lobatto_weights = lobatto_rule(NODES)[1]
    quadrature = jnp.asarray(np.outer(lobatto_weights, lobatto_weights), jnp.float32)[:, :, None]
    mass = quadrature * jacobian
    radial_stiff = mass * (radial_dx * radial_dx + radial_dy * radial_dy)
    cross_stiff = mass * (radial_dx * around_dx + radial_dy * around_dy)
    around_stiff = mass * (around_dx * around_dx + around_dy * around_dy)
    return (radial_stiff, cross_stiff, around_stiff, mass)


def node_weights(layers):
    layer = jnp.arange(layers, dtype=jnp.int32).reshape(layers, 1, 1, 1)
    node = jnp.arange(NODES, dtype=jnp.int32)
    radial_node = node.reshape(1, NODES, 1, 1)
    around_node = node.reshape(1, 1, NODES, 1)
    shared_radial = (radial_node == NODES - 1) & (layer < layers - 1) | (radial_node == 0) & (
        layer > 0
    )
    shared_around = (around_node == 0) | (around_node == NODES - 1)
    multiplicity = (1.0 + shared_radial.astype(jnp.float32)) * (
        1.0 + shared_around.astype(jnp.float32)
    )
    boundary = (radial_node == NODES - 1) & (layer == layers - 1)
    mask = 1.0 - boundary.astype(jnp.float32)
    return (mask, mask / multiplicity)


def plane_shift(first_plane, count, planes):
    plane = first_plane + jnp.arange(count, dtype=jnp.int32)
    order = jnp.where(plane == 1, planes // 2, plane // 2)
    wave = order.astype(jnp.float32) * spanwise_wave
    return (wave * wave).reshape(count, 1, 1, 1, 1)


def helmholtz_local(table, field, shift, metrics):
    radial_stiff, cross_stiff, around_stiff, mass = metrics
    radial = radial_derivative(table, field)
    beside_all = around_derivative(table, field)
    return (
        radial_transpose(table, radial_stiff * radial + cross_stiff * beside_all)
        + around_transpose(table, cross_stiff * radial + around_stiff * beside_all)
        + shift * mass * field
    )


def assemble(field):
    lower = field[:, :-1, -1] + field[:, 1:, 0]
    field = field.at[:, :-1, -1].set(lower).at[:, 1:, 0].set(lower)
    first = field[:, :, :, 0]
    last = field[:, :, :, -1]
    rims = jnp.concatenate([first[..., :1], last[..., -1:]], axis=3)
    padded = padded_2(rims, (("elem", 3),), 1)
    after = jnp.concatenate([first[..., 1:], padded[..., 3:4]], axis=3)
    right = last + after
    left = jnp.concatenate([padded[..., 0:1] + first[..., :1], right[..., :-1]], axis=3)
    return field.at[:, :, :, -1].set(right).at[:, :, :, 0].set(left)


def inner(first, second, weight):
    return jnp.sum(first * second * weight, axis=(1, 2, 3, 4))


def expand(scalar):
    return scalar.reshape(-1, 1, 1, 1, 1)


def squared_norm(residual, weight):
    return lax.psum(inner(residual, residual, weight), "elem")


def on_device(velocity, radial_dx, radial_dy, around_dx, around_dy, jacobian):
    table = jnp.asarray(derivative_table(), jnp.float32)
    modes = lax.axis_size("mode")
    local_planes = velocity.shape[1]
    planes = local_planes * modes
    first_plane = lax.axis_index("mode") * local_planes
    layers = velocity.shape[2]
    columns = velocity.shape[5]
    basis, inverse, slope = transform_tables(planes)
    radial = radial_derivative(table, velocity)
    beside_all = around_derivative(table, velocity)
    along_x = radial_dx * radial + around_dx * beside_all
    along_y = radial_dy * radial + around_dy * beside_all
    fields = jnp.concatenate([velocity, along_x, along_y], axis=0)
    count = fields.shape[0]
    cells = layers * NODES * NODES * columns
    packed = fields.reshape(count, local_planes, modes, cells // modes)
    flat = lax.all_to_all(packed, "mode", split_axis=2, concat_axis=1, tiled=True)[:, :, 0, :]
    values = jnp.einsum("jp,fpc->fjc", basis, flat, precision=lax.Precision.HIGHEST)
    speed = values[0:3]
    slope_x = values[3:6]
    slope_y = values[6:9]
    slope_z = jnp.einsum("jp,fpc->fjc", slope, flat[0:3], precision=lax.Precision.HIGHEST)
    product = -(speed[0:1] * slope_x + speed[1:2] * slope_y + speed[2:3] * slope_z)
    spectral = jnp.einsum("pj,fjc->fpc", inverse, product, precision=lax.Precision.HIGHEST)
    returned = lax.all_to_all(
        spectral[:, :, None, :], "mode", split_axis=1, concat_axis=2, tiled=True
    )
    advection = returned.reshape(velocity.shape)
    metrics = geometry(radial_dx, radial_dy, around_dx, around_dy, jacobian)
    mask, weight = node_weights(layers)
    predicted = velocity + time_step * advection
    radial = radial_derivative(table, predicted[0:2])
    beside_all = around_derivative(table, predicted[0:2])
    divergence = (
        radial_dx * radial[0]
        + around_dx * beside_all[0]
        + (radial_dy * radial[1] + around_dy * beside_all[1])
        + z_derivative(predicted[2:3], first_plane // 2)[0]
    )
    shift = plane_shift(first_plane, local_planes, planes)
    right_side = mask * assemble(-(metrics[3] * divergence) / time_step)
    solution = jnp.zeros_like(right_side)
    residual = right_side
    direction = right_side
    norm_now = squared_norm(residual, weight)
    for _ in range(ITERS):
        image = mask * assemble(helmholtz_local(table, direction, shift, metrics))
        alpha = norm_now / lax.psum(inner(direction, image, weight), "elem")
        solution = solution + expand(alpha) * direction
        residual = residual - expand(alpha) * image
        norm_next = squared_norm(residual, weight)
        direction = residual + expand(norm_next / norm_now) * direction
        norm_now = norm_next
    return (advection, solution)


def split_bf16(table):
    high = table.astype(jnp.bfloat16)
    low = (table - high.astype(np.float64)).astype(jnp.bfloat16)
    return np.concatenate([high, high, low], axis=1)


def paired_tables(planes):
    position = np.arange(planes)
    plane = np.arange(planes)
    order = plane // 2
    angle = 2.0 * np.pi / planes * (position[:, None] * order[None, :] % planes)
    cosine, sine = (np.cos(angle), np.sin(angle))
    odd = (plane % 2 == 1)[None, :]
    parity = (1.0 - 2.0 * (position % 2))[:, None]
    basis = np.where((plane == 1)[None, :], parity, np.where(odd, sine, cosine))
    wave = (order * spanwise_wave)[None, :]
    slope = np.where(odd, wave * cosine, -wave * sine)
    scaling = np.where(order == 0, 1.0, 2.0) / planes
    inverse = -(basis * scaling[None, :]).T

    def columns(matrix):
        return np.concatenate([matrix[:, 0::2], matrix[:, 1::2]], axis=1)

    forward = np.concatenate([columns(basis), columns(slope)])
    backward = columns(inverse.T).T
    return (split_bf16(forward), split_bf16(backward))


def apply_line(matrix, line):
    n = NODES
    m = n // 2
    sums = [line[a] + line[n - 1 - a] for a in range(m)]
    gaps = [line[a] - line[n - 1 - a] for a in range(m)]

    def total(parts):
        out = parts[0]
        for part in parts[1:]:
            out = out + part
        return out

    out = [None] * n
    for i in range(m + 1):
        plus = total(
            [float(0.5 * (matrix[i, a] - matrix[i, n - 1 - a])) * gaps[a] for a in range(m)]
        )
        if i == m:
            out[i] = plus
            continue
        minus = total(
            [float(0.5 * (matrix[i, a] + matrix[i, n - 1 - a])) * sums[a] for a in range(m)]
            + [float(matrix[i, m]) * line[m]]
        )
        out[i] = plus + minus
        out[n - 1 - i] = plus - minus
    return out


def lanes_of(shape):
    return lax.broadcasted_iota(jnp.int32, shape, len(shape) - 1)


def row_of(ref, row, rows):
    return ref[pl.ds(row, rows, stride=0), :]


def call(body, grid, ins, outs, out_shape, scratch=(), flops=0, moved=0, aliases=None, grant=GRANT):
    return pl.pallas_call(
        body,
        grid=grid,
        in_specs=ins,
        out_specs=outs,
        out_shape=out_shape,
        scratch_shapes=list(scratch),
        input_output_aliases=aliases or {},
        compiler_params=pltpu.CompilerParams(
            dimension_semantics=("arbitrary",) * len(grid), vmem_limit_bytes=grant
        ),
        cost_estimate=pl.CostEstimate(
            flops=int(flops), bytes_accessed=int(moved), transcendentals=0
        ),
    )


def held(count):
    return [pl.BlockSpec(memory_space=pltpu.VMEM)] * count


def whole(shape):
    return pl.BlockSpec(shape, lambda *_: (0,) * len(shape))


def turn(tiles):
    tiles = list(tiles)
    sub = lax.broadcasted_iota(jnp.int32, tiles[0].shape, 0)
    size = len(tiles)
    step = size // 2
    while step:
        keep = (sub & step) == 0
        for i in range(size):
            if not i & step:
                one, two = (tiles[i], tiles[i + step])
                tiles[i] = jnp.where(keep, one, pltpu.roll(two, step, 0))
                tiles[i + step] = jnp.where(keep, pltpu.roll(one, size - step, 0), two)
        step //= 2
    return tiles


def turn_all(read, write, count):
    def some(s, carry):
        for i in range(NODES):
            t = s * NODES + i
            for r, tile in enumerate(turn([read(k, t) for k in range(8)])):
                write(t, r, tile)
        return carry

    lax.fori_loop(0, count // NODES, some, 0)


def rows_at(k, unit, t):
    return pl.ds(pl.multiple_of(k * unit + 8 * t, 8), 8)


def pack_one(x_ref, write_out, mid, layers, lanes):
    square = NODES * NODES
    per_plane = square * layers
    unit = 2 * per_plane
    half = lanes // 2
    low = lanes_of((8, lanes)) < half

    def write(t, r, tile):
        mid[8 * t + r] = tile

    turn_all(lambda k, t: x_ref[0, rows_at(k, unit, t), :], write, unit // 8)

    def layer(e, carry):
        for n in range(square):
            cos = mid[n * layers + e]
            sin = mid[per_plane + n * layers + e]
            write_out(2 * e, n, jnp.where(low, cos, pltpu.roll(sin, half, 1)))
            write_out(2 * e + 1, n, jnp.where(low, pltpu.roll(cos, half, 1), sin))
        return carry

    lax.fori_loop(0, layers, layer, 0)


def pack_specs(layers, pairs, lanes, nodes):
    return (
        pl.BlockSpec((2 * layers, nodes, 8, lanes), lambda g: (0, 0, g, 0)),
        jax.ShapeDtypeStruct((2 * layers, nodes, pairs, lanes), jnp.float32),
    )


def pack_first(rows, layers, pairs, lanes):
    square = NODES * NODES
    unit = 2 * square * layers

    def body(x_ref, o_ref, mid):
        def write(d, n, value):
            o_ref[d, n] = value

        pack_one(x_ref, write, mid, layers, lanes)

    spec, shape = pack_specs(layers, pairs, lanes, square)
    return call(
        body,
        (pairs // 8,),
        [pl.BlockSpec((1, 8 * unit, lanes), lambda g: (0, g, 0))],
        spec,
        shape,
        scratch=[pltpu.VMEM((unit, 8, lanes), jnp.float32)],
        grant=WHOLE_GRANT,
        moved=2 * rows.shape[1] * lanes * 4,
    )(rows)


def pack_rest(rows, layers, pairs, lanes, early):
    square = NODES * NODES
    unit = 2 * square * layers

    def body(x_ref, y_ref, o_ref, late_ref, whole_ref, mid):
        def first(d, n, value):
            o_ref[d, n] = value

        def second(d, n, value):
            whole_ref[d, n] = value
            if n < early:
                o_ref[d, square + n] = value
            else:
                late_ref[d, n - early] = value

        pack_one(x_ref, first, mid, layers, lanes)
        pack_one(y_ref, second, mid, layers, lanes)

    parts = [
        pack_specs(layers, pairs, lanes, nodes)
        for nodes in (square + early, square - early, square)
    ]
    return call(
        body,
        (pairs // 8,),
        [
            pl.BlockSpec((1, 8 * unit, lanes), lambda g: (1, g, 0)),
            pl.BlockSpec((1, 8 * unit, lanes), lambda g: (2, g, 0)),
        ],
        [part[0] for part in parts],
        [part[1] for part in parts],
        scratch=[pltpu.VMEM((unit, 8, lanes), jnp.float32)],
        grant=WHOLE_GRANT,
        moved=5 * rows.shape[1] * lanes * 4,
    )(rows, rows)


def unpack(arrays, specs, read_from, slots, layers, buffer, total, steps=2):
    lanes = arrays[0].shape[-1]
    square = NODES * NODES
    per_plane = square * layers
    unit = 2 * per_plane
    half = lanes // 2

    def body(*refs):
        o_ref, mid = refs[-2:]
        low = lanes_of((8, lanes)) < half
        read = read_from(refs, pl.program_id(0))

        def layer(e, carry):
            for n in range(square):
                left, right = (read(2 * e, n), read(2 * e + 1, n))
                mid[n * layers + e] = jnp.where(low, left, pltpu.roll(right, half, 1))
                mid[per_plane + n * layers + e] = jnp.where(low, pltpu.roll(left, half, 1), right)
            return carry

        lax.fori_loop(0, layers, layer, 0)

        def write(t, r, tile):
            o_ref[rows_at(r, unit, t), :] = tile

        turn_all(lambda k, t: mid[8 * t + k], write, unit // 8)

    extra = [] if buffer is None else [buffer]
    return call(
        body,
        (steps,),
        list(specs) + [pl.BlockSpec(memory_space=pl.ANY)] * len(extra),
        pl.BlockSpec((8 * unit, lanes), lambda i: (slots[0] + i * slots[1], 0)),
        jax.ShapeDtypeStruct((total, lanes), jnp.float32),
        scratch=[pltpu.VMEM((unit, 8, lanes), jnp.float32)],
        moved=4 * 8 * unit * lanes * 4,
        aliases={len(arrays): 0} if extra else None,
    )(*arrays, *extra)


def paired_nodes():
    return [(b, min(b + 1, NODES - 1)) for b in range(0, NODES, 2)]


def three_pass(table, rhs_ref, tiles):
    rows, lanes = tiles[0].shape
    half = lanes // 2
    low = lanes_of((rows, lanes)) < half
    depth = 2 * rows
    for place, (one, two) in enumerate(paired_nodes()):
        first, second = (tiles[one], tiles[two])
        cut = pl.ds(place * lanes, lanes)
        for part in range(2):
            if part == 0:
                value = jnp.where(low, first, pltpu.roll(second, half, 1))
            else:
                value = jnp.where(low, pltpu.roll(first, half, 1), second)
            high = value.astype(jnp.bfloat16)
            rest = (value - high.astype(jnp.float32)).astype(jnp.bfloat16)
            rhs_ref[pl.ds(part * rows, rows), cut] = high
            rhs_ref[pl.ds(depth + part * rows, rows), cut] = rest
            rhs_ref[pl.ds(2 * depth + part * rows, rows), cut] = high
    out = jnp.dot(table, rhs_ref[...], preferred_element_type=jnp.float32)
    fields = []
    for field in range(table.shape[0] // depth):
        nodes = [None] * NODES
        for place, (one, two) in enumerate(paired_nodes()):
            cut = slice(place * lanes, (place + 1) * lanes)
            top = out[field * depth : field * depth + rows, cut]
            bottom = out[field * depth + rows : (field + 1) * depth, cut]
            nodes[one] = jnp.where(low, top, pltpu.roll(bottom, half, 1))
            if two != one:
                nodes[two] = jnp.where(low, pltpu.roll(top, half, 1), bottom)
        fields.append(nodes)
    return fields


def rhs_scratch(table, lanes):
    return pltpu.VMEM((table.shape[1], len(paired_nodes()) * lanes), jnp.bfloat16)


def read_tiles(x_ref, rows, lanes):
    return [x_ref[:, b].reshape(rows, lanes) for b in range(NODES)]


def to_points(blocks, table):
    shares, _, pairs, lanes = blocks.shape
    square = NODES * NODES
    rows = shares * pairs

    def body(t_ref, x_ref, v_ref, z_ref, rhs_ref):
        fields = three_pass(t_ref[...], rhs_ref, read_tiles(x_ref, rows, lanes))
        for b in range(NODES):
            v_ref[b] = fields[0][b]
            z_ref[b] = fields[1][b]

    spec = pl.BlockSpec((NODES, rows, lanes), lambda a: (a, 0, 0))
    shape = jax.ShapeDtypeStruct((square, rows, lanes), jnp.float32)
    return call(
        body,
        (NODES,),
        [
            whole(table.shape),
            pl.BlockSpec((shares, NODES, pairs, lanes), lambda a: (0, a, 0, 0)),
        ],
        [spec, spec],
        [shape, shape],
        scratch=[rhs_scratch(table, lanes)],
        flops=2 * table.shape[0] * table.shape[1] * square * lanes,
        grant=WHOLE_GRANT,
        moved=3 * square * rows * lanes * 4,
    )(table, blocks)


def turn_around(blocks, skip, start, count, partial, slope_z, table, back, fields, out):
    shares, _, pairs, lanes = blocks.shape
    rows = shares * pairs
    square = NODES * NODES
    group = pairs // 2
    shape = jax.ShapeDtypeStruct((square, rows, lanes), jnp.float32)

    def body(t_ref, i_ref, x_ref, g_ref, s_ref, *refs):
        w_ref, z_ref = refs[len(fields) : len(fields) + 2]
        outs, rhs_ref = (refs[len(fields) + 2 : -1], refs[-1])
        points = three_pass(t_ref[...], rhs_ref, read_tiles(x_ref, rows, lanes))
        for b in range(NODES):
            w_ref[b] = points[0][b]
            z_ref[b] = points[1][b]
        tiles = [g_ref[b] + w_ref[b] * s_ref[b] for b in range(NODES)]
        spectral = three_pass(i_ref[...], rhs_ref, tiles)[0]
        for b in range(NODES):
            value = spectral[b].reshape(shares, pairs, lanes)
            if out is None:
                for k in range(shares):
                    outs[k][b] = value[k]
            else:
                for g in range(2):
                    outs[0][:, g * NODES + b] = value[:, g * group : (g + 1) * group]

    spec = pl.BlockSpec((NODES, rows, lanes), lambda a: (start + a, 0, 0))
    if out is None:
        out_spec = [pl.BlockSpec((NODES, pairs, lanes), lambda a: (a, 0, 0))] * shares
        out_shape = [jax.ShapeDtypeStruct((count * NODES, pairs, lanes), jnp.float32)] * shares
    else:
        first = out[1]
        out_spec = [pl.BlockSpec((shares, 2 * NODES, group, lanes), lambda a: (0, first + a, 0, 0))]
        out_shape = [jax.ShapeDtypeStruct(out[0], jnp.float32)]
    return call(
        body,
        (count,),
        [
            whole(table.shape),
            whole(back.shape),
            pl.BlockSpec((shares, NODES, pairs, lanes), lambda a: (0, skip + a, 0, 0)),
            spec,
            spec,
        ]
        + [pl.BlockSpec(memory_space=pl.ANY)] * len(fields),
        [spec, spec] + out_spec,
        [shape, shape] + out_shape,
        scratch=[rhs_scratch(table, lanes)],
        flops=3 * table.shape[0] * table.shape[1] * count * NODES * lanes,
        aliases={5: 0, 6: 1} if fields else None,
        grant=WHOLE_GRANT,
        moved=6 * count * NODES * rows * lanes * 4,
    )(table, back, blocks, partial, slope_z, *fields)


def in_plane(speeds, fields, metrics, table):
    square, rows, lanes = speeds[0].shape
    count = len(fields)
    step = 32
    own = [i for i, f in enumerate(fields) if all(f is not s for s in speeds)]
    arrays = list(speeds) + [fields[i] for i in own]

    def body(m_ref, *refs):
        ins, outs = (refs[: len(arrays)], refs[len(arrays) :])
        u_ref, v_ref = ins[:2]
        sources = []
        extra = 2
        for i, f in enumerate(fields):
            if i in own:
                sources.append(ins[extra])
                extra += 1
            else:
                sources.append(u_ref if f is speeds[0] else v_ref)

        def block(s, carry):
            r = pl.ds(s * 8, 8)

            def metric(kind, n):
                return row_of(m_ref, kind * square + n, 8)

            for a in range(NODES):
                ns = [a * NODES + b for b in range(NODES)]
                drift = [
                    u_ref[n, r] * metric(2, n) + v_ref[n, r] * metric(3, n) for n in ns
                ]
                for f in range(count):
                    beside = apply_line(table, [sources[f][n, r] for n in ns])
                    for b, n in enumerate(ns):
                        outs[f][n, r] = drift[b] * beside[b]
            for b in range(NODES):
                ns = [a * NODES + b for a in range(NODES)]
                drift = [
                    u_ref[n, r] * metric(0, n) + v_ref[n, r] * metric(1, n) for n in ns
                ]
                for f in range(count):
                    radial = apply_line(table, [sources[f][n, r] for n in ns])
                    for a, n in enumerate(ns):
                        outs[f][n, r] = outs[f][n, r] + drift[a] * radial[a]
            return carry

        lax.fori_loop(0, step // 8, block, 0)

    spec = pl.BlockSpec((square, step, lanes), lambda i: (0, i, 0))
    shape = jax.ShapeDtypeStruct((square, rows, lanes), jnp.float32)
    return call(
        body,
        (rows // step,),
        [whole(metrics.shape)] + [spec] * len(arrays),
        [spec] * count,
        [shape] * count,
        flops=30 * count * square * rows * lanes,
        grant=WHOLE_GRANT,
        moved=(len(arrays) + count) * square * rows * lanes * 4,
    )(metrics, *arrays)


def by_source(strips, place):
    count = len(strips)
    nodes = strips[0].shape[0]

    def body(place_ref, *refs):
        o_ref = refs[-1]
        here = place_ref[0]

        def node(n, carry):
            for k in range(count):
                o_ref[lax.rem(here - k + count, count), n] = refs[k][n]
            return carry

        lax.fori_loop(0, nodes, node, 0)

    return call(
        body,
        (1,),
        [pl.BlockSpec(memory_space=pltpu.SMEM)] + [whole(strips[0].shape)] * count,
        whole((count,) + strips[0].shape),
        jax.ShapeDtypeStruct((count,) + strips[0].shape, jnp.float32),
        grant=WHOLE_GRANT,
        moved=8 * count * strips[0].size,
    )(jnp.full((1,), place, jnp.int32), *strips)


def to_planes(partial, speed_z, slope_z, table, shares, place, shapes, buffers):
    square, rows, lanes = partial.shape
    pairs = rows // shares
    group = pairs // 2

    def body(t_ref, g_ref, w_ref, z_ref, *refs):
        outs, rhs_ref = (refs[-3:-1], refs[-1])
        tiles = [g_ref[b] + w_ref[b] * z_ref[b] for b in range(NODES)]
        nodes = three_pass(t_ref[...], rhs_ref, tiles)[0]
        for b in range(NODES):
            out = nodes[b].reshape(shares, pairs, lanes)
            for i in range(2):
                outs[i][:, b] = out[:, i * group : (i + 1) * group]

    spec = pl.BlockSpec((NODES, rows, lanes), lambda a: (a, 0, 0))
    out_spec = pl.BlockSpec((shares, NODES, group, lanes), lambda a: (0, place * NODES + a, 0, 0))
    shapes = [jax.ShapeDtypeStruct(shape, jnp.float32) for shape in shapes]
    return call(
        body,
        (NODES,),
        [whole(table.shape), spec, spec, spec]
        + [pl.BlockSpec(memory_space=pl.ANY)] * len(buffers),
        [out_spec, out_spec],
        shapes,
        scratch=[rhs_scratch(table, lanes)],
        flops=2 * table.shape[0] * table.shape[1] * square * lanes,
        grant=WHOLE_GRANT,
        moved=4 * square * rows * lanes * 4,
        aliases={4 + k: k for k in range(len(buffers))},
    )(table, partial, speed_z, slope_z, *buffers)


def velocity_part(sent, metrics, weights, waves, table):
    shares, square, pairs, lanes = sent[0].shape
    half = lanes // 2

    def body(m_ref, q_ref, k_ref, s0, s1, s2, o_ref):
        d = pl.program_id(0)

        def rows_of(s):
            r = pl.ds(s * 8, 8)
            wave = k_ref[r]

            def metric(kind, n):
                return row_of(m_ref, (kind * shares + d) * square + n, 8)

            for a in range(NODES):
                ns = [a * NODES + b for b in range(NODES)]
                first = apply_line(table, [s0[0, n, r] for n in ns])
                second = apply_line(table, [s1[0, n, r] for n in ns])
                for b, n in enumerate(ns):
                    along = pltpu.roll(s2[0, n, r], half, 1) * wave
                    o_ref[0, n, r] = (
                        metric(2, n) * first[b]
                        + metric(3, n) * second[b]
                        + row_of(q_ref, d * square + n, 8) * along
                    )
            for b in range(NODES):
                ns = [a * NODES + b for a in range(NODES)]
                first = apply_line(table, [s0[0, n, r] for n in ns])
                second = apply_line(table, [s1[0, n, r] for n in ns])
                for a, n in enumerate(ns):
                    o_ref[0, n, r] = o_ref[0, n, r] + (
                        metric(0, n) * first[a] + metric(1, n) * second[a]
                    )

        lax.fori_loop(0, pairs // 8, lambda s, carry: (rows_of(s), carry)[1], 0)

    spec = pl.BlockSpec((1, square, pairs, lanes), lambda d: (d, 0, 0, 0))
    return call(
        body,
        (shares,),
        [whole(metrics.shape), whole(weights.shape), whole(waves.shape)] + [spec] * 3,
        spec,
        jax.ShapeDtypeStruct(sent[0].shape, jnp.float32),
        flops=60 * shares * square * pairs * lanes,
        grant=WHOLE_GRANT,
        moved=4 * shares * square * pairs * lanes * 4,
    )(metrics, weights, waves, *sent)


def first_part(base, early, rest, rest_at, metrics, table):
    shares, square, pairs, lanes = base.shape

    some = early.shape[1]
    count = (square - some) // NODES
    group = pairs // 2

    def body(m_ref, s0, r0, *refs):
        others, (o_ref, p0) = (refs[:count], refs[count:])
        d = pl.program_id(0)

        def block(s, carry):
            r = pl.ds(s * 8, 8)
            for n in range(square):
                if n < some:
                    home = r0[0, n, r]
                else:
                    a, b = divmod(n - some, NODES)
                    home = others[a][0, s * NODES + b]
                p0[n] = home

            def metric(kind, n):
                return row_of(m_ref, (kind * shares + d) * square + n, 8)

            for a in range(NODES):
                ns = [a * NODES + b for b in range(NODES)]
                line = apply_line(table, [p0[n] for n in ns])
                for b, n in enumerate(ns):
                    o_ref[0, n, r] = s0[0, n, r] + metric(2, n) * line[b]
            for b in range(NODES):
                ns = [a * NODES + b for a in range(NODES)]
                line = apply_line(table, [p0[n] for n in ns])
                for a, n in enumerate(ns):
                    o_ref[0, n, r] = o_ref[0, n, r] + metric(0, n) * line[a]
            return carry

        lax.fori_loop(0, pairs // 8, block, 0)

    spec = pl.BlockSpec((1, square, pairs, lanes), lambda d: (d, 0, 0, 0))
    return call(
        body,
        (shares,),
        [whole(metrics.shape), spec, pl.BlockSpec((1, some, pairs, lanes), lambda d: (d, 0, 0, 0))]
        + [
            pl.BlockSpec(
                (1, 2 * NODES, group, lanes), functools.partial(lambda i, d: (d, i, 0, 0), rest_at + k)
            )
            for k in range(count)
        ],
        spec,
        jax.ShapeDtypeStruct(base.shape, jnp.float32),
        scratch=[pltpu.VMEM((square, 8, lanes), jnp.float32)],
        flops=30 * shares * square * pairs * lanes,
        grant=WHOLE_GRANT,
        moved=3 * shares * square * pairs * lanes * 4,
    )(metrics, base, early, *[rest] * count)


def join_layers(y_ref, layers):
    square = NODES * NODES
    last = (NODES - 1) * NODES
    for e in range(layers - 1):
        for b in range(NODES):
            upper, lower = (e * square + last + b, (e + 1) * square + b)
            total = y_ref[upper] + y_ref[lower]
            y_ref[upper] = total
            y_ref[lower] = total
    for b in range(NODES):
        node = (layers - 1) * square + last + b
        y_ref[node] = jnp.zeros_like(y_ref[node])


def rim_messages(read, layers, shape, partials):
    lane = lanes_of(shape)
    lanes = shape[-1]
    axis = len(shape) - 1
    first = jnp.zeros(shape, jnp.float32)
    last = jnp.zeros(shape, jnp.float32)
    square = NODES * NODES
    for e in range(layers):
        for a in range(NODES):
            spot = e * NODES + a
            here = lane == spot
            node = e * square + a * NODES
            first = jnp.where(here, pltpu.roll(read(node), spot, axis), first)
            last = jnp.where(
                here, pltpu.roll(read(node + NODES - 1), (spot + 1) % lanes, axis), last
            )
    for i, partial in enumerate(partials):
        here = lane == layers * NODES + i
        first = jnp.where(here, partial, first)
        last = jnp.where(here, partial, last)
    return (first, last)


def right_side(flat, returned, metrics, weights, waves, table, layers, place):
    shares, square, _, lanes = flat.shape
    half = lanes // 2

    def body(m_ref, q_ref, k_ref, f_ref, r1, r2, o_ref, first_ref, last_ref, c0, c1):
        e = pl.program_id(0)
        lane = lanes_of((8, lanes))
        low = lane < half
        wave = k_ref[...]
        sides = (c0, c1)

        @pl.when(e == 0)
        def _():
            first_ref[...] = jnp.zeros_like(first_ref)
            last_ref[...] = jnp.zeros_like(last_ref)

        for h in range(2):
            d = 2 * e + h
            side = sides[h]
            for n in range(square):
                along = pltpu.roll(r2[h, n], half, 1) * wave
                side[n] = f_ref[h, n] + row_of(q_ref, d * square + n, 8) * along

            def metric(kind, n):
                return row_of(m_ref, (kind * shares + d) * square + n, 8)

            for a in range(NODES):
                ns = [a * NODES + b for b in range(NODES)]
                line = apply_line(table, [r1[h, n] for n in ns])
                for b, n in enumerate(ns):
                    side[n] = side[n] + metric(3, n) * line[b]
            for b in range(NODES):
                ns = [a * NODES + b for a in range(NODES)]
                line = apply_line(table, [r1[h, n] for n in ns])
                for a, n in enumerate(ns):
                    side[n] = side[n] + metric(1, n) * line[a]
        rims = [[first_ref[0], last_ref[0]], [first_ref[1], last_ref[1]]]
        for n in range(square):
            left, right = (c0[n], c1[n])
            parts = (
                jnp.where(low, left, pltpu.roll(right, half, 1)),
                jnp.where(low, pltpu.roll(left, half, 1), right),
            )
            for i in range(2):
                o_ref[n, i] = parts[i]
                a, b = divmod(n, NODES)
                spot = e * NODES + a
                if b == 0:
                    rims[i][0] = jnp.where(lane == spot, pltpu.roll(parts[i], spot, 1), rims[i][0])
                if b == NODES - 1:
                    rims[i][1] = jnp.where(
                        lane == spot, pltpu.roll(parts[i], spot + 1, 1), rims[i][1]
                    )
        for i in range(2):
            first_ref[i] = rims[i][0]
            last_ref[i] = rims[i][1]

    spec = pl.BlockSpec((2, square, 8, lanes), lambda e: (e, 0, place, 0))
    nodes = layers * square
    rim_shape = jax.ShapeDtypeStruct((2, 8, lanes), jnp.float32)
    scratch = pltpu.VMEM((square, 8, lanes), jnp.float32)
    return call(
        body,
        (layers,),
        [
            whole(metrics.shape),
            whole(weights.shape),
            pl.BlockSpec((8, lanes), lambda e: (place, 0)),
            spec,
            pl.BlockSpec((2, square, 8, lanes), lambda e: (e, 0, 0, 0)),
            pl.BlockSpec((2, square, 8, lanes), lambda e: (e, 1, 0, 0)),
        ],
        [
            pl.BlockSpec((square, 2, 8, lanes), lambda e: (e, 0, 0, 0)),
            whole((2, 8, lanes)),
            whole((2, 8, lanes)),
        ],
        [jax.ShapeDtypeStruct((nodes, 2, 8, lanes), jnp.float32), rim_shape, rim_shape],
        scratch=[scratch] * 2,
        flops=40 * shares * square * 8 * lanes,
        moved=4 * shares * square * 8 * lanes * 4,
    )(metrics, weights, waves, flat, returned, returned)


def swap_rims(first, last):
    size = lax.axis_size("elem")
    up = [(i, (i + 1) % size) for i in range(size)]
    down = [(j, i) for i, j in up]
    return (lax.ppermute(last, "elem", up), lax.ppermute(first, "elem", down))


def opposite(first):
    size = lax.axis_size("elem")
    return lax.ppermute(first, "elem", [(i, (i + 2) % size) for i in range(size)])


def join_columns(read, ref, before, after, layers):
    lanes = before.shape[-1]
    axis = len(before.shape) - 1
    lane = lanes_of(before.shape)
    square = NODES * NODES
    for e in range(layers):
        for a in range(NODES):
            spot = e * NODES + a
            node = e * square + a * NODES
            first, last = (read(node), read(node + NODES - 1))
            beyond = pltpu.roll(after, lanes - 1 - spot, axis)
            ahead = jnp.where(lane == lanes - 1, beyond, pltpu.roll(first, lanes - 1, axis))
            right = last + ahead
            mine = first + (pltpu.roll(before, lanes - spot, axis) if spot else before)
            ref[node + NODES - 1] = right
            ref[node] = jnp.where(lane == 0, mine, pltpu.roll(right, 1, axis))


def join(source, ref, before, after, layers):
    square = NODES * NODES

    def copy(e, carry):
        for n in range(square):
            if 0 < n % NODES < NODES - 1:
                ref[e * square + n] = source[e * square + n]
        return carry

    lax.fori_loop(0, layers, copy, 0)
    join_columns(lambda n: source[n], ref, before, after, layers)
    join_layers(ref, layers)


def each_node(layers, step):
    def layer(e, carry):
        for n in range(NODES * NODES):
            step(e * NODES * NODES + n)
        return carry

    lax.fori_loop(0, layers, layer, 0)


def share_of(layers, e, a):
    if a == 0:
        return jnp.where(e > 0, 0.5, 1.0)
    if a == NODES - 1:
        return jnp.where(e < layers - 1, 0.5, 0.0)
    return 1.0


def helmholtz(r_ref, y_ref, flux_ref, g_ref, shift, layers, table, dot_only=False):
    square = NODES * NODES
    nodes = layers * square
    turned = table.T
    zero = jnp.zeros(shift.shape, jnp.float32)

    def layer(e, carry):
        norm, energy = carry
        base = e * square

        def metric(kind, n):
            return row_of(g_ref, kind * nodes + base + n, 8)

        for b in range(NODES):
            ns = [a * NODES + b for a in range(NODES)]
            radial = apply_line(table, [r_ref[base + n] for n in ns])
            for a, n in enumerate(ns):
                flux_ref[n] = radial[a]
        for a in range(NODES):
            ns = [a * NODES + b for b in range(NODES)]
            line = [r_ref[base + n] for n in ns]
            beside = apply_line(table, line)
            second = []
            rest = []
            part = zero
            for b, n in enumerate(ns):
                radial = flux_ref[n]
                cross = metric(1, n)
                one = metric(0, n) * radial + cross * beside[b]
                two = cross * radial + metric(2, n) * beside[b]
                same = shift * metric(3, n) * line[b]
                whole_weight = line[b] * line[b]
                part = part + (0.5 * whole_weight if b in (0, NODES - 1) else whole_weight)
                if dot_only:
                    energy = energy + (radial * one + beside[b] * two + same * line[b])
                else:
                    flux_ref[n] = one
                    second.append(two)
                    rest.append(same)
            norm = norm + part * share_of(layers, e, a)
            if not dot_only:
                back = apply_line(turned, second)
                for b, n in enumerate(ns):
                    y_ref[base + n] = rest[b] + back[b]
        if not dot_only:
            for b in range(NODES):
                ns = [a * NODES + b for a in range(NODES)]
                back = apply_line(turned, [flux_ref[n] for n in ns])
                for a, n in enumerate(ns):
                    value = y_ref[base + n] + back[a]
                    y_ref[base + n] = value
                    energy = energy + value * r_ref[base + n]
        return (norm, energy)

    norm, energy = lax.fori_loop(0, layers, layer, (zero, zero))
    axis = len(shift.shape) - 1
    return (
        jnp.sum(norm, axis=axis, keepdims=True),
        jnp.sum(energy, axis=axis, keepdims=True),
    )


def lane_value(block, lane):
    return block[..., lane : lane + 1]


def sums_from(own, left, right, far, layers):
    total = (own[...] + far[...]) + (left[...] + right[...])
    spot = layers * NODES
    return (lane_value(total, spot), lane_value(total, spot + 1))


def scalars_block(shape, values, spot=0):
    lane = lanes_of(shape)
    out = jnp.zeros(shape, jnp.float32)
    for i, value in enumerate(values):
        out = jnp.where(lane == spot + i, value, out)
    return out


def shapes_of(field):
    return (
        jax.ShapeDtypeStruct(field.shape, jnp.float32),
        jax.ShapeDtypeStruct(field.shape[1:], jnp.float32),
        pltpu.VMEM((NODES * NODES,) + field.shape[1:], jnp.float32),
    )


def first_image(raw, before, after, shift, geo, layers, table):
    field, small, flux_scratch = shapes_of(raw)
    shape = raw.shape[1:]

    def body(g_ref, k_ref, f_ref, b_ref, a_ref, r_ref, y_ref, first_ref, last_ref, flux):
        join(f_ref, r_ref, b_ref[...], a_ref[...], layers)
        sums = helmholtz(r_ref, y_ref, flux, g_ref, k_ref[...], layers, table)
        first_ref[...], last_ref[...] = rim_messages(lambda n: y_ref[n], layers, shape, sums)

    return call(
        body,
        (),
        held(5),
        held(4),
        [field, field, small, small],
        scratch=[flux_scratch],
        flops=80 * raw.size,
        moved=12 * raw.size,
    )(geo, shift, raw, before, after)


def second_image(start, image, messages, shift, geo, layers, table):
    field, small, flux_scratch = shapes_of(start)
    shape = start.shape[1:]

    def body(g_ref, k_ref, r0, y0, own, left, right, far, *rest):
        w_ref, y_ref, first_ref, last_ref, scalar_ref, r1, flux = rest
        norm, energy = sums_from(own, left, right, far, layers)
        alpha = jnp.broadcast_to(norm / energy, shape)
        join(y0, w_ref, left[...], right[...], layers)

        def move(node):
            r1[node] = r0[node] - alpha * w_ref[node]

        each_node(layers, move)
        sums = helmholtz(r1, y_ref, flux, g_ref, k_ref[...], layers, table)
        first_ref[...], last_ref[...] = rim_messages(lambda n: y_ref[n], layers, shape, sums)
        scalar_ref[...] = scalars_block(shape, (alpha, norm, energy))

    return call(
        body,
        (),
        held(8),
        held(5),
        [field, field, small, small, small],
        scratch=[pltpu.VMEM(start.shape, jnp.float32), flux_scratch],
        flops=80 * start.size,
        moved=16 * start.size,
    )(geo, shift, start, image, *messages)


def third_energy(start, joined, image, messages, scalars, shift, geo, layers, table):
    field, small, flux_scratch = shapes_of(start)
    shape = start.shape[1:]

    def body(g_ref, k_ref, r0, w0, y1, own, left, right, far, old, *rest):
        r2, d2, sums_ref, scalar_ref, w1, flux = rest
        norm, energy = sums_from(own, left, right, far, layers)
        before = old[...]
        alpha = jnp.broadcast_to(lane_value(before, 0), shape)
        ratio = norm / lane_value(before, 1)
        curve = energy - ratio * ratio * lane_value(before, 2)
        step = jnp.broadcast_to(norm / curve, shape)
        beta = jnp.broadcast_to(ratio, shape)
        join(y1, w1, left[...], right[...], layers)

        def move(node):
            w = w0[node]
            start_value = r0[node]
            moved = start_value - alpha * w
            d2[node] = moved + beta * start_value
            r2[node] = moved - step * (w1[node] + beta * w)

        each_node(layers, move)
        sums = helmholtz(r2, None, flux, g_ref, k_ref[...], layers, table, dot_only=True)
        sums_ref[...] = scalars_block(shape, sums, layers * NODES)
        scalar_ref[...] = scalars_block(shape, (alpha, norm, curve, step))

    return call(
        body,
        (),
        held(10),
        held(4),
        [field, field, small, small],
        scratch=[pltpu.VMEM(start.shape, jnp.float32), flux_scratch],
        flops=60 * start.size,
        moved=20 * start.size,
    )(geo, shift, start, joined, image, *messages, scalars)


def finish(start, direction, residual, messages, scalars, layers, place, buffer, total):
    nodes, _, rows, lanes = start.shape
    shape = start.shape[1:]
    square = NODES * NODES

    unit = 2 * nodes

    def body(r0, d2, r2, own, left, right, far, old, *refs):
        o_ref, mid = refs[-2:]
        norm, energy = sums_from(own, left, right, far, layers)
        before = old[...]
        ratio = norm / lane_value(before, 1)
        curve = energy - ratio * ratio * lane_value(before, 2)
        step = norm / curve
        third = jnp.broadcast_to(step, shape)
        second = jnp.broadcast_to(lane_value(before, 3) + step * ratio, shape)
        first = jnp.broadcast_to(lane_value(before, 0), shape)

        def layer(e, carry):
            for n in range(square):
                node = e * square + n
                value = first * r0[node] + second * d2[node] + third * r2[node]
                for i in range(2):
                    mid[i * nodes + n * layers + e] = value[i]
            return carry

        lax.fori_loop(0, layers, layer, 0)

        def write(t, r, tile):
            o_ref[rows_at(r, unit, t), :] = tile

        turn_all(lambda k, t: mid[8 * t + k], write, unit // 8)

    extra = [] if buffer is None else [buffer]
    return call(
        body,
        (1,),
        [whole(start.shape)] * 3
        + [whole(shape)] * 5
        + [pl.BlockSpec(memory_space=pl.ANY)] * len(extra),
        pl.BlockSpec((2 * rows * nodes, lanes), lambda i: (place, 0)),
        jax.ShapeDtypeStruct((total, lanes), jnp.float32),
        scratch=[pltpu.VMEM((unit, rows, lanes), jnp.float32)],
        flops=6 * start.size,
        moved=16 * start.size,
        aliases={8: 0} if extra else None,
    )(start, direction, residual, *messages, scalars, *extra)


def halves(values, shares):
    half = values.shape[-1] // 2
    parts = [jnp.concatenate([p, p], axis=-1) for p in (values[..., :half], values[..., half:])]
    return jnp.stack(parts, axis=2).reshape(values.shape[0], shares, NODES * NODES, 2 * half)


def on_device_paired(*arrays):
    return paired_step(*arrays)


def paired_step(velocity, radial_dx, radial_dy, around_dx, around_dy, jacobian):
    table = derivative_table()
    modes = lax.axis_size("mode")
    mode = lax.axis_index("mode")
    _, local_planes, layers, _, _, lanes = velocity.shape
    planes = local_planes * modes
    pairs = local_planes // 2
    first_plane = mode * local_planes
    square = NODES * NODES
    forward, backward = (jnp.asarray(t) for t in paired_tables(planes))

    rows = velocity.transpose(0, 1, 3, 4, 2, 5).reshape(3, local_planes * square * layers, lanes)
    plain = jnp.stack([radial_dx, radial_dy, around_dx, around_dy]).reshape(
        4, layers, square, lanes
    )
    both = halves(plain, modes)
    here = lax.dynamic_index_in_dim(both, mode, 1, keepdims=False).reshape(4 * square, lanes)
    metrics = geometry(radial_dx, radial_dy, around_dx, around_dy, jacobian)
    geo = jnp.stack(metrics).reshape(4 * layers * square, lanes)
    scaled = halves((metrics[3] * (-1.0 / time_step)).reshape(1, layers, square, lanes), modes)
    flux = (both * scaled).reshape(4 * modes * square, lanes)
    small_flux = flux * time_step
    scaled = scaled.reshape(modes * square, lanes)
    turned = lax.optimization_barrier(backward).reshape(2, modes, pairs, -1)
    turned = jnp.roll(turned, -mode, axis=1)
    turned = turned.reshape(backward.shape)
    pair = (first_plane // 2 + jnp.arange(pairs, dtype=jnp.int32)).astype(jnp.float32)
    wave = pair[:, None] * spanwise_wave
    low = (jnp.arange(lanes) < lanes // 2)[None, :]
    waves = jnp.where(low, wave, -wave)
    small_waves = waves * time_step
    shift = plane_shift(first_plane, local_planes, planes).reshape(pairs, 2).T
    shift = jnp.broadcast_to(shift.reshape(2, 2, pairs // 2, 1), (2, 2, pairs // 2, lanes))
    shift = (shift[:, 0], shift[:, 1])

    def exchange(blocks):
        return lax.all_to_all(blocks, "mode", split_axis=0, concat_axis=0, tiled=True)

    some = (NODES // 2 + 1) * NODES
    group = pairs // 2
    first_shape = (modes, 4 * square - 2 * some, group, lanes)
    second_shape = (modes, 2 * square, group, lanes)
    sent_0 = pack_first(rows, layers, pairs, lanes)
    sent_1, late_2, sent_2 = pack_rest(rows, layers, pairs, lanes, some)
    arrived_0 = exchange(sent_0)
    sent_1, here, geo, flux, small_flux, scaled, waves, small_waves, shift, turned = (
        lax.optimization_barrier(
            (sent_1, here, geo, flux, small_flux, scaled, waves, small_waves, shift, turned)
        )
    )
    arrived_1 = exchange(sent_1)
    arrived_2 = exchange(late_2)
    speed_x, slope_0 = to_points(arrived_0, forward)
    speed_y, slope_1 = to_points(arrived_1, forward)
    speeds = [speed_x, speed_y]
    partial = in_plane(speeds, speeds[:1], here, table)
    rows_early = some // NODES
    speed_z, slope_2, *strips = turn_around(
        arrived_1, NODES, 0, rows_early, partial[0], slope_0, forward, turned, (), None
    )
    for k in range(1, modes):
        strips[k] = lax.ppermute(strips[k], "mode", [(i, (i + k) % modes) for i in range(modes)])
    speed_z, slope_2, first_buffer = turn_around(
        arrived_2,
        0,
        rows_early,
        NODES - rows_early,
        partial[0],
        slope_0,
        forward,
        backward,
        (speed_z, slope_2),
        (first_shape, NODES),
    )
    middle, last = in_plane(speeds, [speed_y, speed_z], here, table)
    shapes = (first_shape, second_shape)
    blocks = to_planes(
        middle, speed_z, slope_1, backward, modes, 0, shapes, (first_buffer,)
    )
    blocks = to_planes(last, speed_z, slope_2, backward, modes, 1, shapes, blocks)
    home_0 = by_source(strips, mode)
    home_1 = exchange(blocks[0])
    home_2 = exchange(blocks[1])
    returned = (home_1, home_2)
    base = velocity_part((sent_0, sent_1, sent_2), flux, scaled, waves, table)

    own_rows = local_planes * square * layers

    def read_first(refs, g):
        def read(d, n):
            if n < some:
                return refs[0][d, n]
            a, b = divmod(n - some, NODES)
            return refs[1 + a][d, g * NODES + b]

        return read

    def read_part(refs, i):
        return lambda d, n: refs[0][d, n]

    first_specs = [pl.BlockSpec((modes, some, group, lanes), lambda i: (0, 0, i, 0))] + [
        pl.BlockSpec(
            (modes, 2 * NODES, group, lanes), functools.partial(lambda k, i: (0, k, 0, 0), NODES + k)
        )
        for k in range(NODES - rows_early)
    ]
    part_specs = [pl.BlockSpec((modes, square, group, lanes), lambda i: (0, i, 0, 0))]
    advection = unpack(
        [home_0] + [home_1] * (NODES - rows_early),
        first_specs,
        read_first,
        (0, 1),
        layers,
        None,
        3 * own_rows,
    )
    flat = first_part(base, home_0, home_1, NODES, small_flux, table)

    def solve(place, flat, own_shift, buffer):
        raw, first, last = right_side(
            flat, returned[place], small_flux, scaled, small_waves, table, layers, place
        )
        before, after = swap_rims(first, last)
        start, image, first, last = first_image(raw, before, after, own_shift, geo, layers, table)
        messages = (first,) + swap_rims(first, last) + (opposite(first),)
        joined, image, first, last, scalars = second_image(
            start, image, messages, own_shift, geo, layers, table
        )
        messages = (first,) + swap_rims(first, last) + (opposite(first),)
        residual, direction, sums, scalars = third_energy(
            start, joined, image, messages, scalars, own_shift, geo, layers, table
        )
        messages = (sums,) + swap_rims(sums, sums) + (opposite(sums),)
        return finish(
            start, direction, residual, messages, scalars, layers, place, buffer, own_rows
        )

    pressure = solve(0, flat, shift[0], None)
    advection = unpack(
        [home_1], part_specs, read_part, (2, 2), layers, advection, 3 * own_rows
    )
    flat, pressure, advection, shift = lax.optimization_barrier(
        (flat, pressure, advection, shift)
    )

    def unpack_late(comp, buffer):
        spec = pl.BlockSpec((modes, square, group, lanes), lambda i: (0, comp, 0, 0))
        return unpack(
            [home_2], [spec], read_part, (3 + 2 * comp, 1), layers, buffer, 3 * own_rows, 1
        )

    pressure = solve(1, flat, shift[1], pressure)
    advection = unpack_late(1, unpack_late(0, advection))
    advection = advection.reshape(3, local_planes, NODES, NODES, layers, lanes)
    pressure = pressure.reshape(local_planes, NODES, NODES, layers, lanes)
    return (advection.transpose(0, 1, 4, 2, 3, 5), pressure.transpose(0, 3, 1, 2, 4))


def paired_fits(mesh, shape):
    modes, ring = (mesh.shape["mode"], mesh.shape["elem"])
    _, planes, layers, _, _, columns = shape
    return (
        ring == 4
        and columns == 128 * ring
        and modes == 2 * layers
        and layers % 4 == 0
        and planes == 32 * modes
        and (layers * NODES + 2 <= 128)
    )


def solution(mesh):
    placed = (
        P(None, "mode", None, None, None, "elem"),
        P(None, None, None, "elem"),
        P(None, None, None, "elem"),
        P(None, None, None, "elem"),
        P(None, None, None, "elem"),
        P(None, None, None, "elem"),
    )


    def step(velocity, *rest):
        body = on_device_paired if paired_fits(mesh, velocity.shape) else on_device
        return jax.shard_map(
            body,
            mesh=mesh,
            in_specs=placed,
            out_specs=(
                P(None, "mode", None, None, None, "elem"),
                P("mode", None, None, None, "elem"),
            ),
            check_vma=False,
        )(velocity, *rest)

    return step
```

```python
import functools
import math

import jax
import jax.numpy as jnp
import numpy as np
from jax import lax
from jax.experimental import pallas as pl
from jax.experimental.pallas import tpu as pltpu
from jax.sharding import PartitionSpec as P

NODES = 7
ITERS = 3
GRANT = 24 * 2**20
WHOLE_GRANT = 67043328


spanwise_wave = 2.0 * math.pi / 64.0
time_step = 0.1


def padded_2(value, sides, width):
    for axis, dim in sides:
        size, length = (lax.axis_size(axis), value.shape[dim])
        up = [(i, (i + 1) % size) for i in range(size)]
        down = [(j, i) for i, j in up]
        last = lax.slice_in_dim(value, length - width, length, axis=dim)
        leading = lax.slice_in_dim(value, 0, width, axis=dim)
        before = lax.ppermute(last, axis, up)
        after = lax.ppermute(leading, axis, down)
        value = jnp.concatenate([before, value, after], axis=dim)
    return value


def lobatto_rule(count):
    degree = count - 1
    points = np.cos(np.pi * np.arange(count) / degree)
    legendre = np.zeros((count, count))
    for _ in range(60):
        legendre[:, 0] = 1.0
        legendre[:, 1] = points
        for order in range(2, count):
            legendre[:, order] = (
                (2 * order - 1) * points * legendre[:, order - 1]
                - (order - 1) * legendre[:, order - 2]
            ) / order
        points = points - (points * legendre[:, degree] - legendre[:, degree - 1]) / (
            count * legendre[:, degree]
        )
    legendre[:, 0] = 1.0
    legendre[:, 1] = points
    for order in range(2, count):
        legendre[:, order] = (
            (2 * order - 1) * points * legendre[:, order - 1] - (order - 1) * legendre[:, order - 2]
        ) / order
    weights = 2.0 / (degree * count * legendre[:, degree] ** 2)
    return (points[::-1].copy(), weights[::-1].copy())


def derivative_table():
    lobatto_nodes = lobatto_rule(NODES)[0]
    total = lobatto_nodes.shape[0]
    scales = np.ones(total)
    for column in range(total):
        for other in range(total):
            if other != column:
                scales[column] = scales[column] / (lobatto_nodes[column] - lobatto_nodes[other])
    table = np.zeros((total, total))
    for row in range(total):
        for column in range(total):
            if row != column:
                table[row, column] = (
                    scales[column] / scales[row] / (lobatto_nodes[row] - lobatto_nodes[column])
                )
        table[row, row] = -np.sum(table[row])
    return table


def radial_derivative(table, field):
    return jnp.einsum("ia,...abe->...ibe", table, field, precision=lax.Precision.HIGHEST)


def around_derivative(table, field):
    return jnp.einsum("jb,...abe->...aje", table, field, precision=lax.Precision.HIGHEST)


def radial_transpose(table, field):
    return jnp.einsum("ia,...ibe->...abe", table, field, precision=lax.Precision.HIGHEST)


def around_transpose(table, field):
    return jnp.einsum("jb,...aje->...abe", table, field, precision=lax.Precision.HIGHEST)


def z_derivative(field, first_pair):
    shape = field.shape
    count = shape[1] // 2
    pairs = field.reshape((shape[0], count, 2) + shape[2:])
    waves = (first_pair + jnp.arange(count, dtype=jnp.int32)).astype(jnp.float32) * spanwise_wave
    waves = waves.reshape((1, count) + (1,) * (len(shape) - 2))
    return jnp.stack([waves * pairs[:, :, 1], -waves * pairs[:, :, 0]], axis=2).reshape(shape)


def transform_tables(planes):
    position = jnp.arange(planes, dtype=jnp.int32)
    plane = jnp.arange(planes, dtype=jnp.int32)
    order = plane // 2
    turns = position[:, None] * order[None, :] % planes
    angle = 2.0 * math.pi / planes * turns.astype(jnp.float32)
    cosine = jnp.cos(angle)
    sine = jnp.sin(angle)
    is_sine = (plane % 2 == 1)[None, :]
    is_top = (plane == 1)[None, :]
    parity = jnp.cos(math.pi * (position % 2).astype(jnp.float32))[:, None]
    basis = jnp.where(is_top, parity, jnp.where(is_sine, sine, cosine))
    scaling = jnp.where(order == 0, 1.0, 2.0).astype(jnp.float32) / planes
    inverse = jnp.transpose(basis * scaling[None, :])
    wave = (order.astype(jnp.float32) * spanwise_wave)[None, :]
    slope = jnp.where(is_sine, wave * cosine, -wave * sine)
    return (basis, inverse, slope)


def geometry(radial_dx, radial_dy, around_dx, around_dy, jacobian):
    lobatto_weights = lobatto_rule(NODES)[1]
    quadrature = jnp.asarray(np.outer(lobatto_weights, lobatto_weights), jnp.float32)[:, :, None]
    mass = quadrature * jacobian
    radial_stiff = mass * (radial_dx * radial_dx + radial_dy * radial_dy)
    cross_stiff = mass * (radial_dx * around_dx + radial_dy * around_dy)
    around_stiff = mass * (around_dx * around_dx + around_dy * around_dy)
    return (radial_stiff, cross_stiff, around_stiff, mass)


def node_weights(layers):
    layer = jnp.arange(layers, dtype=jnp.int32).reshape(layers, 1, 1, 1)
    node = jnp.arange(NODES, dtype=jnp.int32)
    radial_node = node.reshape(1, NODES, 1, 1)
    around_node = node.reshape(1, 1, NODES, 1)
    shared_radial = (radial_node == NODES - 1) & (layer < layers - 1) | (radial_node == 0) & (
        layer > 0
    )
    shared_around = (around_node == 0) | (around_node == NODES - 1)
    multiplicity = (1.0 + shared_radial.astype(jnp.float32)) * (
        1.0 + shared_around.astype(jnp.float32)
    )
    boundary = (radial_node == NODES - 1) & (layer == layers - 1)
    mask = 1.0 - boundary.astype(jnp.float32)
    return (mask, mask / multiplicity)


def plane_shift(first_plane, count, planes):
    plane = first_plane + jnp.arange(count, dtype=jnp.int32)
    order = jnp.where(plane == 1, planes // 2, plane // 2)
    wave = order.astype(jnp.float32) * spanwise_wave
    return (wave * wave).reshape(count, 1, 1, 1, 1)


def helmholtz_local(table, field, shift, metrics):
    radial_stiff, cross_stiff, around_stiff, mass = metrics
    radial = radial_derivative(table, field)
    beside_all = around_derivative(table, field)
    return (
        radial_transpose(table, radial_stiff * radial + cross_stiff * beside_all)
        + around_transpose(table, cross_stiff * radial + around_stiff * beside_all)
        + shift * mass * field
    )


def assemble(field):
    lower = field[:, :-1, -1] + field[:, 1:, 0]
    field = field.at[:, :-1, -1].set(lower).at[:, 1:, 0].set(lower)
    first = field[:, :, :, 0]
    last = field[:, :, :, -1]
    rims = jnp.concatenate([first[..., :1], last[..., -1:]], axis=3)
    padded = padded_2(rims, (("elem", 3),), 1)
    after = jnp.concatenate([first[..., 1:], padded[..., 3:4]], axis=3)
    right = last + after
    left = jnp.concatenate([padded[..., 0:1] + first[..., :1], right[..., :-1]], axis=3)
    return field.at[:, :, :, -1].set(right).at[:, :, :, 0].set(left)


def inner(first, second, weight):
    return jnp.sum(first * second * weight, axis=(1, 2, 3, 4))


def expand(scalar):
    return scalar.reshape(-1, 1, 1, 1, 1)


def squared_norm(residual, weight):
    return lax.psum(inner(residual, residual, weight), "elem")


def on_device(velocity, radial_dx, radial_dy, around_dx, around_dy, jacobian):
    table = jnp.asarray(derivative_table(), jnp.float32)
    modes = lax.axis_size("mode")
    local_planes = velocity.shape[1]
    planes = local_planes * modes
    first_plane = lax.axis_index("mode") * local_planes
    layers = velocity.shape[2]
    columns = velocity.shape[5]
    basis, inverse, slope = transform_tables(planes)
    radial = radial_derivative(table, velocity)
    beside_all = around_derivative(table, velocity)
    along_x = radial_dx * radial + around_dx * beside_all
    along_y = radial_dy * radial + around_dy * beside_all
    fields = jnp.concatenate([velocity, along_x, along_y], axis=0)
    count = fields.shape[0]
    cells = layers * NODES * NODES * columns
    packed = fields.reshape(count, local_planes, modes, cells // modes)
    flat = lax.all_to_all(packed, "mode", split_axis=2, concat_axis=1, tiled=True)[:, :, 0, :]
    values = jnp.einsum("jp,fpc->fjc", basis, flat, precision=lax.Precision.HIGHEST)
    speed = values[0:3]
    slope_x = values[3:6]
    slope_y = values[6:9]
    slope_z = jnp.einsum("jp,fpc->fjc", slope, flat[0:3], precision=lax.Precision.HIGHEST)
    product = -(speed[0:1] * slope_x + speed[1:2] * slope_y + speed[2:3] * slope_z)
    spectral = jnp.einsum("pj,fjc->fpc", inverse, product, precision=lax.Precision.HIGHEST)
    returned = lax.all_to_all(
        spectral[:, :, None, :], "mode", split_axis=1, concat_axis=2, tiled=True
    )
    advection = returned.reshape(velocity.shape)
    metrics = geometry(radial_dx, radial_dy, around_dx, around_dy, jacobian)
    mask, weight = node_weights(layers)
    predicted = velocity + time_step * advection
    radial = radial_derivative(table, predicted[0:2])
    beside_all = around_derivative(table, predicted[0:2])
    divergence = (
        radial_dx * radial[0]
        + around_dx * beside_all[0]
        + (radial_dy * radial[1] + around_dy * beside_all[1])
        + z_derivative(predicted[2:3], first_plane // 2)[0]
    )
    shift = plane_shift(first_plane, local_planes, planes)
    right_side = mask * assemble(-(metrics[3] * divergence) / time_step)
    solution = jnp.zeros_like(right_side)
    residual = right_side
    direction = right_side
    norm_now = squared_norm(residual, weight)
    for _ in range(ITERS):
        image = mask * assemble(helmholtz_local(table, direction, shift, metrics))
        alpha = norm_now / lax.psum(inner(direction, image, weight), "elem")
        solution = solution + expand(alpha) * direction
        residual = residual - expand(alpha) * image
        norm_next = squared_norm(residual, weight)
        direction = residual + expand(norm_next / norm_now) * direction
        norm_now = norm_next
    return (advection, solution)


def split_bf16(table):
    high = table.astype(jnp.bfloat16)
    low = (table - high.astype(np.float64)).astype(jnp.bfloat16)
    return np.concatenate([high, high, low], axis=1)


def paired_tables(planes):
    position = np.arange(planes)
    plane = np.arange(planes)
    order = plane // 2
    angle = 2.0 * np.pi / planes * (position[:, None] * order[None, :] % planes)
    cosine, sine = (np.cos(angle), np.sin(angle))
    odd = (plane % 2 == 1)[None, :]
    parity = (1.0 - 2.0 * (position % 2))[:, None]
    basis = np.where((plane == 1)[None, :], parity, np.where(odd, sine, cosine))
    wave = (order * spanwise_wave)[None, :]
    slope = np.where(odd, wave * cosine, -wave * sine)
    scaling = np.where(order == 0, 1.0, 2.0) / planes
    inverse = -(basis * scaling[None, :]).T

    def columns(matrix):
        return np.concatenate([matrix[:, 0::2], matrix[:, 1::2]], axis=1)

    forward = np.concatenate([columns(basis), columns(slope)])
    backward = columns(inverse.T).T
    return (split_bf16(forward), split_bf16(backward))


def apply_line(matrix, line):
    n = NODES
    m = n // 2
    sums = [line[a] + line[n - 1 - a] for a in range(m)]
    gaps = [line[a] - line[n - 1 - a] for a in range(m)]

    def total(parts):
        out = parts[0]
        for part in parts[1:]:
            out = out + part
        return out

    out = [None] * n
    for i in range(m + 1):
        plus = total(
            [float(0.5 * (matrix[i, a] - matrix[i, n - 1 - a])) * gaps[a] for a in range(m)]
        )
        if i == m:
            out[i] = plus
            continue
        minus = total(
            [float(0.5 * (matrix[i, a] + matrix[i, n - 1 - a])) * sums[a] for a in range(m)]
            + [float(matrix[i, m]) * line[m]]
        )
        out[i] = plus + minus
        out[n - 1 - i] = plus - minus
    return out


def lanes_of(shape):
    return lax.broadcasted_iota(jnp.int32, shape, len(shape) - 1)


def row_of(ref, row, rows):
    return ref[pl.ds(row, rows, stride=0), :]


def call(body, grid, ins, outs, out_shape, scratch=(), flops=0, moved=0, aliases=None, grant=GRANT):
    return pl.pallas_call(
        body,
        grid=grid,
        in_specs=ins,
        out_specs=outs,
        out_shape=out_shape,
        scratch_shapes=list(scratch),
        input_output_aliases=aliases or {},
        compiler_params=pltpu.CompilerParams(
            dimension_semantics=("arbitrary",) * len(grid), vmem_limit_bytes=grant
        ),
        cost_estimate=pl.CostEstimate(
            flops=int(flops), bytes_accessed=int(moved), transcendentals=0
        ),
    )


def held(count):
    return [pl.BlockSpec(memory_space=pltpu.VMEM)] * count


def whole(shape):
    return pl.BlockSpec(shape, lambda *_: (0,) * len(shape))


def turn(tiles):
    tiles = list(tiles)
    sub = lax.broadcasted_iota(jnp.int32, tiles[0].shape, 0)
    size = len(tiles)
    step = size // 2
    while step:
        keep = (sub & step) == 0
        for i in range(size):
            if not i & step:
                one, two = (tiles[i], tiles[i + step])
                tiles[i] = jnp.where(keep, one, pltpu.roll(two, step, 0))
                tiles[i + step] = jnp.where(keep, pltpu.roll(one, size - step, 0), two)
        step //= 2
    return tiles


def turn_all(read, write, count):
    def some(s, carry):
        for i in range(NODES):
            t = s * NODES + i
            for r, tile in enumerate(turn([read(k, t) for k in range(8)])):
                write(t, r, tile)
        return carry

    lax.fori_loop(0, count // NODES, some, 0)


def rows_at(k, unit, t):
    return pl.ds(pl.multiple_of(k * unit + 8 * t, 8), 8)


def pack_one(x_ref, write_out, mid, layers, lanes):
    square = NODES * NODES
    per_plane = square * layers
    unit = 2 * per_plane
    half = lanes // 2
    low = lanes_of((8, lanes)) < half

    def write(t, r, tile):
        mid[8 * t + r] = tile

    turn_all(lambda k, t: x_ref[0, rows_at(k, unit, t), :], write, unit // 8)

    def layer(e, carry):
        for n in range(square):
            cos = mid[n * layers + e]
            sin = mid[per_plane + n * layers + e]
            write_out(2 * e, n, jnp.where(low, cos, pltpu.roll(sin, half, 1)))
            write_out(2 * e + 1, n, jnp.where(low, pltpu.roll(cos, half, 1), sin))
        return carry

    lax.fori_loop(0, layers, layer, 0)


def pack_specs(layers, pairs, lanes, nodes):
    return (
        pl.BlockSpec((2 * layers, nodes, 8, lanes), lambda g: (0, 0, g, 0)),
        jax.ShapeDtypeStruct((2 * layers, nodes, pairs, lanes), jnp.float32),
    )


def pack_first(rows, place, layers, pairs, lanes):
    square = NODES * NODES
    unit = 2 * square * layers
    shares = 2 * layers

    def body(place_ref, x_ref, *refs):
        outs, (mid, held_ref) = (refs[:shares], refs[shares:])
        here = place_ref[0]

        def write(d, n, value):
            held_ref[d, n] = value

        pack_one(x_ref, write, mid, layers, lanes)

        def row(a, carry):
            for k in range(shares):
                d = lax.rem(here + k, shares)
                for b in range(NODES):
                    outs[k][a * NODES + b] = held_ref[d, a * NODES + b]
            return carry

        lax.fori_loop(0, NODES, row, 0)

    return call(
        body,
        (pairs // 8,),
        [
            pl.BlockSpec(memory_space=pltpu.SMEM),
            pl.BlockSpec((1, 8 * unit, lanes), lambda g: (0, g, 0)),
        ],
        [pl.BlockSpec((square, 8, lanes), lambda g: (0, g, 0))] * shares,
        [jax.ShapeDtypeStruct((square, pairs, lanes), jnp.float32)] * shares,
        scratch=[
            pltpu.VMEM((unit, 8, lanes), jnp.float32),
            pltpu.VMEM((shares, square, 8, lanes), jnp.float32),
        ],
        grant=WHOLE_GRANT,
        moved=2 * rows.shape[1] * lanes * 4,
    )(jnp.full((1,), place, jnp.int32), rows)


def pack_rest(rows, layers, pairs, lanes, early):
    square = NODES * NODES
    unit = 2 * square * layers

    def body(u_ref, x_ref, y_ref, o_ref, late_ref, whole_ref, zero_ref, mid):
        def zeroth(d, n, value):
            zero_ref[d, n] = value

        def first(d, n, value):
            o_ref[d, n] = value

        def second(d, n, value):
            whole_ref[d, n] = value
            if n < early:
                o_ref[d, square + n] = value
            else:
                late_ref[d, n - early] = value

        pack_one(x_ref, first, mid, layers, lanes)
        pack_one(y_ref, second, mid, layers, lanes)
        pack_one(u_ref, zeroth, mid, layers, lanes)

    parts = [
        pack_specs(layers, pairs, lanes, nodes)
        for nodes in (square + early, square - early, square, square)
    ]
    return call(
        body,
        (pairs // 8,),
        [
            pl.BlockSpec((1, 8 * unit, lanes), lambda g: (0, g, 0)),
            pl.BlockSpec((1, 8 * unit, lanes), lambda g: (1, g, 0)),
            pl.BlockSpec((1, 8 * unit, lanes), lambda g: (2, g, 0)),
        ],
        [part[0] for part in parts],
        [part[1] for part in parts],
        scratch=[pltpu.VMEM((unit, 8, lanes), jnp.float32)],
        grant=WHOLE_GRANT,
        moved=5 * rows.shape[1] * lanes * 4,
    )(rows, rows, rows)


def unpack(arrays, specs, read_from, slots, layers, buffer, total, steps=2):
    lanes = arrays[0].shape[-1]
    square = NODES * NODES
    per_plane = square * layers
    unit = 2 * per_plane
    half = lanes // 2

    def body(*refs):
        o_ref, mid = refs[-2:]
        low = lanes_of((8, lanes)) < half
        read = read_from(refs, pl.program_id(0))

        def layer(e, carry):
            for n in range(square):
                left, right = (read(2 * e, n), read(2 * e + 1, n))
                mid[n * layers + e] = jnp.where(low, left, pltpu.roll(right, half, 1))
                mid[per_plane + n * layers + e] = jnp.where(low, pltpu.roll(left, half, 1), right)
            return carry

        lax.fori_loop(0, layers, layer, 0)

        def write(t, r, tile):
            o_ref[rows_at(r, unit, t), :] = tile

        turn_all(lambda k, t: mid[8 * t + k], write, unit // 8)

    extra = [] if buffer is None else [buffer]
    return call(
        body,
        (steps,),
        list(specs) + [pl.BlockSpec(memory_space=pl.ANY)] * len(extra),
        pl.BlockSpec((8 * unit, lanes), lambda i: (slots[0] + i * slots[1], 0)),
        jax.ShapeDtypeStruct((total, lanes), jnp.float32),
        scratch=[pltpu.VMEM((unit, 8, lanes), jnp.float32)],
        moved=4 * 8 * unit * lanes * 4,
        aliases={len(arrays): 0} if extra else None,
    )(*arrays, *extra)


def paired_nodes():
    return [(b, min(b + 1, NODES - 1)) for b in range(0, NODES, 2)]


def three_pass(table, rhs_ref, tiles):
    rows, lanes = tiles[0].shape
    half = lanes // 2
    low = lanes_of((rows, lanes)) < half
    depth = 2 * rows
    for place, (one, two) in enumerate(paired_nodes()):
        first, second = (tiles[one], tiles[two])
        cut = pl.ds(place * lanes, lanes)
        for part in range(2):
            if part == 0:
                value = jnp.where(low, first, pltpu.roll(second, half, 1))
            else:
                value = jnp.where(low, pltpu.roll(first, half, 1), second)
            high = value.astype(jnp.bfloat16)
            rest = (value - high.astype(jnp.float32)).astype(jnp.bfloat16)
            rhs_ref[pl.ds(part * rows, rows), cut] = high
            rhs_ref[pl.ds(depth + part * rows, rows), cut] = rest
            rhs_ref[pl.ds(2 * depth + part * rows, rows), cut] = high
    out = jnp.dot(table, rhs_ref[...], preferred_element_type=jnp.float32)
    fields = []
    for field in range(table.shape[0] // depth):
        nodes = [None] * NODES
        for place, (one, two) in enumerate(paired_nodes()):
            cut = slice(place * lanes, (place + 1) * lanes)
            top = out[field * depth : field * depth + rows, cut]
            bottom = out[field * depth + rows : (field + 1) * depth, cut]
            nodes[one] = jnp.where(low, top, pltpu.roll(bottom, half, 1))
            if two != one:
                nodes[two] = jnp.where(low, pltpu.roll(top, half, 1), bottom)
        fields.append(nodes)
    return fields


def rhs_scratch(table, lanes):
    return pltpu.VMEM((table.shape[1], len(paired_nodes()) * lanes), jnp.bfloat16)


def read_tiles(x_ref, rows, lanes):
    return [x_ref[:, b].reshape(rows, lanes) for b in range(NODES)]


def to_points(blocks, table):
    shares, _, pairs, lanes = blocks.shape
    square = NODES * NODES
    rows = shares * pairs

    def body(t_ref, x_ref, v_ref, z_ref, rhs_ref):
        fields = three_pass(t_ref[...], rhs_ref, read_tiles(x_ref, rows, lanes))
        for b in range(NODES):
            v_ref[b] = fields[0][b]
            z_ref[b] = fields[1][b]

    spec = pl.BlockSpec((NODES, rows, lanes), lambda a: (a, 0, 0))
    shape = jax.ShapeDtypeStruct((square, rows, lanes), jnp.float32)
    return call(
        body,
        (NODES,),
        [
            whole(table.shape),
            pl.BlockSpec((shares, NODES, pairs, lanes), lambda a: (0, a, 0, 0)),
        ],
        [spec, spec],
        [shape, shape],
        scratch=[rhs_scratch(table, lanes)],
        flops=2 * table.shape[0] * table.shape[1] * square * lanes,
        grant=WHOLE_GRANT,
        moved=3 * square * rows * lanes * 4,
    )(table, blocks)


def turn_around(blocks, skip, start, count, partial, slope_z, table, back, fields, out):
    shares, _, pairs, lanes = blocks.shape
    rows = shares * pairs
    square = NODES * NODES
    group = pairs // 2
    shape = jax.ShapeDtypeStruct((square, rows, lanes), jnp.float32)

    def body(t_ref, i_ref, x_ref, g_ref, s_ref, *refs):
        w_ref, z_ref, o_ref, rhs_ref = refs[-4:]
        points = three_pass(t_ref[...], rhs_ref, read_tiles(x_ref, rows, lanes))
        for b in range(NODES):
            w_ref[b] = points[0][b]
            z_ref[b] = points[1][b]
        tiles = [g_ref[b] + w_ref[b] * s_ref[b] for b in range(NODES)]
        spectral = three_pass(i_ref[...], rhs_ref, tiles)[0]
        for b in range(NODES):
            value = spectral[b].reshape(shares, pairs, lanes)
            if out is None:
                o_ref[:, b] = value
            else:
                for g in range(2):
                    o_ref[:, g * NODES + b] = value[:, g * group : (g + 1) * group]

    spec = pl.BlockSpec((NODES, rows, lanes), lambda a: (start + a, 0, 0))
    if out is None:
        out_spec = pl.BlockSpec((shares, NODES, pairs, lanes), lambda a: (0, a, 0, 0))
        out_shape = jax.ShapeDtypeStruct((shares, count * NODES, pairs, lanes), jnp.float32)
    else:
        first = out[1]
        out_spec = pl.BlockSpec((shares, 2 * NODES, group, lanes), lambda a: (0, first + a, 0, 0))
        out_shape = jax.ShapeDtypeStruct(out[0], jnp.float32)
    return call(
        body,
        (count,),
        [
            whole(table.shape),
            whole(back.shape),
            pl.BlockSpec((shares, NODES, pairs, lanes), lambda a: (0, skip + a, 0, 0)),
            spec,
            spec,
        ]
        + [pl.BlockSpec(memory_space=pl.ANY)] * len(fields),
        [spec, spec, out_spec],
        [shape, shape, out_shape],
        scratch=[rhs_scratch(table, lanes)],
        flops=3 * table.shape[0] * table.shape[1] * count * NODES * lanes,
        aliases={5: 0, 6: 1} if fields else None,
        grant=WHOLE_GRANT,
        moved=6 * count * NODES * rows * lanes * 4,
    )(table, back, blocks, partial, slope_z, *fields)


def in_plane(speeds, fields, metrics, table):
    square, rows, lanes = speeds[0].shape
    count = len(fields)
    step = 32
    own = [i for i, f in enumerate(fields) if all(f is not s for s in speeds)]
    arrays = list(speeds) + [fields[i] for i in own]

    def body(m_ref, *refs):
        ins, outs = (refs[: len(arrays)], refs[len(arrays) :])
        u_ref, v_ref = ins[:2]
        sources = []
        extra = 2
        for i, f in enumerate(fields):
            if i in own:
                sources.append(ins[extra])
                extra += 1
            else:
                sources.append(u_ref if f is speeds[0] else v_ref)

        def block(s, carry):
            r = pl.ds(s * 8, 8)

            def metric(kind, n):
                return row_of(m_ref, kind * square + n, 8)

            for a in range(NODES):
                ns = [a * NODES + b for b in range(NODES)]
                drift = [
                    u_ref[n, r] * metric(2, n) + v_ref[n, r] * metric(3, n) for n in ns
                ]
                for f in range(count):
                    beside = apply_line(table, [sources[f][n, r] for n in ns])
                    for b, n in enumerate(ns):
                        outs[f][n, r] = drift[b] * beside[b]
            for b in range(NODES):
                ns = [a * NODES + b for a in range(NODES)]
                drift = [
                    u_ref[n, r] * metric(0, n) + v_ref[n, r] * metric(1, n) for n in ns
                ]
                for f in range(count):
                    radial = apply_line(table, [sources[f][n, r] for n in ns])
                    for a, n in enumerate(ns):
                        outs[f][n, r] = outs[f][n, r] + drift[a] * radial[a]
            return carry

        lax.fori_loop(0, step // 8, block, 0)

    spec = pl.BlockSpec((square, step, lanes), lambda i: (0, i, 0))
    shape = jax.ShapeDtypeStruct((square, rows, lanes), jnp.float32)
    return call(
        body,
        (rows // step,),
        [whole(metrics.shape)] + [spec] * len(arrays),
        [spec] * count,
        [shape] * count,
        flops=30 * count * square * rows * lanes,
        grant=WHOLE_GRANT,
        moved=(len(arrays) + count) * square * rows * lanes * 4,
    )(metrics, *arrays)


def by_source(strips, place):
    count = len(strips)
    nodes = strips[0].shape[0]

    def body(place_ref, *refs):
        o_ref = refs[-1]
        here = place_ref[0]

        def node(n, carry):
            for k in range(count):
                o_ref[lax.rem(here - k + count, count), n] = refs[k][n]
            return carry

        lax.fori_loop(0, nodes, node, 0)

    return call(
        body,
        (1,),
        [pl.BlockSpec(memory_space=pltpu.SMEM)] + [whole(strips[0].shape)] * count,
        whole((count,) + strips[0].shape),
        jax.ShapeDtypeStruct((count,) + strips[0].shape, jnp.float32),
        grant=WHOLE_GRANT,
        moved=8 * count * strips[0].size,
    )(jnp.full((1,), place, jnp.int32), *strips)


def to_planes(partial, speed_z, slope_z, table, shares, place, shapes, buffers):
    square, rows, lanes = partial.shape
    pairs = rows // shares
    group = pairs // 2

    def body(t_ref, g_ref, w_ref, z_ref, *refs):
        outs, rhs_ref = (refs[-3:-1], refs[-1])
        tiles = [g_ref[b] + w_ref[b] * z_ref[b] for b in range(NODES)]
        nodes = three_pass(t_ref[...], rhs_ref, tiles)[0]
        for b in range(NODES):
            out = nodes[b].reshape(shares, pairs, lanes)
            for i in range(2):
                outs[i][:, b] = out[:, i * group : (i + 1) * group]

    spec = pl.BlockSpec((NODES, rows, lanes), lambda a: (a, 0, 0))
    out_spec = pl.BlockSpec((shares, NODES, group, lanes), lambda a: (0, place * NODES + a, 0, 0))
    shapes = [jax.ShapeDtypeStruct(shape, jnp.float32) for shape in shapes]
    return call(
        body,
        (NODES,),
        [whole(table.shape), spec, spec, spec]
        + [pl.BlockSpec(memory_space=pl.ANY)] * len(buffers),
        [out_spec, out_spec],
        shapes,
        scratch=[rhs_scratch(table, lanes)],
        flops=2 * table.shape[0] * table.shape[1] * square * lanes,
        grant=WHOLE_GRANT,
        moved=4 * square * rows * lanes * 4,
        aliases={4 + k: k for k in range(len(buffers))},
    )(table, partial, speed_z, slope_z, *buffers)


def velocity_part(sent, metrics, weights, waves, table):
    shares, square, pairs, lanes = sent[0].shape
    half = lanes // 2

    def body(m_ref, q_ref, k_ref, s0, s1, s2, o_ref):
        d = pl.program_id(0)

        def rows_of(s):
            r = pl.ds(s * 8, 8)
            wave = k_ref[r]

            def metric(kind, n):
                return row_of(m_ref, (kind * shares + d) * square + n, 8)

            for a in range(NODES):
                ns = [a * NODES + b for b in range(NODES)]
                first = apply_line(table, [s0[0, n, r] for n in ns])
                second = apply_line(table, [s1[0, n, r] for n in ns])
                for b, n in enumerate(ns):
                    along = pltpu.roll(s2[0, n, r], half, 1) * wave
                    o_ref[0, n, r] = (
                        metric(2, n) * first[b]
                        + metric(3, n) * second[b]
                        + row_of(q_ref, d * square + n, 8) * along
                    )
            for b in range(NODES):
                ns = [a * NODES + b for a in range(NODES)]
                first = apply_line(table, [s0[0, n, r] for n in ns])
                second = apply_line(table, [s1[0, n, r] for n in ns])
                for a, n in enumerate(ns):
                    o_ref[0, n, r] = o_ref[0, n, r] + (
                        metric(0, n) * first[a] + metric(1, n) * second[a]
                    )

        lax.fori_loop(0, pairs // 8, lambda s, carry: (rows_of(s), carry)[1], 0)

    spec = pl.BlockSpec((1, square, pairs, lanes), lambda d: (d, 0, 0, 0))
    return call(
        body,
        (shares,),
        [whole(metrics.shape), whole(weights.shape), whole(waves.shape)] + [spec] * 3,
        spec,
        jax.ShapeDtypeStruct(sent[0].shape, jnp.float32),
        flops=60 * shares * square * pairs * lanes,
        grant=WHOLE_GRANT,
        moved=4 * shares * square * pairs * lanes * 4,
    )(metrics, weights, waves, *sent)


def first_part(base, early, rest, rest_at, metrics, table):
    shares, square, pairs, lanes = base.shape

    some = early.shape[1]
    count = (square - some) // NODES
    group = pairs // 2

    def body(m_ref, s0, r0, *refs):
        others, (o_ref, p0) = (refs[:count], refs[count:])
        d = pl.program_id(0)

        def block(s, carry):
            r = pl.ds(s * 8, 8)
            for n in range(square):
                if n < some:
                    home = r0[0, n, r]
                else:
                    a, b = divmod(n - some, NODES)
                    home = others[a][0, s * NODES + b]
                p0[n] = home

            def metric(kind, n):
                return row_of(m_ref, (kind * shares + d) * square + n, 8)

            for a in range(NODES):
                ns = [a * NODES + b for b in range(NODES)]
                line = apply_line(table, [p0[n] for n in ns])
                for b, n in enumerate(ns):
                    o_ref[0, n, r] = s0[0, n, r] + metric(2, n) * line[b]
            for b in range(NODES):
                ns = [a * NODES + b for a in range(NODES)]
                line = apply_line(table, [p0[n] for n in ns])
                for a, n in enumerate(ns):
                    o_ref[0, n, r] = o_ref[0, n, r] + metric(0, n) * line[a]
            return carry

        lax.fori_loop(0, pairs // 8, block, 0)

    spec = pl.BlockSpec((1, square, pairs, lanes), lambda d: (d, 0, 0, 0))
    return call(
        body,
        (shares,),
        [whole(metrics.shape), spec, pl.BlockSpec((1, some, pairs, lanes), lambda d: (d, 0, 0, 0))]
        + [
            pl.BlockSpec(
                (1, 2 * NODES, group, lanes), functools.partial(lambda i, d: (d, i, 0, 0), rest_at + k)
            )
            for k in range(count)
        ],
        spec,
        jax.ShapeDtypeStruct(base.shape, jnp.float32),
        scratch=[pltpu.VMEM((square, 8, lanes), jnp.float32)],
        flops=30 * shares * square * pairs * lanes,
        grant=WHOLE_GRANT,
        moved=3 * shares * square * pairs * lanes * 4,
    )(metrics, base, early, *[rest] * count)


def join_layers(y_ref, layers):
    square = NODES * NODES
    last = (NODES - 1) * NODES
    for e in range(layers - 1):
        for b in range(NODES):
            upper, lower = (e * square + last + b, (e + 1) * square + b)
            total = y_ref[upper] + y_ref[lower]
            y_ref[upper] = total
            y_ref[lower] = total
    for b in range(NODES):
        node = (layers - 1) * square + last + b
        y_ref[node] = jnp.zeros_like(y_ref[node])


def rim_messages(read, layers, shape, partials):
    lane = lanes_of(shape)
    lanes = shape[-1]
    axis = len(shape) - 1
    first = jnp.zeros(shape, jnp.float32)
    last = jnp.zeros(shape, jnp.float32)
    square = NODES * NODES
    for e in range(layers):
        for a in range(NODES):
            spot = e * NODES + a
            here = lane == spot
            node = e * square + a * NODES
            first = jnp.where(here, pltpu.roll(read(node), spot, axis), first)
            last = jnp.where(
                here, pltpu.roll(read(node + NODES - 1), (spot + 1) % lanes, axis), last
            )
    for i, partial in enumerate(partials):
        here = lane == layers * NODES + i
        first = jnp.where(here, partial, first)
        last = jnp.where(here, partial, last)
    return (first, last)


def right_side(flat, returned, metrics, weights, waves, table, layers, place):
    shares, square, _, lanes = flat.shape
    half = lanes // 2

    def body(m_ref, q_ref, k_ref, f_ref, r1, r2, o_ref, first_ref, last_ref, c0, c1):
        e = pl.program_id(0)
        lane = lanes_of((8, lanes))
        low = lane < half
        wave = k_ref[...]
        sides = (c0, c1)

        @pl.when(e == 0)
        def _():
            first_ref[...] = jnp.zeros_like(first_ref)
            last_ref[...] = jnp.zeros_like(last_ref)

        for h in range(2):
            d = 2 * e + h
            side = sides[h]
            for n in range(square):
                along = pltpu.roll(r2[h, n], half, 1) * wave
                side[n] = f_ref[h, n] + row_of(q_ref, d * square + n, 8) * along

            def metric(kind, n):
                return row_of(m_ref, (kind * shares + d) * square + n, 8)

            for a in range(NODES):
                ns = [a * NODES + b for b in range(NODES)]
                line = apply_line(table, [r1[h, n] for n in ns])
                for b, n in enumerate(ns):
                    side[n] = side[n] + metric(3, n) * line[b]
            for b in range(NODES):
                ns = [a * NODES + b for a in range(NODES)]
                line = apply_line(table, [r1[h, n] for n in ns])
                for a, n in enumerate(ns):
                    side[n] = side[n] + metric(1, n) * line[a]
        rims = [[first_ref[0], last_ref[0]], [first_ref[1], last_ref[1]]]
        for n in range(square):
            left, right = (c0[n], c1[n])
            parts = (
                jnp.where(low, left, pltpu.roll(right, half, 1)),
                jnp.where(low, pltpu.roll(left, half, 1), right),
            )
            for i in range(2):
                o_ref[n, i] = parts[i]
                a, b = divmod(n, NODES)
                spot = e * NODES + a
                if b == 0:
                    rims[i][0] = jnp.where(lane == spot, pltpu.roll(parts[i], spot, 1), rims[i][0])
                if b == NODES - 1:
                    rims[i][1] = jnp.where(
                        lane == spot, pltpu.roll(parts[i], spot + 1, 1), rims[i][1]
                    )
        for i in range(2):
            first_ref[i] = rims[i][0]
            last_ref[i] = rims[i][1]

    spec = pl.BlockSpec((2, square, 8, lanes), lambda e: (e, 0, place, 0))
    nodes = layers * square
    rim_shape = jax.ShapeDtypeStruct((2, 8, lanes), jnp.float32)
    scratch = pltpu.VMEM((square, 8, lanes), jnp.float32)
    return call(
        body,
        (layers,),
        [
            whole(metrics.shape),
            whole(weights.shape),
            pl.BlockSpec((8, lanes), lambda e: (place, 0)),
            spec,
            pl.BlockSpec((2, square, 8, lanes), lambda e: (e, 0, 0, 0)),
            pl.BlockSpec((2, square, 8, lanes), lambda e: (e, 1, 0, 0)),
        ],
        [
            pl.BlockSpec((square, 2, 8, lanes), lambda e: (e, 0, 0, 0)),
            whole((2, 8, lanes)),
            whole((2, 8, lanes)),
        ],
        [jax.ShapeDtypeStruct((nodes, 2, 8, lanes), jnp.float32), rim_shape, rim_shape],
        scratch=[scratch] * 2,
        flops=40 * shares * square * 8 * lanes,
        moved=4 * shares * square * 8 * lanes * 4,
    )(metrics, weights, waves, flat, returned, returned)


def swap_rims(first, last):
    size = lax.axis_size("elem")
    up = [(i, (i + 1) % size) for i in range(size)]
    down = [(j, i) for i, j in up]
    return (lax.ppermute(last, "elem", up), lax.ppermute(first, "elem", down))


def opposite(first):
    size = lax.axis_size("elem")
    return lax.ppermute(first, "elem", [(i, (i + 2) % size) for i in range(size)])


def join_columns(read, ref, before, after, layers):
    lanes = before.shape[-1]
    axis = len(before.shape) - 1
    lane = lanes_of(before.shape)
    square = NODES * NODES
    for e in range(layers):
        for a in range(NODES):
            spot = e * NODES + a
            node = e * square + a * NODES
            first, last = (read(node), read(node + NODES - 1))
            beyond = pltpu.roll(after, lanes - 1 - spot, axis)
            ahead = jnp.where(lane == lanes - 1, beyond, pltpu.roll(first, lanes - 1, axis))
            right = last + ahead
            mine = first + (pltpu.roll(before, lanes - spot, axis) if spot else before)
            ref[node + NODES - 1] = right
            ref[node] = jnp.where(lane == 0, mine, pltpu.roll(right, 1, axis))


def join(source, ref, before, after, layers):
    square = NODES * NODES

    def copy(e, carry):
        for n in range(square):
            if 0 < n % NODES < NODES - 1:
                ref[e * square + n] = source[e * square + n]
        return carry

    lax.fori_loop(0, layers, copy, 0)
    join_columns(lambda n: source[n], ref, before, after, layers)
    join_layers(ref, layers)


def each_node(layers, step):
    def layer(e, carry):
        for n in range(NODES * NODES):
            step(e * NODES * NODES + n)
        return carry

    lax.fori_loop(0, layers, layer, 0)


def share_of(layers, e, a):
    if a == 0:
        return jnp.where(e > 0, 0.5, 1.0)
    if a == NODES - 1:
        return jnp.where(e < layers - 1, 0.5, 0.0)
    return 1.0


def helmholtz(r_ref, y_ref, flux_ref, g_ref, shift, layers, table, dot_only=False):
    square = NODES * NODES
    nodes = layers * square
    turned = table.T
    zero = jnp.zeros(shift.shape, jnp.float32)

    def layer(e, carry):
        norm, energy = carry
        base = e * square

        def metric(kind, n):
            return row_of(g_ref, kind * nodes + base + n, 8)

        for b in range(NODES):
            ns = [a * NODES + b for a in range(NODES)]
            radial = apply_line(table, [r_ref[base + n] for n in ns])
            for a, n in enumerate(ns):
                flux_ref[n] = radial[a]
        for a in range(NODES):
            ns = [a * NODES + b for b in range(NODES)]
            line = [r_ref[base + n] for n in ns]
            beside = apply_line(table, line)
            second = []
            rest = []
            part = zero
            for b, n in enumerate(ns):
                radial = flux_ref[n]
                cross = metric(1, n)
                one = metric(0, n) * radial + cross * beside[b]
                two = cross * radial + metric(2, n) * beside[b]
                same = shift * metric(3, n) * line[b]
                whole_weight = line[b] * line[b]
                part = part + (0.5 * whole_weight if b in (0, NODES - 1) else whole_weight)
                if dot_only:
                    energy = energy + (radial * one + beside[b] * two + same * line[b])
                else:
                    flux_ref[n] = one
                    second.append(two)
                    rest.append(same)
            norm = norm + part * share_of(layers, e, a)
            if not dot_only:
                back = apply_line(turned, second)
                for b, n in enumerate(ns):
                    y_ref[base + n] = rest[b] + back[b]
        if not dot_only:
            for b in range(NODES):
                ns = [a * NODES + b for a in range(NODES)]
                back = apply_line(turned, [flux_ref[n] for n in ns])
                for a, n in enumerate(ns):
                    value = y_ref[base + n] + back[a]
                    y_ref[base + n] = value
                    energy = energy + value * r_ref[base + n]
        return (norm, energy)

    norm, energy = lax.fori_loop(0, layers, layer, (zero, zero))
    axis = len(shift.shape) - 1
    return (
        jnp.sum(norm, axis=axis, keepdims=True),
        jnp.sum(energy, axis=axis, keepdims=True),
    )


def lane_value(block, lane):
    return block[..., lane : lane + 1]


def sums_from(own, left, right, far, layers):
    total = (own[...] + far[...]) + (left[...] + right[...])
    spot = layers * NODES
    return (lane_value(total, spot), lane_value(total, spot + 1))


def scalars_block(shape, values, spot=0):
    lane = lanes_of(shape)
    out = jnp.zeros(shape, jnp.float32)
    for i, value in enumerate(values):
        out = jnp.where(lane == spot + i, value, out)
    return out


def shapes_of(field):
    return (
        jax.ShapeDtypeStruct(field.shape, jnp.float32),
        jax.ShapeDtypeStruct(field.shape[1:], jnp.float32),
        pltpu.VMEM((NODES * NODES,) + field.shape[1:], jnp.float32),
    )


def first_image(raw, before, after, shift, geo, layers, table):
    field, small, flux_scratch = shapes_of(raw)
    shape = raw.shape[1:]

    def body(g_ref, k_ref, f_ref, b_ref, a_ref, r_ref, y_ref, first_ref, last_ref, flux):
        join(f_ref, r_ref, b_ref[...], a_ref[...], layers)
        sums = helmholtz(r_ref, y_ref, flux, g_ref, k_ref[...], layers, table)
        first_ref[...], last_ref[...] = rim_messages(lambda n: y_ref[n], layers, shape, sums)

    return call(
        body,
        (),
        held(5),
        held(4),
        [field, field, small, small],
        scratch=[flux_scratch],
        flops=80 * raw.size,
        moved=12 * raw.size,
    )(geo, shift, raw, before, after)


def second_image(start, image, messages, shift, geo, layers, table):
    field, small, flux_scratch = shapes_of(start)
    shape = start.shape[1:]

    def body(g_ref, k_ref, r0, y0, own, left, right, far, *rest):
        w_ref, y_ref, first_ref, last_ref, scalar_ref, r1, flux = rest
        norm, energy = sums_from(own, left, right, far, layers)
        alpha = jnp.broadcast_to(norm / energy, shape)
        join(y0, w_ref, left[...], right[...], layers)

        def move(node):
            r1[node] = r0[node] - alpha * w_ref[node]

        each_node(layers, move)
        sums = helmholtz(r1, y_ref, flux, g_ref, k_ref[...], layers, table)
        first_ref[...], last_ref[...] = rim_messages(lambda n: y_ref[n], layers, shape, sums)
        scalar_ref[...] = scalars_block(shape, (alpha, norm, energy))

    return call(
        body,
        (),
        held(8),
        held(5),
        [field, field, small, small, small],
        scratch=[pltpu.VMEM(start.shape, jnp.float32), flux_scratch],
        flops=80 * start.size,
        moved=16 * start.size,
    )(geo, shift, start, image, *messages)


def third_energy(start, joined, image, messages, scalars, shift, geo, layers, table):
    field, small, flux_scratch = shapes_of(start)
    shape = start.shape[1:]

    def body(g_ref, k_ref, r0, w0, y1, own, left, right, far, old, *rest):
        r2, d2, sums_ref, scalar_ref, w1, flux = rest
        norm, energy = sums_from(own, left, right, far, layers)
        before = old[...]
        alpha = jnp.broadcast_to(lane_value(before, 0), shape)
        ratio = norm / lane_value(before, 1)
        curve = energy - ratio * ratio * lane_value(before, 2)
        step = jnp.broadcast_to(norm / curve, shape)
        beta = jnp.broadcast_to(ratio, shape)
        join(y1, w1, left[...], right[...], layers)

        def move(node):
            w = w0[node]
            start_value = r0[node]
            moved = start_value - alpha * w
            d2[node] = moved + beta * start_value
            r2[node] = moved - step * (w1[node] + beta * w)

        each_node(layers, move)
        sums = helmholtz(r2, None, flux, g_ref, k_ref[...], layers, table, dot_only=True)
        sums_ref[...] = scalars_block(shape, sums, layers * NODES)
        scalar_ref[...] = scalars_block(shape, (alpha, norm, curve, step))

    return call(
        body,
        (),
        held(10),
        held(4),
        [field, field, small, small],
        scratch=[pltpu.VMEM(start.shape, jnp.float32), flux_scratch],
        flops=60 * start.size,
        moved=20 * start.size,
    )(geo, shift, start, joined, image, *messages, scalars)


def finish(start, direction, residual, messages, scalars, layers, place, buffer, total):
    nodes, _, rows, lanes = start.shape
    shape = start.shape[1:]
    square = NODES * NODES

    unit = 2 * nodes

    def body(r0, d2, r2, own, left, right, far, old, *refs):
        o_ref, mid = refs[-2:]
        norm, energy = sums_from(own, left, right, far, layers)
        before = old[...]
        ratio = norm / lane_value(before, 1)
        curve = energy - ratio * ratio * lane_value(before, 2)
        step = norm / curve
        third = jnp.broadcast_to(step, shape)
        second = jnp.broadcast_to(lane_value(before, 3) + step * ratio, shape)
        first = jnp.broadcast_to(lane_value(before, 0), shape)

        def layer(e, carry):
            for n in range(square):
                node = e * square + n
                value = first * r0[node] + second * d2[node] + third * r2[node]
                for i in range(2):
                    mid[i * nodes + n * layers + e] = value[i]
            return carry

        lax.fori_loop(0, layers, layer, 0)

        def write(t, r, tile):
            o_ref[rows_at(r, unit, t), :] = tile

        turn_all(lambda k, t: mid[8 * t + k], write, unit // 8)

    extra = [] if buffer is None else [buffer]
    return call(
        body,
        (1,),
        [whole(start.shape)] * 3
        + [whole(shape)] * 5
        + [pl.BlockSpec(memory_space=pl.ANY)] * len(extra),
        pl.BlockSpec((2 * rows * nodes, lanes), lambda i: (place, 0)),
        jax.ShapeDtypeStruct((total, lanes), jnp.float32),
        scratch=[pltpu.VMEM((unit, rows, lanes), jnp.float32)],
        flops=6 * start.size,
        moved=16 * start.size,
        aliases={8: 0} if extra else None,
    )(start, direction, residual, *messages, scalars, *extra)


def halves(values, shares):
    half = values.shape[-1] // 2
    parts = [jnp.concatenate([p, p], axis=-1) for p in (values[..., :half], values[..., half:])]
    return jnp.stack(parts, axis=2).reshape(values.shape[0], shares, NODES * NODES, 2 * half)


def on_device_paired(*arrays):
    return paired_step(*arrays)


def paired_step(velocity, radial_dx, radial_dy, around_dx, around_dy, jacobian):
    table = derivative_table()
    modes = lax.axis_size("mode")
    mode = lax.axis_index("mode")
    _, local_planes, layers, _, _, lanes = velocity.shape
    planes = local_planes * modes
    pairs = local_planes // 2
    first_plane = mode * local_planes
    square = NODES * NODES
    forward, backward = (jnp.asarray(t) for t in paired_tables(planes))

    rows = velocity.transpose(0, 1, 3, 4, 2, 5).reshape(3, local_planes * square * layers, lanes)
    plain = jnp.stack([radial_dx, radial_dy, around_dx, around_dy]).reshape(
        4, layers, square, lanes
    )
    both = halves(plain, modes)
    here = lax.dynamic_index_in_dim(both, mode, 1, keepdims=False).reshape(4 * square, lanes)
    metrics = geometry(radial_dx, radial_dy, around_dx, around_dy, jacobian)
    geo = jnp.stack(metrics).reshape(4 * layers * square, lanes)
    scaled = halves((metrics[3] * (-1.0 / time_step)).reshape(1, layers, square, lanes), modes)
    flux = (both * scaled).reshape(4 * modes * square, lanes)
    small_flux = flux * time_step
    scaled = scaled.reshape(modes * square, lanes)
    pair = (first_plane // 2 + jnp.arange(pairs, dtype=jnp.int32)).astype(jnp.float32)
    wave = pair[:, None] * spanwise_wave
    low = (jnp.arange(lanes) < lanes // 2)[None, :]
    waves = jnp.where(low, wave, -wave)
    small_waves = waves * time_step
    shift = plane_shift(first_plane, local_planes, planes).reshape(pairs, 2).T
    shift = jnp.broadcast_to(shift.reshape(2, 2, pairs // 2, 1), (2, 2, pairs // 2, lanes))
    shift = (shift[:, 0], shift[:, 1])

    def exchange(blocks):
        return lax.all_to_all(blocks, "mode", split_axis=0, concat_axis=0, tiled=True)

    some = (NODES // 2 + 1) * NODES
    group = pairs // 2
    first_shape = (modes, 4 * square - 2 * some, group, lanes)
    second_shape = (modes, 2 * square, group, lanes)
    strips = list(pack_first(rows, mode, layers, pairs, lanes))
    sent_1, late_2, sent_2, sent_0 = pack_rest(rows, layers, pairs, lanes, some)
    for k in range(1, modes):
        strips[k] = lax.ppermute(strips[k], "mode", [(i, (i + k) % modes) for i in range(modes)])
    sent_1, here, geo, flux, small_flux, scaled, waves, small_waves, shift = (
        lax.optimization_barrier(
            (sent_1, here, geo, flux, small_flux, scaled, waves, small_waves, shift)
        )
    )
    arrived_1 = exchange(sent_1)
    arrived_2 = exchange(late_2)
    speed_x, slope_0 = to_points(by_source(strips, mode), forward)
    speed_y, slope_1 = to_points(arrived_1, forward)
    speeds = [speed_x, speed_y]
    partial = in_plane(speeds, speeds, here, table)
    rows_early = some // NODES
    speed_z, slope_2, blocks = turn_around(
        arrived_1, NODES, 0, rows_early, partial[0], slope_0, forward, backward, (), None
    )
    home_0 = exchange(blocks)
    speed_z, slope_2, first_buffer = turn_around(
        arrived_2,
        0,
        rows_early,
        NODES - rows_early,
        partial[0],
        slope_0,
        forward,
        backward,
        (speed_z, slope_2),
        (first_shape, NODES),
    )
    last = in_plane(speeds, [speed_z], here, table)[0]
    shapes = (first_shape, second_shape)
    blocks = to_planes(partial[1], speed_z, slope_1, backward, modes, 0, shapes, (first_buffer,))
    blocks = to_planes(last, speed_z, slope_2, backward, modes, 1, shapes, blocks)
    home_1 = exchange(blocks[0])
    home_2 = exchange(blocks[1])
    returned = (home_1, home_2)
    base = velocity_part((sent_0, sent_1, sent_2), flux, scaled, waves, table)

    own_rows = local_planes * square * layers

    def read_first(refs, g):
        def read(d, n):
            if n < some:
                return refs[0][d, n]
            a, b = divmod(n - some, NODES)
            return refs[1 + a][d, g * NODES + b]

        return read

    def read_part(refs, i):
        return lambda d, n: refs[0][d, n]

    first_specs = [pl.BlockSpec((modes, some, group, lanes), lambda i: (0, 0, i, 0))] + [
        pl.BlockSpec(
            (modes, 2 * NODES, group, lanes), functools.partial(lambda k, i: (0, k, 0, 0), NODES + k)
        )
        for k in range(NODES - rows_early)
    ]
    part_specs = [pl.BlockSpec((modes, square, group, lanes), lambda i: (0, i, 0, 0))]
    advection = unpack(
        [home_0] + [home_1] * (NODES - rows_early),
        first_specs,
        read_first,
        (0, 1),
        layers,
        None,
        3 * own_rows,
    )
    flat = first_part(base, home_0, home_1, NODES, small_flux, table)

    def solve(place, flat, own_shift, buffer):
        raw, first, last = right_side(
            flat, returned[place], small_flux, scaled, small_waves, table, layers, place
        )
        before, after = swap_rims(first, last)
        start, image, first, last = first_image(raw, before, after, own_shift, geo, layers, table)
        messages = (first,) + swap_rims(first, last) + (opposite(first),)
        joined, image, first, last, scalars = second_image(
            start, image, messages, own_shift, geo, layers, table
        )
        messages = (first,) + swap_rims(first, last) + (opposite(first),)
        residual, direction, sums, scalars = third_energy(
            start, joined, image, messages, scalars, own_shift, geo, layers, table
        )
        messages = (sums,) + swap_rims(sums, sums) + (opposite(sums),)
        return finish(
            start, direction, residual, messages, scalars, layers, place, buffer, own_rows
        )

    pressure = solve(0, flat, shift[0], None)
    advection = unpack(
        [home_1], part_specs, read_part, (2, 2), layers, advection, 3 * own_rows
    )
    flat, pressure, advection, shift = lax.optimization_barrier(
        (flat, pressure, advection, shift)
    )

    def unpack_late(comp, buffer):
        spec = pl.BlockSpec((modes, square, group, lanes), lambda i: (0, comp, 0, 0))
        return unpack(
            [home_2], [spec], read_part, (3 + 2 * comp, 1), layers, buffer, 3 * own_rows, 1
        )

    pressure = solve(1, flat, shift[1], pressure)
    advection = unpack_late(1, unpack_late(0, advection))
    advection = advection.reshape(3, local_planes, NODES, NODES, layers, lanes)
    pressure = pressure.reshape(local_planes, NODES, NODES, layers, lanes)
    return (advection.transpose(0, 1, 4, 2, 3, 5), pressure.transpose(0, 3, 1, 2, 4))


def paired_fits(mesh, shape):
    modes, ring = (mesh.shape["mode"], mesh.shape["elem"])
    _, planes, layers, _, _, columns = shape
    return (
        ring == 4
        and columns == 128 * ring
        and modes == 2 * layers
        and layers % 4 == 0
        and planes == 32 * modes
        and (layers * NODES + 2 <= 128)
    )


def solution(mesh):
    placed = (
        P(None, "mode", None, None, None, "elem"),
        P(None, None, None, "elem"),
        P(None, None, None, "elem"),
        P(None, None, None, "elem"),
        P(None, None, None, "elem"),
        P(None, None, None, "elem"),
    )


    def step(velocity, *rest):
        body = on_device_paired if paired_fits(mesh, velocity.shape) else on_device
        return jax.shard_map(
            body,
            mesh=mesh,
            in_specs=placed,
            out_specs=(
                P(None, "mode", None, None, None, "elem"),
                P("mode", None, None, None, "elem"),
            ),
            check_vma=False,
        )(velocity, *rest)

    return step
```

```python
import functools
import math

import jax
import jax.numpy as jnp
import numpy as np
from jax import lax
from jax.experimental import pallas as pl
from jax.experimental.pallas import tpu as pltpu
from jax.sharding import PartitionSpec as P

NODES = 7
ITERS = 3
GRANT = 24 * 2**20
WHOLE_GRANT = 67043328


spanwise_wave = 2.0 * math.pi / 64.0
time_step = 0.1


def padded_2(value, sides, width):
    for axis, dim in sides:
        size, length = (lax.axis_size(axis), value.shape[dim])
        up = [(i, (i + 1) % size) for i in range(size)]
        down = [(j, i) for i, j in up]
        last = lax.slice_in_dim(value, length - width, length, axis=dim)
        leading = lax.slice_in_dim(value, 0, width, axis=dim)
        before = lax.ppermute(last, axis, up)
        after = lax.ppermute(leading, axis, down)
        value = jnp.concatenate([before, value, after], axis=dim)
    return value


def lobatto_rule(count):
    degree = count - 1
    points = np.cos(np.pi * np.arange(count) / degree)
    legendre = np.zeros((count, count))
    for _ in range(60):
        legendre[:, 0] = 1.0
        legendre[:, 1] = points
        for order in range(2, count):
            legendre[:, order] = (
                (2 * order - 1) * points * legendre[:, order - 1]
                - (order - 1) * legendre[:, order - 2]
            ) / order
        points = points - (points * legendre[:, degree] - legendre[:, degree - 1]) / (
            count * legendre[:, degree]
        )
    legendre[:, 0] = 1.0
    legendre[:, 1] = points
    for order in range(2, count):
        legendre[:, order] = (
            (2 * order - 1) * points * legendre[:, order - 1] - (order - 1) * legendre[:, order - 2]
        ) / order
    weights = 2.0 / (degree * count * legendre[:, degree] ** 2)
    return (points[::-1].copy(), weights[::-1].copy())


def derivative_table():
    lobatto_nodes = lobatto_rule(NODES)[0]
    total = lobatto_nodes.shape[0]
    scales = np.ones(total)
    for column in range(total):
        for other in range(total):
            if other != column:
                scales[column] = scales[column] / (lobatto_nodes[column] - lobatto_nodes[other])
    table = np.zeros((total, total))
    for row in range(total):
        for column in range(total):
            if row != column:
                table[row, column] = (
                    scales[column] / scales[row] / (lobatto_nodes[row] - lobatto_nodes[column])
                )
        table[row, row] = -np.sum(table[row])
    return table


def radial_derivative(table, field):
    return jnp.einsum("ia,...abe->...ibe", table, field, precision=lax.Precision.HIGHEST)


def around_derivative(table, field):
    return jnp.einsum("jb,...abe->...aje", table, field, precision=lax.Precision.HIGHEST)


def radial_transpose(table, field):
    return jnp.einsum("ia,...ibe->...abe", table, field, precision=lax.Precision.HIGHEST)


def around_transpose(table, field):
    return jnp.einsum("jb,...aje->...abe", table, field, precision=lax.Precision.HIGHEST)


def z_derivative(field, first_pair):
    shape = field.shape
    count = shape[1] // 2
    pairs = field.reshape((shape[0], count, 2) + shape[2:])
    waves = (first_pair + jnp.arange(count, dtype=jnp.int32)).astype(jnp.float32) * spanwise_wave
    waves = waves.reshape((1, count) + (1,) * (len(shape) - 2))
    return jnp.stack([waves * pairs[:, :, 1], -waves * pairs[:, :, 0]], axis=2).reshape(shape)


def transform_tables(planes):
    position = jnp.arange(planes, dtype=jnp.int32)
    plane = jnp.arange(planes, dtype=jnp.int32)
    order = plane // 2
    turns = position[:, None] * order[None, :] % planes
    angle = 2.0 * math.pi / planes * turns.astype(jnp.float32)
    cosine = jnp.cos(angle)
    sine = jnp.sin(angle)
    is_sine = (plane % 2 == 1)[None, :]
    is_top = (plane == 1)[None, :]
    parity = jnp.cos(math.pi * (position % 2).astype(jnp.float32))[:, None]
    basis = jnp.where(is_top, parity, jnp.where(is_sine, sine, cosine))
    scaling = jnp.where(order == 0, 1.0, 2.0).astype(jnp.float32) / planes
    inverse = jnp.transpose(basis * scaling[None, :])
    wave = (order.astype(jnp.float32) * spanwise_wave)[None, :]
    slope = jnp.where(is_sine, wave * cosine, -wave * sine)
    return (basis, inverse, slope)


def geometry(radial_dx, radial_dy, around_dx, around_dy, jacobian):
    lobatto_weights = lobatto_rule(NODES)[1]
    quadrature = jnp.asarray(np.outer(lobatto_weights, lobatto_weights), jnp.float32)[:, :, None]
    mass = quadrature * jacobian
    radial_stiff = mass * (radial_dx * radial_dx + radial_dy * radial_dy)
    cross_stiff = mass * (radial_dx * around_dx + radial_dy * around_dy)
    around_stiff = mass * (around_dx * around_dx + around_dy * around_dy)
    return (radial_stiff, cross_stiff, around_stiff, mass)


def node_weights(layers):
    layer = jnp.arange(layers, dtype=jnp.int32).reshape(layers, 1, 1, 1)
    node = jnp.arange(NODES, dtype=jnp.int32)
    radial_node = node.reshape(1, NODES, 1, 1)
    around_node = node.reshape(1, 1, NODES, 1)
    shared_radial = (radial_node == NODES - 1) & (layer < layers - 1) | (radial_node == 0) & (
        layer > 0
    )
    shared_around = (around_node == 0) | (around_node == NODES - 1)
    multiplicity = (1.0 + shared_radial.astype(jnp.float32)) * (
        1.0 + shared_around.astype(jnp.float32)
    )
    boundary = (radial_node == NODES - 1) & (layer == layers - 1)
    mask = 1.0 - boundary.astype(jnp.float32)
    return (mask, mask / multiplicity)


def plane_shift(first_plane, count, planes):
    plane = first_plane + jnp.arange(count, dtype=jnp.int32)
    order = jnp.where(plane == 1, planes // 2, plane // 2)
    wave = order.astype(jnp.float32) * spanwise_wave
    return (wave * wave).reshape(count, 1, 1, 1, 1)


def helmholtz_local(table, field, shift, metrics):
    radial_stiff, cross_stiff, around_stiff, mass = metrics
    radial = radial_derivative(table, field)
    beside_all = around_derivative(table, field)
    return (
        radial_transpose(table, radial_stiff * radial + cross_stiff * beside_all)
        + around_transpose(table, cross_stiff * radial + around_stiff * beside_all)
        + shift * mass * field
    )


def assemble(field):
    lower = field[:, :-1, -1] + field[:, 1:, 0]
    field = field.at[:, :-1, -1].set(lower).at[:, 1:, 0].set(lower)
    first = field[:, :, :, 0]
    last = field[:, :, :, -1]
    rims = jnp.concatenate([first[..., :1], last[..., -1:]], axis=3)
    padded = padded_2(rims, (("elem", 3),), 1)
    after = jnp.concatenate([first[..., 1:], padded[..., 3:4]], axis=3)
    right = last + after
    left = jnp.concatenate([padded[..., 0:1] + first[..., :1], right[..., :-1]], axis=3)
    return field.at[:, :, :, -1].set(right).at[:, :, :, 0].set(left)


def inner(first, second, weight):
    return jnp.sum(first * second * weight, axis=(1, 2, 3, 4))


def expand(scalar):
    return scalar.reshape(-1, 1, 1, 1, 1)


def squared_norm(residual, weight):
    return lax.psum(inner(residual, residual, weight), "elem")


def on_device(velocity, radial_dx, radial_dy, around_dx, around_dy, jacobian):
    table = jnp.asarray(derivative_table(), jnp.float32)
    modes = lax.axis_size("mode")
    local_planes = velocity.shape[1]
    planes = local_planes * modes
    first_plane = lax.axis_index("mode") * local_planes
    layers = velocity.shape[2]
    columns = velocity.shape[5]
    basis, inverse, slope = transform_tables(planes)
    radial = radial_derivative(table, velocity)
    beside_all = around_derivative(table, velocity)
    along_x = radial_dx * radial + around_dx * beside_all
    along_y = radial_dy * radial + around_dy * beside_all
    fields = jnp.concatenate([velocity, along_x, along_y], axis=0)
    count = fields.shape[0]
    cells = layers * NODES * NODES * columns
    packed = fields.reshape(count, local_planes, modes, cells // modes)
    flat = lax.all_to_all(packed, "mode", split_axis=2, concat_axis=1, tiled=True)[:, :, 0, :]
    values = jnp.einsum("jp,fpc->fjc", basis, flat, precision=lax.Precision.HIGHEST)
    speed = values[0:3]
    slope_x = values[3:6]
    slope_y = values[6:9]
    slope_z = jnp.einsum("jp,fpc->fjc", slope, flat[0:3], precision=lax.Precision.HIGHEST)
    product = -(speed[0:1] * slope_x + speed[1:2] * slope_y + speed[2:3] * slope_z)
    spectral = jnp.einsum("pj,fjc->fpc", inverse, product, precision=lax.Precision.HIGHEST)
    returned = lax.all_to_all(
        spectral[:, :, None, :], "mode", split_axis=1, concat_axis=2, tiled=True
    )
    advection = returned.reshape(velocity.shape)
    metrics = geometry(radial_dx, radial_dy, around_dx, around_dy, jacobian)
    mask, weight = node_weights(layers)
    predicted = velocity + time_step * advection
    radial = radial_derivative(table, predicted[0:2])
    beside_all = around_derivative(table, predicted[0:2])
    divergence = (
        radial_dx * radial[0]
        + around_dx * beside_all[0]
        + (radial_dy * radial[1] + around_dy * beside_all[1])
        + z_derivative(predicted[2:3], first_plane // 2)[0]
    )
    shift = plane_shift(first_plane, local_planes, planes)
    right_side = mask * assemble(-(metrics[3] * divergence) / time_step)
    solution = jnp.zeros_like(right_side)
    residual = right_side
    direction = right_side
    norm_now = squared_norm(residual, weight)
    for _ in range(ITERS):
        image = mask * assemble(helmholtz_local(table, direction, shift, metrics))
        alpha = norm_now / lax.psum(inner(direction, image, weight), "elem")
        solution = solution + expand(alpha) * direction
        residual = residual - expand(alpha) * image
        norm_next = squared_norm(residual, weight)
        direction = residual + expand(norm_next / norm_now) * direction
        norm_now = norm_next
    return (advection, solution)


def split_bf16(table):
    high = table.astype(jnp.bfloat16)
    low = (table - high.astype(np.float64)).astype(jnp.bfloat16)
    return np.concatenate([high, high, low], axis=1)


def paired_tables(planes):
    position = np.arange(planes)
    plane = np.arange(planes)
    order = plane // 2
    angle = 2.0 * np.pi / planes * (position[:, None] * order[None, :] % planes)
    cosine, sine = (np.cos(angle), np.sin(angle))
    odd = (plane % 2 == 1)[None, :]
    parity = (1.0 - 2.0 * (position % 2))[:, None]
    basis = np.where((plane == 1)[None, :], parity, np.where(odd, sine, cosine))
    wave = (order * spanwise_wave)[None, :]
    slope = np.where(odd, wave * cosine, -wave * sine)
    scaling = np.where(order == 0, 1.0, 2.0) / planes
    inverse = -(basis * scaling[None, :]).T

    def columns(matrix):
        return np.concatenate([matrix[:, 0::2], matrix[:, 1::2]], axis=1)

    forward = np.concatenate([columns(basis), columns(slope)])
    backward = columns(inverse.T).T
    return (split_bf16(forward), split_bf16(backward))


def apply_line(matrix, line):
    n = NODES
    m = n // 2
    sums = [line[a] + line[n - 1 - a] for a in range(m)]
    gaps = [line[a] - line[n - 1 - a] for a in range(m)]

    def total(parts):
        out = parts[0]
        for part in parts[1:]:
            out = out + part
        return out

    out = [None] * n
    for i in range(m + 1):
        plus = total(
            [float(0.5 * (matrix[i, a] - matrix[i, n - 1 - a])) * gaps[a] for a in range(m)]
        )
        if i == m:
            out[i] = plus
            continue
        minus = total(
            [float(0.5 * (matrix[i, a] + matrix[i, n - 1 - a])) * sums[a] for a in range(m)]
            + [float(matrix[i, m]) * line[m]]
        )
        out[i] = plus + minus
        out[n - 1 - i] = plus - minus
    return out


def lanes_of(shape):
    return lax.broadcasted_iota(jnp.int32, shape, len(shape) - 1)


def row_of(ref, row, rows):
    return ref[pl.ds(row, rows, stride=0), :]


def call(body, grid, ins, outs, out_shape, scratch=(), flops=0, moved=0, aliases=None, grant=GRANT):
    return pl.pallas_call(
        body,
        grid=grid,
        in_specs=ins,
        out_specs=outs,
        out_shape=out_shape,
        scratch_shapes=list(scratch),
        input_output_aliases=aliases or {},
        compiler_params=pltpu.CompilerParams(
            dimension_semantics=("arbitrary",) * len(grid), vmem_limit_bytes=grant
        ),
        cost_estimate=pl.CostEstimate(
            flops=int(flops), bytes_accessed=int(moved), transcendentals=0
        ),
    )


def held(count):
    return [pl.BlockSpec(memory_space=pltpu.VMEM)] * count


def whole(shape):
    return pl.BlockSpec(shape, lambda *_: (0,) * len(shape))


def turn(tiles):
    tiles = list(tiles)
    sub = lax.broadcasted_iota(jnp.int32, tiles[0].shape, 0)
    size = len(tiles)
    step = size // 2
    while step:
        keep = (sub & step) == 0
        for i in range(size):
            if not i & step:
                one, two = (tiles[i], tiles[i + step])
                tiles[i] = jnp.where(keep, one, pltpu.roll(two, step, 0))
                tiles[i + step] = jnp.where(keep, pltpu.roll(one, size - step, 0), two)
        step //= 2
    return tiles


def turn_all(read, write, count):
    def some(s, carry):
        for i in range(NODES):
            t = s * NODES + i
            for r, tile in enumerate(turn([read(k, t) for k in range(8)])):
                write(t, r, tile)
        return carry

    lax.fori_loop(0, count // NODES, some, 0)


def rows_at(k, unit, t):
    return pl.ds(pl.multiple_of(k * unit + 8 * t, 8), 8)


def pack_one(x_ref, write_out, mid, layers, lanes):
    square = NODES * NODES
    per_plane = square * layers
    unit = 2 * per_plane
    half = lanes // 2
    low = lanes_of((8, lanes)) < half

    def write(t, r, tile):
        mid[8 * t + r] = tile

    turn_all(lambda k, t: x_ref[0, rows_at(k, unit, t), :], write, unit // 8)

    def layer(e, carry):
        for n in range(square):
            cos = mid[n * layers + e]
            sin = mid[per_plane + n * layers + e]
            write_out(2 * e, n, jnp.where(low, cos, pltpu.roll(sin, half, 1)))
            write_out(2 * e + 1, n, jnp.where(low, pltpu.roll(cos, half, 1), sin))
        return carry

    lax.fori_loop(0, layers, layer, 0)


def pack_specs(layers, pairs, lanes, nodes):
    return (
        pl.BlockSpec((2 * layers, nodes, 8, lanes), lambda g: (0, 0, g, 0)),
        jax.ShapeDtypeStruct((2 * layers, nodes, pairs, lanes), jnp.float32),
    )


def pack_first(rows, place, layers, pairs, lanes):
    square = NODES * NODES
    unit = 2 * square * layers
    shares = 2 * layers

    def body(place_ref, x_ref, *refs):
        outs, (mid, held_ref) = (refs[:shares], refs[shares:])
        here = place_ref[0]

        def write(d, n, value):
            held_ref[d, n] = value

        pack_one(x_ref, write, mid, layers, lanes)

        def row(a, carry):
            for k in range(shares):
                d = lax.rem(here + k, shares)
                for b in range(NODES):
                    outs[k][a * NODES + b] = held_ref[d, a * NODES + b]
            return carry

        lax.fori_loop(0, NODES, row, 0)

    return call(
        body,
        (pairs // 8,),
        [
            pl.BlockSpec(memory_space=pltpu.SMEM),
            pl.BlockSpec((1, 8 * unit, lanes), lambda g: (0, g, 0)),
        ],
        [pl.BlockSpec((square, 8, lanes), lambda g: (0, g, 0))] * shares,
        [jax.ShapeDtypeStruct((square, pairs, lanes), jnp.float32)] * shares,
        scratch=[
            pltpu.VMEM((unit, 8, lanes), jnp.float32),
            pltpu.VMEM((shares, square, 8, lanes), jnp.float32),
        ],
        grant=WHOLE_GRANT,
        moved=2 * rows.shape[1] * lanes * 4,
    )(jnp.full((1,), place, jnp.int32), rows)


def pack_rest(rows, layers, pairs, lanes, early):
    square = NODES * NODES
    unit = 2 * square * layers

    def body(u_ref, x_ref, y_ref, o_ref, late_ref, whole_ref, zero_ref, mid):
        def zeroth(d, n, value):
            zero_ref[d, n] = value

        def first(d, n, value):
            o_ref[d, n] = value

        def second(d, n, value):
            whole_ref[d, n] = value
            if n < early:
                o_ref[d, square + n] = value
            else:
                late_ref[d, n - early] = value

        pack_one(x_ref, first, mid, layers, lanes)
        pack_one(y_ref, second, mid, layers, lanes)
        pack_one(u_ref, zeroth, mid, layers, lanes)

    parts = [
        pack_specs(layers, pairs, lanes, nodes)
        for nodes in (square + early, square - early, square, square)
    ]
    return call(
        body,
        (pairs // 8,),
        [
            pl.BlockSpec((1, 8 * unit, lanes), lambda g: (0, g, 0)),
            pl.BlockSpec((1, 8 * unit, lanes), lambda g: (1, g, 0)),
            pl.BlockSpec((1, 8 * unit, lanes), lambda g: (2, g, 0)),
        ],
        [part[0] for part in parts],
        [part[1] for part in parts],
        scratch=[pltpu.VMEM((unit, 8, lanes), jnp.float32)],
        grant=WHOLE_GRANT,
        moved=5 * rows.shape[1] * lanes * 4,
    )(rows, rows, rows)


def unpack(arrays, specs, read_from, slots, layers, buffer, total, steps=2):
    lanes = arrays[0].shape[-1]
    square = NODES * NODES
    per_plane = square * layers
    unit = 2 * per_plane
    half = lanes // 2

    def body(*refs):
        o_ref, mid = refs[-2:]
        low = lanes_of((8, lanes)) < half
        read = read_from(refs, pl.program_id(0))

        def layer(e, carry):
            for n in range(square):
                left, right = (read(2 * e, n), read(2 * e + 1, n))
                mid[n * layers + e] = jnp.where(low, left, pltpu.roll(right, half, 1))
                mid[per_plane + n * layers + e] = jnp.where(low, pltpu.roll(left, half, 1), right)
            return carry

        lax.fori_loop(0, layers, layer, 0)

        def write(t, r, tile):
            o_ref[rows_at(r, unit, t), :] = tile

        turn_all(lambda k, t: mid[8 * t + k], write, unit // 8)

    extra = [] if buffer is None else [buffer]
    return call(
        body,
        (steps,),
        list(specs) + [pl.BlockSpec(memory_space=pl.ANY)] * len(extra),
        pl.BlockSpec((8 * unit, lanes), lambda i: (slots[0] + i * slots[1], 0)),
        jax.ShapeDtypeStruct((total, lanes), jnp.float32),
        scratch=[pltpu.VMEM((unit, 8, lanes), jnp.float32)],
        moved=4 * 8 * unit * lanes * 4,
        aliases={len(arrays): 0} if extra else None,
    )(*arrays, *extra)


def paired_nodes():
    return [(b, min(b + 1, NODES - 1)) for b in range(0, NODES, 2)]


def three_pass(table, rhs_ref, tiles):
    rows, lanes = tiles[0].shape
    half = lanes // 2
    low = lanes_of((rows, lanes)) < half
    depth = 2 * rows
    for place, (one, two) in enumerate(paired_nodes()):
        first, second = (tiles[one], tiles[two])
        cut = pl.ds(place * lanes, lanes)
        for part in range(2):
            if part == 0:
                value = jnp.where(low, first, pltpu.roll(second, half, 1))
            else:
                value = jnp.where(low, pltpu.roll(first, half, 1), second)
            high = value.astype(jnp.bfloat16)
            rest = (value - high.astype(jnp.float32)).astype(jnp.bfloat16)
            rhs_ref[pl.ds(part * rows, rows), cut] = high
            rhs_ref[pl.ds(depth + part * rows, rows), cut] = rest
            rhs_ref[pl.ds(2 * depth + part * rows, rows), cut] = high
    out = jnp.dot(table, rhs_ref[...], preferred_element_type=jnp.float32)
    fields = []
    for field in range(table.shape[0] // depth):
        nodes = [None] * NODES
        for place, (one, two) in enumerate(paired_nodes()):
            cut = slice(place * lanes, (place + 1) * lanes)
            top = out[field * depth : field * depth + rows, cut]
            bottom = out[field * depth + rows : (field + 1) * depth, cut]
            nodes[one] = jnp.where(low, top, pltpu.roll(bottom, half, 1))
            if two != one:
                nodes[two] = jnp.where(low, pltpu.roll(top, half, 1), bottom)
        fields.append(nodes)
    return fields


def rhs_scratch(table, lanes):
    return pltpu.VMEM((table.shape[1], len(paired_nodes()) * lanes), jnp.bfloat16)


def read_tiles(x_ref, rows, lanes):
    return [x_ref[:, b].reshape(rows, lanes) for b in range(NODES)]


def to_points(blocks, table):
    shares, _, pairs, lanes = blocks.shape
    square = NODES * NODES
    rows = shares * pairs

    def body(t_ref, x_ref, v_ref, z_ref, rhs_ref):
        fields = three_pass(t_ref[...], rhs_ref, read_tiles(x_ref, rows, lanes))
        for b in range(NODES):
            v_ref[b] = fields[0][b]
            z_ref[b] = fields[1][b]

    spec = pl.BlockSpec((NODES, rows, lanes), lambda a: (a, 0, 0))
    shape = jax.ShapeDtypeStruct((square, rows, lanes), jnp.float32)
    return call(
        body,
        (NODES,),
        [
            whole(table.shape),
            pl.BlockSpec((shares, NODES, pairs, lanes), lambda a: (0, a, 0, 0)),
        ],
        [spec, spec],
        [shape, shape],
        scratch=[rhs_scratch(table, lanes)],
        flops=2 * table.shape[0] * table.shape[1] * square * lanes,
        grant=WHOLE_GRANT,
        moved=3 * square * rows * lanes * 4,
    )(table, blocks)


def turn_around(blocks, skip, start, count, partial, slope_z, table, back, fields, out):
    shares, _, pairs, lanes = blocks.shape
    rows = shares * pairs
    square = NODES * NODES
    group = pairs // 2
    shape = jax.ShapeDtypeStruct((square, rows, lanes), jnp.float32)

    def body(t_ref, i_ref, x_ref, g_ref, s_ref, *refs):
        w_ref, z_ref = refs[len(fields) : len(fields) + 2]
        outs, rhs_ref = (refs[len(fields) + 2 : -1], refs[-1])
        points = three_pass(t_ref[...], rhs_ref, read_tiles(x_ref, rows, lanes))
        for b in range(NODES):
            w_ref[b] = points[0][b]
            z_ref[b] = points[1][b]
        tiles = [g_ref[b] + w_ref[b] * s_ref[b] for b in range(NODES)]
        spectral = three_pass(i_ref[...], rhs_ref, tiles)[0]
        for b in range(NODES):
            value = spectral[b].reshape(shares, pairs, lanes)
            if out is None:
                outs[0][:, b] = value
            else:
                for k in range(shares):
                    for g in range(2):
                        outs[k][g * NODES + b] = value[k, g * group : (g + 1) * group]

    spec = pl.BlockSpec((NODES, rows, lanes), lambda a: (start + a, 0, 0))
    if out is None:
        out_spec = [pl.BlockSpec((shares, NODES, pairs, lanes), lambda a: (0, a, 0, 0))]
        out_shape = [jax.ShapeDtypeStruct((shares, count * NODES, pairs, lanes), jnp.float32)]
    else:
        first = out[1]
        out_spec = [pl.BlockSpec((2 * NODES, group, lanes), lambda a: (first + a, 0, 0))] * shares
        out_shape = [jax.ShapeDtypeStruct(out[0], jnp.float32)] * shares
    return call(
        body,
        (count,),
        [
            whole(table.shape),
            whole(back.shape),
            pl.BlockSpec((shares, NODES, pairs, lanes), lambda a: (0, skip + a, 0, 0)),
            spec,
            spec,
        ]
        + [pl.BlockSpec(memory_space=pl.ANY)] * len(fields),
        [spec, spec] + out_spec,
        [shape, shape] + out_shape,
        scratch=[rhs_scratch(table, lanes)],
        flops=3 * table.shape[0] * table.shape[1] * count * NODES * lanes,
        aliases={5: 0, 6: 1} if fields else None,
        grant=WHOLE_GRANT,
        moved=6 * count * NODES * rows * lanes * 4,
    )(table, back, blocks, partial, slope_z, *fields)


def in_plane(speeds, fields, metrics, table):
    square, rows, lanes = speeds[0].shape
    count = len(fields)
    step = 32
    own = [i for i, f in enumerate(fields) if all(f is not s for s in speeds)]
    arrays = list(speeds) + [fields[i] for i in own]

    def body(m_ref, *refs):
        ins, outs = (refs[: len(arrays)], refs[len(arrays) :])
        u_ref, v_ref = ins[:2]
        sources = []
        extra = 2
        for i, f in enumerate(fields):
            if i in own:
                sources.append(ins[extra])
                extra += 1
            else:
                sources.append(u_ref if f is speeds[0] else v_ref)

        def block(s, carry):
            r = pl.ds(s * 8, 8)

            def metric(kind, n):
                return row_of(m_ref, kind * square + n, 8)

            for a in range(NODES):
                ns = [a * NODES + b for b in range(NODES)]
                drift = [
                    u_ref[n, r] * metric(2, n) + v_ref[n, r] * metric(3, n) for n in ns
                ]
                for f in range(count):
                    beside = apply_line(table, [sources[f][n, r] for n in ns])
                    for b, n in enumerate(ns):
                        outs[f][n, r] = drift[b] * beside[b]
            for b in range(NODES):
                ns = [a * NODES + b for a in range(NODES)]
                drift = [
                    u_ref[n, r] * metric(0, n) + v_ref[n, r] * metric(1, n) for n in ns
                ]
                for f in range(count):
                    radial = apply_line(table, [sources[f][n, r] for n in ns])
                    for a, n in enumerate(ns):
                        outs[f][n, r] = outs[f][n, r] + drift[a] * radial[a]
            return carry

        lax.fori_loop(0, step // 8, block, 0)

    spec = pl.BlockSpec((square, step, lanes), lambda i: (0, i, 0))
    shape = jax.ShapeDtypeStruct((square, rows, lanes), jnp.float32)
    return call(
        body,
        (rows // step,),
        [whole(metrics.shape)] + [spec] * len(arrays),
        [spec] * count,
        [shape] * count,
        flops=30 * count * square * rows * lanes,
        grant=WHOLE_GRANT,
        moved=(len(arrays) + count) * square * rows * lanes * 4,
    )(metrics, *arrays)


def by_source(strips, place):
    count = len(strips)
    nodes, rows, lanes = strips[0].shape
    step = 2 * NODES if nodes % (2 * NODES) == 0 else NODES

    def body(place_ref, *refs):
        o_ref = refs[-1]
        here = place_ref[0]
        for k in range(count):
            source = lax.rem(here - k + count, count)
            for n in range(step):
                o_ref[source, n] = refs[k][n]

    return call(
        body,
        (nodes // step,),
        [pl.BlockSpec(memory_space=pltpu.SMEM)]
        + [pl.BlockSpec((step, rows, lanes), lambda i: (i, 0, 0))] * count,
        pl.BlockSpec((count, step, rows, lanes), lambda i: (0, i, 0, 0)),
        jax.ShapeDtypeStruct((count,) + strips[0].shape, jnp.float32),
        grant=WHOLE_GRANT,
        moved=8 * count * strips[0].size,
    )(jnp.full((1,), place, jnp.int32), *strips)


def to_planes(partial, speed_z, slope_z, table, place, comp, shapes, buffers):
    square, rows, lanes = partial.shape
    shares = shapes[1][0]
    pairs = rows // shares
    group = pairs // 2

    def body(place_ref, t_ref, g_ref, w_ref, z_ref, *refs):
        strips, o_ref, rhs_ref = (refs[-shares - 2 : -2], refs[-2], refs[-1])
        here = place_ref[0]
        tiles = [g_ref[b] + w_ref[b] * z_ref[b] for b in range(NODES)]
        nodes = three_pass(t_ref[...], rhs_ref, tiles)[0]
        for b in range(NODES):
            out = nodes[b].reshape(shares, pairs, lanes)
            for k in range(shares):
                strips[k][b] = out[k, :group]
                o_ref[lax.rem(here + k, shares), b] = out[k, group:]

    spec = pl.BlockSpec((NODES, rows, lanes), lambda a: (a, 0, 0))
    return call(
        body,
        (NODES,),
        [pl.BlockSpec(memory_space=pltpu.SMEM), whole(table.shape), spec, spec, spec]
        + [pl.BlockSpec(memory_space=pl.ANY)] * len(buffers),
        [pl.BlockSpec((NODES, group, lanes), lambda a: (comp * NODES + a, 0, 0))] * shares
        + [pl.BlockSpec((shares, NODES, group, lanes), lambda a: (0, comp * NODES + a, 0, 0))],
        [jax.ShapeDtypeStruct(shapes[0], jnp.float32)] * shares
        + [jax.ShapeDtypeStruct(shapes[1], jnp.float32)],
        scratch=[rhs_scratch(table, lanes)],
        flops=2 * table.shape[0] * table.shape[1] * square * lanes,
        aliases={5 + k: k for k in range(len(buffers))},
        grant=WHOLE_GRANT,
        moved=4 * square * rows * lanes * 4,
    )(jnp.full((1,), place, jnp.int32), table, partial, speed_z, slope_z, *buffers)


def velocity_part(sent, metrics, weights, waves, table):
    shares, square, pairs, lanes = sent[0].shape
    half = lanes // 2

    def body(m_ref, q_ref, k_ref, s0, s1, s2, o_ref):
        d = pl.program_id(0)

        def rows_of(s):
            r = pl.ds(s * 8, 8)
            wave = k_ref[r]

            def metric(kind, n):
                return row_of(m_ref, (kind * shares + d) * square + n, 8)

            for a in range(NODES):
                ns = [a * NODES + b for b in range(NODES)]
                first = apply_line(table, [s0[0, n, r] for n in ns])
                second = apply_line(table, [s1[0, n, r] for n in ns])
                for b, n in enumerate(ns):
                    along = pltpu.roll(s2[0, n, r], half, 1) * wave
                    o_ref[0, n, r] = (
                        metric(2, n) * first[b]
                        + metric(3, n) * second[b]
                        + row_of(q_ref, d * square + n, 8) * along
                    )
            for b in range(NODES):
                ns = [a * NODES + b for a in range(NODES)]
                first = apply_line(table, [s0[0, n, r] for n in ns])
                second = apply_line(table, [s1[0, n, r] for n in ns])
                for a, n in enumerate(ns):
                    o_ref[0, n, r] = o_ref[0, n, r] + (
                        metric(0, n) * first[a] + metric(1, n) * second[a]
                    )

        lax.fori_loop(0, pairs // 8, lambda s, carry: (rows_of(s), carry)[1], 0)

    spec = pl.BlockSpec((1, square, pairs, lanes), lambda d: (d, 0, 0, 0))
    return call(
        body,
        (shares,),
        [whole(metrics.shape), whole(weights.shape), whole(waves.shape)] + [spec] * 3,
        spec,
        jax.ShapeDtypeStruct(sent[0].shape, jnp.float32),
        flops=60 * shares * square * pairs * lanes,
        grant=WHOLE_GRANT,
        moved=4 * shares * square * pairs * lanes * 4,
    )(metrics, weights, waves, *sent)


def first_part(base, early, rest, rest_at, metrics, table):
    shares, square, pairs, lanes = base.shape

    some = early.shape[1]
    count = (square - some) // NODES
    group = pairs // 2

    def body(m_ref, s0, r0, *refs):
        others, (o_ref, p0) = (refs[:count], refs[count:])
        d = pl.program_id(0)

        def block(s, carry):
            r = pl.ds(s * 8, 8)
            for n in range(square):
                if n < some:
                    home = r0[0, n, r]
                else:
                    a, b = divmod(n - some, NODES)
                    home = others[a][0, s * NODES + b]
                p0[n] = home

            def metric(kind, n):
                return row_of(m_ref, (kind * shares + d) * square + n, 8)

            for a in range(NODES):
                ns = [a * NODES + b for b in range(NODES)]
                line = apply_line(table, [p0[n] for n in ns])
                for b, n in enumerate(ns):
                    o_ref[0, n, r] = s0[0, n, r] + metric(2, n) * line[b]
            for b in range(NODES):
                ns = [a * NODES + b for a in range(NODES)]
                line = apply_line(table, [p0[n] for n in ns])
                for a, n in enumerate(ns):
                    o_ref[0, n, r] = o_ref[0, n, r] + metric(0, n) * line[a]
            return carry

        lax.fori_loop(0, pairs // 8, block, 0)

    spec = pl.BlockSpec((1, square, pairs, lanes), lambda d: (d, 0, 0, 0))
    return call(
        body,
        (shares,),
        [whole(metrics.shape), spec, pl.BlockSpec((1, some, pairs, lanes), lambda d: (d, 0, 0, 0))]
        + [
            pl.BlockSpec(
                (1, 2 * NODES, group, lanes), functools.partial(lambda i, d: (d, i, 0, 0), rest_at + k)
            )
            for k in range(count)
        ],
        spec,
        jax.ShapeDtypeStruct(base.shape, jnp.float32),
        scratch=[pltpu.VMEM((square, 8, lanes), jnp.float32)],
        flops=30 * shares * square * pairs * lanes,
        grant=WHOLE_GRANT,
        moved=3 * shares * square * pairs * lanes * 4,
    )(metrics, base, early, *[rest] * count)


def join_layers(y_ref, layers):
    square = NODES * NODES
    last = (NODES - 1) * NODES
    for e in range(layers - 1):
        for b in range(NODES):
            upper, lower = (e * square + last + b, (e + 1) * square + b)
            total = y_ref[upper] + y_ref[lower]
            y_ref[upper] = total
            y_ref[lower] = total
    for b in range(NODES):
        node = (layers - 1) * square + last + b
        y_ref[node] = jnp.zeros_like(y_ref[node])


def rim_messages(read, layers, shape, partials):
    lane = lanes_of(shape)
    lanes = shape[-1]
    axis = len(shape) - 1
    first = jnp.zeros(shape, jnp.float32)
    last = jnp.zeros(shape, jnp.float32)
    square = NODES * NODES
    for e in range(layers):
        for a in range(NODES):
            spot = e * NODES + a
            here = lane == spot
            node = e * square + a * NODES
            first = jnp.where(here, pltpu.roll(read(node), spot, axis), first)
            last = jnp.where(
                here, pltpu.roll(read(node + NODES - 1), (spot + 1) % lanes, axis), last
            )
    for i, partial in enumerate(partials):
        here = lane == layers * NODES + i
        first = jnp.where(here, partial, first)
        last = jnp.where(here, partial, last)
    return (first, last)


def right_side(flat, returned, metrics, weights, waves, table, layers, place):
    shares, square, _, lanes = flat.shape
    half = lanes // 2

    def body(m_ref, q_ref, k_ref, f_ref, r1, r2, o_ref, first_ref, last_ref, c0, c1):
        e = pl.program_id(0)
        lane = lanes_of((8, lanes))
        low = lane < half
        wave = k_ref[...]
        sides = (c0, c1)

        @pl.when(e == 0)
        def _():
            first_ref[...] = jnp.zeros_like(first_ref)
            last_ref[...] = jnp.zeros_like(last_ref)

        for h in range(2):
            d = 2 * e + h
            side = sides[h]
            for n in range(square):
                along = pltpu.roll(r2[h, n], half, 1) * wave
                side[n] = f_ref[h, n] + row_of(q_ref, d * square + n, 8) * along

            def metric(kind, n):
                return row_of(m_ref, (kind * shares + d) * square + n, 8)

            for a in range(NODES):
                ns = [a * NODES + b for b in range(NODES)]
                line = apply_line(table, [r1[h, n] for n in ns])
                for b, n in enumerate(ns):
                    side[n] = side[n] + metric(3, n) * line[b]
            for b in range(NODES):
                ns = [a * NODES + b for a in range(NODES)]
                line = apply_line(table, [r1[h, n] for n in ns])
                for a, n in enumerate(ns):
                    side[n] = side[n] + metric(1, n) * line[a]
        rims = [[first_ref[0], last_ref[0]], [first_ref[1], last_ref[1]]]
        for n in range(square):
            left, right = (c0[n], c1[n])
            parts = (
                jnp.where(low, left, pltpu.roll(right, half, 1)),
                jnp.where(low, pltpu.roll(left, half, 1), right),
            )
            for i in range(2):
                o_ref[n, i] = parts[i]
                a, b = divmod(n, NODES)
                spot = e * NODES + a
                if b == 0:
                    rims[i][0] = jnp.where(lane == spot, pltpu.roll(parts[i], spot, 1), rims[i][0])
                if b == NODES - 1:
                    rims[i][1] = jnp.where(
                        lane == spot, pltpu.roll(parts[i], spot + 1, 1), rims[i][1]
                    )
        for i in range(2):
            first_ref[i] = rims[i][0]
            last_ref[i] = rims[i][1]

    spec = pl.BlockSpec((2, square, 8, lanes), lambda e: (e, 0, place, 0))
    nodes = layers * square
    rim_shape = jax.ShapeDtypeStruct((2, 8, lanes), jnp.float32)
    scratch = pltpu.VMEM((square, 8, lanes), jnp.float32)
    return call(
        body,
        (layers,),
        [
            whole(metrics.shape),
            whole(weights.shape),
            pl.BlockSpec((8, lanes), lambda e: (place, 0)),
            spec,
            pl.BlockSpec((2, square, 8, lanes), lambda e: (e, 0, 0, 0)),
            pl.BlockSpec((2, square, 8, lanes), lambda e: (e, 1, 0, 0)),
        ],
        [
            pl.BlockSpec((square, 2, 8, lanes), lambda e: (e, 0, 0, 0)),
            whole((2, 8, lanes)),
            whole((2, 8, lanes)),
        ],
        [jax.ShapeDtypeStruct((nodes, 2, 8, lanes), jnp.float32), rim_shape, rim_shape],
        scratch=[scratch] * 2,
        flops=40 * shares * square * 8 * lanes,
        moved=4 * shares * square * 8 * lanes * 4,
    )(metrics, weights, waves, flat, returned, returned)


def swap_rims(first, last):
    size = lax.axis_size("elem")
    up = [(i, (i + 1) % size) for i in range(size)]
    down = [(j, i) for i, j in up]
    return (lax.ppermute(last, "elem", up), lax.ppermute(first, "elem", down))


def opposite(first):
    size = lax.axis_size("elem")
    return lax.ppermute(first, "elem", [(i, (i + 2) % size) for i in range(size)])


def join_columns(read, ref, before, after, layers):
    lanes = before.shape[-1]
    axis = len(before.shape) - 1
    lane = lanes_of(before.shape)
    square = NODES * NODES
    for e in range(layers):
        for a in range(NODES):
            spot = e * NODES + a
            node = e * square + a * NODES
            first, last = (read(node), read(node + NODES - 1))
            beyond = pltpu.roll(after, lanes - 1 - spot, axis)
            ahead = jnp.where(lane == lanes - 1, beyond, pltpu.roll(first, lanes - 1, axis))
            right = last + ahead
            mine = first + (pltpu.roll(before, lanes - spot, axis) if spot else before)
            ref[node + NODES - 1] = right
            ref[node] = jnp.where(lane == 0, mine, pltpu.roll(right, 1, axis))


def join(source, ref, before, after, layers):
    square = NODES * NODES

    def copy(e, carry):
        for n in range(square):
            if 0 < n % NODES < NODES - 1:
                ref[e * square + n] = source[e * square + n]
        return carry

    lax.fori_loop(0, layers, copy, 0)
    join_columns(lambda n: source[n], ref, before, after, layers)
    join_layers(ref, layers)


def each_node(layers, step):
    def layer(e, carry):
        for n in range(NODES * NODES):
            step(e * NODES * NODES + n)
        return carry

    lax.fori_loop(0, layers, layer, 0)


def share_of(layers, e, a):
    if a == 0:
        return jnp.where(e > 0, 0.5, 1.0)
    if a == NODES - 1:
        return jnp.where(e < layers - 1, 0.5, 0.0)
    return 1.0


def helmholtz(r_ref, y_ref, flux_ref, g_ref, shift, layers, table, dot_only=False):
    square = NODES * NODES
    nodes = layers * square
    turned = table.T
    zero = jnp.zeros(shift.shape, jnp.float32)

    def layer(e, carry):
        norm, energy = carry
        base = e * square

        def metric(kind, n):
            return row_of(g_ref, kind * nodes + base + n, 8)

        for b in range(NODES):
            ns = [a * NODES + b for a in range(NODES)]
            radial = apply_line(table, [r_ref[base + n] for n in ns])
            for a, n in enumerate(ns):
                flux_ref[n] = radial[a]
        for a in range(NODES):
            ns = [a * NODES + b for b in range(NODES)]
            line = [r_ref[base + n] for n in ns]
            beside = apply_line(table, line)
            second = []
            rest = []
            part = zero
            for b, n in enumerate(ns):
                radial = flux_ref[n]
                cross = metric(1, n)
                one = metric(0, n) * radial + cross * beside[b]
                two = cross * radial + metric(2, n) * beside[b]
                same = shift * metric(3, n) * line[b]
                whole_weight = line[b] * line[b]
                part = part + (0.5 * whole_weight if b in (0, NODES - 1) else whole_weight)
                if dot_only:
                    energy = energy + (radial * one + beside[b] * two + same * line[b])
                else:
                    flux_ref[n] = one
                    second.append(two)
                    rest.append(same)
            norm = norm + part * share_of(layers, e, a)
            if not dot_only:
                back = apply_line(turned, second)
                for b, n in enumerate(ns):
                    y_ref[base + n] = rest[b] + back[b]
        if not dot_only:
            for b in range(NODES):
                ns = [a * NODES + b for a in range(NODES)]
                back = apply_line(turned, [flux_ref[n] for n in ns])
                for a, n in enumerate(ns):
                    value = y_ref[base + n] + back[a]
                    y_ref[base + n] = value
                    energy = energy + value * r_ref[base + n]
        return (norm, energy)

    norm, energy = lax.fori_loop(0, layers, layer, (zero, zero))
    axis = len(shift.shape) - 1
    return (
        jnp.sum(norm, axis=axis, keepdims=True),
        jnp.sum(energy, axis=axis, keepdims=True),
    )


def lane_value(block, lane):
    return block[..., lane : lane + 1]


def sums_from(own, left, right, far, layers):
    total = (own[...] + far[...]) + (left[...] + right[...])
    spot = layers * NODES
    return (lane_value(total, spot), lane_value(total, spot + 1))


def scalars_block(shape, values, spot=0):
    lane = lanes_of(shape)
    out = jnp.zeros(shape, jnp.float32)
    for i, value in enumerate(values):
        out = jnp.where(lane == spot + i, value, out)
    return out


def shapes_of(field):
    return (
        jax.ShapeDtypeStruct(field.shape, jnp.float32),
        jax.ShapeDtypeStruct(field.shape[1:], jnp.float32),
        pltpu.VMEM((NODES * NODES,) + field.shape[1:], jnp.float32),
    )


def first_image(raw, before, after, shift, geo, layers, table):
    field, small, flux_scratch = shapes_of(raw)
    shape = raw.shape[1:]

    def body(g_ref, k_ref, f_ref, b_ref, a_ref, r_ref, y_ref, first_ref, last_ref, flux):
        join(f_ref, r_ref, b_ref[...], a_ref[...], layers)
        sums = helmholtz(r_ref, y_ref, flux, g_ref, k_ref[...], layers, table)
        first_ref[...], last_ref[...] = rim_messages(lambda n: y_ref[n], layers, shape, sums)

    return call(
        body,
        (),
        held(5),
        held(4),
        [field, field, small, small],
        scratch=[flux_scratch],
        flops=80 * raw.size,
        moved=12 * raw.size,
    )(geo, shift, raw, before, after)


def second_image(start, image, messages, shift, geo, layers, table):
    field, small, flux_scratch = shapes_of(start)
    shape = start.shape[1:]

    def body(g_ref, k_ref, r0, y0, own, left, right, far, *rest):
        w_ref, y_ref, first_ref, last_ref, scalar_ref, r1, flux = rest
        norm, energy = sums_from(own, left, right, far, layers)
        alpha = jnp.broadcast_to(norm / energy, shape)
        join(y0, w_ref, left[...], right[...], layers)

        def move(node):
            r1[node] = r0[node] - alpha * w_ref[node]

        each_node(layers, move)
        sums = helmholtz(r1, y_ref, flux, g_ref, k_ref[...], layers, table)
        first_ref[...], last_ref[...] = rim_messages(lambda n: y_ref[n], layers, shape, sums)
        scalar_ref[...] = scalars_block(shape, (alpha, norm, energy))

    return call(
        body,
        (),
        held(8),
        held(5),
        [field, field, small, small, small],
        scratch=[pltpu.VMEM(start.shape, jnp.float32), flux_scratch],
        flops=80 * start.size,
        moved=16 * start.size,
    )(geo, shift, start, image, *messages)


def third_energy(start, joined, image, messages, scalars, shift, geo, layers, table):
    field, small, flux_scratch = shapes_of(start)
    shape = start.shape[1:]

    def body(g_ref, k_ref, r0, w0, y1, own, left, right, far, old, *rest):
        r2, d2, sums_ref, scalar_ref, w1, flux = rest
        norm, energy = sums_from(own, left, right, far, layers)
        before = old[...]
        alpha = jnp.broadcast_to(lane_value(before, 0), shape)
        ratio = norm / lane_value(before, 1)
        curve = energy - ratio * ratio * lane_value(before, 2)
        step = jnp.broadcast_to(norm / curve, shape)
        beta = jnp.broadcast_to(ratio, shape)
        join(y1, w1, left[...], right[...], layers)

        def move(node):
            w = w0[node]
            start_value = r0[node]
            moved = start_value - alpha * w
            d2[node] = moved + beta * start_value
            r2[node] = moved - step * (w1[node] + beta * w)

        each_node(layers, move)
        sums = helmholtz(r2, None, flux, g_ref, k_ref[...], layers, table, dot_only=True)
        sums_ref[...] = scalars_block(shape, sums, layers * NODES)
        scalar_ref[...] = scalars_block(shape, (alpha, norm, curve, step))

    return call(
        body,
        (),
        held(10),
        held(4),
        [field, field, small, small],
        scratch=[pltpu.VMEM(start.shape, jnp.float32), flux_scratch],
        flops=60 * start.size,
        moved=20 * start.size,
    )(geo, shift, start, joined, image, *messages, scalars)


def finish(start, direction, residual, messages, scalars, layers, place, buffer, total):
    nodes, _, rows, lanes = start.shape
    shape = start.shape[1:]
    square = NODES * NODES

    unit = 2 * nodes

    def body(r0, d2, r2, own, left, right, far, old, *refs):
        o_ref, mid = refs[-2:]
        norm, energy = sums_from(own, left, right, far, layers)
        before = old[...]
        ratio = norm / lane_value(before, 1)
        curve = energy - ratio * ratio * lane_value(before, 2)
        step = norm / curve
        third = jnp.broadcast_to(step, shape)
        second = jnp.broadcast_to(lane_value(before, 3) + step * ratio, shape)
        first = jnp.broadcast_to(lane_value(before, 0), shape)

        def layer(e, carry):
            for n in range(square):
                node = e * square + n
                value = first * r0[node] + second * d2[node] + third * r2[node]
                for i in range(2):
                    mid[i * nodes + n * layers + e] = value[i]
            return carry

        lax.fori_loop(0, layers, layer, 0)

        def write(t, r, tile):
            o_ref[rows_at(r, unit, t), :] = tile

        turn_all(lambda k, t: mid[8 * t + k], write, unit // 8)

    extra = [] if buffer is None else [buffer]
    return call(
        body,
        (1,),
        [whole(start.shape)] * 3
        + [whole(shape)] * 5
        + [pl.BlockSpec(memory_space=pl.ANY)] * len(extra),
        pl.BlockSpec((2 * rows * nodes, lanes), lambda i: (place, 0)),
        jax.ShapeDtypeStruct((total, lanes), jnp.float32),
        scratch=[pltpu.VMEM((unit, rows, lanes), jnp.float32)],
        flops=6 * start.size,
        moved=16 * start.size,
        aliases={8: 0} if extra else None,
    )(start, direction, residual, *messages, scalars, *extra)


def halves(values, shares):
    half = values.shape[-1] // 2
    parts = [jnp.concatenate([p, p], axis=-1) for p in (values[..., :half], values[..., half:])]
    return jnp.stack(parts, axis=2).reshape(values.shape[0], shares, NODES * NODES, 2 * half)


def on_device_paired(*arrays):
    return paired_step(*arrays)


def paired_step(velocity, radial_dx, radial_dy, around_dx, around_dy, jacobian):
    table = derivative_table()
    modes = lax.axis_size("mode")
    mode = lax.axis_index("mode")
    _, local_planes, layers, _, _, lanes = velocity.shape
    planes = local_planes * modes
    pairs = local_planes // 2
    first_plane = mode * local_planes
    square = NODES * NODES
    forward, backward = (jnp.asarray(t) for t in paired_tables(planes))

    rows = velocity.transpose(0, 1, 3, 4, 2, 5).reshape(3, local_planes * square * layers, lanes)
    plain = jnp.stack([radial_dx, radial_dy, around_dx, around_dy]).reshape(
        4, layers, square, lanes
    )
    both = halves(plain, modes)
    here = lax.dynamic_index_in_dim(both, mode, 1, keepdims=False).reshape(4 * square, lanes)
    metrics = geometry(radial_dx, radial_dy, around_dx, around_dy, jacobian)
    geo = jnp.stack(metrics).reshape(4 * layers * square, lanes)
    scaled = halves((metrics[3] * (-1.0 / time_step)).reshape(1, layers, square, lanes), modes)
    flux = (both * scaled).reshape(4 * modes * square, lanes)
    small_flux = flux * time_step
    scaled = scaled.reshape(modes * square, lanes)
    turned = lax.optimization_barrier(backward).reshape(2, modes, pairs, -1)
    turned = jnp.roll(turned, -mode, axis=1).reshape(backward.shape)
    pair = (first_plane // 2 + jnp.arange(pairs, dtype=jnp.int32)).astype(jnp.float32)
    wave = pair[:, None] * spanwise_wave
    low = (jnp.arange(lanes) < lanes // 2)[None, :]
    waves = jnp.where(low, wave, -wave)
    small_waves = waves * time_step
    shift = plane_shift(first_plane, local_planes, planes).reshape(pairs, 2).T
    shift = jnp.broadcast_to(shift.reshape(2, 2, pairs // 2, 1), (2, 2, pairs // 2, lanes))
    shift = (shift[:, 0], shift[:, 1])

    def exchange(blocks):
        return lax.all_to_all(blocks, "mode", split_axis=0, concat_axis=0, tiled=True)

    some = (NODES // 2 + 1) * NODES
    group = pairs // 2
    first_shape = (4 * square - 2 * some, group, lanes)
    second_shape = (modes, 2 * square, group, lanes)
    strips = list(pack_first(rows, mode, layers, pairs, lanes))
    sent_1, late_2, sent_2, sent_0 = pack_rest(rows, layers, pairs, lanes, some)
    for k in range(1, modes):
        strips[k] = lax.ppermute(strips[k], "mode", [(i, (i + k) % modes) for i in range(modes)])
    sent_1, here, geo, flux, small_flux, scaled, waves, small_waves, shift, turned = (
        lax.optimization_barrier(
            (sent_1, here, geo, flux, small_flux, scaled, waves, small_waves, shift, turned)
        )
    )
    arrived_1 = exchange(sent_1)
    arrived_2 = exchange(late_2)
    speed_x, slope_0 = to_points(by_source(strips, mode), forward)
    speed_y, slope_1 = to_points(arrived_1, forward)
    speeds = [speed_x, speed_y]
    partial = in_plane(speeds, speeds, here, table)
    rows_early = some // NODES
    speed_z, slope_2, blocks = turn_around(
        arrived_1, NODES, 0, rows_early, partial[0], slope_0, forward, backward, (), None
    )
    home_0 = exchange(blocks)
    speed_z, slope_2, *buffers = turn_around(
        arrived_2,
        0,
        rows_early,
        NODES - rows_early,
        partial[0],
        slope_0,
        forward,
        turned,
        (speed_z, slope_2),
        (first_shape, NODES),
    )
    last = in_plane(speeds, [speed_z], here, table)[0]
    shapes = (first_shape, second_shape)
    buffers = to_planes(partial[1], speed_z, slope_1, turned, mode, 0, shapes, buffers)
    *home_strips, second = to_planes(last, speed_z, slope_2, turned, mode, 1, shapes, buffers)
    for k in range(1, modes):
        home_strips[k] = lax.ppermute(
            home_strips[k], "mode", [(i, (i + k) % modes) for i in range(modes)]
        )
    home_1 = by_source(home_strips, mode)
    home_2 = exchange(second)
    returned = (home_1, home_2)
    base = velocity_part((sent_0, sent_1, sent_2), flux, scaled, waves, table)

    own_rows = local_planes * square * layers

    def read_first(refs, g):
        def read(d, n):
            if n < some:
                return refs[0][d, n]
            a, b = divmod(n - some, NODES)
            return refs[1 + a][d, g * NODES + b]

        return read

    def read_part(refs, i):
        return lambda d, n: refs[0][d, n]

    first_specs = [pl.BlockSpec((modes, some, group, lanes), lambda i: (0, 0, i, 0))] + [
        pl.BlockSpec(
            (modes, 2 * NODES, group, lanes), functools.partial(lambda k, i: (0, k, 0, 0), NODES + k)
        )
        for k in range(NODES - rows_early)
    ]
    part_specs = [pl.BlockSpec((modes, square, group, lanes), lambda i: (0, i, 0, 0))]
    advection = unpack(
        [home_0] + [home_1] * (NODES - rows_early),
        first_specs,
        read_first,
        (0, 1),
        layers,
        None,
        3 * own_rows,
    )
    flat = first_part(base, home_0, home_1, NODES, small_flux, table)

    def solve(place, flat, own_shift, buffer):
        raw, first, last = right_side(
            flat, returned[place], small_flux, scaled, small_waves, table, layers, place
        )
        before, after = swap_rims(first, last)
        start, image, first, last = first_image(raw, before, after, own_shift, geo, layers, table)
        messages = (first,) + swap_rims(first, last) + (opposite(first),)
        joined, image, first, last, scalars = second_image(
            start, image, messages, own_shift, geo, layers, table
        )
        messages = (first,) + swap_rims(first, last) + (opposite(first),)
        residual, direction, sums, scalars = third_energy(
            start, joined, image, messages, scalars, own_shift, geo, layers, table
        )
        messages = (sums,) + swap_rims(sums, sums) + (opposite(sums),)
        return finish(
            start, direction, residual, messages, scalars, layers, place, buffer, own_rows
        )

    pressure = solve(0, flat, shift[0], None)
    advection = unpack(
        [home_1], part_specs, read_part, (2, 2), layers, advection, 3 * own_rows
    )
    flat, pressure, advection, shift = lax.optimization_barrier(
        (flat, pressure, advection, shift)
    )

    def unpack_late(comp, buffer):
        spec = pl.BlockSpec((modes, square, group, lanes), lambda i: (0, comp, 0, 0))
        return unpack(
            [home_2], [spec], read_part, (3 + 2 * comp, 1), layers, buffer, 3 * own_rows, 1
        )

    pressure = solve(1, flat, shift[1], pressure)
    advection = unpack_late(1, unpack_late(0, advection))
    advection = advection.reshape(3, local_planes, NODES, NODES, layers, lanes)
    pressure = pressure.reshape(local_planes, NODES, NODES, layers, lanes)
    return (advection.transpose(0, 1, 4, 2, 3, 5), pressure.transpose(0, 3, 1, 2, 4))


def paired_fits(mesh, shape):
    modes, ring = (mesh.shape["mode"], mesh.shape["elem"])
    _, planes, layers, _, _, columns = shape
    return (
        ring == 4
        and columns == 128 * ring
        and modes == 2 * layers
        and layers % 4 == 0
        and planes == 32 * modes
        and (layers * NODES + 2 <= 128)
    )


def solution(mesh):
    placed = (
        P(None, "mode", None, None, None, "elem"),
        P(None, None, None, "elem"),
        P(None, None, None, "elem"),
        P(None, None, None, "elem"),
        P(None, None, None, "elem"),
        P(None, None, None, "elem"),
    )


    def step(velocity, *rest):
        body = on_device_paired if paired_fits(mesh, velocity.shape) else on_device
        return jax.shard_map(
            body,
            mesh=mesh,
            in_specs=placed,
            out_specs=(
                P(None, "mode", None, None, None, "elem"),
                P("mode", None, None, None, "elem"),
            ),
            check_vma=False,
        )(velocity, *rest)

    return step
```

```python
import functools
import math

import jax
import jax.numpy as jnp
import numpy as np
from jax import lax
from jax.experimental import pallas as pl
from jax.experimental.pallas import tpu as pltpu
from jax.sharding import PartitionSpec as P

NODES = 7
ITERS = 3
GRANT = 24 * 2**20
WHOLE_GRANT = 67043328


spanwise_wave = 2.0 * math.pi / 64.0
time_step = 0.1


def padded_2(value, sides, width):
    for axis, dim in sides:
        size, length = (lax.axis_size(axis), value.shape[dim])
        up = [(i, (i + 1) % size) for i in range(size)]
        down = [(j, i) for i, j in up]
        last = lax.slice_in_dim(value, length - width, length, axis=dim)
        leading = lax.slice_in_dim(value, 0, width, axis=dim)
        before = lax.ppermute(last, axis, up)
        after = lax.ppermute(leading, axis, down)
        value = jnp.concatenate([before, value, after], axis=dim)
    return value


def lobatto_rule(count):
    degree = count - 1
    points = np.cos(np.pi * np.arange(count) / degree)
    legendre = np.zeros((count, count))
    for _ in range(60):
        legendre[:, 0] = 1.0
        legendre[:, 1] = points
        for order in range(2, count):
            legendre[:, order] = (
                (2 * order - 1) * points * legendre[:, order - 1]
                - (order - 1) * legendre[:, order - 2]
            ) / order
        points = points - (points * legendre[:, degree] - legendre[:, degree - 1]) / (
            count * legendre[:, degree]
        )
    legendre[:, 0] = 1.0
    legendre[:, 1] = points
    for order in range(2, count):
        legendre[:, order] = (
            (2 * order - 1) * points * legendre[:, order - 1] - (order - 1) * legendre[:, order - 2]
        ) / order
    weights = 2.0 / (degree * count * legendre[:, degree] ** 2)
    return (points[::-1].copy(), weights[::-1].copy())


def derivative_table():
    lobatto_nodes = lobatto_rule(NODES)[0]
    total = lobatto_nodes.shape[0]
    scales = np.ones(total)
    for column in range(total):
        for other in range(total):
            if other != column:
                scales[column] = scales[column] / (lobatto_nodes[column] - lobatto_nodes[other])
    table = np.zeros((total, total))
    for row in range(total):
        for column in range(total):
            if row != column:
                table[row, column] = (
                    scales[column] / scales[row] / (lobatto_nodes[row] - lobatto_nodes[column])
                )
        table[row, row] = -np.sum(table[row])
    return table


def radial_derivative(table, field):
    return jnp.einsum("ia,...abe->...ibe", table, field, precision=lax.Precision.HIGHEST)


def around_derivative(table, field):
    return jnp.einsum("jb,...abe->...aje", table, field, precision=lax.Precision.HIGHEST)


def radial_transpose(table, field):
    return jnp.einsum("ia,...ibe->...abe", table, field, precision=lax.Precision.HIGHEST)


def around_transpose(table, field):
    return jnp.einsum("jb,...aje->...abe", table, field, precision=lax.Precision.HIGHEST)


def z_derivative(field, first_pair):
    shape = field.shape
    count = shape[1] // 2
    pairs = field.reshape((shape[0], count, 2) + shape[2:])
    waves = (first_pair + jnp.arange(count, dtype=jnp.int32)).astype(jnp.float32) * spanwise_wave
    waves = waves.reshape((1, count) + (1,) * (len(shape) - 2))
    return jnp.stack([waves * pairs[:, :, 1], -waves * pairs[:, :, 0]], axis=2).reshape(shape)


def transform_tables(planes):
    position = jnp.arange(planes, dtype=jnp.int32)
    plane = jnp.arange(planes, dtype=jnp.int32)
    order = plane // 2
    turns = position[:, None] * order[None, :] % planes
    angle = 2.0 * math.pi / planes * turns.astype(jnp.float32)
    cosine = jnp.cos(angle)
    sine = jnp.sin(angle)
    is_sine = (plane % 2 == 1)[None, :]
    is_top = (plane == 1)[None, :]
    parity = jnp.cos(math.pi * (position % 2).astype(jnp.float32))[:, None]
    basis = jnp.where(is_top, parity, jnp.where(is_sine, sine, cosine))
    scaling = jnp.where(order == 0, 1.0, 2.0).astype(jnp.float32) / planes
    inverse = jnp.transpose(basis * scaling[None, :])
    wave = (order.astype(jnp.float32) * spanwise_wave)[None, :]
    slope = jnp.where(is_sine, wave * cosine, -wave * sine)
    return (basis, inverse, slope)


def geometry(radial_dx, radial_dy, around_dx, around_dy, jacobian):
    lobatto_weights = lobatto_rule(NODES)[1]
    quadrature = jnp.asarray(np.outer(lobatto_weights, lobatto_weights), jnp.float32)[:, :, None]
    mass = quadrature * jacobian
    radial_stiff = mass * (radial_dx * radial_dx + radial_dy * radial_dy)
    cross_stiff = mass * (radial_dx * around_dx + radial_dy * around_dy)
    around_stiff = mass * (around_dx * around_dx + around_dy * around_dy)
    return (radial_stiff, cross_stiff, around_stiff, mass)


def node_weights(layers):
    layer = jnp.arange(layers, dtype=jnp.int32).reshape(layers, 1, 1, 1)
    node = jnp.arange(NODES, dtype=jnp.int32)
    radial_node = node.reshape(1, NODES, 1, 1)
    around_node = node.reshape(1, 1, NODES, 1)
    shared_radial = (radial_node == NODES - 1) & (layer < layers - 1) | (radial_node == 0) & (
        layer > 0
    )
    shared_around = (around_node == 0) | (around_node == NODES - 1)
    multiplicity = (1.0 + shared_radial.astype(jnp.float32)) * (
        1.0 + shared_around.astype(jnp.float32)
    )
    boundary = (radial_node == NODES - 1) & (layer == layers - 1)
    mask = 1.0 - boundary.astype(jnp.float32)
    return (mask, mask / multiplicity)


def plane_shift(first_plane, count, planes):
    plane = first_plane + jnp.arange(count, dtype=jnp.int32)
    order = jnp.where(plane == 1, planes // 2, plane // 2)
    wave = order.astype(jnp.float32) * spanwise_wave
    return (wave * wave).reshape(count, 1, 1, 1, 1)


def helmholtz_local(table, field, shift, metrics):
    radial_stiff, cross_stiff, around_stiff, mass = metrics
    radial = radial_derivative(table, field)
    beside_all = around_derivative(table, field)
    return (
        radial_transpose(table, radial_stiff * radial + cross_stiff * beside_all)
        + around_transpose(table, cross_stiff * radial + around_stiff * beside_all)
        + shift * mass * field
    )


def assemble(field):
    lower = field[:, :-1, -1] + field[:, 1:, 0]
    field = field.at[:, :-1, -1].set(lower).at[:, 1:, 0].set(lower)
    first = field[:, :, :, 0]
    last = field[:, :, :, -1]
    rims = jnp.concatenate([first[..., :1], last[..., -1:]], axis=3)
    padded = padded_2(rims, (("elem", 3),), 1)
    after = jnp.concatenate([first[..., 1:], padded[..., 3:4]], axis=3)
    right = last + after
    left = jnp.concatenate([padded[..., 0:1] + first[..., :1], right[..., :-1]], axis=3)
    return field.at[:, :, :, -1].set(right).at[:, :, :, 0].set(left)


def inner(first, second, weight):
    return jnp.sum(first * second * weight, axis=(1, 2, 3, 4))


def expand(scalar):
    return scalar.reshape(-1, 1, 1, 1, 1)


def squared_norm(residual, weight):
    return lax.psum(inner(residual, residual, weight), "elem")


def on_device(velocity, radial_dx, radial_dy, around_dx, around_dy, jacobian):
    table = jnp.asarray(derivative_table(), jnp.float32)
    modes = lax.axis_size("mode")
    local_planes = velocity.shape[1]
    planes = local_planes * modes
    first_plane = lax.axis_index("mode") * local_planes
    layers = velocity.shape[2]
    columns = velocity.shape[5]
    basis, inverse, slope = transform_tables(planes)
    radial = radial_derivative(table, velocity)
    beside_all = around_derivative(table, velocity)
    along_x = radial_dx * radial + around_dx * beside_all
    along_y = radial_dy * radial + around_dy * beside_all
    fields = jnp.concatenate([velocity, along_x, along_y], axis=0)
    count = fields.shape[0]
    cells = layers * NODES * NODES * columns
    packed = fields.reshape(count, local_planes, modes, cells // modes)
    flat = lax.all_to_all(packed, "mode", split_axis=2, concat_axis=1, tiled=True)[:, :, 0, :]
    values = jnp.einsum("jp,fpc->fjc", basis, flat, precision=lax.Precision.HIGHEST)
    speed = values[0:3]
    slope_x = values[3:6]
    slope_y = values[6:9]
    slope_z = jnp.einsum("jp,fpc->fjc", slope, flat[0:3], precision=lax.Precision.HIGHEST)
    product = -(speed[0:1] * slope_x + speed[1:2] * slope_y + speed[2:3] * slope_z)
    spectral = jnp.einsum("pj,fjc->fpc", inverse, product, precision=lax.Precision.HIGHEST)
    returned = lax.all_to_all(
        spectral[:, :, None, :], "mode", split_axis=1, concat_axis=2, tiled=True
    )
    advection = returned.reshape(velocity.shape)
    metrics = geometry(radial_dx, radial_dy, around_dx, around_dy, jacobian)
    mask, weight = node_weights(layers)
    predicted = velocity + time_step * advection
    radial = radial_derivative(table, predicted[0:2])
    beside_all = around_derivative(table, predicted[0:2])
    divergence = (
        radial_dx * radial[0]
        + around_dx * beside_all[0]
        + (radial_dy * radial[1] + around_dy * beside_all[1])
        + z_derivative(predicted[2:3], first_plane // 2)[0]
    )
    shift = plane_shift(first_plane, local_planes, planes)
    right_side = mask * assemble(-(metrics[3] * divergence) / time_step)
    solution = jnp.zeros_like(right_side)
    residual = right_side
    direction = right_side
    norm_now = squared_norm(residual, weight)
    for _ in range(ITERS):
        image = mask * assemble(helmholtz_local(table, direction, shift, metrics))
        alpha = norm_now / lax.psum(inner(direction, image, weight), "elem")
        solution = solution + expand(alpha) * direction
        residual = residual - expand(alpha) * image
        norm_next = squared_norm(residual, weight)
        direction = residual + expand(norm_next / norm_now) * direction
        norm_now = norm_next
    return (advection, solution)


def split_bf16(table):
    high = table.astype(jnp.bfloat16)
    low = (table - high.astype(np.float64)).astype(jnp.bfloat16)
    return np.concatenate([high, high, low], axis=1)


def paired_tables(planes):
    position = np.arange(planes)
    plane = np.arange(planes)
    order = plane // 2
    angle = 2.0 * np.pi / planes * (position[:, None] * order[None, :] % planes)
    cosine, sine = (np.cos(angle), np.sin(angle))
    odd = (plane % 2 == 1)[None, :]
    parity = (1.0 - 2.0 * (position % 2))[:, None]
    basis = np.where((plane == 1)[None, :], parity, np.where(odd, sine, cosine))
    wave = (order * spanwise_wave)[None, :]
    slope = np.where(odd, wave * cosine, -wave * sine)
    scaling = np.where(order == 0, 1.0, 2.0) / planes
    inverse = -(basis * scaling[None, :]).T

    def columns(matrix):
        return np.concatenate([matrix[:, 0::2], matrix[:, 1::2]], axis=1)

    forward = np.concatenate([columns(basis), columns(slope)])
    backward = columns(inverse.T).T
    return (split_bf16(forward), split_bf16(backward))


def apply_line(matrix, line):
    n = NODES
    m = n // 2
    sums = [line[a] + line[n - 1 - a] for a in range(m)]
    gaps = [line[a] - line[n - 1 - a] for a in range(m)]

    def total(parts):
        out = parts[0]
        for part in parts[1:]:
            out = out + part
        return out

    out = [None] * n
    for i in range(m + 1):
        plus = total(
            [float(0.5 * (matrix[i, a] - matrix[i, n - 1 - a])) * gaps[a] for a in range(m)]
        )
        if i == m:
            out[i] = plus
            continue
        minus = total(
            [float(0.5 * (matrix[i, a] + matrix[i, n - 1 - a])) * sums[a] for a in range(m)]
            + [float(matrix[i, m]) * line[m]]
        )
        out[i] = plus + minus
        out[n - 1 - i] = plus - minus
    return out


def lanes_of(shape):
    return lax.broadcasted_iota(jnp.int32, shape, len(shape) - 1)


def row_of(ref, row, rows):
    return ref[pl.ds(row, rows, stride=0), :]


def call(body, grid, ins, outs, out_shape, scratch=(), flops=0, moved=0, aliases=None, grant=GRANT):
    return pl.pallas_call(
        body,
        grid=grid,
        in_specs=ins,
        out_specs=outs,
        out_shape=out_shape,
        scratch_shapes=list(scratch),
        input_output_aliases=aliases or {},
        compiler_params=pltpu.CompilerParams(
            dimension_semantics=("arbitrary",) * len(grid), vmem_limit_bytes=grant
        ),
        cost_estimate=pl.CostEstimate(
            flops=int(flops), bytes_accessed=int(moved), transcendentals=0
        ),
    )


def held(count):
    return [pl.BlockSpec(memory_space=pltpu.VMEM)] * count


def whole(shape):
    return pl.BlockSpec(shape, lambda *_: (0,) * len(shape))


def turn(tiles):
    tiles = list(tiles)
    sub = lax.broadcasted_iota(jnp.int32, tiles[0].shape, 0)
    size = len(tiles)
    step = size // 2
    while step:
        keep = (sub & step) == 0
        for i in range(size):
            if not i & step:
                one, two = (tiles[i], tiles[i + step])
                tiles[i] = jnp.where(keep, one, pltpu.roll(two, step, 0))
                tiles[i + step] = jnp.where(keep, pltpu.roll(one, size - step, 0), two)
        step //= 2
    return tiles


def turn_all(read, write, count):
    def some(s, carry):
        for i in range(NODES):
            t = s * NODES + i
            for r, tile in enumerate(turn([read(k, t) for k in range(8)])):
                write(t, r, tile)
        return carry

    lax.fori_loop(0, count // NODES, some, 0)


def rows_at(k, unit, t):
    return pl.ds(pl.multiple_of(k * unit + 8 * t, 8), 8)


def pack_one(x_ref, write_out, mid, layers, lanes):
    square = NODES * NODES
    per_plane = square * layers
    unit = 2 * per_plane
    half = lanes // 2
    low = lanes_of((8, lanes)) < half

    def write(t, r, tile):
        mid[8 * t + r] = tile

    turn_all(lambda k, t: x_ref[0, rows_at(k, unit, t), :], write, unit // 8)

    def layer(e, carry):
        for n in range(square):
            cos = mid[n * layers + e]
            sin = mid[per_plane + n * layers + e]
            write_out(2 * e, n, jnp.where(low, cos, pltpu.roll(sin, half, 1)))
            write_out(2 * e + 1, n, jnp.where(low, pltpu.roll(cos, half, 1), sin))
        return carry

    lax.fori_loop(0, layers, layer, 0)


def pack_specs(layers, pairs, lanes, nodes):
    return (
        pl.BlockSpec((2 * layers, nodes, 8, lanes), lambda g: (0, 0, g, 0)),
        jax.ShapeDtypeStruct((2 * layers, nodes, pairs, lanes), jnp.float32),
    )


def pack_first(rows, place, layers, pairs, lanes):
    square = NODES * NODES
    unit = 2 * square * layers
    shares = 2 * layers

    def body(place_ref, x_ref, *refs):
        outs, (mid, held_ref) = (refs[:shares], refs[shares:])
        here = place_ref[0]

        def write(d, n, value):
            held_ref[d, n] = value

        pack_one(x_ref, write, mid, layers, lanes)

        def row(a, carry):
            for k in range(shares):
                d = lax.rem(here + k, shares)
                for b in range(NODES):
                    outs[k][a * NODES + b] = held_ref[d, a * NODES + b]
            return carry

        lax.fori_loop(0, NODES, row, 0)

    return call(
        body,
        (pairs // 8,),
        [
            pl.BlockSpec(memory_space=pltpu.SMEM),
            pl.BlockSpec((1, 8 * unit, lanes), lambda g: (0, g, 0)),
        ],
        [pl.BlockSpec((square, 8, lanes), lambda g: (0, g, 0))] * shares,
        [jax.ShapeDtypeStruct((square, pairs, lanes), jnp.float32)] * shares,
        scratch=[
            pltpu.VMEM((unit, 8, lanes), jnp.float32),
            pltpu.VMEM((shares, square, 8, lanes), jnp.float32),
        ],
        grant=WHOLE_GRANT,
        moved=2 * rows.shape[1] * lanes * 4,
    )(jnp.full((1,), place, jnp.int32), rows)


def pack_rest(rows, layers, pairs, lanes, early):
    square = NODES * NODES
    unit = 2 * square * layers

    def body(u_ref, x_ref, y_ref, o_ref, late_ref, whole_ref, zero_ref, mid):
        def zeroth(d, n, value):
            zero_ref[d, n] = value

        def first(d, n, value):
            o_ref[d, n] = value

        def second(d, n, value):
            whole_ref[d, n] = value
            if n < early:
                o_ref[d, square + n] = value
            else:
                late_ref[d, n - early] = value

        pack_one(x_ref, first, mid, layers, lanes)
        pack_one(y_ref, second, mid, layers, lanes)
        pack_one(u_ref, zeroth, mid, layers, lanes)

    parts = [
        pack_specs(layers, pairs, lanes, nodes)
        for nodes in (square + early, square - early, square, square)
    ]
    return call(
        body,
        (pairs // 8,),
        [
            pl.BlockSpec((1, 8 * unit, lanes), lambda g: (0, g, 0)),
            pl.BlockSpec((1, 8 * unit, lanes), lambda g: (1, g, 0)),
            pl.BlockSpec((1, 8 * unit, lanes), lambda g: (2, g, 0)),
        ],
        [part[0] for part in parts],
        [part[1] for part in parts],
        scratch=[pltpu.VMEM((unit, 8, lanes), jnp.float32)],
        grant=WHOLE_GRANT,
        moved=5 * rows.shape[1] * lanes * 4,
    )(rows, rows, rows)


def unpack(arrays, specs, read_from, slots, layers, buffer, total, steps=2):
    lanes = arrays[0].shape[-1]
    square = NODES * NODES
    per_plane = square * layers
    unit = 2 * per_plane
    half = lanes // 2

    def body(*refs):
        o_ref, mid = refs[-2:]
        low = lanes_of((8, lanes)) < half
        read = read_from(refs, pl.program_id(0))

        def layer(e, carry):
            for n in range(square):
                left, right = (read(2 * e, n), read(2 * e + 1, n))
                mid[n * layers + e] = jnp.where(low, left, pltpu.roll(right, half, 1))
                mid[per_plane + n * layers + e] = jnp.where(low, pltpu.roll(left, half, 1), right)
            return carry

        lax.fori_loop(0, layers, layer, 0)

        def write(t, r, tile):
            o_ref[rows_at(r, unit, t), :] = tile

        turn_all(lambda k, t: mid[8 * t + k], write, unit // 8)

    extra = [] if buffer is None else [buffer]
    return call(
        body,
        (steps,),
        list(specs) + [pl.BlockSpec(memory_space=pl.ANY)] * len(extra),
        pl.BlockSpec((8 * unit, lanes), lambda i: (slots[0] + i * slots[1], 0)),
        jax.ShapeDtypeStruct((total, lanes), jnp.float32),
        scratch=[pltpu.VMEM((unit, 8, lanes), jnp.float32)],
        moved=4 * 8 * unit * lanes * 4,
        aliases={len(arrays): 0} if extra else None,
    )(*arrays, *extra)


def paired_nodes():
    return [(b, min(b + 1, NODES - 1)) for b in range(0, NODES, 2)]


def three_pass(table, rhs_ref, tiles):
    rows, lanes = tiles[0].shape
    half = lanes // 2
    low = lanes_of((rows, lanes)) < half
    depth = 2 * rows
    for place, (one, two) in enumerate(paired_nodes()):
        first, second = (tiles[one], tiles[two])
        cut = pl.ds(place * lanes, lanes)
        for part in range(2):
            if part == 0:
                value = jnp.where(low, first, pltpu.roll(second, half, 1))
            else:
                value = jnp.where(low, pltpu.roll(first, half, 1), second)
            high = value.astype(jnp.bfloat16)
            rest = (value - high.astype(jnp.float32)).astype(jnp.bfloat16)
            rhs_ref[pl.ds(part * rows, rows), cut] = high
            rhs_ref[pl.ds(depth + part * rows, rows), cut] = rest
            rhs_ref[pl.ds(2 * depth + part * rows, rows), cut] = high
    out = jnp.dot(table, rhs_ref[...], preferred_element_type=jnp.float32)
    fields = []
    for field in range(table.shape[0] // depth):
        nodes = [None] * NODES
        for place, (one, two) in enumerate(paired_nodes()):
            cut = slice(place * lanes, (place + 1) * lanes)
            top = out[field * depth : field * depth + rows, cut]
            bottom = out[field * depth + rows : (field + 1) * depth, cut]
            nodes[one] = jnp.where(low, top, pltpu.roll(bottom, half, 1))
            if two != one:
                nodes[two] = jnp.where(low, pltpu.roll(top, half, 1), bottom)
        fields.append(nodes)
    return fields


def rhs_scratch(table, lanes):
    return pltpu.VMEM((table.shape[1], len(paired_nodes()) * lanes), jnp.bfloat16)


def read_tiles(x_ref, rows, lanes):
    return [x_ref[:, b].reshape(rows, lanes) for b in range(NODES)]


def to_points(blocks, table):
    shares, _, pairs, lanes = blocks.shape
    square = NODES * NODES
    rows = shares * pairs

    def body(t_ref, x_ref, v_ref, z_ref, rhs_ref):
        fields = three_pass(t_ref[...], rhs_ref, read_tiles(x_ref, rows, lanes))
        for b in range(NODES):
            v_ref[b] = fields[0][b]
            z_ref[b] = fields[1][b]

    spec = pl.BlockSpec((NODES, rows, lanes), lambda a: (a, 0, 0))
    shape = jax.ShapeDtypeStruct((square, rows, lanes), jnp.float32)
    return call(
        body,
        (NODES,),
        [
            whole(table.shape),
            pl.BlockSpec((shares, NODES, pairs, lanes), lambda a: (0, a, 0, 0)),
        ],
        [spec, spec],
        [shape, shape],
        scratch=[rhs_scratch(table, lanes)],
        flops=2 * table.shape[0] * table.shape[1] * square * lanes,
        grant=WHOLE_GRANT,
        moved=3 * square * rows * lanes * 4,
    )(table, blocks)


def turn_around(blocks, skip, start, count, partial, slope_z, table, back, fields, out):
    shares, _, pairs, lanes = blocks.shape
    rows = shares * pairs
    square = NODES * NODES
    group = pairs // 2
    shape = jax.ShapeDtypeStruct((square, rows, lanes), jnp.float32)

    def body(t_ref, i_ref, x_ref, g_ref, s_ref, *refs):
        w_ref, z_ref = refs[len(fields) : len(fields) + 2]
        outs, rhs_ref = (refs[len(fields) + 2 : -1], refs[-1])
        points = three_pass(t_ref[...], rhs_ref, read_tiles(x_ref, rows, lanes))
        for b in range(NODES):
            w_ref[b] = points[0][b]
            z_ref[b] = points[1][b]
        tiles = [g_ref[b] + w_ref[b] * s_ref[b] for b in range(NODES)]
        spectral = three_pass(i_ref[...], rhs_ref, tiles)[0]
        for b in range(NODES):
            value = spectral[b].reshape(shares, pairs, lanes)
            if out is None:
                outs[0][:, b] = value
            else:
                for k in range(shares):
                    for g in range(2):
                        outs[k][g * NODES + b] = value[k, g * group : (g + 1) * group]

    spec = pl.BlockSpec((NODES, rows, lanes), lambda a: (start + a, 0, 0))
    if out is None:
        out_spec = [pl.BlockSpec((shares, NODES, pairs, lanes), lambda a: (0, a, 0, 0))]
        out_shape = [jax.ShapeDtypeStruct((shares, count * NODES, pairs, lanes), jnp.float32)]
    else:
        first = out[1]
        out_spec = [pl.BlockSpec((2 * NODES, group, lanes), lambda a: (first + a, 0, 0))] * shares
        out_shape = [jax.ShapeDtypeStruct(out[0], jnp.float32)] * shares
    return call(
        body,
        (count,),
        [
            whole(table.shape),
            whole(back.shape),
            pl.BlockSpec((shares, NODES, pairs, lanes), lambda a: (0, skip + a, 0, 0)),
            spec,
            spec,
        ]
        + [pl.BlockSpec(memory_space=pl.ANY)] * len(fields),
        [spec, spec] + out_spec,
        [shape, shape] + out_shape,
        scratch=[rhs_scratch(table, lanes)],
        flops=3 * table.shape[0] * table.shape[1] * count * NODES * lanes,
        aliases={5: 0, 6: 1} if fields else None,
        grant=WHOLE_GRANT,
        moved=6 * count * NODES * rows * lanes * 4,
    )(table, back, blocks, partial, slope_z, *fields)


def in_plane(speeds, fields, metrics, table):
    square, rows, lanes = speeds[0].shape
    count = len(fields)
    step = 32
    own = [i for i, f in enumerate(fields) if all(f is not s for s in speeds)]
    arrays = list(speeds) + [fields[i] for i in own]

    def body(m_ref, *refs):
        ins, outs = (refs[: len(arrays)], refs[len(arrays) :])
        u_ref, v_ref = ins[:2]
        sources = []
        extra = 2
        for i, f in enumerate(fields):
            if i in own:
                sources.append(ins[extra])
                extra += 1
            else:
                sources.append(u_ref if f is speeds[0] else v_ref)

        def block(s, carry):
            r = pl.ds(s * 8, 8)

            def metric(kind, n):
                return row_of(m_ref, kind * square + n, 8)

            for a in range(NODES):
                ns = [a * NODES + b for b in range(NODES)]
                drift = [
                    u_ref[n, r] * metric(2, n) + v_ref[n, r] * metric(3, n) for n in ns
                ]
                for f in range(count):
                    beside = apply_line(table, [sources[f][n, r] for n in ns])
                    for b, n in enumerate(ns):
                        outs[f][n, r] = drift[b] * beside[b]
            for b in range(NODES):
                ns = [a * NODES + b for a in range(NODES)]
                drift = [
                    u_ref[n, r] * metric(0, n) + v_ref[n, r] * metric(1, n) for n in ns
                ]
                for f in range(count):
                    radial = apply_line(table, [sources[f][n, r] for n in ns])
                    for a, n in enumerate(ns):
                        outs[f][n, r] = outs[f][n, r] + drift[a] * radial[a]
            return carry

        lax.fori_loop(0, step // 8, block, 0)

    spec = pl.BlockSpec((square, step, lanes), lambda i: (0, i, 0))
    shape = jax.ShapeDtypeStruct((square, rows, lanes), jnp.float32)
    return call(
        body,
        (rows // step,),
        [whole(metrics.shape)] + [spec] * len(arrays),
        [spec] * count,
        [shape] * count,
        flops=30 * count * square * rows * lanes,
        grant=WHOLE_GRANT,
        moved=(len(arrays) + count) * square * rows * lanes * 4,
    )(metrics, *arrays)


def by_source(strips, place):
    count = len(strips)
    nodes, rows, lanes = strips[0].shape
    step = 2 * NODES if nodes % (2 * NODES) == 0 else NODES

    def body(place_ref, *refs):
        o_ref = refs[-1]
        here = place_ref[0]
        for k in range(count):
            source = lax.rem(here - k + count, count)
            for n in range(step):
                o_ref[source, n] = refs[k][n]

    return call(
        body,
        (nodes // step,),
        [pl.BlockSpec(memory_space=pltpu.SMEM)]
        + [pl.BlockSpec((step, rows, lanes), lambda i: (i, 0, 0))] * count,
        pl.BlockSpec((count, step, rows, lanes), lambda i: (0, i, 0, 0)),
        jax.ShapeDtypeStruct((count,) + strips[0].shape, jnp.float32),
        grant=WHOLE_GRANT,
        moved=8 * count * strips[0].size,
    )(jnp.full((1,), place, jnp.int32), *strips)


def to_planes(partial, speed_z, slope_z, table, place, comp, shapes, buffers):
    square, rows, lanes = partial.shape
    shares = shapes[1][0]
    pairs = rows // shares
    group = pairs // 2

    def body(place_ref, t_ref, g_ref, w_ref, z_ref, *refs):
        strips, o_ref, rhs_ref = (refs[-shares - 2 : -2], refs[-2], refs[-1])
        here = place_ref[0]
        tiles = [g_ref[b] + w_ref[b] * z_ref[b] for b in range(NODES)]
        nodes = three_pass(t_ref[...], rhs_ref, tiles)[0]
        for b in range(NODES):
            out = nodes[b].reshape(shares, pairs, lanes)
            for k in range(shares):
                strips[k][b] = out[k, :group]
                o_ref[lax.rem(here + k, shares), b] = out[k, group:]

    spec = pl.BlockSpec((NODES, rows, lanes), lambda a: (a, 0, 0))
    return call(
        body,
        (NODES,),
        [pl.BlockSpec(memory_space=pltpu.SMEM), whole(table.shape), spec, spec, spec]
        + [pl.BlockSpec(memory_space=pl.ANY)] * len(buffers),
        [pl.BlockSpec((NODES, group, lanes), lambda a: (comp * NODES + a, 0, 0))] * shares
        + [pl.BlockSpec((shares, NODES, group, lanes), lambda a: (0, comp * NODES + a, 0, 0))],
        [jax.ShapeDtypeStruct(shapes[0], jnp.float32)] * shares
        + [jax.ShapeDtypeStruct(shapes[1], jnp.float32)],
        scratch=[rhs_scratch(table, lanes)],
        flops=2 * table.shape[0] * table.shape[1] * square * lanes,
        aliases={5 + k: k for k in range(len(buffers))},
        grant=WHOLE_GRANT,
        moved=4 * square * rows * lanes * 4,
    )(jnp.full((1,), place, jnp.int32), table, partial, speed_z, slope_z, *buffers)


def velocity_part(sent, metrics, weights, waves, table):
    shares, square, pairs, lanes = sent[0].shape
    half = lanes // 2

    def body(m_ref, q_ref, k_ref, s0, s1, s2, o_ref):
        d = pl.program_id(0)

        def rows_of(s):
            r = pl.ds(s * 8, 8)
            wave = k_ref[r]

            def metric(kind, n):
                return row_of(m_ref, (kind * shares + d) * square + n, 8)

            for a in range(NODES):
                ns = [a * NODES + b for b in range(NODES)]
                first = apply_line(table, [s0[0, n, r] for n in ns])
                second = apply_line(table, [s1[0, n, r] for n in ns])
                for b, n in enumerate(ns):
                    along = pltpu.roll(s2[0, n, r], half, 1) * wave
                    o_ref[0, n, r] = (
                        metric(2, n) * first[b]
                        + metric(3, n) * second[b]
                        + row_of(q_ref, d * square + n, 8) * along
                    )
            for b in range(NODES):
                ns = [a * NODES + b for a in range(NODES)]
                first = apply_line(table, [s0[0, n, r] for n in ns])
                second = apply_line(table, [s1[0, n, r] for n in ns])
                for a, n in enumerate(ns):
                    o_ref[0, n, r] = o_ref[0, n, r] + (
                        metric(0, n) * first[a] + metric(1, n) * second[a]
                    )

        lax.fori_loop(0, pairs // 8, lambda s, carry: (rows_of(s), carry)[1], 0)

    spec = pl.BlockSpec((1, square, pairs, lanes), lambda d: (d, 0, 0, 0))
    return call(
        body,
        (shares,),
        [whole(metrics.shape), whole(weights.shape), whole(waves.shape)] + [spec] * 3,
        spec,
        jax.ShapeDtypeStruct(sent[0].shape, jnp.float32),
        flops=60 * shares * square * pairs * lanes,
        grant=WHOLE_GRANT,
        moved=4 * shares * square * pairs * lanes * 4,
    )(metrics, weights, waves, *sent)


def first_part(base, early, rest, rest_at, metrics, table):
    shares, square, pairs, lanes = base.shape

    some = early.shape[1]
    count = (square - some) // NODES
    group = pairs // 2

    def body(m_ref, s0, r0, *refs):
        others, (o_ref, p0) = (refs[:count], refs[count:])
        d = pl.program_id(0)

        def block(s, carry):
            r = pl.ds(s * 8, 8)
            for n in range(square):
                if n < some:
                    home = r0[0, n, r]
                else:
                    a, b = divmod(n - some, NODES)
                    home = others[a][0, s * NODES + b]
                p0[n] = home

            def metric(kind, n):
                return row_of(m_ref, (kind * shares + d) * square + n, 8)

            for a in range(NODES):
                ns = [a * NODES + b for b in range(NODES)]
                line = apply_line(table, [p0[n] for n in ns])
                for b, n in enumerate(ns):
                    o_ref[0, n, r] = s0[0, n, r] + metric(2, n) * line[b]
            for b in range(NODES):
                ns = [a * NODES + b for a in range(NODES)]
                line = apply_line(table, [p0[n] for n in ns])
                for a, n in enumerate(ns):
                    o_ref[0, n, r] = o_ref[0, n, r] + metric(0, n) * line[a]
            return carry

        lax.fori_loop(0, pairs // 8, block, 0)

    spec = pl.BlockSpec((1, square, pairs, lanes), lambda d: (d, 0, 0, 0))
    return call(
        body,
        (shares,),
        [whole(metrics.shape), spec, pl.BlockSpec((1, some, pairs, lanes), lambda d: (d, 0, 0, 0))]
        + [
            pl.BlockSpec(
                (1, 2 * NODES, group, lanes), functools.partial(lambda i, d: (d, i, 0, 0), rest_at + k)
            )
            for k in range(count)
        ],
        spec,
        jax.ShapeDtypeStruct(base.shape, jnp.float32),
        scratch=[pltpu.VMEM((square, 8, lanes), jnp.float32)],
        flops=30 * shares * square * pairs * lanes,
        grant=WHOLE_GRANT,
        moved=3 * shares * square * pairs * lanes * 4,
    )(metrics, base, early, *[rest] * count)


def join_layers(y_ref, layers):
    square = NODES * NODES
    last = (NODES - 1) * NODES
    for e in range(layers - 1):
        for b in range(NODES):
            upper, lower = (e * square + last + b, (e + 1) * square + b)
            total = y_ref[upper] + y_ref[lower]
            y_ref[upper] = total
            y_ref[lower] = total
    for b in range(NODES):
        node = (layers - 1) * square + last + b
        y_ref[node] = jnp.zeros_like(y_ref[node])


def rim_messages(read, layers, shape, partials):
    lane = lanes_of(shape)
    lanes = shape[-1]
    axis = len(shape) - 1
    first = jnp.zeros(shape, jnp.float32)
    last = jnp.zeros(shape, jnp.float32)
    square = NODES * NODES
    for e in range(layers):
        for a in range(NODES):
            spot = e * NODES + a
            here = lane == spot
            node = e * square + a * NODES
            first = jnp.where(here, pltpu.roll(read(node), spot, axis), first)
            last = jnp.where(
                here, pltpu.roll(read(node + NODES - 1), (spot + 1) % lanes, axis), last
            )
    for i, partial in enumerate(partials):
        here = lane == layers * NODES + i
        first = jnp.where(here, partial, first)
        last = jnp.where(here, partial, last)
    return (first, last)


def right_side(flat, returned, metrics, weights, waves, table, layers, place):
    shares, square, _, lanes = flat.shape
    half = lanes // 2

    def body(m_ref, q_ref, k_ref, f_ref, r1, r2, o_ref, first_ref, last_ref, c0, c1):
        e = pl.program_id(0)
        lane = lanes_of((8, lanes))
        low = lane < half
        wave = k_ref[...]
        sides = (c0, c1)

        @pl.when(e == 0)
        def _():
            first_ref[...] = jnp.zeros_like(first_ref)
            last_ref[...] = jnp.zeros_like(last_ref)

        for h in range(2):
            d = 2 * e + h
            side = sides[h]
            for n in range(square):
                along = pltpu.roll(r2[h, n], half, 1) * wave
                side[n] = f_ref[h, n] + row_of(q_ref, d * square + n, 8) * along

            def metric(kind, n):
                return row_of(m_ref, (kind * shares + d) * square + n, 8)

            for a in range(NODES):
                ns = [a * NODES + b for b in range(NODES)]
                line = apply_line(table, [r1[h, n] for n in ns])
                for b, n in enumerate(ns):
                    side[n] = side[n] + metric(1, n) * line[b]
            for b in range(NODES):
                ns = [a * NODES + b for a in range(NODES)]
                line = apply_line(table, [r1[h, n] for n in ns])
                for a, n in enumerate(ns):
                    side[n] = side[n] + metric(0, n) * line[a]
        rims = [[first_ref[0], last_ref[0]], [first_ref[1], last_ref[1]]]
        for n in range(square):
            left, right = (c0[n], c1[n])
            parts = (
                jnp.where(low, left, pltpu.roll(right, half, 1)),
                jnp.where(low, pltpu.roll(left, half, 1), right),
            )
            for i in range(2):
                o_ref[n, i] = parts[i]
                a, b = divmod(n, NODES)
                spot = e * NODES + a
                if b == 0:
                    rims[i][0] = jnp.where(lane == spot, pltpu.roll(parts[i], spot, 1), rims[i][0])
                if b == NODES - 1:
                    rims[i][1] = jnp.where(
                        lane == spot, pltpu.roll(parts[i], spot + 1, 1), rims[i][1]
                    )
        for i in range(2):
            first_ref[i] = rims[i][0]
            last_ref[i] = rims[i][1]

    spec = pl.BlockSpec((2, square, 8, lanes), lambda e: (e, 0, place, 0))
    nodes = layers * square
    rim_shape = jax.ShapeDtypeStruct((2, 8, lanes), jnp.float32)
    scratch = pltpu.VMEM((square, 8, lanes), jnp.float32)
    return call(
        body,
        (layers,),
        [
            whole(metrics.shape),
            whole(weights.shape),
            pl.BlockSpec((8, lanes), lambda e: (place, 0)),
            spec,
            pl.BlockSpec((2, square, 8, lanes), lambda e: (e, 0, 0, 0)),
            pl.BlockSpec((2, square, 8, lanes), lambda e: (e, 1, 0, 0)),
        ],
        [
            pl.BlockSpec((square, 2, 8, lanes), lambda e: (e, 0, 0, 0)),
            whole((2, 8, lanes)),
            whole((2, 8, lanes)),
        ],
        [jax.ShapeDtypeStruct((nodes, 2, 8, lanes), jnp.float32), rim_shape, rim_shape],
        scratch=[scratch] * 2,
        flops=40 * shares * square * 8 * lanes,
        moved=4 * shares * square * 8 * lanes * 4,
    )(metrics, weights, waves, flat, returned, returned)


def swap_rims(first, last):
    size = lax.axis_size("elem")
    up = [(i, (i + 1) % size) for i in range(size)]
    down = [(j, i) for i, j in up]
    return (lax.ppermute(last, "elem", up), lax.ppermute(first, "elem", down))


def opposite(first):
    size = lax.axis_size("elem")
    return lax.ppermute(first, "elem", [(i, (i + 2) % size) for i in range(size)])


def join_columns(read, ref, before, after, layers):
    lanes = before.shape[-1]
    axis = len(before.shape) - 1
    lane = lanes_of(before.shape)
    square = NODES * NODES
    for e in range(layers):
        for a in range(NODES):
            spot = e * NODES + a
            node = e * square + a * NODES
            first, last = (read(node), read(node + NODES - 1))
            beyond = pltpu.roll(after, lanes - 1 - spot, axis)
            ahead = jnp.where(lane == lanes - 1, beyond, pltpu.roll(first, lanes - 1, axis))
            right = last + ahead
            mine = first + (pltpu.roll(before, lanes - spot, axis) if spot else before)
            ref[node + NODES - 1] = right
            ref[node] = jnp.where(lane == 0, mine, pltpu.roll(right, 1, axis))


def join(source, ref, before, after, layers):
    square = NODES * NODES

    def copy(e, carry):
        for n in range(square):
            if 0 < n % NODES < NODES - 1:
                ref[e * square + n] = source[e * square + n]
        return carry

    lax.fori_loop(0, layers, copy, 0)
    join_columns(lambda n: source[n], ref, before, after, layers)
    join_layers(ref, layers)


def each_node(layers, step):
    def layer(e, carry):
        for n in range(NODES * NODES):
            step(e * NODES * NODES + n)
        return carry

    lax.fori_loop(0, layers, layer, 0)


def share_of(layers, e, a):
    if a == 0:
        return jnp.where(e > 0, 0.5, 1.0)
    if a == NODES - 1:
        return jnp.where(e < layers - 1, 0.5, 0.0)
    return 1.0


def helmholtz(r_ref, y_ref, flux_ref, g_ref, shift, layers, table, dot_only=False):
    square = NODES * NODES
    nodes = layers * square
    turned = table.T
    zero = jnp.zeros(shift.shape, jnp.float32)

    def layer(e, carry):
        norm, energy = carry
        base = e * square

        def metric(kind, n):
            return row_of(g_ref, kind * nodes + base + n, 8)

        for b in range(NODES):
            ns = [a * NODES + b for a in range(NODES)]
            radial = apply_line(table, [r_ref[base + n] for n in ns])
            for a, n in enumerate(ns):
                flux_ref[n] = radial[a]
        for a in range(NODES):
            ns = [a * NODES + b for b in range(NODES)]
            line = [r_ref[base + n] for n in ns]
            beside = apply_line(table, line)
            second = []
            rest = []
            part = zero
            for b, n in enumerate(ns):
                radial = flux_ref[n]
                cross = metric(1, n)
                one = metric(0, n) * radial + cross * beside[b]
                two = cross * radial + metric(2, n) * beside[b]
                same = shift * metric(3, n) * line[b]
                whole_weight = line[b] * line[b]
                part = part + (0.5 * whole_weight if b in (0, NODES - 1) else whole_weight)
                if dot_only:
                    energy = energy + (radial * one + beside[b] * two + same * line[b])
                else:
                    flux_ref[n] = one
                    second.append(two)
                    rest.append(same)
            norm = norm + part * share_of(layers, e, a)
            if not dot_only:
                back = apply_line(turned, second)
                for b, n in enumerate(ns):
                    y_ref[base + n] = rest[b] + back[b]
        if not dot_only:
            for b in range(NODES):
                ns = [a * NODES + b for a in range(NODES)]
                back = apply_line(turned, [flux_ref[n] for n in ns])
                for a, n in enumerate(ns):
                    value = y_ref[base + n] + back[a]
                    y_ref[base + n] = value
                    energy = energy + value * r_ref[base + n]
        return (norm, energy)

    norm, energy = lax.fori_loop(0, layers, layer, (zero, zero))
    axis = len(shift.shape) - 1
    return (
        jnp.sum(norm, axis=axis, keepdims=True),
        jnp.sum(energy, axis=axis, keepdims=True),
    )


def lane_value(block, lane):
    return block[..., lane : lane + 1]


def sums_from(own, left, right, far, layers):
    total = (own[...] + far[...]) + (left[...] + right[...])
    spot = layers * NODES
    return (lane_value(total, spot), lane_value(total, spot + 1))


def scalars_block(shape, values, spot=0):
    lane = lanes_of(shape)
    out = jnp.zeros(shape, jnp.float32)
    for i, value in enumerate(values):
        out = jnp.where(lane == spot + i, value, out)
    return out


def shapes_of(field):
    return (
        jax.ShapeDtypeStruct(field.shape, jnp.float32),
        jax.ShapeDtypeStruct(field.shape[1:], jnp.float32),
        pltpu.VMEM((NODES * NODES,) + field.shape[1:], jnp.float32),
    )


def first_image(raw, before, after, shift, geo, layers, table):
    field, small, flux_scratch = shapes_of(raw)
    shape = raw.shape[1:]

    def body(g_ref, k_ref, f_ref, b_ref, a_ref, r_ref, y_ref, first_ref, last_ref, flux):
        join(f_ref, r_ref, b_ref[...], a_ref[...], layers)
        sums = helmholtz(r_ref, y_ref, flux, g_ref, k_ref[...], layers, table)
        first_ref[...], last_ref[...] = rim_messages(lambda n: y_ref[n], layers, shape, sums)

    return call(
        body,
        (),
        held(5),
        held(4),
        [field, field, small, small],
        scratch=[flux_scratch],
        flops=80 * raw.size,
        moved=12 * raw.size,
    )(geo, shift, raw, before, after)


def second_image(start, image, messages, shift, geo, layers, table):
    field, small, flux_scratch = shapes_of(start)
    shape = start.shape[1:]

    def body(g_ref, k_ref, r0, y0, own, left, right, far, *rest):
        w_ref, y_ref, first_ref, last_ref, scalar_ref, r1, flux = rest
        norm, energy = sums_from(own, left, right, far, layers)
        alpha = jnp.broadcast_to(norm / energy, shape)
        join(y0, w_ref, left[...], right[...], layers)

        def move(node):
            r1[node] = r0[node] - alpha * w_ref[node]

        each_node(layers, move)
        sums = helmholtz(r1, y_ref, flux, g_ref, k_ref[...], layers, table)
        first_ref[...], last_ref[...] = rim_messages(lambda n: y_ref[n], layers, shape, sums)
        scalar_ref[...] = scalars_block(shape, (alpha, norm, energy))

    return call(
        body,
        (),
        held(8),
        held(5),
        [field, field, small, small, small],
        scratch=[pltpu.VMEM(start.shape, jnp.float32), flux_scratch],
        flops=80 * start.size,
        moved=16 * start.size,
    )(geo, shift, start, image, *messages)


def third_energy(start, joined, image, messages, scalars, shift, geo, layers, table):
    field, small, flux_scratch = shapes_of(start)
    shape = start.shape[1:]

    def body(g_ref, k_ref, r0, w0, y1, own, left, right, far, old, *rest):
        r2, d2, sums_ref, scalar_ref, w1, flux = rest
        norm, energy = sums_from(own, left, right, far, layers)
        before = old[...]
        alpha = jnp.broadcast_to(lane_value(before, 0), shape)
        ratio = norm / lane_value(before, 1)
        curve = energy - ratio * ratio * lane_value(before, 2)
        step = jnp.broadcast_to(norm / curve, shape)
        beta = jnp.broadcast_to(ratio, shape)
        join(y1, w1, left[...], right[...], layers)

        def move(node):
            w = w0[node]
            start_value = r0[node]
            moved = start_value - alpha * w
            d2[node] = moved + beta * start_value
            r2[node] = moved - step * (w1[node] + beta * w)

        each_node(layers, move)
        sums = helmholtz(r2, None, flux, g_ref, k_ref[...], layers, table, dot_only=True)
        sums_ref[...] = scalars_block(shape, sums, layers * NODES)
        scalar_ref[...] = scalars_block(shape, (alpha, norm, curve, step))

    return call(
        body,
        (),
        held(10),
        held(4),
        [field, field, small, small],
        scratch=[pltpu.VMEM(start.shape, jnp.float32), flux_scratch],
        flops=60 * start.size,
        moved=20 * start.size,
    )(geo, shift, start, joined, image, *messages, scalars)


def finish(start, direction, residual, messages, scalars, layers, place, buffer, total):
    nodes, _, rows, lanes = start.shape
    shape = start.shape[1:]
    square = NODES * NODES

    unit = 2 * nodes

    def body(r0, d2, r2, own, left, right, far, old, *refs):
        o_ref, mid = refs[-2:]
        norm, energy = sums_from(own, left, right, far, layers)
        before = old[...]
        ratio = norm / lane_value(before, 1)
        curve = energy - ratio * ratio * lane_value(before, 2)
        step = norm / curve
        third = jnp.broadcast_to(step, shape)
        second = jnp.broadcast_to(lane_value(before, 3) + step * ratio, shape)
        first = jnp.broadcast_to(lane_value(before, 0), shape)

        def layer(e, carry):
            for n in range(square):
                node = e * square + n
                value = first * r0[node] + second * d2[node] + third * r2[node]
                for i in range(2):
                    mid[i * nodes + n * layers + e] = value[i]
            return carry

        lax.fori_loop(0, layers, layer, 0)

        def write(t, r, tile):
            o_ref[rows_at(r, unit, t), :] = tile

        turn_all(lambda k, t: mid[8 * t + k], write, unit // 8)

    extra = [] if buffer is None else [buffer]
    return call(
        body,
        (1,),
        [whole(start.shape)] * 3
        + [whole(shape)] * 5
        + [pl.BlockSpec(memory_space=pl.ANY)] * len(extra),
        pl.BlockSpec((2 * rows * nodes, lanes), lambda i: (place, 0)),
        jax.ShapeDtypeStruct((total, lanes), jnp.float32),
        scratch=[pltpu.VMEM((unit, rows, lanes), jnp.float32)],
        flops=6 * start.size,
        moved=16 * start.size,
        aliases={8: 0} if extra else None,
    )(start, direction, residual, *messages, scalars, *extra)


def halves(values, shares):
    half = values.shape[-1] // 2
    parts = [jnp.concatenate([p, p], axis=-1) for p in (values[..., :half], values[..., half:])]
    return jnp.stack(parts, axis=2).reshape(values.shape[0], shares, NODES * NODES, 2 * half)


def on_device_paired(*arrays):
    return paired_step(*arrays)


def paired_step(velocity, radial_dx, radial_dy, around_dx, around_dy, jacobian):
    table = derivative_table()
    modes = lax.axis_size("mode")
    mode = lax.axis_index("mode")
    _, local_planes, layers, _, _, lanes = velocity.shape
    planes = local_planes * modes
    pairs = local_planes // 2
    first_plane = mode * local_planes
    square = NODES * NODES
    forward, backward = (jnp.asarray(t) for t in paired_tables(planes))

    rows = velocity.transpose(0, 1, 3, 4, 2, 5).reshape(3, local_planes * square * layers, lanes)
    plain = jnp.stack([radial_dx, radial_dy, around_dx, around_dy]).reshape(
        4, layers, square, lanes
    )
    both = halves(plain, modes)
    here = lax.dynamic_index_in_dim(both, mode, 1, keepdims=False).reshape(4 * square, lanes)
    metrics = geometry(radial_dx, radial_dy, around_dx, around_dy, jacobian)
    geo = jnp.stack(metrics).reshape(4 * layers * square, lanes)
    scaled = halves((metrics[3] * (-1.0 / time_step)).reshape(1, layers, square, lanes), modes)
    flux = (both * scaled).reshape(4 * modes * square, lanes)
    small_flux = flux * time_step
    part = modes * square
    side_flux = jnp.concatenate([small_flux[part : 2 * part], small_flux[3 * part :]])
    scaled = scaled.reshape(modes * square, lanes)
    turned = lax.optimization_barrier(backward).reshape(2, modes, pairs, -1)
    turned = jnp.roll(turned, -mode, axis=1).reshape(backward.shape)
    pair = (first_plane // 2 + jnp.arange(pairs, dtype=jnp.int32)).astype(jnp.float32)
    wave = pair[:, None] * spanwise_wave
    low = (jnp.arange(lanes) < lanes // 2)[None, :]
    waves = jnp.where(low, wave, -wave)
    small_waves = waves * time_step
    shift = plane_shift(first_plane, local_planes, planes).reshape(pairs, 2).T
    shift = jnp.broadcast_to(shift.reshape(2, 2, pairs // 2, 1), (2, 2, pairs // 2, lanes))
    shift = (shift[:, 0], shift[:, 1])

    def exchange(blocks):
        return lax.all_to_all(blocks, "mode", split_axis=0, concat_axis=0, tiled=True)

    some = (NODES // 2 + 1) * NODES
    group = pairs // 2
    first_shape = (4 * square - 2 * some, group, lanes)
    second_shape = (modes, 2 * square, group, lanes)
    strips = list(pack_first(rows, mode, layers, pairs, lanes))
    sent_1, late_2, sent_2, sent_0 = pack_rest(rows, layers, pairs, lanes, some)
    for k in range(1, modes):
        strips[k] = lax.ppermute(strips[k], "mode", [(i, (i + k) % modes) for i in range(modes)])
    sent_1, here, geo, flux, small_flux, side_flux, scaled, waves, small_waves, shift, turned = (
        lax.optimization_barrier(
            (sent_1, here, geo, flux, small_flux, side_flux, scaled, waves, small_waves, shift, turned)
        )
    )
    arrived_1 = exchange(sent_1)
    arrived_2 = exchange(late_2)
    speed_x, slope_0 = to_points(by_source(strips, mode), forward)
    speed_y, slope_1 = to_points(arrived_1, forward)
    speeds = [speed_x, speed_y]
    partial = in_plane(speeds, speeds, here, table)
    rows_early = some // NODES
    speed_z, slope_2, blocks = turn_around(
        arrived_1, NODES, 0, rows_early, partial[0], slope_0, forward, backward, (), None
    )
    home_0 = exchange(blocks)
    speed_z, slope_2, *buffers = turn_around(
        arrived_2,
        0,
        rows_early,
        NODES - rows_early,
        partial[0],
        slope_0,
        forward,
        turned,
        (speed_z, slope_2),
        (first_shape, NODES),
    )
    last = in_plane(speeds, [speed_z], here, table)[0]
    shapes = (first_shape, second_shape)
    buffers = to_planes(partial[1], speed_z, slope_1, turned, mode, 0, shapes, buffers)
    *home_strips, second = to_planes(last, speed_z, slope_2, turned, mode, 1, shapes, buffers)
    for k in range(1, modes):
        home_strips[k] = lax.ppermute(
            home_strips[k], "mode", [(i, (i + k) % modes) for i in range(modes)]
        )
    home_1 = by_source(home_strips, mode)
    home_2 = exchange(second)
    returned = (home_1, home_2)
    base = velocity_part((sent_0, sent_1, sent_2), flux, scaled, waves, table)

    own_rows = local_planes * square * layers

    def read_first(refs, g):
        def read(d, n):
            if n < some:
                return refs[0][d, n]
            a, b = divmod(n - some, NODES)
            return refs[1 + a][d, g * NODES + b]

        return read

    def read_part(refs, i):
        return lambda d, n: refs[0][d, n]

    first_specs = [pl.BlockSpec((modes, some, group, lanes), lambda i: (0, 0, i, 0))] + [
        pl.BlockSpec(
            (modes, 2 * NODES, group, lanes), functools.partial(lambda k, i: (0, k, 0, 0), NODES + k)
        )
        for k in range(NODES - rows_early)
    ]
    part_specs = [pl.BlockSpec((modes, square, group, lanes), lambda i: (0, i, 0, 0))]
    advection = unpack(
        [home_0] + [home_1] * (NODES - rows_early),
        first_specs,
        read_first,
        (0, 1),
        layers,
        None,
        3 * own_rows,
    )
    flat = first_part(base, home_0, home_1, NODES, small_flux, table)

    def solve(place, flat, own_shift, buffer):
        raw, first, last = right_side(
            flat, returned[place], side_flux, scaled, small_waves, table, layers, place
        )
        before, after = swap_rims(first, last)
        start, image, first, last = first_image(raw, before, after, own_shift, geo, layers, table)
        messages = (first,) + swap_rims(first, last) + (opposite(first),)
        joined, image, first, last, scalars = second_image(
            start, image, messages, own_shift, geo, layers, table
        )
        messages = (first,) + swap_rims(first, last) + (opposite(first),)
        residual, direction, sums, scalars = third_energy(
            start, joined, image, messages, scalars, own_shift, geo, layers, table
        )
        messages = (sums,) + swap_rims(sums, sums) + (opposite(sums),)
        return finish(
            start, direction, residual, messages, scalars, layers, place, buffer, own_rows
        )

    pressure = solve(0, flat, shift[0], None)
    advection = unpack(
        [home_1], part_specs, read_part, (2, 2), layers, advection, 3 * own_rows
    )
    flat, pressure, advection, shift = lax.optimization_barrier(
        (flat, pressure, advection, shift)
    )

    def unpack_late(comp, buffer):
        spec = pl.BlockSpec((modes, square, group, lanes), lambda i: (0, comp, 0, 0))
        return unpack(
            [home_2], [spec], read_part, (3 + 2 * comp, 1), layers, buffer, 3 * own_rows, 1
        )

    pressure = solve(1, flat, shift[1], pressure)
    advection = unpack_late(1, unpack_late(0, advection))
    advection = advection.reshape(3, local_planes, NODES, NODES, layers, lanes)
    pressure = pressure.reshape(local_planes, NODES, NODES, layers, lanes)
    return (advection.transpose(0, 1, 4, 2, 3, 5), pressure.transpose(0, 3, 1, 2, 4))


def paired_fits(mesh, shape):
    modes, ring = (mesh.shape["mode"], mesh.shape["elem"])
    _, planes, layers, _, _, columns = shape
    return (
        ring == 4
        and columns == 128 * ring
        and modes == 2 * layers
        and layers % 4 == 0
        and planes == 32 * modes
        and (layers * NODES + 2 <= 128)
    )


def solution(mesh):
    placed = (
        P(None, "mode", None, None, None, "elem"),
        P(None, None, None, "elem"),
        P(None, None, None, "elem"),
        P(None, None, None, "elem"),
        P(None, None, None, "elem"),
        P(None, None, None, "elem"),
    )


    def step(velocity, *rest):
        body = on_device_paired if paired_fits(mesh, velocity.shape) else on_device
        return jax.shard_map(
            body,
            mesh=mesh,
            in_specs=placed,
            out_specs=(
                P(None, "mode", None, None, None, "elem"),
                P("mode", None, None, None, "elem"),
            ),
            check_vma=False,
        )(velocity, *rest)

    return step
```
